32 devices in a mesh: fsdp: 4 (over z), ctx: 2 (over y), tp: 4 (over x, core).
Axes of the slice: x: 2, y: 2, z: 4, core: 2. Of those that a mesh axis runs over, the one named last changes fastest.
Arguments:
- tokens: bfloat16 [8192, 2048], P(('fsdp', 'ctx')), may hold values from -6 to 6
- out_grad: bfloat16 [8192, 2048], P(('fsdp', 'ctx')), may hold values from -6 to 6
- routes: int32 [8192, 6], P(('fsdp', 'ctx')), may hold values from 0 to 15, as said below
- slot_index: int32 [8192, 6], P(('fsdp', 'ctx')), may hold values from 0 to 384, as said below
- prefix: int32 [4], replicated, may hold values from 204 to 1024
- attn_gain: bfloat16 [2048], P(('fsdp', 'ctx')), may hold values from 0.5 to 1.5
- query_weight: bfloat16 [2048, 3072], P(('fsdp', 'ctx'), 'tp'), may hold values from -0.125 to 0.125
- latent_down: bfloat16 [2048, 576], P(('fsdp', 'ctx')), may hold values from -0.125 to 0.125
- latent_gain: bfloat16 [512], P(('fsdp', 'ctx')), may hold values from 0.5 to 1.5
- latent_up: bfloat16 [512, 4096], P(('fsdp', 'ctx'), 'tp'), may hold values from -0.25 to 0.25
- out_weight: bfloat16 [2048, 2048], P('tp', ('fsdp', 'ctx')), may hold values from -2 to 2
- moe_gain: bfloat16 [2048], P(('fsdp', 'ctx')), may hold values from 0.5 to 1.5
- router_weight: bfloat16 [2048, 16], P(('fsdp', 'ctx')), may hold values from -0.0625 to 0.0625
- shared_gate: bfloat16 [2048, 2816], P(('fsdp', 'ctx'), 'tp'), may hold values from -0.125 to 0.125
- shared_up: bfloat16 [2048, 2816], P(('fsdp', 'ctx'), 'tp'), may hold values from -0.125 to 0.125
- shared_down: bfloat16 [2816, 2048], P('tp', ('fsdp', 'ctx')), may hold values from -0.109375 to 0.109375
- expert_gate: bfloat16 [16, 2048, 1408], P(None, ('fsdp', 'ctx'), 'tp'), may hold values from -0.125 to 0.125
- expert_up: bfloat16 [16, 2048, 1408], P(None, ('fsdp', 'ctx'), 'tp'), may hold values from -0.125 to 0.125
- expert_down: bfloat16 [16, 1408, 2048], P(None, 'tp', ('fsdp', 'ctx')), may hold values from -1.25 to 1.25
Outputs:
- output: bfloat16 [8192, 2048], P(('fsdp', 'ctx'))
- token_grad: float32 [8192, 2048], P(('fsdp', 'ctx'))
- attn_gain_grad: float32 [2048], P(('fsdp', 'ctx'))
- query_weight_grad: float32 [2048, 3072], P(('fsdp', 'ctx'), 'tp')
- latent_down_grad: float32 [2048, 576], P(('fsdp', 'ctx'))
- latent_gain_grad: float32 [512], P(('fsdp', 'ctx'))
- latent_up_grad: float32 [512, 4096], P(('fsdp', 'ctx'), 'tp')
- out_weight_grad: float32 [2048, 2048], P('tp', ('fsdp', 'ctx'))
- moe_gain_grad: float32 [2048], P(('fsdp', 'ctx'))
- router_weight_grad: float32 [2048, 16], P(('fsdp', 'ctx'))
- shared_gate_grad: float32 [2048, 2816], P(('fsdp', 'ctx'), 'tp')
- shared_up_grad: float32 [2048, 2816], P(('fsdp', 'ctx'), 'tp')
- shared_down_grad: float32 [2816, 2048], P('tp', ('fsdp', 'ctx'))
- expert_gate_grad: float32 [16, 2048, 1408], P(None, ('fsdp', 'ctx'), 'tp')
- expert_up_grad: float32 [16, 2048, 1408], P(None, ('fsdp', 'ctx'), 'tp')
- expert_down_grad: float32 [16, 1408, 2048], P(None, 'tp', ('fsdp', 'ctx'))
The draws below stay inside these ranges and needn't reach their ends.
Inputs may be any that keep to these rules, and one draw needn't show every extreme that they name: `routes`: each row names 6 different experts; in every aligned block of 1024 rows (the rows of one device) some expert is named by more than 384 rows. `slot_index`: for each row and route, the number of earlier pairs of the same aligned block of 1024 rows (rows in order, routes in order within a row) naming the same expert, or 384 where that number is 384 or more; the value 384 marks a dropped pair.
All inputs are finite; a program needn't handle non-finite values.
Results may differ from the reference program's by a relative error of at most 0.028.
Values may be sent and summed in bfloat16 or wider, within the bound.
A program may use at most 512 MiB of HBM per device.

```python
import math
import jax
import jax.numpy as jnp
from jax import lax

D = 2048
H = 16
NOPE = 128
ROPE = 64
KVR = 512
VDIM = 128
FF = 1408
TOPK = 6
EXPERTS = 16
TOK_DEV = 1024
SFF = 2816
CAP = 384
SEQ = 2048
NSEQ = 4
TOKENS = 8192


def routing_tables(key):
    base = jax.random.fold_in(key, 11)
    key_raw, key_rank, key_hot, key_pick = jax.random.split(base, 4)
    block_count = TOKENS // TOK_DEV
    raw_score = jax.random.randint(key_raw, (block_count, TOK_DEV, EXPERTS), 0, 65536)
    favour = jax.random.permutation(key_rank, EXPERTS).astype(jnp.int32) * 2048
    hot_expert = jax.random.randint(key_hot, (block_count, 1, 1), 0, EXPERTS)
    order_key = jax.random.randint(key_pick, (block_count, TOK_DEV), 0, 65536) * TOK_DEV + jnp.arange(TOK_DEV, dtype=jnp.int32)[None, :]
    order_rank = jnp.argsort(jnp.argsort(order_key, axis=1), axis=1)
    expert_ids = jnp.arange(EXPERTS, dtype=jnp.int32)
    forced = (order_rank <= CAP)[..., None] & (expert_ids[None, None, :] == hot_expert)
    score = (raw_score + favour[None, None, :] + forced.astype(jnp.int32) * 1048576) * EXPERTS + expert_ids[None, None, :]
    unused, route_ids = lax.top_k(score, TOPK)
    route_ids = route_ids.astype(jnp.int32)
    one_hot = (route_ids[..., None] == expert_ids).astype(jnp.int32).reshape(block_count, TOK_DEV * TOPK, EXPERTS)
    earlier = jnp.cumsum(one_hot, axis=1) - one_hot
    rank_in = jnp.sum(earlier * one_hot, axis=-1).reshape(block_count, TOK_DEV, TOPK)
    slot_ids = jnp.minimum(rank_in, CAP)
    return (route_ids.reshape(TOKENS, TOPK), slot_ids.reshape(TOKENS, TOPK).astype(jnp.int32))


def draw_routes(key, part):
    return routing_tables(key)[0]


def draw_slot_index(key, part):
    return routing_tables(key)[1]


def draw_prefix(key, part):
    base = jax.random.fold_in(key, 23)
    key_len, key_first = jax.random.split(base, 2)
    lengths = jax.random.randint(key_len, (NSEQ,), SEQ // 10, SEQ // 2 + 1)
    first_seq = jax.random.randint(key_first, (), 0, NSEQ)
    seq_ids = jnp.arange(NSEQ, dtype=jnp.int32)
    lengths = jnp.where(seq_ids == first_seq, SEQ // 2, lengths)
    lengths = jnp.where(seq_ids == (first_seq + 1) % NSEQ, SEQ // 10, lengths)
    return lengths.astype(jnp.int32)


def shard_levels(own_key, dims, cuts, low, largest):
    factor_of, own = 1.0, jax.random.fold_in(own_key, 6)
    for axis_at, parts in cuts:
        draws = jnp.exp(jax.random.uniform(jax.random.fold_in(own, axis_at), (parts,), jnp.float32, low / len(cuts), largest / len(cuts)))
        factor_of = factor_of * jnp.repeat(draws, dims[axis_at] // parts).reshape([-1 if axis == axis_at else 1 for axis in range(len(dims))])
    return factor_of


def centred(rng, extent, spread, bound, cuts=(), kind=jnp.bfloat16):
    loudness = shard_levels(rng, extent, cuts, -0.22, 0.18) if cuts else 1.0
    entries = jax.random.normal(rng, extent, jnp.float32) * spread * loudness
    return jnp.minimum(jnp.maximum(entries, -bound), bound).astype(kind)


def setup_inputs(seed: int = 0) -> dict:
    seeds = jax.random.split(jax.random.key(seed), 20)
    return {
        "tokens": centred(seeds[0], (TOKENS, D), 1.0, 6.0, ((0, 8),)),
        "out_grad": centred(seeds[1], (TOKENS, D), 1.0, 6.0, ((0, 8),)),
        "routes": draw_routes(jax.random.fold_in(seeds[19], 71), 0),
        "slot_index": draw_slot_index(jax.random.fold_in(seeds[19], 71), 0),
        "prefix": draw_prefix(jax.random.fold_in(seeds[19], 71), 0),
        "attn_gain": jnp.clip(1.0 + 0.1 * jax.random.normal(seeds[5], (D,), jnp.float32), 0.5, 1.5).astype(jnp.bfloat16),
        "query_weight": centred(seeds[6], (D, H * (NOPE + ROPE)), D ** -0.5, 0.125, ((0, 8), (1, 4))),
        "latent_down": centred(seeds[7], (D, KVR + ROPE), D ** -0.5, 0.125, ((0, 8),)),
        "latent_gain": jnp.clip(1.0 + 0.1 * jax.random.normal(seeds[8], (KVR,), jnp.float32), 0.5, 1.5).astype(jnp.bfloat16),
        "latent_up": centred(seeds[9], (KVR, H * (NOPE + VDIM)), KVR ** -0.5, 0.25, ((0, 8), (1, 4))),
        "out_weight": centred(seeds[10], (H * VDIM, D), (max(H * VDIM // 256, 1)) ** -0.5, 2.0, ((0, 4), (1, 8))),
        "moe_gain": jnp.clip(1.0 + 0.1 * jax.random.normal(seeds[11], (D,), jnp.float32), 0.5, 1.5).astype(jnp.bfloat16),
        "router_weight": centred(seeds[12], (D, EXPERTS), (4 * D) ** -0.5, 0.0625, ((0, 8),)),
        "shared_gate": centred(seeds[13], (D, SFF), D ** -0.5, 0.125, ((0, 8), (1, 4))),
        "shared_up": centred(seeds[14], (D, SFF), D ** -0.5, 0.125, ((0, 8), (1, 4))),
        "shared_down": centred(seeds[15], (SFF, D), SFF ** -0.5, 0.109375, ((0, 4), (1, 8))),
        "expert_gate": centred(seeds[16], (EXPERTS, D, FF), D ** -0.5, 0.125, ((1, 8), (2, 4))),
        "expert_up": centred(seeds[17], (EXPERTS, D, FF), D ** -0.5, 0.125, ((1, 8), (2, 4))),
        "expert_down": centred(seeds[18], (EXPERTS, FF, D), (max(FF // 64, 1)) ** -0.5, 1.25, ((1, 4), (2, 8))),
    }


EPSILON = 1e-06
THETA_BASE = 10000.0
HIGHEST = lax.Precision.HIGHEST

@jax.custom_vjp
def low(v):
    return lax.optimization_barrier(v.astype(jnp.bfloat16)).astype(jnp.float32)

@jax.custom_vjp
def low_back(v):
    return v

def low_keep(v):
    return (low(v), None)

def low_pass(kept, grad):
    return (grad,)

def back_keep(v):
    return (v, None)

def back_low(kept, grad):
    return (low(grad),)
low.defvjp(low_keep, low_pass)
low_back.defvjp(back_keep, back_low)

def matmul(left, right):
    return jnp.dot(left, right, precision=HIGHEST)

def rms_scale(values):
    return lax.rsqrt(lax.optimization_barrier(jnp.mean(values * values, axis=-1, keepdims=True)) + EPSILON)

def rotation_tables(positions, half_width):
    freq_table = jnp.exp(jnp.arange(half_width, dtype=jnp.float32) * (-math.log(THETA_BASE) / half_width))
    angle_table = positions.astype(jnp.float32)[:, None] * freq_table[None, :]
    return (jnp.cos(angle_table), jnp.sin(angle_table))

def rotate(values, cos_table, sin_table):
    half_width = values.shape[-1] // 2
    first_half = values[..., :half_width]
    second_half = values[..., half_width:]
    return jnp.concatenate([first_half * cos_table - second_half * sin_table, second_half * cos_table + first_half * sin_table], axis=-1)

def layer(hidden, weights, route_ids, slot_ids, prefix_len):
    attn_gain, query_weight, latent_down, latent_gain, latent_up, out_weight, moe_gain, router_weight, shared_gate, shared_up, shared_down, expert_gate, expert_up, expert_down = weights
    length = hidden.shape[0]
    positions = jnp.arange(length, dtype=jnp.int32)
    cos_table, sin_table = rotation_tables(positions, ROPE // 2)
    normed_in = low(hidden * rms_scale(hidden) * attn_gain)
    query_raw = low_back(matmul(normed_in, query_weight)).reshape(length, H, NOPE + ROPE)
    query_in = low(jnp.concatenate([query_raw[..., :NOPE], rotate(query_raw[..., NOPE:], cos_table[:, None], sin_table[:, None])], axis=-1))
    latent_raw = low_back(matmul(normed_in, latent_down))
    latent_part = latent_raw[:, :KVR]
    latent = low(latent_part * rms_scale(latent_part) * latent_gain)
    key_rope = low(rotate(latent_raw[:, KVR:], cos_table, sin_table))
    key_value = low(low_back(matmul(latent, latent_up))).reshape(length, H, NOPE + VDIM)
    key_nope = key_value[..., :NOPE]
    value_part = key_value[..., NOPE:]
    block_rows = min(512, length)
    score_scale = (NOPE + ROPE) ** (-0.5)

    def attend(block_index):
        first_row = block_index * block_rows
        query_block = lax.dynamic_slice_in_dim(query_in, first_row, block_rows, 0)
        limit_row = jnp.maximum(first_row + jnp.arange(block_rows, dtype=jnp.int32), prefix_len - 1)
        scores = jnp.einsum('qhd,khd->hqk', query_block[..., :NOPE], key_nope, precision=HIGHEST)
        scores = scores + jnp.einsum('qhd,kd->hqk', query_block[..., NOPE:], key_rope, precision=HIGHEST)
        scores = low_back(scores * score_scale)
        allowed = positions[None, :] <= limit_row[:, None]
        scores = jnp.where(allowed[None], scores, -1e+30)
        top_score = lax.optimization_barrier(jnp.max(scores, axis=-1, keepdims=True))
        exponent = jnp.exp(scores - top_score)
        weights_soft = exponent / lax.optimization_barrier(jnp.sum(exponent, axis=-1, keepdims=True))
        return jnp.einsum('hqk,khd->qhd', low(weights_soft), value_part, precision=HIGHEST)
    attended = lax.map(jax.checkpoint(attend), jnp.arange(length // block_rows, dtype=jnp.int32))
    attended = low(low_back(attended.reshape(length, H * VDIM)))
    attn_out = low_back(matmul(attended, out_weight))
    residual = hidden + attn_out
    normed_mid = low(residual * rms_scale(residual) * moe_gain)
    logits = low_back(matmul(normed_mid, router_weight))
    router_prob = jax.nn.softmax(logits, axis=-1)
    gates = jnp.take_along_axis(router_prob, route_ids, axis=1)
    gate_pre = low_back(matmul(normed_mid, shared_gate))
    up_pre = low_back(matmul(normed_mid, shared_up))
    shared_act = low(jax.nn.silu(gate_pre) * up_pre)
    shared_out = matmul(shared_act, shared_down)
    block_count = length // TOK_DEV
    block_ids = (positions // TOK_DEV)[:, None]
    slot_pos = jnp.where(slot_ids < CAP, (block_ids * EXPERTS + route_ids) * CAP + slot_ids, block_count * EXPERTS * CAP)
    owners = jnp.full((block_count * EXPERTS * CAP,), length, jnp.int32).at[slot_pos.reshape(-1)].set(jnp.repeat(positions, TOPK), mode='drop')
    capacity_slot_rows = jnp.take(normed_mid, owners, axis=0, mode='fill', fill_value=0.0).reshape(block_count, EXPERTS, CAP, D)
    expert_gpre = low_back(jnp.einsum('becd,edf->becf', capacity_slot_rows, expert_gate, precision=HIGHEST))
    expert_upre = low_back(jnp.einsum('becd,edf->becf', capacity_slot_rows, expert_up, precision=HIGHEST))
    expert_act = low(jax.nn.silu(expert_gpre) * expert_upre)
    expert_out = low_back(jnp.einsum('becf,efd->becd', expert_act, expert_down, precision=HIGHEST)).reshape(block_count * EXPERTS * CAP, D)
    picked = jnp.take(expert_out, slot_pos, axis=0, mode='fill', fill_value=0.0)
    routed = lax.optimization_barrier(jnp.sum(gates[..., None] * picked, axis=1))
    return residual + shared_out + routed

def reference(tokens, out_grad, routes, slot_index, prefix, attn_gain, query_weight, latent_down, latent_gain, latent_up, out_weight, moe_gain, router_weight, shared_gate, shared_up, shared_down, expert_gate, expert_up, expert_down):
    weights = tuple((weight_arg.astype(jnp.float32) for weight_arg in (attn_gain, query_weight, latent_down, latent_gain, latent_up, out_weight, moe_gain, router_weight, shared_gate, shared_up, shared_down, expert_gate, expert_up, expert_down)))
    hidden_all = tokens.astype(jnp.float32).reshape(NSEQ, SEQ, D)
    grad_all = out_grad.astype(jnp.float32).reshape(NSEQ, SEQ, D)
    route_all = routes.reshape(NSEQ, SEQ, TOPK)
    slot_all = slot_index.reshape(NSEQ, SEQ, TOPK)

    def one_sequence(running, items):
        hidden_seq, grad_seq, route_seq, slot_seq, prefix_len = items

        def run_layer(hidden_arg, *weight_args):
            return layer(hidden_arg, weight_args, route_seq, slot_seq, prefix_len)
        result, pull_back = jax.vjp(run_layer, hidden_seq, *weights)
        grads = pull_back(grad_seq)
        updated = tuple((left + right for left, right in zip(running, grads[1:])))
        return (updated, (result.astype(jnp.bfloat16), grads[0]))
    zero_grads = tuple((jnp.zeros_like(weight_arg) for weight_arg in weights))
    totals, (outputs, token_grads) = lax.scan(one_sequence, zero_grads, (hidden_all, grad_all, route_all, slot_all, prefix))
    return (outputs.reshape(TOKENS, D), token_grads.reshape(TOKENS, D), totals[0], totals[1], totals[2], totals[3], totals[4], totals[5], totals[6], totals[7], totals[8], totals[9], totals[10], totals[11], totals[12], totals[13])
```

```python
import functools
import math

import jax
import jax.numpy as jnp
from jax import lax
from jax.experimental import pallas as pl
from jax.experimental.pallas import tpu as pltpu
from jax.sharding import Mesh
from jax.sharding import PartitionSpec as P

NOPE = 128
ROPE = 64
KVR = 512
VDIM = 128
HEAD = 256

EPSILON = 1e-06
THETA_BASE = 10000.0
F32 = jnp.float32
BF16 = jnp.bfloat16
MESH_ID = pl.DeviceIdType.MESH

ROWS = ("fo", "fi", "ctx")
TP = ("tpx", "tpc")
PLANE = ("ctx", "tpx", "tpc")
CHIPS = ("fi", "ctx", "tpx")


def rotation_tables(positions, half_width):
    freq_table = jnp.exp(jnp.arange(half_width, dtype=F32) * (-math.log(THETA_BASE) / half_width))
    angle_table = positions.astype(F32)[:, None] * freq_table[None, :]
    return (jnp.cos(angle_table), jnp.sin(angle_table))


def rotate(values, cos_table, sin_table):
    half_width = values.shape[-1] // 2
    first_half = values[..., :half_width]
    second_half = values[..., half_width:]
    return jnp.concatenate(
        [
            first_half * cos_table - second_half * sin_table,
            second_half * cos_table + first_half * sin_table,
        ],
        axis=-1,
    )


def silu_parts(values):
    sigma = jax.nn.sigmoid(values)
    return (values * sigma, sigma * (1.0 + values * (1.0 - sigma)))


def rms_scale(values):
    return lax.rsqrt(jnp.mean(values * values, axis=-1, keepdims=True) + EPSILON)


def norm_back(grad_normed, normed, scale_rows):
    return scale_rows * (
        grad_normed - normed * jnp.mean(grad_normed * normed, axis=-1, keepdims=True)
    )


def dot(left, right):
    return jnp.dot(left, right, preferred_element_type=F32)


def dot_nt(left, right):
    return lax.dot_general(left, right, (((1,), (1,)), ((), ())), preferred_element_type=F32)


def dot_tn(left, right):
    return lax.dot_general(left, right, (((0,), (0,)), ((), ())), preferred_element_type=F32)


def ein(spec, left, right):
    return jnp.einsum(spec, left, right, preferred_element_type=F32)


def plane_place(sizes):
    tpx_n, tpc_n = sizes["tpx"], sizes["tpc"]
    fo, z, y, x, c = (lax.axis_index(name) for name in ("fo", "fi", "ctx", "tpx", "tpc"))
    own = (y * tpx_n + x) * tpc_n + c

    def device(index, z_at=None):
        return (
            fo,
            z if z_at is None else z_at,
            index // (tpx_n * tpc_n),
            lax.rem(index // tpc_n, tpx_n),
            lax.rem(index, tpc_n),
        )

    return z, y, x, c, own, device


def greet_plane(sizes, z, own, device):
    fi_n = sizes["fi"]
    plane_n = sizes["ctx"] * sizes["tpx"] * sizes["tpc"]
    barrier = pltpu.get_barrier_semaphore()
    for step in range(1, plane_n):
        pl.semaphore_signal(
            barrier,
            inc=1,
            device_id=device(lax.rem(own + step, plane_n)),
            device_id_type=MESH_ID,
        )
    for near in (-1, 1):

        @pl.when((z + near >= 0) & (z + near < fi_n))
        def _():
            pl.semaphore_signal(
                barrier, inc=1, device_id=device(own, z + near), device_id_type=MESH_ID
            )

    sides = (z > 0).astype(jnp.int32) + (z < fi_n - 1).astype(jnp.int32)
    pl.semaphore_wait(barrier, plane_n - 1 + sides)


def dispatch_body(
    sizes,
    slots_ref,
    rows_ref,
    out_ref,
    held,
    picked,
    own_sem,
    line_send,
    line_recv,
    plane_send,
    plane_recv,
):
    fi_n, tpx_n, tpc_n = sizes["fi"], sizes["tpx"], sizes["tpc"]
    plane_n = sizes["ctx"] * tpx_n * tpc_n
    chips = sizes["ctx"] * tpx_n
    z_part = fi_n // tpc_n
    capacity, quarter = picked.shape[2:]
    tokens = held.shape[1]
    z, y, x, c, own, device = plane_place(sizes)
    greet_plane(sizes, z, own, device)
    columns = pl.ds(pl.multiple_of((x * tpc_n + c) * quarter, quarter), quarter)

    load = pltpu.make_async_copy(rows_ref, held.at[z], own_sem)
    load.start()
    load.wait()

    def line(side, step):
        block = z - step if side == 0 else z + step
        to = z + 1 if side == 0 else z - 1
        return block, to, pltpu.make_async_remote_copy(
            src_ref=held.at[block],
            dst_ref=held.at[block],
            send_sem=line_send.at[side, step],
            recv_sem=line_recv.at[side, step],
            device_id=device(own, to),
            device_id_type=MESH_ID,
        )

    def sends(side, step):
        block = z - step if side == 0 else z + step
        to = z + 1 if side == 0 else z - 1
        return (block >= 0) & (block < fi_n) & (to >= 0) & (to < fi_n)

    def plane_copy(block, chip):
        target = chip * tpc_n + block // z_part
        at = lax.rem(block, z_part)
        return pltpu.make_async_remote_copy(
            src_ref=picked.at[block, chip],
            dst_ref=out_ref.at[at, y, :, columns],
            send_sem=plane_send.at[block, chip],
            recv_sem=plane_recv.at[own, at],
            device_id=device(target),
            device_id_type=MESH_ID,
        )

    def keep_copy(block, chip):
        return pltpu.make_async_copy(
            picked.at[block, chip],
            out_ref.at[lax.rem(block, z_part), y, :, columns],
            plane_send.at[block, chip],
        )

    def at_home(block, chip):
        return chip * tpc_n + block // z_part == own

    def pick(block):
        def one(chip, carry):
            wanted = slots_ref[block, pl.ds(chip, 1), :]
            rank = lax.broadcasted_iota(jnp.int32, (capacity, tokens), 0)
            hits = jnp.where(rank == wanted, 1.0, 0.0).astype(BF16)
            picked[block, chip] = jnp.dot(
                hits, held[block], preferred_element_type=F32
            ).astype(BF16)

            @pl.when(at_home(block, chip))
            def _():
                keep_copy(block, chip).start()

            @pl.when(jnp.logical_not(at_home(block, chip)))
            def _():
                plane_copy(block, chip).start()

            return carry

        lax.fori_loop(0, chips, one, 0)

    for step in range(fi_n):
        for side in (0, 1):
            if step < fi_n - 1:

                @pl.when(sends(side, step))
                def _():
                    line(side, step)[2].start()

        if step == 0:
            pick(z)
        else:
            for side in (0, 1):
                block = z - step if side == 0 else z + step

                @pl.when((block >= 0) & (block < fi_n))
                def _():
                    pick(block)

        if step < fi_n - 1:
            for side in (0, 1):
                block = z - 1 - step if side == 0 else z + 1 + step

                @pl.when((block >= 0) & (block < fi_n))
                def _():
                    pltpu.make_async_remote_copy(
                        src_ref=held.at[block],
                        dst_ref=held.at[block],
                        send_sem=line_send.at[side, step],
                        recv_sem=line_recv.at[side, step],
                        device_id=device(own, z),
                        device_id_type=MESH_ID,
                    ).wait_recv()

    for step in range(fi_n - 1):
        for side in (0, 1):

            @pl.when(sends(side, step))
            def _():
                line(side, step)[2].wait_send()

    def settle(index, carry):
        block, chip = index // chips, lax.rem(index, chips)

        @pl.when(at_home(block, chip))
        def _():
            keep_copy(block, chip).wait()

        @pl.when(jnp.logical_not(at_home(block, chip)))
        def _():
            plane_copy(block, chip).wait_send()

        return carry

    lax.fori_loop(0, fi_n * chips, settle, 0)

    def arrive(index, carry):
        source, at = index // z_part, lax.rem(index, z_part)

        @pl.when(source != own)
        def _():
            pltpu.make_async_remote_copy(
                src_ref=picked.at[0, 0],
                dst_ref=out_ref.at[at, y, :, columns],
                send_sem=plane_send.at[0, 0],
                recv_sem=plane_recv.at[source, at],
                device_id=device(own),
                device_id_type=MESH_ID,
            ).wait_recv()

        return carry

    lax.fori_loop(0, plane_n * z_part, arrive, 0)


def dispatch_rows(sizes, part_rows, plane_slots, capacity, collective_id):
    tokens, quarter = part_rows.shape
    fi_n, ctx_n, tpx_n, tpc_n = (sizes[n] for n in ("fi", "ctx", "tpx", "tpc"))
    z_part, plane_n, chips = fi_n // tpc_n, ctx_n * tpx_n * tpc_n, ctx_n * tpx_n
    return pl.pallas_call(
        functools.partial(dispatch_body, sizes),
        out_shape=jax.ShapeDtypeStruct(
            (z_part, ctx_n, capacity, quarter * tpx_n * tpc_n), BF16
        ),
        in_specs=[
            pl.BlockSpec(memory_space=pltpu.VMEM),
            pl.BlockSpec(memory_space=pl.ANY),
        ],
        out_specs=pl.BlockSpec(memory_space=pl.ANY),
        scratch_shapes=[
            pltpu.VMEM((fi_n, tokens, quarter), BF16),
            pltpu.VMEM((fi_n, chips, capacity, quarter), BF16),
            pltpu.SemaphoreType.DMA,
            pltpu.SemaphoreType.DMA((2, fi_n)),
            pltpu.SemaphoreType.DMA((2, fi_n)),
            pltpu.SemaphoreType.DMA((fi_n, chips)),
            pltpu.SemaphoreType.DMA((plane_n, z_part)),
        ],
        compiler_params=pltpu.CompilerParams(
            collective_id=collective_id, has_side_effects=True, vmem_limit_bytes=40 << 20
        ),
        cost_estimate=pl.CostEstimate(
            flops=2 * fi_n * chips * capacity * tokens * quarter,
            bytes_accessed=100_000_000,
            transcendentals=0,
        ),
        name="dispatch",
    )(plane_slots, part_rows)


def give_back_body(
    sizes,
    slots_ref,
    rows_ref,
    out_ref,
    got,
    total,
    going,
    coming,
    plane_send,
    plane_recv,
    line_send,
    line_recv,
):
    fi_n, tpx_n, tpc_n = sizes["fi"], sizes["tpx"], sizes["tpc"]
    plane_n = sizes["ctx"] * tpx_n * tpc_n
    chips = sizes["ctx"] * tpx_n
    z_part = fi_n // tpc_n
    capacity, quarter = got.shape[2:]
    tokens = total.shape[0]
    z, y, x, c, own, device = plane_place(sizes)
    greet_plane(sizes, z, own, device)
    tile = min(256, tokens)

    def piece(target, at):
        side = lax.rem(target, tpx_n * tpc_n)
        return rows_ref.at[
            at,
            target // (tpx_n * tpc_n),
            :,
            pl.ds(pl.multiple_of(side * quarter, quarter), quarter),
        ]

    def plane_copy(target, at):
        return pltpu.make_async_remote_copy(
            src_ref=piece(target, at),
            dst_ref=got.at[c * z_part + at, own // tpc_n],
            send_sem=plane_send.at[target, at],
            recv_sem=plane_recv.at[own, at],
            device_id=device(target),
            device_id_type=MESH_ID,
        )

    def keep_copy(at):
        return pltpu.make_async_copy(
            piece(own, at), got.at[c * z_part + at, own // tpc_n], plane_recv.at[own, at]
        )

    far_first = z < fi_n // 2
    for turn in range(z_part):
        at = jnp.where(far_first, z_part - 1 - turn, turn)

        def one(step, carry):
            plane_copy(lax.rem(own + step, plane_n), at).start()
            return carry

        keep_copy(at).start()
        lax.fori_loop(1, plane_n, one, 0)

    def gathered(block):
        def one(chip, carry):
            source, at = chip * tpc_n + block // z_part, lax.rem(block, z_part)

            @pl.when(source == own)
            def _():
                keep_copy(at).wait()

            @pl.when(source != own)
            def _():
                pltpu.make_async_remote_copy(
                    src_ref=got.at[block, chip],
                    dst_ref=got.at[block, chip],
                    send_sem=plane_send.at[own, at],
                    recv_sem=plane_recv.at[source, at],
                    device_id=device(own),
                    device_id_type=MESH_ID,
                ).wait_recv()

            return carry

        lax.fori_loop(0, chips, one, 0)

        def rows(step, carry):
            first = pl.multiple_of(step * tile, tile)
            spots = slots_ref[block, pl.ds(first, tile), :]
            rank = lax.broadcasted_iota(jnp.int32, (tile, capacity), 1)
            summed = jnp.zeros((tile, quarter), F32)
            for chip in range(chips):
                hits = jnp.where(rank == spots[:, chip : chip + 1], 1.0, 0.0).astype(BF16)
                summed = summed + jnp.dot(hits, got[block, chip], preferred_element_type=F32)
            total[pl.ds(first, tile), :] = summed
            return carry

        lax.fori_loop(0, tokens // tile, rows, 0)

    def line(side, target):
        return pltpu.make_async_remote_copy(
            src_ref=going.at[target],
            dst_ref=coming.at[side, target],
            send_sem=line_send.at[side, target],
            recv_sem=line_recv.at[side, target],
            device_id=device(own, z + 1 if side == 0 else z - 1),
            device_id_type=MESH_ID,
        )

    def came(side, target):
        pltpu.make_async_remote_copy(
            src_ref=going.at[target],
            dst_ref=coming.at[side, target],
            send_sem=line_send.at[side, target],
            recv_sem=line_recv.at[side, target],
            device_id=device(own, z),
            device_id_type=MESH_ID,
        ).wait_recv()

    for step in range(fi_n - 1):
        for side in (0, 1):
            target = fi_n - 1 - step if side == 0 else step
            passes = (z < target) if side == 0 else (z > target)
            inner = (z > 0) if side == 0 else (z < fi_n - 1)

            @pl.when(passes)
            def _():
                gathered(target)

                @pl.when(inner)
                def _():
                    came(side, target)
                    going[target] = (total[...] + coming[side, target].astype(F32)).astype(BF16)

                @pl.when(jnp.logical_not(inner))
                def _():
                    going[target] = total[...].astype(BF16)

                line(side, target).start()

    gathered(z)
    for side in (0, 1):

        @pl.when((z > 0) if side == 0 else (z < fi_n - 1))
        def _():
            came(side, z)
            total[...] += coming[side, z].astype(F32)

    out_ref[...] = total[...]

    for target in range(fi_n):
        for side in (0, 1):

            @pl.when((z < target) if side == 0 else (z > target))
            def _():
                line(side, target).wait_send()

    def settle(index, carry):
        target, at = index // z_part, lax.rem(index, z_part)

        @pl.when(target != own)
        def _():
            plane_copy(target, at).wait_send()

        return carry

    lax.fori_loop(0, plane_n * z_part, settle, 0)


def give_back_rows(sizes, rows, token_slots, collective_id):
    fi_n, ctx_n, tpx_n, tpc_n = (sizes[n] for n in ("fi", "ctx", "tpx", "tpc"))
    z_part, plane_n, chips = fi_n // tpc_n, ctx_n * tpx_n * tpc_n, ctx_n * tpx_n
    capacity, width = rows.shape[2:]
    quarter = width // (tpx_n * tpc_n)
    tokens = token_slots.shape[1]
    return pl.pallas_call(
        functools.partial(give_back_body, sizes),
        out_shape=jax.ShapeDtypeStruct((tokens, quarter), F32),
        in_specs=[
            pl.BlockSpec(memory_space=pltpu.VMEM),
            pl.BlockSpec(memory_space=pl.ANY),
        ],
        out_specs=pl.BlockSpec(memory_space=pltpu.VMEM),
        scratch_shapes=[
            pltpu.VMEM((fi_n, chips, capacity, quarter), BF16),
            pltpu.VMEM((tokens, quarter), F32),
            pltpu.VMEM((fi_n, tokens, quarter), BF16),
            pltpu.VMEM((2, fi_n, tokens, quarter), BF16),
            pltpu.SemaphoreType.DMA((plane_n, z_part)),
            pltpu.SemaphoreType.DMA((plane_n, z_part)),
            pltpu.SemaphoreType.DMA((2, fi_n)),
            pltpu.SemaphoreType.DMA((2, fi_n)),
        ],
        compiler_params=pltpu.CompilerParams(
            collective_id=collective_id, has_side_effects=True, vmem_limit_bytes=48 << 20
        ),
        cost_estimate=pl.CostEstimate(
            flops=2 * fi_n * chips * capacity * tokens * quarter,
            bytes_accessed=100_000_000,
            transcendentals=0,
        ),
        name="give_back",
    )(token_slots, rows)


def attend_body(place_ref, q_ref, kv_ref, rope_ref, out_ref, log_ref):
    block_rows, key_count = q_ref.shape[0], kv_ref.shape[0]
    first = place_ref[0] + pl.program_id(1) * block_rows
    keys = jnp.concatenate([kv_ref[:, :NOPE], rope_ref[...]], axis=1)
    scores = dot_nt(q_ref[...], keys)
    row = first + lax.broadcasted_iota(jnp.int32, (block_rows, 1), 0)
    limit = jnp.maximum(row, place_ref[1] - 1)
    key = lax.broadcasted_iota(jnp.int32, (block_rows, key_count), 1)
    scores = jnp.where(key <= limit, scores, -1e30)
    top = jnp.max(scores, axis=1, keepdims=True)
    exponent = jnp.exp(scores - top)
    row_total = jnp.sum(exponent, axis=1, keepdims=True)
    summed = jnp.dot(exponent.astype(BF16), kv_ref[:, NOPE:], preferred_element_type=F32)
    out_ref[...] = (summed / row_total).astype(BF16)
    log_total = jnp.broadcast_to(top + jnp.log(row_total), (block_rows, 128))
    log_ref[0] = log_total.T[:1]

def attend(place, query, key_value, rope, block_rows):
    rows, key_count = query.shape[0], key_value.shape[0]
    heads = query.shape[1] // HEAD
    return pl.pallas_call(
        attend_body,
        out_shape=(jax.ShapeDtypeStruct((rows, heads * VDIM), BF16), jax.ShapeDtypeStruct((heads, 1, rows), F32)),
        grid_spec=pltpu.PrefetchScalarGridSpec(
            num_scalar_prefetch=1,
            grid=(heads, rows // block_rows),
            in_specs=[
                pl.BlockSpec((block_rows, HEAD), lambda h, i, s: (i, h)),
                pl.BlockSpec((key_count, HEAD), lambda h, i, s: (0, h)),
                pl.BlockSpec((key_count, NOPE), lambda h, i, s: (0, 0)),
            ],
            out_specs=[
                pl.BlockSpec((block_rows, VDIM), lambda h, i, s: (i, h)),
                pl.BlockSpec((1, 1, block_rows), lambda h, i, s: (h, 0, i)),
            ],
        ),
        compiler_params=pltpu.CompilerParams(vmem_limit_bytes=48 << 20),
        cost_estimate=pl.CostEstimate(flops=4 * rows * key_count * heads * HEAD, bytes_accessed=20_000_000, transcendentals=rows * key_count * heads),
        name="attend",
    )(place, query, key_value, rope)

def attend_back_body(place_ref, q_ref, kv_ref, rope_ref, dout_ref, log_ref, table_ref, dq_ref, dkv_ref, drope_ref, keys_acc, values_acc):
    block_rows, key_count = q_ref.shape[0], kv_ref.shape[0]
    head, step = pl.program_id(0), pl.program_id(1)
    first = place_ref[0] + step * block_rows
    keys = jnp.concatenate([kv_ref[:, :NOPE], rope_ref[...]], axis=1)
    scores = dot_nt(keys, q_ref[...])
    row = first + lax.broadcasted_iota(jnp.int32, (1, block_rows), 1)
    limit = jnp.maximum(row, place_ref[1] - 1)
    key = lax.broadcasted_iota(jnp.int32, (key_count, block_rows), 0)
    soft = jnp.exp(jnp.where(key <= limit, scores, -1e30) - log_ref[0])
    soft_grad = dot_nt(kv_ref[:, NOPE:], dout_ref[...])
    mean = jnp.sum(soft * soft_grad, axis=0, keepdims=True)
    score_grad = (soft * (soft_grad - mean)).astype(BF16)
    values = jnp.dot(soft.astype(BF16), dout_ref[...], preferred_element_type=F32)
    keys_grad = jnp.dot(score_grad, q_ref[...], preferred_element_type=F32)
    dq_ref[...] = (dot_tn(score_grad, keys) * table_ref[...]).astype(BF16)

    @pl.when(step == 0)
    def _():
        keys_acc[...] = keys_grad
        values_acc[...] = values

    @pl.when(step > 0)
    def _():
        keys_acc[...] += keys_grad
        values_acc[...] += values

    @pl.when(step == pl.num_programs(1) - 1)
    def _():
        dkv_ref[...] = jnp.concatenate([keys_acc[:, :NOPE], values_acc[...]], axis=1).astype(BF16)

        @pl.when(head == 0)
        def _():
            drope_ref[...] = keys_acc[:, NOPE:]

        @pl.when(head > 0)
        def _():
            drope_ref[...] += keys_acc[:, NOPE:]

def attend_back(place, query, key_value, rope, dout, log_total, table, block_rows):
    rows, key_count = query.shape[0], key_value.shape[0]
    heads = query.shape[1] // HEAD
    return pl.pallas_call(
        attend_back_body,
        out_shape=(jax.ShapeDtypeStruct((rows, heads * HEAD), BF16), jax.ShapeDtypeStruct((key_count, heads * HEAD), BF16), jax.ShapeDtypeStruct((key_count, NOPE), F32)),
        grid_spec=pltpu.PrefetchScalarGridSpec(
            num_scalar_prefetch=1,
            grid=(heads, rows // block_rows),
            in_specs=[
                pl.BlockSpec((block_rows, HEAD), lambda h, i, s: (i, h)),
                pl.BlockSpec((key_count, HEAD), lambda h, i, s: (0, h)),
                pl.BlockSpec((key_count, NOPE), lambda h, i, s: (0, 0)),
                pl.BlockSpec((block_rows, VDIM), lambda h, i, s: (i, h)),
                pl.BlockSpec((1, 1, block_rows), lambda h, i, s: (h, 0, i)),
                pl.BlockSpec((block_rows, HEAD), lambda h, i, s: (i, 0)),
            ],
            out_specs=[
                pl.BlockSpec((block_rows, HEAD), lambda h, i, s: (i, h)),
                pl.BlockSpec((key_count, HEAD), lambda h, i, s: (0, h)),
                pl.BlockSpec((key_count, NOPE), lambda h, i, s: (0, 0)),
            ],
            scratch_shapes=[pltpu.VMEM((key_count, HEAD), F32), pltpu.VMEM((key_count, VDIM), F32)],
        ),
        compiler_params=pltpu.CompilerParams(vmem_limit_bytes=56 << 20),
        cost_estimate=pl.CostEstimate(flops=10 * rows * key_count * heads * HEAD, bytes_accessed=40_000_000, transcendentals=rows * key_count * heads),
        name="attend_back",
    )(place, query, key_value, rope, dout, log_total, table)


def build(sizes):
    fo_n, fi_n, ctx_n, tpx_n, tpc_n = (sizes[name] for name in ("fo", "fi", "ctx", "tpx", "tpc"))
    tp_n = tpx_n * tpc_n
    row_shards = fo_n * fi_n * ctx_n
    plane_experts = ctx_n * tpx_n
    z_part = fi_n // tpc_n

    def expert_weights(gate, up, down):
        local = jnp.stack([gate.transpose(0, 2, 1), up.transpose(0, 2, 1), down], axis=1)
        if fo_n > 1:
            local = lax.all_gather(local, "fo", axis=0)
        else:
            local = local[None]
        got = lax.all_to_all(local, CHIPS, split_axis=1, concat_axis=1, tiled=True)
        got = lax.all_gather(got, "tpc", axis=0)
        a, b = got.shape[-2:]
        got = got.reshape(tpc_n, fo_n, fi_n, ctx_n, tpx_n, 3, a, b)
        return got.transpose(5, 4, 0, 6, 1, 2, 3, 7).reshape(3, tp_n * a, row_shards * b)

    def split_expert_grads(grads):
        a, b = grads[0].shape[0] // tp_n, grads[0].shape[1] // row_shards
        parts = jnp.stack(
            [
                grad.astype(BF16)
                .reshape(tpx_n, tpc_n, a, fo_n, fi_n, ctx_n, b)
                .transpose(1, 3, 4, 5, 0, 2, 6)
                .reshape(tpc_n, fo_n, fi_n * ctx_n * tpx_n, a, b)
                for grad in grads
            ],
            axis=3,
        )
        return lax.psum_scatter(parts, "tpc", scatter_dimension=0, tiled=True)[0]

    def own_expert_grads(mine):
        got = lax.all_to_all(mine, CHIPS, split_axis=1, concat_axis=1, tiled=True)
        if fo_n > 1:
            got = lax.psum_scatter(got, "fo", scatter_dimension=0, tiled=True)
        got = got[0].astype(F32)
        return (got[:, 0].transpose(0, 2, 1), got[:, 1].transpose(0, 2, 1), got[:, 2])

    def shards(
        tokens,
        out_grad,
        routes,
        slot_index,
        prefix,
        attn_gain,
        query_weight,
        latent_down,
        latent_gain,
        latent_up,
        out_weight,
        moe_gain,
        router_weight,
        shared_gate,
        shared_up,
        shared_down,
        expert_gate,
        expert_up,
        expert_down,
    ):
        row_count, width = tokens.shape
        expert_count = expert_gate.shape[0]
        capacity = row_count * routes.shape[1] // expert_count
        quarter = width // tp_n
        tp_index = lax.axis_index(TP)
        own_expert = lax.axis_index(CHIPS)
        plane_base = lax.axis_index("fi") * plane_experts

        def columns(values):
            return lax.dynamic_slice_in_dim(values, tp_index * quarter, quarter, values.ndim - 1)

        depth = latent_down.shape[0]
        small = jnp.concatenate(
            [
                latent_down,
                attn_gain[:, None],
                moe_gain[:, None],
                jnp.pad(latent_gain, (0, depth - latent_gain.shape[0]))[:, None],
                router_weight,
            ],
            axis=1,
        )
        used = small.shape[1]
        part = -(-used // (32 * tp_n)) * 32
        small = jnp.pad(small, ((0, 0), (0, part * tp_n - used)))
        small = lax.dynamic_slice_in_dim(small, tp_index * part, part, 1)
        small = lax.all_gather(small, ROWS + TP, axis=0)
        small = (
            small.reshape(row_shards, tp_n, depth, part)
            .transpose(0, 2, 1, 3)
            .reshape(row_shards * depth, tp_n * part)
        )
        down_width = latent_down.shape[1]
        down_full = small[:, :down_width]
        gain_one = small[:, down_width].astype(F32)
        gain_two = small[:, down_width + 1].astype(F32)
        gain_latent = (
            small[:, down_width + 2]
            .reshape(row_shards, depth)[:, : latent_gain.shape[0]]
            .reshape(-1)
            .astype(F32)
        )
        router_full = small[:, down_width + 3 : used]

        query_full = lax.all_gather(query_weight, ROWS, axis=0, tiled=True)
        up_full = lax.all_gather(latent_up, ROWS, axis=0, tiled=True)
        out_full = lax.all_gather(out_weight, ROWS, axis=1, tiled=True)

        keys = jnp.where(slot_index < capacity, routes * capacity + slot_index, -1)
        keys_all = lax.all_gather(keys, ("fi", "ctx"), axis=0).reshape(
            fi_n, ctx_n, row_count, routes.shape[1]
        )

        def slots_of(key_rows, expert_ids):
            rel = key_rows[..., None, :, :] - expert_ids[:, None, None] * capacity
            return jnp.max(jnp.where((rel >= 0) & (rel < capacity), rel, -1), axis=-1)

        slot_ids = jnp.arange(capacity, dtype=jnp.int32)
        keys_column = lax.dynamic_index_in_dim(keys_all, lax.axis_index("ctx"), 1, keepdims=False)
        plane_slots = slots_of(
            keys_column, plane_base + jnp.arange(plane_experts, dtype=jnp.int32)
        )
        token_slots = plane_slots.transpose(0, 2, 1)
        z_first = lax.axis_index("tpc") * z_part
        keys_mine = lax.dynamic_slice_in_dim(keys_all, z_first, z_part, 0)
        my_slots = slots_of(keys_mine, own_expert[None])[:, :, 0]
        own_slots = slots_of(keys, jnp.arange(expert_count, dtype=jnp.int32))

        def dispatch(part_rows, collective_id):
            got = dispatch_rows(sizes, part_rows, plane_slots, capacity, collective_id)
            return got.reshape(-1, width)

        def give_back(rows, collective_id):
            rows = rows.reshape(z_part, ctx_n, capacity, width)
            return give_back_rows(sizes, rows, token_slots, collective_id)

        slot_grads = dispatch(columns(out_grad), 0)
        routed_weights = expert_weights(expert_gate, expert_up, expert_down)
        gate_full, expert_up_full, down_weight = (routed_weights[k] for k in range(3))
        shared_gate_full = lax.all_gather(shared_gate, ROWS, axis=0, tiled=True)
        shared_up_full = lax.all_gather(shared_up, ROWS, axis=0, tiled=True)
        shared_down_full = lax.all_gather(shared_down, ROWS, axis=1, tiled=True)

        head_count = query_full.shape[1] // (NOPE + ROPE)
        hidden = tokens.astype(F32)
        scale_one = rms_scale(hidden)
        normed_one = hidden * scale_one
        normed_in = (normed_one * gain_one).astype(BF16)
        seq_index = lax.axis_index(("fo", "fi"))
        prefix_len = lax.dynamic_index_in_dim(prefix, seq_index, keepdims=False)
        row_offset = lax.axis_index("ctx") * row_count
        query_pos = row_offset + jnp.arange(row_count, dtype=jnp.int32)
        cos_table, sin_table = rotation_tables(query_pos, ROPE // 2)
        score_scale = (NOPE + ROPE) ** (-0.5)
        cos_wide = jnp.concatenate([cos_table, cos_table], axis=1)
        sin_wide = jnp.concatenate([sin_table, sin_table], axis=1)
        table = score_scale * jnp.concatenate(
            [jnp.ones((row_count, NOPE), F32), cos_wide, sin_wide], axis=1
        )

        def turned(weight):
            half = weight.shape[-1] // 2
            return jnp.concatenate([-weight[..., half:], weight[..., :half]], axis=-1)

        latent_raw = dot(normed_in, jnp.concatenate([down_full, turned(down_full[:, KVR:])], axis=1))
        latent_part = latent_raw[:, :KVR]
        scale_latent = rms_scale(latent_part)
        normed_latent = latent_part * scale_latent
        latent = (normed_latent * gain_latent).astype(BF16)
        key_rope = (
            latent_raw[:, KVR : KVR + ROPE] * cos_wide + latent_raw[:, KVR + ROPE :] * sin_wide
        ).astype(BF16)
        both = lax.all_gather(
            jnp.concatenate([latent, key_rope, key_rope], axis=1), "ctx", axis=0, tiled=True
        )
        latent_all, rope_all = both[:, :KVR], both[:, KVR:]
        query_heads = query_full.reshape(width, head_count, NOPE + ROPE)
        query_wide = jnp.concatenate(
            [query_heads, turned(query_heads[..., NOPE:])], axis=-1
        ).reshape(width, head_count * HEAD)
        query_in = (
            dot(normed_in, query_wide).reshape(row_count, head_count, HEAD) * table[:, None]
        ).astype(BF16).reshape(row_count, head_count * HEAD)
        key_value = dot(latent_all, up_full).astype(BF16)
        place = jnp.stack([row_offset, prefix_len]).astype(jnp.int32)
        block_rows = min(256, row_count)
        attended, log_totals = attend(place, query_in, key_value, rope_all, block_rows)

        def tp_scatter(partial):
            parts = partial.astype(BF16).reshape(row_count, tp_n, quarter).transpose(1, 0, 2)
            return lax.psum_scatter(parts, TP, scatter_dimension=0, tiled=True)[0].astype(F32)

        def tp_gather(part_rows):
            got = lax.all_gather(part_rows, TP, axis=0)
            return got.transpose(1, 0, 2).reshape(row_count, width)

        residual = columns(tokens).astype(F32) + tp_scatter(dot(attended, out_full))
        scale_two = lax.rsqrt(
            lax.psum(jnp.sum(residual * residual, axis=-1, keepdims=True), TP) / width + EPSILON
        )
        normed_two = residual * scale_two
        gain_two_part = columns(gain_two[None])
        mid_part = (normed_two * gain_two_part).astype(BF16)

        slot_rows = dispatch(mid_part, 1)
        normed_mid = tp_gather(mid_part)

        logits = dot(normed_mid, router_full)
        router_prob = jax.nn.softmax(logits, axis=-1)
        prob_all = lax.all_gather(router_prob, ("fi", "ctx"), axis=0).reshape(
            fi_n, ctx_n, row_count, expert_count
        )
        prob_mine = lax.dynamic_slice_in_dim(prob_all, z_first, z_part, 0)
        prob_mine = lax.dynamic_index_in_dim(prob_mine, own_expert, 3, keepdims=False)
        slot_gate = jnp.sum(
            jnp.where(my_slots[:, :, None, :] == slot_ids[:, None], prob_mine[:, :, None, :], 0.0),
            axis=-1,
        ).reshape(-1, 1)

        gate_pre = dot(normed_mid, shared_gate_full)
        up_pre = dot(normed_mid, shared_up_full)
        shared_dact = dot_nt(out_grad, shared_down_full)
        shared_silu, shared_slope = silu_parts(gate_pre)
        shared_act = (shared_silu * up_pre).astype(BF16)
        shared_dgate = (shared_dact * up_pre * shared_slope).astype(BF16)
        shared_dup = (shared_dact * shared_silu).astype(BF16)
        mid_shared = tp_scatter(
            dot_nt(shared_dgate, shared_gate_full) + dot_nt(shared_dup, shared_up_full)
        )
        out_shared = tp_scatter(dot(shared_act, shared_down_full))

        expert_dact_raw = dot_nt(slot_grads, down_weight)
        expert_gpre = dot_nt(slot_rows, gate_full)
        expert_upre = dot_nt(slot_rows, expert_up_full)
        expert_silu, expert_slope = silu_parts(expert_gpre)
        expert_act_wide = expert_silu * expert_upre
        expert_act = expert_act_wide.astype(BF16)
        slot_gate_grad = jnp.sum(expert_act.astype(F32) * expert_dact_raw, axis=-1)
        expert_dact = expert_dact_raw * slot_gate
        expert_dgate = (expert_dact * expert_upre * expert_slope).astype(BF16)
        expert_dup = (expert_dact * expert_silu).astype(BF16)
        slot_drows = dot(expert_dgate, gate_full) + dot(expert_dup, expert_up_full)
        mid_routed = give_back(slot_drows.astype(BF16), 2)
        gate_back = lax.all_gather(
            slot_gate_grad.reshape(z_part, ctx_n, capacity), CHIPS + ("tpc",), axis=0
        ).reshape(expert_count, fi_n, ctx_n, capacity)
        gate_back = lax.dynamic_index_in_dim(gate_back, lax.axis_index("fi"), 1, keepdims=False)
        gate_back = lax.dynamic_index_in_dim(gate_back, lax.axis_index("ctx"), 1, keepdims=False)
        prob_grad = jnp.sum(
            jnp.where(own_slots[:, None, :] == slot_ids[None, :, None], gate_back[:, :, None], 0.0),
            axis=1,
        ).T
        logit_grad = (
            router_prob * (prob_grad - jnp.sum(router_prob * prob_grad, axis=-1, keepdims=True))
        ).astype(BF16)

        expert_out = (dot(expert_act, down_weight) * slot_gate).astype(BF16)
        output = residual + out_shared + give_back(expert_out, 3)
        output = tp_gather(output.astype(BF16))
        slot_dout = (slot_grads.astype(F32) * slot_gate).astype(BF16)
        routed_grads = split_expert_grads(
            (
                dot_tn(expert_dgate, slot_rows),
                dot_tn(expert_dup, slot_rows),
                dot_tn(expert_act, slot_dout),
            )
        )
        sdown_grad = dot_tn(shared_act, out_grad)
        sgate_grad = dot_tn(normed_mid, shared_dgate)
        sup_grad = dot_tn(normed_mid, shared_dup)

        def own_rows(grad, axis):
            return lax.psum_scatter(
                grad.astype(BF16), ROWS, scatter_dimension=axis, tiled=True
            ).astype(F32)

        sgate_grad = own_rows(sgate_grad, 0)
        sup_grad = own_rows(sup_grad, 0)
        sdown_grad = own_rows(sdown_grad, 1)

        mid_total = mid_shared + mid_routed + dot_nt(logit_grad, columns(router_full.T).T)
        gain_two_grad = jnp.sum(mid_total * normed_two, axis=0)
        dn_two = mid_total * gain_two_part
        dot_two = lax.psum(jnp.sum(dn_two * normed_two, axis=-1, keepdims=True), TP) / width
        residual_grad = columns(out_grad).astype(F32) + scale_two * (dn_two - normed_two * dot_two)
        attn_dout = tp_gather(residual_grad.astype(BF16))

        out_weight_grad = dot_tn(attended, attn_dout)
        attended_grad = dot_nt(attn_dout, out_full).astype(BF16)
        attended_grad, routed_grads = lax.optimization_barrier((attended_grad, routed_grads))
        egate_grad, eup_grad, edown_grad = own_expert_grads(routed_grads)
        query_grad, kv_grad, rope_grad = attend_back(
            place, query_in, key_value, rope_all, attended_grad, log_totals, table,
            min(512, row_count),
        )
        up_grad = dot_tn(latent_all, kv_grad)
        latent_grad = dot_nt(kv_grad, up_full)
        query_wide_grad = dot_tn(normed_in, query_grad).reshape(width, head_count, HEAD)
        query_weight_grad = jnp.concatenate(
            [
                query_wide_grad[..., :NOPE],
                query_wide_grad[..., NOPE : NOPE + ROPE] - turned(query_wide_grad[..., NOPE + ROPE :]),
            ],
            axis=-1,
        ).reshape(width, head_count * (NOPE + ROPE))
        input_part = tp_scatter(dot_nt(query_grad, query_wide))
        both_grad = lax.psum_scatter(
            jnp.concatenate([latent_grad, rope_grad], axis=1).astype(BF16),
            "ctx",
            scatter_dimension=0,
            tiled=True,
        )
        both_grad = lax.psum(both_grad, TP).astype(F32)
        latent_own = both_grad[:, :KVR]
        rope_own = both_grad[:, KVR : KVR + ROPE] + both_grad[:, KVR + ROPE :]
        gain_latent_grad = jnp.sum(latent_own * normed_latent, axis=0)
        latent_raw_grad = norm_back(latent_own * gain_latent, normed_latent, scale_latent)
        down_out_grad = jnp.concatenate(
            [latent_raw_grad, rotate(rope_own, cos_table, -sin_table)], axis=-1
        ).astype(BF16)
        down_part = down_width // tp_n
        down_grad = dot_tn(
            normed_in, lax.dynamic_slice_in_dim(down_out_grad, tp_index * down_part, down_part, 1)
        )
        input_total = input_part + dot_nt(
            down_out_grad, lax.dynamic_slice_in_dim(down_full, tp_index * quarter, quarter, 0)
        )
        normed_one_part = columns(normed_one)
        gain_one_grad = jnp.sum(input_total * normed_one_part, axis=0)
        dn_one = input_total * columns(gain_one[None])
        dot_one = lax.psum(jnp.sum(dn_one * normed_one_part, axis=-1, keepdims=True), TP) / width
        token_grad = residual_grad + scale_one * (dn_one - normed_one_part * dot_one)
        token_grad = tp_gather(token_grad.astype(BF16)).astype(F32)

        query_weight_grad = own_rows(query_weight_grad, 0)
        up_grad = own_rows(up_grad, 0)
        out_weight_grad = own_rows(out_weight_grad, 1)

        router_grad = dot_tn(normed_mid, logit_grad)
        own_down = lax.psum_scatter(
            down_grad.astype(BF16), ROWS, scatter_dimension=0, tiled=True
        )
        own_down = lax.all_gather(own_down, TP, axis=0)
        down_grad = own_down.transpose(1, 0, 2).reshape(depth, down_width).astype(F32)
        gains = jnp.stack([gain_one_grad, gain_two_grad], axis=1)
        gains = lax.dynamic_update_slice_in_dim(
            jnp.zeros((width, 2), F32), gains, tp_index * quarter, 0
        )
        latent_rows = jnp.pad(
            gain_latent_grad.reshape(row_shards, -1),
            ((0, 0), (0, depth - latent_gain.shape[0])),
        ).reshape(-1, 1)
        owner = (tp_index == 0).astype(F32)
        tiny = jnp.concatenate([gains, latent_rows * owner, router_grad * owner], axis=1)
        tiny = lax.psum_scatter(tiny, ROWS, scatter_dimension=0, tiled=True)
        tiny = lax.psum(tiny, TP)
        return (
            output,
            token_grad,
            tiny[:, 0],
            query_weight_grad,
            down_grad,
            tiny[: latent_gain.shape[0], 2],
            up_grad,
            out_weight_grad,
            tiny[:, 1],
            tiny[:, 3:],
            sgate_grad,
            sup_grad,
            sdown_grad,
            egate_grad,
            eup_grad,
            edown_grad,
        )

    return shards


EXPERTS = 16


def solution(mesh):
    ctx_n, tp_n = mesh.shape["ctx"], mesh.shape["tp"]
    tpc_n = 2
    tpx_n = tp_n // tpc_n
    fi_n = EXPERTS // (ctx_n * tpx_n)
    sizes = {
        "fo": mesh.shape["fsdp"] // fi_n,
        "fi": fi_n,
        "ctx": ctx_n,
        "tpx": tpx_n,
        "tpc": tpc_n,
    }
    fine = Mesh(mesh.devices.reshape(tuple(sizes.values())), tuple(sizes))
    rows = P(ROWS)
    rows_two = P(ROWS, None)
    rows_tp = P(ROWS, TP)
    tp_rows = P(TP, ROWS)
    wide_in = P(None, ROWS, TP)
    wide_out = P(None, TP, ROWS)
    weights = (
        rows,
        rows_tp,
        rows_two,
        rows,
        rows_tp,
        tp_rows,
        rows,
        rows_two,
        rows_tp,
        rows_tp,
        tp_rows,
        wide_in,
        wide_in,
        wide_out,
    )
    return jax.shard_map(
        build(sizes),
        mesh=fine,
        in_specs=(rows_two, rows_two, rows_two, rows_two, P()) + weights,
        out_specs=(rows_two, rows_two) + weights,
        check_vma=False,
    )
```

```python
import functools
import math

import jax
import jax.numpy as jnp
from jax import lax
from jax.experimental import pallas as pl
from jax.experimental.pallas import tpu as pltpu
from jax.sharding import Mesh
from jax.sharding import PartitionSpec as P

NOPE = 128
ROPE = 64
KVR = 512
VDIM = 128
HEAD = 256

EPSILON = 1e-06
THETA_BASE = 10000.0
F32 = jnp.float32
BF16 = jnp.bfloat16
MESH_ID = pl.DeviceIdType.MESH

ROWS = ("fo", "fi", "ctx")
TP = ("tpx", "tpc")
PLANE = ("ctx", "tpx", "tpc")
CHIPS = ("fi", "ctx", "tpx")


def rotation_tables(positions, half_width):
    freq_table = jnp.exp(jnp.arange(half_width, dtype=F32) * (-math.log(THETA_BASE) / half_width))
    angle_table = positions.astype(F32)[:, None] * freq_table[None, :]
    return (jnp.cos(angle_table), jnp.sin(angle_table))


def rotate(values, cos_table, sin_table):
    half_width = values.shape[-1] // 2
    first_half = values[..., :half_width]
    second_half = values[..., half_width:]
    return jnp.concatenate(
        [
            first_half * cos_table - second_half * sin_table,
            second_half * cos_table + first_half * sin_table,
        ],
        axis=-1,
    )


def silu_parts(values):
    sigma = jax.nn.sigmoid(values)
    return (values * sigma, sigma * (1.0 + values * (1.0 - sigma)))


def rms_scale(values):
    return lax.rsqrt(jnp.mean(values * values, axis=-1, keepdims=True) + EPSILON)


def norm_back(grad_normed, normed, scale_rows):
    return scale_rows * (
        grad_normed - normed * jnp.mean(grad_normed * normed, axis=-1, keepdims=True)
    )


def dot(left, right):
    return jnp.dot(left, right, preferred_element_type=F32)


def dot_nt(left, right):
    return lax.dot_general(left, right, (((1,), (1,)), ((), ())), preferred_element_type=F32)


def dot_tn(left, right):
    return lax.dot_general(left, right, (((0,), (0,)), ((), ())), preferred_element_type=F32)


def ein(spec, left, right):
    return jnp.einsum(spec, left, right, preferred_element_type=F32)


def plane_place(sizes):
    tpx_n, tpc_n = sizes["tpx"], sizes["tpc"]
    fo, z, y, x, c = (lax.axis_index(name) for name in ("fo", "fi", "ctx", "tpx", "tpc"))
    own = (y * tpx_n + x) * tpc_n + c

    def device(index, z_at=None):
        return (
            fo,
            z if z_at is None else z_at,
            index // (tpx_n * tpc_n),
            lax.rem(index // tpc_n, tpx_n),
            lax.rem(index, tpc_n),
        )

    return z, y, x, c, own, device


def greet_plane(sizes, z, own, device):
    fi_n = sizes["fi"]
    plane_n = sizes["ctx"] * sizes["tpx"] * sizes["tpc"]
    barrier = pltpu.get_barrier_semaphore()
    for step in range(1, plane_n):
        pl.semaphore_signal(
            barrier,
            inc=1,
            device_id=device(lax.rem(own + step, plane_n)),
            device_id_type=MESH_ID,
        )
    for near in (-1, 1):

        @pl.when((z + near >= 0) & (z + near < fi_n))
        def _():
            pl.semaphore_signal(
                barrier, inc=1, device_id=device(own, z + near), device_id_type=MESH_ID
            )

    sides = (z > 0).astype(jnp.int32) + (z < fi_n - 1).astype(jnp.int32)
    pl.semaphore_wait(barrier, plane_n - 1 + sides)


def dispatch_body(
    sizes,
    slots_ref,
    rows_ref,
    out_ref,
    held,
    picked,
    own_sem,
    line_send,
    line_recv,
    plane_send,
    plane_recv,
):
    fi_n, tpx_n, tpc_n = sizes["fi"], sizes["tpx"], sizes["tpc"]
    plane_n = sizes["ctx"] * tpx_n * tpc_n
    chips = sizes["ctx"] * tpx_n
    z_part = fi_n // tpc_n
    capacity, quarter = picked.shape[2:]
    tokens = held.shape[1]
    z, y, x, c, own, device = plane_place(sizes)
    greet_plane(sizes, z, own, device)
    columns = pl.ds(pl.multiple_of((x * tpc_n + c) * quarter, quarter), quarter)

    load = pltpu.make_async_copy(rows_ref, held.at[z], own_sem)
    load.start()
    load.wait()

    def line(side, step):
        block = z - step if side == 0 else z + step
        to = z + 1 if side == 0 else z - 1
        return block, to, pltpu.make_async_remote_copy(
            src_ref=held.at[block],
            dst_ref=held.at[block],
            send_sem=line_send.at[side, step],
            recv_sem=line_recv.at[side, step],
            device_id=device(own, to),
            device_id_type=MESH_ID,
        )

    def sends(side, step):
        block = z - step if side == 0 else z + step
        to = z + 1 if side == 0 else z - 1
        return (block >= 0) & (block < fi_n) & (to >= 0) & (to < fi_n)

    def plane_copy(block, chip):
        target = chip * tpc_n + block // z_part
        at = lax.rem(block, z_part)
        return pltpu.make_async_remote_copy(
            src_ref=picked.at[block, chip],
            dst_ref=out_ref.at[at, y, :, columns],
            send_sem=plane_send.at[block, chip],
            recv_sem=plane_recv.at[own, at],
            device_id=device(target),
            device_id_type=MESH_ID,
        )

    def keep_copy(block, chip):
        return pltpu.make_async_copy(
            picked.at[block, chip],
            out_ref.at[lax.rem(block, z_part), y, :, columns],
            plane_send.at[block, chip],
        )

    def at_home(block, chip):
        return chip * tpc_n + block // z_part == own

    def pick(block):
        def one(chip, carry):
            wanted = slots_ref[block, pl.ds(chip, 1), :]
            rank = lax.broadcasted_iota(jnp.int32, (capacity, tokens), 0)
            hits = jnp.where(rank == wanted, 1.0, 0.0).astype(BF16)
            picked[block, chip] = jnp.dot(
                hits, held[block], preferred_element_type=F32
            ).astype(BF16)

            @pl.when(at_home(block, chip))
            def _():
                keep_copy(block, chip).start()

            @pl.when(jnp.logical_not(at_home(block, chip)))
            def _():
                plane_copy(block, chip).start()

            return carry

        lax.fori_loop(0, chips, one, 0)

    for step in range(fi_n):
        for side in (0, 1):
            if step < fi_n - 1:

                @pl.when(sends(side, step))
                def _():
                    line(side, step)[2].start()

        if step == 0:
            pick(z)
        else:
            for side in (0, 1):
                block = z - step if side == 0 else z + step

                @pl.when((block >= 0) & (block < fi_n))
                def _():
                    pick(block)

        if step < fi_n - 1:
            for side in (0, 1):
                block = z - 1 - step if side == 0 else z + 1 + step

                @pl.when((block >= 0) & (block < fi_n))
                def _():
                    pltpu.make_async_remote_copy(
                        src_ref=held.at[block],
                        dst_ref=held.at[block],
                        send_sem=line_send.at[side, step],
                        recv_sem=line_recv.at[side, step],
                        device_id=device(own, z),
                        device_id_type=MESH_ID,
                    ).wait_recv()

    for step in range(fi_n - 1):
        for side in (0, 1):

            @pl.when(sends(side, step))
            def _():
                line(side, step)[2].wait_send()

    def settle(index, carry):
        block, chip = index // chips, lax.rem(index, chips)

        @pl.when(at_home(block, chip))
        def _():
            keep_copy(block, chip).wait()

        @pl.when(jnp.logical_not(at_home(block, chip)))
        def _():
            plane_copy(block, chip).wait_send()

        return carry

    lax.fori_loop(0, fi_n * chips, settle, 0)

    def arrive(index, carry):
        source, at = index // z_part, lax.rem(index, z_part)

        @pl.when(source != own)
        def _():
            pltpu.make_async_remote_copy(
                src_ref=picked.at[0, 0],
                dst_ref=out_ref.at[at, y, :, columns],
                send_sem=plane_send.at[0, 0],
                recv_sem=plane_recv.at[source, at],
                device_id=device(own),
                device_id_type=MESH_ID,
            ).wait_recv()

        return carry

    lax.fori_loop(0, plane_n * z_part, arrive, 0)


def dispatch_rows(sizes, part_rows, plane_slots, capacity, collective_id):
    tokens, quarter = part_rows.shape
    fi_n, ctx_n, tpx_n, tpc_n = (sizes[n] for n in ("fi", "ctx", "tpx", "tpc"))
    z_part, plane_n, chips = fi_n // tpc_n, ctx_n * tpx_n * tpc_n, ctx_n * tpx_n
    return pl.pallas_call(
        functools.partial(dispatch_body, sizes),
        out_shape=jax.ShapeDtypeStruct(
            (z_part, ctx_n, capacity, quarter * tpx_n * tpc_n), BF16
        ),
        in_specs=[
            pl.BlockSpec(memory_space=pltpu.VMEM),
            pl.BlockSpec(memory_space=pl.ANY),
        ],
        out_specs=pl.BlockSpec(memory_space=pl.ANY),
        scratch_shapes=[
            pltpu.VMEM((fi_n, tokens, quarter), BF16),
            pltpu.VMEM((fi_n, chips, capacity, quarter), BF16),
            pltpu.SemaphoreType.DMA,
            pltpu.SemaphoreType.DMA((2, fi_n)),
            pltpu.SemaphoreType.DMA((2, fi_n)),
            pltpu.SemaphoreType.DMA((fi_n, chips)),
            pltpu.SemaphoreType.DMA((plane_n, z_part)),
        ],
        compiler_params=pltpu.CompilerParams(
            collective_id=collective_id, has_side_effects=True, vmem_limit_bytes=40 << 20
        ),
        cost_estimate=pl.CostEstimate(
            flops=2 * fi_n * chips * capacity * tokens * quarter,
            bytes_accessed=100_000_000,
            transcendentals=0,
        ),
        name="dispatch",
    )(plane_slots, part_rows)


def give_back_body(
    sizes,
    slots_ref,
    rows_ref,
    out_ref,
    got,
    total,
    going,
    coming,
    plane_send,
    plane_recv,
    line_send,
    line_recv,
):
    fi_n, tpx_n, tpc_n = sizes["fi"], sizes["tpx"], sizes["tpc"]
    plane_n = sizes["ctx"] * tpx_n * tpc_n
    chips = sizes["ctx"] * tpx_n
    z_part = fi_n // tpc_n
    capacity, quarter = got.shape[2:]
    tokens = total.shape[0]
    z, y, x, c, own, device = plane_place(sizes)
    greet_plane(sizes, z, own, device)
    tile = min(256, tokens)

    def piece(target, at):
        side = lax.rem(target, tpx_n * tpc_n)
        return rows_ref.at[
            at,
            target // (tpx_n * tpc_n),
            :,
            pl.ds(pl.multiple_of(side * quarter, quarter), quarter),
        ]

    def plane_copy(target, at):
        return pltpu.make_async_remote_copy(
            src_ref=piece(target, at),
            dst_ref=got.at[c * z_part + at, own // tpc_n],
            send_sem=plane_send.at[target, at],
            recv_sem=plane_recv.at[own, at],
            device_id=device(target),
            device_id_type=MESH_ID,
        )

    def keep_copy(at):
        return pltpu.make_async_copy(
            piece(own, at), got.at[c * z_part + at, own // tpc_n], plane_recv.at[own, at]
        )

    far_first = z < fi_n // 2
    for turn in range(z_part):
        at = jnp.where(far_first, z_part - 1 - turn, turn)

        def one(step, carry):
            plane_copy(lax.rem(own + step, plane_n), at).start()
            return carry

        keep_copy(at).start()
        lax.fori_loop(1, plane_n, one, 0)

    def gathered(block):
        def one(chip, carry):
            source, at = chip * tpc_n + block // z_part, lax.rem(block, z_part)

            @pl.when(source == own)
            def _():
                keep_copy(at).wait()

            @pl.when(source != own)
            def _():
                pltpu.make_async_remote_copy(
                    src_ref=got.at[block, chip],
                    dst_ref=got.at[block, chip],
                    send_sem=plane_send.at[own, at],
                    recv_sem=plane_recv.at[source, at],
                    device_id=device(own),
                    device_id_type=MESH_ID,
                ).wait_recv()

            return carry

        lax.fori_loop(0, chips, one, 0)

        def rows(step, carry):
            first = pl.multiple_of(step * tile, tile)
            spots = slots_ref[block, pl.ds(first, tile), :]
            rank = lax.broadcasted_iota(jnp.int32, (tile, capacity), 1)
            summed = jnp.zeros((tile, quarter), F32)
            for chip in range(chips):
                hits = jnp.where(rank == spots[:, chip : chip + 1], 1.0, 0.0).astype(BF16)
                summed = summed + jnp.dot(hits, got[block, chip], preferred_element_type=F32)
            total[pl.ds(first, tile), :] = summed
            return carry

        lax.fori_loop(0, tokens // tile, rows, 0)

    def line(side, target):
        return pltpu.make_async_remote_copy(
            src_ref=going.at[target],
            dst_ref=coming.at[side, target],
            send_sem=line_send.at[side, target],
            recv_sem=line_recv.at[side, target],
            device_id=device(own, z + 1 if side == 0 else z - 1),
            device_id_type=MESH_ID,
        )

    def came(side, target):
        pltpu.make_async_remote_copy(
            src_ref=going.at[target],
            dst_ref=coming.at[side, target],
            send_sem=line_send.at[side, target],
            recv_sem=line_recv.at[side, target],
            device_id=device(own, z),
            device_id_type=MESH_ID,
        ).wait_recv()

    for step in range(fi_n - 1):
        for side in (0, 1):
            target = fi_n - 1 - step if side == 0 else step
            passes = (z < target) if side == 0 else (z > target)
            inner = (z > 0) if side == 0 else (z < fi_n - 1)

            @pl.when(passes)
            def _():
                gathered(target)

                @pl.when(inner)
                def _():
                    came(side, target)
                    going[target] = (total[...] + coming[side, target].astype(F32)).astype(BF16)

                @pl.when(jnp.logical_not(inner))
                def _():
                    going[target] = total[...].astype(BF16)

                line(side, target).start()

    gathered(z)
    for side in (0, 1):

        @pl.when((z > 0) if side == 0 else (z < fi_n - 1))
        def _():
            came(side, z)
            total[...] += coming[side, z].astype(F32)

    out_ref[...] = total[...]

    for target in range(fi_n):
        for side in (0, 1):

            @pl.when((z < target) if side == 0 else (z > target))
            def _():
                line(side, target).wait_send()

    def settle(index, carry):
        target, at = index // z_part, lax.rem(index, z_part)

        @pl.when(target != own)
        def _():
            plane_copy(target, at).wait_send()

        return carry

    lax.fori_loop(0, plane_n * z_part, settle, 0)


def give_back_rows(sizes, rows, token_slots, collective_id):
    fi_n, ctx_n, tpx_n, tpc_n = (sizes[n] for n in ("fi", "ctx", "tpx", "tpc"))
    z_part, plane_n, chips = fi_n // tpc_n, ctx_n * tpx_n * tpc_n, ctx_n * tpx_n
    capacity, width = rows.shape[2:]
    quarter = width // (tpx_n * tpc_n)
    tokens = token_slots.shape[1]
    return pl.pallas_call(
        functools.partial(give_back_body, sizes),
        out_shape=jax.ShapeDtypeStruct((tokens, quarter), F32),
        in_specs=[
            pl.BlockSpec(memory_space=pltpu.VMEM),
            pl.BlockSpec(memory_space=pl.ANY),
        ],
        out_specs=pl.BlockSpec(memory_space=pltpu.VMEM),
        scratch_shapes=[
            pltpu.VMEM((fi_n, chips, capacity, quarter), BF16),
            pltpu.VMEM((tokens, quarter), F32),
            pltpu.VMEM((fi_n, tokens, quarter), BF16),
            pltpu.VMEM((2, fi_n, tokens, quarter), BF16),
            pltpu.SemaphoreType.DMA((plane_n, z_part)),
            pltpu.SemaphoreType.DMA((plane_n, z_part)),
            pltpu.SemaphoreType.DMA((2, fi_n)),
            pltpu.SemaphoreType.DMA((2, fi_n)),
        ],
        compiler_params=pltpu.CompilerParams(
            collective_id=collective_id, has_side_effects=True, vmem_limit_bytes=48 << 20
        ),
        cost_estimate=pl.CostEstimate(
            flops=2 * fi_n * chips * capacity * tokens * quarter,
            bytes_accessed=100_000_000,
            transcendentals=0,
        ),
        name="give_back",
    )(token_slots, rows)


def moves(count, sizes):
    ctx_n, tpx_n = sizes["ctx"], sizes["tpx"]
    return [(s // (ctx_n * tpx_n), s // tpx_n % ctx_n, s % tpx_n) for s in range(1, count)]


def collect_body(sizes, kinds, routed, *refs):
    fo_n, fi_n, ctx_n, tpx_n, tpc_n = (sizes[n] for n in ("fo", "fi", "ctx", "tpx", "tpc"))
    tp_n = tpx_n * tpc_n
    chip_n = fi_n * ctx_n * tpx_n
    count = len(kinds)
    shards, refs = refs[:count], refs[count:]
    if routed:
        local, refs = refs[0], refs[1:]
    outs, refs = refs[:count], refs[count:]
    if routed:
        experts, refs = refs[:3], refs[3:]
    own_sem, line_send, line_recv, col_send, col_recv, tp_send, tp_recv = refs[:7]
    fo, z, y, x, c = (lax.axis_index(n) for n in ("fo", "fi", "ctx", "tpx", "tpc"))
    q = x * tpc_n + c
    barrier = pltpu.get_barrier_semaphore()

    def hello(device):
        pl.semaphore_signal(barrier, inc=1, device_id=device, device_id_type=MESH_ID)

    expected = jnp.int32(0)
    if routed:
        for dz, dy, dx in moves(chip_n, sizes):
            hello((fo, lax.rem(z + dz, fi_n), lax.rem(y + dy, ctx_n), lax.rem(x + dx, tpx_n), c))
        for dc in range(1, tpc_n):
            hello((fo, z, y, x, lax.rem(c + dc, tpc_n)))
        expected = expected + (chip_n - 1 + tpc_n - 1)
    else:
        for near in (-1, 1):

            @pl.when((z + near >= 0) & (z + near < fi_n))
            def _():
                hello((fo, z + near, y, x, c))

        for dy in range(1, ctx_n):
            hello((fo, z, lax.rem(y + dy, ctx_n), x, c))
        for step in range(1, tp_n):
            other = lax.rem(q + step, tp_n)
            hello((fo, z, y, other // tpc_n, lax.rem(other, tpc_n)))
        expected = expected + (ctx_n - 1 + tp_n - 1)
        expected = expected + (z > 0).astype(jnp.int32) + (z < fi_n - 1).astype(jnp.int32)
    pl.semaphore_wait(barrier, expected)

    items = [(i, f) for f in range(fo_n) for i in range(count)]

    def source(n):
        i, f = items[n]
        if kinds[i] == "share":
            a = shards[i].shape[1] // tp_n
            return shards[i].at[f, pl.ds(pl.multiple_of(q * a, a), a), :]
        return shards[i].at[f]

    def place(n, zb, yb):
        i, f = items[n]
        a, b = shards[i].shape[1:]
        block = (f * fi_n + zb) * ctx_n + yb
        if kinds[i] == "col":
            return outs[i].at[:, pl.ds(pl.multiple_of(block * b, b), b)]
        if kinds[i] == "share":
            part = a // tp_n
            return outs[i].at[pl.ds(pl.multiple_of(block * a + q * part, part), part), :]
        return outs[i].at[pl.ds(pl.multiple_of(block * a, a), a), :]

    def line(n, side, step, first):
        block = z - step if side == 0 else z + step
        to = z + 1 if side == 0 else z - 1
        return pltpu.make_async_remote_copy(
            src_ref=source(n) if first else place(n, block, y),
            dst_ref=place(n, block, y),
            send_sem=line_send.at[n, side, step],
            recv_sem=line_recv.at[n, side, step],
            device_id=(fo, to, y, x, c),
            device_id_type=MESH_ID,
        )

    def sends(side, step):
        block = z - step if side == 0 else z + step
        to = z + 1 if side == 0 else z - 1
        return (block >= 0) & (block < fi_n) & (to >= 0) & (to < fi_n)

    def across(n, zb, dy, first=False):
        return pltpu.make_async_remote_copy(
            src_ref=source(n) if first else place(n, zb, y),
            dst_ref=place(n, zb, y),
            send_sem=col_send.at[n, zb, dy],
            recv_sem=col_recv.at[n, zb, dy],
            device_id=(fo, z, lax.rem(y + dy, ctx_n), x, c),
            device_id_type=MESH_ID,
        )

    def keep(n):
        return pltpu.make_async_copy(source(n), place(n, z, y), own_sem.at[n])

    for n in range(len(items)):
        for side in (0, 1):

            @pl.when(sends(side, 0))
            def _():
                line(n, side, 0, True).start()

        for dy in range(1, ctx_n):
            across(n, z, dy, True).start()
        keep(n).start()

    if routed:
        expert_send, expert_recv, pair_send, pair_recv = refs[7:]

        def chip_of(offset):
            dz, dy, dx = offset
            return (lax.rem(z + dz, fi_n), lax.rem(y + dy, ctx_n), lax.rem(x + dx, tpx_n))

        def number(chip):
            return (chip[0] * ctx_n + chip[1]) * tpx_n + chip[2]

        def spot(k, f, chip, core):
            rows, depth = local.shape[3:]
            block = (f * fi_n + chip[0]) * ctx_n + chip[1]
            return experts[k].at[
                pl.ds(pl.multiple_of((chip[2] * tpc_n + core) * rows, rows), rows),
                pl.ds(pl.multiple_of(block * depth, depth), depth),
            ]

        def expert_copy(f, k, chip):
            return pltpu.make_async_remote_copy(
                src_ref=local.at[f, number(chip), k],
                dst_ref=spot(k, f, (z, y, x), c),
                send_sem=expert_send.at[f, k, number(chip)],
                recv_sem=expert_recv.at[f, k, number((z, y, x))],
                device_id=(fo, chip[0], chip[1], chip[2], c),
                device_id_type=MESH_ID,
            )

        def expert_keep(f, k):
            me = (z, y, x)
            return pltpu.make_async_copy(
                local.at[f, number(me), k], spot(k, f, me, c), expert_recv.at[f, k, number(me)]
            )

        def pair_copy(f, k, chip, dc):
            return pltpu.make_async_remote_copy(
                src_ref=spot(k, f, chip, c),
                dst_ref=spot(k, f, chip, c),
                send_sem=pair_send.at[f, k, number(chip), dc],
                recv_sem=pair_recv.at[f, k, number(chip), dc],
                device_id=(fo, z, y, x, lax.rem(c + dc, tpc_n)),
                device_id_type=MESH_ID,
            )

        parts = fo_n * 3

        def launch(step, carry):
            f, k = step // 3, lax.rem(step, 3)
            for kk in range(3):

                @pl.when(k == kk)
                def _():
                    for offset in moves(chip_n, sizes):
                        expert_copy(f, kk, chip_of(offset)).start()
                    expert_keep(f, kk).start()

            return carry

        lax.fori_loop(0, parts, launch, 0)

    for step in range(fi_n - 1):
        for n in range(len(items)):
            for side in (0, 1):
                block = z - 1 - step if side == 0 else z + 1 + step

                @pl.when((block >= 0) & (block < fi_n))
                def _():
                    pltpu.make_async_remote_copy(
                        src_ref=place(n, block, y),
                        dst_ref=place(n, block, y),
                        send_sem=line_send.at[n, side, step],
                        recv_sem=line_recv.at[n, side, step],
                        device_id=(fo, z, y, x, c),
                        device_id_type=MESH_ID,
                    ).wait_recv()
                    for dy in range(1, ctx_n):
                        across(n, block, dy).start()

                if step < fi_n - 2:

                    @pl.when(sends(side, step + 1))
                    def _():
                        line(n, side, step + 1, False).start()

    for n in range(len(items)):
        keep(n).wait()
        for dy in range(1, ctx_n):
            for zb in range(fi_n):
                pltpu.make_async_remote_copy(
                    src_ref=place(n, zb, y),
                    dst_ref=place(n, zb, lax.rem(y + ctx_n - dy, ctx_n)),
                    send_sem=col_send.at[n, zb, dy],
                    recv_sem=col_recv.at[n, zb, dy],
                    device_id=(fo, z, y, x, c),
                    device_id_type=MESH_ID,
                ).wait_recv()
        i, f = items[n]
        if kinds[i] == "share":
            a = shards[i].shape[1]
            part = a // tp_n

            def spread(block, step, n=n, i=i, f=f, a=a, part=part):
                other = lax.rem(q + step, tp_n)
                at = (f * fi_n * ctx_n + block) * a + q * part
                return pltpu.make_async_remote_copy(
                    src_ref=outs[i].at[pl.ds(pl.multiple_of(at, part), part), :],
                    dst_ref=outs[i].at[pl.ds(pl.multiple_of(at, part), part), :],
                    send_sem=tp_send.at[n, block, step],
                    recv_sem=tp_recv.at[n, block, step],
                    device_id=(fo, z, y, other // tpc_n, lax.rem(other, tpc_n)),
                    device_id_type=MESH_ID,
                )

            def spread_all(block, carry):
                for step in range(1, tp_n):
                    spread(block, step).start()
                return carry

            lax.fori_loop(0, fi_n * ctx_n, spread_all, 0)

    for n in range(len(items)):
        i, f = items[n]
        if kinds[i] == "share":
            a = shards[i].shape[1]
            part = a // tp_n

            def landed(block, carry, n=n, i=i, f=f, a=a, part=part):
                for step in range(1, tp_n):
                    origin = lax.rem(q + tp_n - step, tp_n)
                    at = (f * fi_n * ctx_n + block) * a
                    mine = pl.ds(pl.multiple_of(at + q * part, part), part)
                    theirs = pl.ds(pl.multiple_of(at + origin * part, part), part)
                    copy = pltpu.make_async_remote_copy(
                        src_ref=outs[i].at[mine, :],
                        dst_ref=outs[i].at[theirs, :],
                        send_sem=tp_send.at[n, block, step],
                        recv_sem=tp_recv.at[n, block, step],
                        device_id=(fo, z, y, x, c),
                        device_id_type=MESH_ID,
                    )
                    copy.wait_send()
                    copy.wait_recv()
                return carry

            lax.fori_loop(0, fi_n * ctx_n, landed, 0)
        for side in (0, 1):
            for step in range(fi_n - 1):

                @pl.when(sends(side, step))
                def _():
                    line(n, side, step, step == 0).wait_send()

        for dy in range(1, ctx_n):
            for zb in range(fi_n):
                across(n, zb, dy).wait_send()

    if routed:

        def arrive(step, carry):
            f, k = step // 3, lax.rem(step, 3)
            for kk in range(3):

                @pl.when(k == kk)
                def _():
                    expert_keep(f, kk).wait()
                    for dc in range(1, tpc_n):
                        pair_copy(f, kk, (z, y, x), dc).start()
                    for dz, dy, dx in moves(chip_n, sizes):
                        chip = chip_of((fi_n - dz, ctx_n - dy, tpx_n - dx))
                        pltpu.make_async_remote_copy(
                            src_ref=spot(kk, f, chip, c),
                            dst_ref=spot(kk, f, chip, c),
                            send_sem=expert_send.at[f, kk, number(chip)],
                            recv_sem=expert_recv.at[f, kk, number(chip)],
                            device_id=(fo, z, y, x, c),
                            device_id_type=MESH_ID,
                        ).wait_recv()
                        for dc in range(1, tpc_n):
                            pair_copy(f, kk, chip, dc).start()

            return carry

        lax.fori_loop(0, parts, arrive, 0)

        def settle(step, carry):
            f, k = step // 3, lax.rem(step, 3)
            for kk in range(3):

                @pl.when(k == kk)
                def _():
                    for offset in [(0, 0, 0)] + moves(chip_n, sizes):
                        chip = chip_of(offset)
                        if offset != (0, 0, 0):
                            expert_copy(f, kk, chip).wait_send()
                        for dc in range(1, tpc_n):
                            pair_copy(f, kk, chip, dc).wait_send()
                            sender = lax.rem(c + tpc_n - dc, tpc_n)
                            pltpu.make_async_remote_copy(
                                src_ref=spot(kk, f, chip, c),
                                dst_ref=spot(kk, f, chip, sender),
                                send_sem=pair_send.at[f, kk, number(chip), dc],
                                recv_sem=pair_recv.at[f, kk, number(chip), dc],
                                device_id=(fo, z, y, x, c),
                                device_id_type=MESH_ID,
                            ).wait_recv()

            return carry

        lax.fori_loop(0, parts, settle, 0)


def collect(sizes, kinds, shards, local, collective_id):
    fo_n, fi_n, ctx_n, tpx_n, tpc_n = (sizes[n] for n in ("fo", "fi", "ctx", "tpx", "tpc"))
    tp_n = tpx_n * tpc_n
    blocks = fo_n * fi_n * ctx_n
    shapes = []
    for kind, shard in zip(kinds, shards):
        _, a, b = shard.shape
        shapes.append((a, blocks * b) if kind == "col" else (blocks * a, b))
    n = len(kinds) * fo_n
    scratch = [
        pltpu.SemaphoreType.DMA((n,)),
        pltpu.SemaphoreType.DMA((n, 2, fi_n)),
        pltpu.SemaphoreType.DMA((n, 2, fi_n)),
        pltpu.SemaphoreType.DMA((n, fi_n, ctx_n)),
        pltpu.SemaphoreType.DMA((n, fi_n, ctx_n)),
        pltpu.SemaphoreType.DMA((n, fi_n * ctx_n, tp_n)),
        pltpu.SemaphoreType.DMA((n, fi_n * ctx_n, tp_n)),
    ]
    args = list(shards)
    routed = local is not None
    if routed:
        args.append(local)
        chip_n = fi_n * ctx_n * tpx_n
        rows, depth = local.shape[3:]
        shapes += [(rows * tp_n, depth * blocks)] * 3
        scratch += [pltpu.SemaphoreType.DMA((fo_n, 3, chip_n))] * 2
        scratch += [pltpu.SemaphoreType.DMA((fo_n, 3, chip_n, tpc_n))] * 2
    return pl.pallas_call(
        functools.partial(collect_body, sizes, tuple(kinds), routed),
        out_shape=tuple(jax.ShapeDtypeStruct(shape, BF16) for shape in shapes),
        in_specs=[pl.BlockSpec(memory_space=pl.ANY)] * len(args),
        out_specs=tuple(pl.BlockSpec(memory_space=pl.ANY) for _ in shapes),
        scratch_shapes=scratch,
        compiler_params=pltpu.CompilerParams(
            collective_id=collective_id, has_side_effects=True
        ),
        cost_estimate=pl.CostEstimate(flops=0, bytes_accessed=100_000_000, transcendentals=0),
        name="collect",
    )(*args)


def finish_body(sizes, kinds, extra, *refs):
    fi_n, ctx_n, tpx_n, tpc_n = (sizes[n] for n in ("fi", "ctx", "tpx", "tpc"))
    tp_n = tpx_n * tpc_n
    count = len(kinds)
    parts, refs = refs[:count], refs[count:]
    quarters, refs = refs[:extra], refs[extra:]
    outs, refs = refs[:count], refs[count:]
    wholes, refs = refs[:extra], refs[extra:]
    mine, refs = refs[:count], refs[count:]
    other, refs = refs[:count], refs[count:]
    coming, refs = refs[:count], refs[count:]
    tiny, refs = refs[0], refs[1:]
    load_sem, col_send, col_recv, line_send, line_recv, tp_send, tp_recv = refs[:7]
    keep_sem, x_send, x_recv, c_send, c_recv = refs[7:]
    fo, z, y, x, c = (lax.axis_index(n) for n in ("fo", "fi", "ctx", "tpx", "tpc"))
    q = x * tpc_n + c
    barrier = pltpu.get_barrier_semaphore()

    def hello(device):
        pl.semaphore_signal(barrier, inc=1, device_id=device, device_id_type=MESH_ID)

    for near in (-1, 1):

        @pl.when((z + near >= 0) & (z + near < fi_n))
        def _():
            hello((fo, z + near, y, x, c))

    for dy in range(1, ctx_n):
        hello((fo, z, lax.rem(y + dy, ctx_n), x, c))
    for step in range(1, tp_n):
        peer = lax.rem(q + step, tp_n)
        hello((fo, z, y, peer // tpc_n, lax.rem(peer, tpc_n)))
    sides = (z > 0).astype(jnp.int32) + (z < fi_n - 1).astype(jnp.int32)
    pl.semaphore_wait(barrier, ctx_n - 1 + tp_n - 1 + sides)

    def slab(j, owner):
        wide = quarters[j].shape[1]
        return wholes[j].at[:, pl.ds(pl.multiple_of(owner * wide, wide), wide)]

    def keep(j):
        return pltpu.make_async_copy(quarters[j], slab(j, q), keep_sem.at[j])

    def to_chip(j, dx):
        return pltpu.make_async_remote_copy(
            src_ref=quarters[j],
            dst_ref=slab(j, q),
            send_sem=x_send.at[j, dx],
            recv_sem=x_recv.at[j, dx],
            device_id=(fo, z, y, lax.rem(x + dx, tpx_n), c),
            device_id_type=MESH_ID,
        )

    def to_core(j, dx, dc):
        owner = lax.rem(x + tpx_n - dx, tpx_n) * tpc_n + c
        return pltpu.make_async_remote_copy(
            src_ref=quarters[j] if dx == 0 else slab(j, owner),
            dst_ref=slab(j, owner),
            send_sem=c_send.at[j, dx, dc],
            recv_sem=c_recv.at[j, dx, dc],
            device_id=(fo, z, y, x, lax.rem(c + dc, tpc_n)),
            device_id_type=MESH_ID,
        )

    for j in range(extra):
        for dx in range(1, tpx_n):
            to_chip(j, dx).start()
        for dc in range(1, tpc_n):
            to_core(j, 0, dc).start()
        keep(j).start()

    def view(n, zb, yb):
        a, b = mine[n].shape[1:]
        block = zb * ctx_n + yb
        if kinds[n] == "col":
            return parts[n].at[:, pl.ds(pl.multiple_of(block * b, b), b)]
        if kinds[n] == "share":
            return parts[n].at[pl.ds(pl.multiple_of(block * a * tp_n + q * a, a), a), :]
        return parts[n].at[pl.ds(pl.multiple_of(block * a, a), a), :]

    def across(n, zb, dy):
        to = lax.rem(y + dy, ctx_n)
        return pltpu.make_async_remote_copy(
            src_ref=view(n, zb, to),
            dst_ref=other[n].at[dy - 1, zb],
            send_sem=col_send.at[n, zb, dy],
            recv_sem=col_recv.at[n, zb, dy],
            device_id=(fo, z, to, x, c),
            device_id_type=MESH_ID,
        )

    def load(n, zb):
        return pltpu.make_async_copy(view(n, zb, y), mine[n].at[zb], load_sem.at[n, zb])

    order = [fi_n - 1 - k // 2 if k % 2 == 0 else k // 2 for k in range(fi_n)]
    for zb in order:
        for n in range(count):
            for dy in range(1, ctx_n):
                across(n, zb, dy).start()
            load(n, zb).start()

    def line(n, side, target):
        at = jnp.where(target == (z + 1 if side == 0 else z - 1), fi_n, target) if side == 1 else target
        return pltpu.make_async_remote_copy(
            src_ref=mine[n].at[target],
            dst_ref=coming[n].at[at],
            send_sem=line_send.at[n, side, target],
            recv_sem=line_recv.at[n, side, target],
            device_id=(fo, z + 1 if side == 0 else z - 1, y, x, c),
            device_id_type=MESH_ID,
        )

    def came(n, side, target, at):
        pltpu.make_async_remote_copy(
            src_ref=mine[n].at[target],
            dst_ref=coming[n].at[at],
            send_sem=line_send.at[n, side, target],
            recv_sem=line_recv.at[n, side, target],
            device_id=(fo, z, y, x, c),
            device_id_type=MESH_ID,
        ).wait_recv()

    def ready(n, target):
        load(n, target).wait()
        for dy in range(1, ctx_n):
            across(n, target, dy).wait_recv()

    def add(n, target, use, store):
        a = mine[n].shape[1]
        tile = math.gcd(a, 64)

        def rows(step, carry):
            at = pl.ds(pl.multiple_of(step * tile, tile), tile)
            summed = mine[n][target, at, :].astype(F32)
            for dy in range(1, ctx_n):
                summed = summed + other[n][dy - 1, target, at, :].astype(F32)
            for slot in use:
                summed = summed + coming[n][slot, at, :].astype(F32)
            store(at, summed.astype(BF16))
            return carry

        lax.fori_loop(0, a // tile, rows, 0)

    for step in range(fi_n - 1):
        for n in range(count):
            for side in (0, 1):
                target = fi_n - 1 - step if side == 0 else step
                passes = (z < target) if side == 0 else (z > target)
                inner = (z > 0) if side == 0 else (z < fi_n - 1)

                def back(at, values, n=n, target=target):
                    mine[n][target, at, :] = values

                @pl.when(passes & inner)
                def _():
                    ready(n, target)
                    came(n, side, target, target)
                    add(n, target, (target,), back)
                    line(n, side, target).start()

                @pl.when(passes & jnp.logical_not(inner))
                def _():
                    ready(n, target)
                    add(n, target, (), back)
                    line(n, side, target).start()

    for n in range(count):
        ready(n, z)

        def out(at, values, n=n):
            if kinds[n] == "share":
                a = mine[n].shape[1]
                outs[n][q, at, :] = values
            elif kinds[n] == "sum":
                tiny[q, at, :] = values
            else:
                outs[n][at, :] = values

        @pl.when(z > 0)
        def _():
            came(n, 0, z, z)

        @pl.when(z < fi_n - 1)
        def _():
            came(n, 1, z, fi_n)

        @pl.when((z > 0) & (z < fi_n - 1))
        def _():
            add(n, z, (z, fi_n), out)

        @pl.when((z == 0) & (z < fi_n - 1))
        def _():
            add(n, z, (fi_n,), out)

        @pl.when((z > 0) & (z == fi_n - 1))
        def _():
            add(n, z, (z,), out)

        @pl.when((z == 0) & (z == fi_n - 1))
        def _():
            add(n, z, (), out)

        if kinds[n] in ("share", "sum"):
            held = outs[n] if kinds[n] == "share" else tiny
            for step in range(1, tp_n):
                peer = lax.rem(q + step, tp_n)
                pltpu.make_async_remote_copy(
                    src_ref=held.at[q],
                    dst_ref=held.at[q],
                    send_sem=tp_send.at[n, step],
                    recv_sem=tp_recv.at[n, step],
                    device_id=(fo, z, y, peer // tpc_n, lax.rem(peer, tpc_n)),
                    device_id_type=MESH_ID,
                ).start()

    for j in range(extra):
        for dx in range(1, tpx_n):
            owner = lax.rem(x + tpx_n - dx, tpx_n) * tpc_n + c
            pltpu.make_async_remote_copy(
                src_ref=quarters[j],
                dst_ref=slab(j, owner),
                send_sem=x_send.at[j, dx],
                recv_sem=x_recv.at[j, dx],
                device_id=(fo, z, y, x, c),
                device_id_type=MESH_ID,
            ).wait_recv()
            for dc in range(1, tpc_n):
                to_core(j, dx, dc).start()

    for n in range(count):
        if kinds[n] in ("share", "sum"):
            held = outs[n] if kinds[n] == "share" else tiny
            for step in range(1, tp_n):
                origin = lax.rem(q + tp_n - step, tp_n)
                copy = pltpu.make_async_remote_copy(
                    src_ref=held.at[q],
                    dst_ref=held.at[origin],
                    send_sem=tp_send.at[n, step],
                    recv_sem=tp_recv.at[n, step],
                    device_id=(fo, z, y, x, c),
                    device_id_type=MESH_ID,
                )
                copy.wait_send()
                copy.wait_recv()
            if kinds[n] == "sum":
                summed = tiny[0].astype(F32)
                for k in range(1, tp_n):
                    summed = summed + tiny[k].astype(F32)
                outs[n][...] = summed.astype(BF16)
        for target in range(fi_n):
            for dy in range(1, ctx_n):
                across(n, target, dy).wait_send()
            for side in (0, 1):

                @pl.when((z < target) if side == 0 else (z > target))
                def _():
                    line(n, side, target).wait_send()

    for j in range(extra):
        keep(j).wait()
        for dx in range(tpx_n):
            if dx > 0:
                to_chip(j, dx).wait_send()
            for dc in range(1, tpc_n):
                to_core(j, dx, dc).wait_send()
                owner = lax.rem(x + tpx_n - dx, tpx_n) * tpc_n + lax.rem(c + tpc_n - dc, tpc_n)
                pltpu.make_async_remote_copy(
                    src_ref=quarters[j],
                    dst_ref=slab(j, owner),
                    send_sem=c_send.at[j, dx, dc],
                    recv_sem=c_recv.at[j, dx, dc],
                    device_id=(fo, z, y, x, c),
                    device_id_type=MESH_ID,
                ).wait_recv()


def finish(sizes, kinds, parts, quarters, collective_id):
    fi_n, ctx_n, tpx_n, tpc_n = (sizes[n] for n in ("fi", "ctx", "tpx", "tpc"))
    tp_n = tpx_n * tpc_n
    blocks = fi_n * ctx_n
    count, extra = len(kinds), len(quarters)
    own, shapes = [], []
    sum_shape = (16, 256)
    for kind, part in zip(kinds, parts):
        a, b = part.shape
        if kind == "col":
            own.append((a, b // blocks))
            shapes.append(own[-1])
        elif kind == "share":
            own.append((a // (blocks * tp_n), b))
            shapes.append((tp_n,) + own[-1])
        else:
            own.append((a // blocks, b))
            shapes.append(own[-1])
        if kind == "sum":
            sum_shape = own[-1]
    wide = [(v.shape[0], v.shape[1] * tp_n) for v in quarters]
    hbm = pl.BlockSpec(memory_space=pl.ANY)
    vmem = pl.BlockSpec(memory_space=pltpu.VMEM)
    some = max(extra, 1)
    return pl.pallas_call(
        functools.partial(finish_body, sizes, tuple(kinds), extra),
        out_shape=tuple(jax.ShapeDtypeStruct(s, BF16) for s in shapes + wide),
        in_specs=[hbm] * (count + extra),
        out_specs=tuple([vmem] * count + [hbm] * extra),
        scratch_shapes=[pltpu.VMEM((fi_n,) + s, BF16) for s in own]
        + [pltpu.VMEM((max(ctx_n - 1, 1), fi_n) + s, BF16) for s in own]
        + [pltpu.VMEM((fi_n + 1,) + s, BF16) for s in own]
        + [
            pltpu.VMEM((tp_n,) + sum_shape, BF16),
            pltpu.SemaphoreType.DMA((count, fi_n)),
            pltpu.SemaphoreType.DMA((count, fi_n, ctx_n)),
            pltpu.SemaphoreType.DMA((count, fi_n, ctx_n)),
            pltpu.SemaphoreType.DMA((count, 2, fi_n)),
            pltpu.SemaphoreType.DMA((count, 2, fi_n)),
            pltpu.SemaphoreType.DMA((count, tp_n)),
            pltpu.SemaphoreType.DMA((count, tp_n)),
            pltpu.SemaphoreType.DMA((some,)),
            pltpu.SemaphoreType.DMA((some, tpx_n)),
            pltpu.SemaphoreType.DMA((some, tpx_n)),
            pltpu.SemaphoreType.DMA((some, tpx_n, tpc_n)),
            pltpu.SemaphoreType.DMA((some, tpx_n, tpc_n)),
        ],
        compiler_params=pltpu.CompilerParams(
            collective_id=collective_id, has_side_effects=True, vmem_limit_bytes=48 << 20
        ),
        cost_estimate=pl.CostEstimate(flops=0, bytes_accessed=100_000_000, transcendentals=0),
        name="finish",
    )(*parts, *quarters)


def attend_body(place_ref, q_ref, kv_ref, rope_ref, out_ref, log_ref):
    block_rows, key_count = q_ref.shape[0], kv_ref.shape[0]
    first = place_ref[0] + pl.program_id(1) * block_rows
    keys = jnp.concatenate([kv_ref[:, :NOPE], rope_ref[...]], axis=1)
    scores = dot_nt(q_ref[...], keys)
    row = first + lax.broadcasted_iota(jnp.int32, (block_rows, 1), 0)
    limit = jnp.maximum(row, place_ref[1] - 1)
    key = lax.broadcasted_iota(jnp.int32, (block_rows, key_count), 1)
    scores = jnp.where(key <= limit, scores, -1e30)
    top = jnp.max(scores, axis=1, keepdims=True)
    exponent = jnp.exp(scores - top)
    row_total = jnp.sum(exponent, axis=1, keepdims=True)
    summed = jnp.dot(exponent.astype(BF16), kv_ref[:, NOPE:], preferred_element_type=F32)
    out_ref[...] = (summed / row_total).astype(BF16)
    log_total = jnp.broadcast_to(top + jnp.log(row_total), (block_rows, 128))
    log_ref[0] = log_total.T[:1]

def attend(place, query, key_value, rope, block_rows):
    rows, key_count = query.shape[0], key_value.shape[0]
    heads = query.shape[1] // HEAD
    return pl.pallas_call(
        attend_body,
        out_shape=(jax.ShapeDtypeStruct((rows, heads * VDIM), BF16), jax.ShapeDtypeStruct((heads, 1, rows), F32)),
        grid_spec=pltpu.PrefetchScalarGridSpec(
            num_scalar_prefetch=1,
            grid=(heads, rows // block_rows),
            in_specs=[
                pl.BlockSpec((block_rows, HEAD), lambda h, i, s: (i, h)),
                pl.BlockSpec((key_count, HEAD), lambda h, i, s: (0, h)),
                pl.BlockSpec((key_count, NOPE), lambda h, i, s: (0, 0)),
            ],
            out_specs=[
                pl.BlockSpec((block_rows, VDIM), lambda h, i, s: (i, h)),
                pl.BlockSpec((1, 1, block_rows), lambda h, i, s: (h, 0, i)),
            ],
        ),
        compiler_params=pltpu.CompilerParams(vmem_limit_bytes=48 << 20),
        cost_estimate=pl.CostEstimate(flops=4 * rows * key_count * heads * HEAD, bytes_accessed=20_000_000, transcendentals=rows * key_count * heads),
        name="attend",
    )(place, query, key_value, rope)

def attend_back_body(place_ref, q_ref, kv_ref, rope_ref, dout_ref, log_ref, table_ref, dq_ref, dkv_ref, drope_ref, keys_acc, values_acc):
    block_rows, key_count = q_ref.shape[0], kv_ref.shape[0]
    head, step = pl.program_id(0), pl.program_id(1)
    first = place_ref[0] + step * block_rows
    keys = jnp.concatenate([kv_ref[:, :NOPE], rope_ref[...]], axis=1)
    scores = dot_nt(keys, q_ref[...])
    row = first + lax.broadcasted_iota(jnp.int32, (1, block_rows), 1)
    limit = jnp.maximum(row, place_ref[1] - 1)
    key = lax.broadcasted_iota(jnp.int32, (key_count, block_rows), 0)
    soft = jnp.exp(jnp.where(key <= limit, scores, -1e30) - log_ref[0])
    soft_grad = dot_nt(kv_ref[:, NOPE:], dout_ref[...])
    mean = jnp.sum(soft * soft_grad, axis=0, keepdims=True)
    score_grad = (soft * (soft_grad - mean)).astype(BF16)
    values = jnp.dot(soft.astype(BF16), dout_ref[...], preferred_element_type=F32)
    keys_grad = jnp.dot(score_grad, q_ref[...], preferred_element_type=F32)
    dq_ref[...] = (dot_tn(score_grad, keys) * table_ref[...]).astype(BF16)

    @pl.when(step == 0)
    def _():
        keys_acc[...] = keys_grad
        values_acc[...] = values

    @pl.when(step > 0)
    def _():
        keys_acc[...] += keys_grad
        values_acc[...] += values

    @pl.when(step == pl.num_programs(1) - 1)
    def _():
        dkv_ref[...] = jnp.concatenate([keys_acc[:, :NOPE], values_acc[...]], axis=1).astype(BF16)

        @pl.when(head == 0)
        def _():
            drope_ref[...] = keys_acc[:, NOPE:]

        @pl.when(head > 0)
        def _():
            drope_ref[...] += keys_acc[:, NOPE:]

def attend_back(place, query, key_value, rope, dout, log_total, table, block_rows):
    rows, key_count = query.shape[0], key_value.shape[0]
    heads = query.shape[1] // HEAD
    return pl.pallas_call(
        attend_back_body,
        out_shape=(jax.ShapeDtypeStruct((rows, heads * HEAD), BF16), jax.ShapeDtypeStruct((key_count, heads * HEAD), BF16), jax.ShapeDtypeStruct((key_count, NOPE), F32)),
        grid_spec=pltpu.PrefetchScalarGridSpec(
            num_scalar_prefetch=1,
            grid=(heads, rows // block_rows),
            in_specs=[
                pl.BlockSpec((block_rows, HEAD), lambda h, i, s: (i, h)),
                pl.BlockSpec((key_count, HEAD), lambda h, i, s: (0, h)),
                pl.BlockSpec((key_count, NOPE), lambda h, i, s: (0, 0)),
                pl.BlockSpec((block_rows, VDIM), lambda h, i, s: (i, h)),
                pl.BlockSpec((1, 1, block_rows), lambda h, i, s: (h, 0, i)),
                pl.BlockSpec((block_rows, HEAD), lambda h, i, s: (i, 0)),
            ],
            out_specs=[
                pl.BlockSpec((block_rows, HEAD), lambda h, i, s: (i, h)),
                pl.BlockSpec((key_count, HEAD), lambda h, i, s: (0, h)),
                pl.BlockSpec((key_count, NOPE), lambda h, i, s: (0, 0)),
            ],
            scratch_shapes=[pltpu.VMEM((key_count, HEAD), F32), pltpu.VMEM((key_count, VDIM), F32)],
        ),
        compiler_params=pltpu.CompilerParams(vmem_limit_bytes=56 << 20),
        cost_estimate=pl.CostEstimate(flops=10 * rows * key_count * heads * HEAD, bytes_accessed=40_000_000, transcendentals=rows * key_count * heads),
        name="attend_back",
    )(place, query, key_value, rope, dout, log_total, table)


def build(sizes):
    fo_n, fi_n, ctx_n, tpx_n, tpc_n = (sizes[name] for name in ("fo", "fi", "ctx", "tpx", "tpc"))
    tp_n = tpx_n * tpc_n
    row_shards = fo_n * fi_n * ctx_n
    plane_experts = ctx_n * tpx_n
    z_part = fi_n // tpc_n

    def expert_weights(gate, up, down):
        local = jnp.stack([gate.transpose(0, 2, 1), up.transpose(0, 2, 1), down], axis=1)
        return lax.all_gather(local, "fo", axis=0) if fo_n > 1 else local[None]

    def shard_of(weight):
        return lax.all_gather(weight, "fo", axis=0) if fo_n > 1 else weight[None]

    def fo_sum(part, kind):
        if fo_n == 1:
            return part
        if kind == "col":
            a = part.shape[0]
            part = part.reshape(a, fo_n, -1)
            return lax.psum_scatter(part, "fo", scatter_dimension=1, tiled=True).reshape(a, -1)
        return lax.psum_scatter(part, "fo", scatter_dimension=0, tiled=True)

    def split_expert_grads(grads):
        a, b = grads[0].shape[0] // tp_n, grads[0].shape[1] // row_shards
        parts = jnp.stack(
            [
                grad.astype(BF16)
                .reshape(tpx_n, tpc_n, a, fo_n, fi_n, ctx_n, b)
                .transpose(1, 3, 4, 5, 0, 2, 6)
                .reshape(tpc_n, fo_n, fi_n * ctx_n * tpx_n, a, b)
                for grad in grads
            ],
            axis=3,
        )
        return lax.psum_scatter(parts, "tpc", scatter_dimension=0, tiled=True)[0]

    def own_expert_grads(mine):
        got = lax.all_to_all(mine, CHIPS, split_axis=1, concat_axis=1, tiled=True)
        if fo_n > 1:
            got = lax.psum_scatter(got, "fo", scatter_dimension=0, tiled=True)
        got = got[0].astype(F32)
        return (got[:, 0].transpose(0, 2, 1), got[:, 1].transpose(0, 2, 1), got[:, 2])

    def shards(
        tokens,
        out_grad,
        routes,
        slot_index,
        prefix,
        attn_gain,
        query_weight,
        latent_down,
        latent_gain,
        latent_up,
        out_weight,
        moe_gain,
        router_weight,
        shared_gate,
        shared_up,
        shared_down,
        expert_gate,
        expert_up,
        expert_down,
    ):
        row_count, width = tokens.shape
        expert_count = expert_gate.shape[0]
        capacity = row_count * routes.shape[1] // expert_count
        quarter = width // tp_n
        tp_index = lax.axis_index(TP)
        own_expert = lax.axis_index(CHIPS)
        plane_base = lax.axis_index("fi") * plane_experts

        def columns(values):
            return lax.dynamic_slice_in_dim(values, tp_index * quarter, quarter, values.ndim - 1)

        depth = latent_down.shape[0]
        down_width = latent_down.shape[1]

        def turned(weight):
            half = weight.shape[-1] // 2
            return jnp.concatenate([-weight[..., half:], weight[..., :half]], axis=-1)

        small = jnp.concatenate(
            [
                latent_down,
                turned(latent_down[:, KVR:]),
                attn_gain[:, None],
                moe_gain[:, None],
                jnp.pad(latent_gain, (0, depth - latent_gain.shape[0]))[:, None],
                router_weight,
            ],
            axis=1,
        )
        used = small.shape[1]
        small = jnp.pad(small, ((0, 0), (0, -used % 128)))
        small, query_full, up_full, out_full = collect(
            sizes,
            ("share", "row", "row", "col"),
            [shard_of(w) for w in (small, query_weight, latent_up, out_weight)],
            None,
            4,
        )
        wide_down = small[:, : down_width + ROPE]
        down_full = small[:, :down_width]
        gain_at = down_width + ROPE
        gain_one = small[:, gain_at].astype(F32)
        gain_two = small[:, gain_at + 1].astype(F32)
        gain_latent = (
            small[:, gain_at + 2]
            .reshape(row_shards, depth)[:, : latent_gain.shape[0]]
            .reshape(-1)
            .astype(F32)
        )
        router_full = small[:, gain_at + 3 : used]

        keys = jnp.where(slot_index < capacity, routes * capacity + slot_index, -1)
        keys_all = lax.all_gather(keys, ("fi", "ctx"), axis=0).reshape(
            fi_n, ctx_n, row_count, routes.shape[1]
        )

        def slots_of(key_rows, expert_ids):
            rel = key_rows[..., None, :, :] - expert_ids[:, None, None] * capacity
            return jnp.max(jnp.where((rel >= 0) & (rel < capacity), rel, -1), axis=-1)

        slot_ids = jnp.arange(capacity, dtype=jnp.int32)
        keys_column = lax.dynamic_index_in_dim(keys_all, lax.axis_index("ctx"), 1, keepdims=False)
        plane_slots = slots_of(
            keys_column, plane_base + jnp.arange(plane_experts, dtype=jnp.int32)
        )
        token_slots = plane_slots.transpose(0, 2, 1)
        own_slots = slots_of(keys, jnp.arange(expert_count, dtype=jnp.int32))

        def dispatch(part_rows, collective_id):
            got = dispatch_rows(sizes, part_rows, plane_slots, capacity, collective_id)
            return got.reshape(-1, width)

        def give_back(rows, collective_id):
            rows = rows.reshape(z_part, ctx_n, capacity, width)
            return give_back_rows(sizes, rows, token_slots, collective_id)

        slot_grads = dispatch(columns(out_grad), 0)
        (
            shared_gate_full,
            shared_up_full,
            shared_down_full,
            gate_full,
            expert_up_full,
            down_weight,
        ) = collect(
            sizes,
            ("row", "row", "col"),
            [shard_of(w) for w in (shared_gate, shared_up, shared_down)],
            expert_weights(expert_gate, expert_up, expert_down),
            5,
        )

        head_count = query_full.shape[1] // (NOPE + ROPE)
        hidden = tokens.astype(F32)
        scale_one = rms_scale(hidden)
        normed_one = hidden * scale_one
        normed_in = (normed_one * gain_one).astype(BF16)
        seq_index = lax.axis_index(("fo", "fi"))
        prefix_len = lax.dynamic_index_in_dim(prefix, seq_index, keepdims=False)
        row_offset = lax.axis_index("ctx") * row_count
        query_pos = row_offset + jnp.arange(row_count, dtype=jnp.int32)
        cos_table, sin_table = rotation_tables(query_pos, ROPE // 2)
        score_scale = (NOPE + ROPE) ** (-0.5)
        cos_wide = jnp.concatenate([cos_table, cos_table], axis=1)
        sin_wide = jnp.concatenate([sin_table, sin_table], axis=1)
        table = score_scale * jnp.concatenate(
            [jnp.ones((row_count, NOPE), F32), cos_wide, sin_wide], axis=1
        )

        latent_raw = dot(normed_in, wide_down)
        latent_part = latent_raw[:, :KVR]
        scale_latent = rms_scale(latent_part)
        normed_latent = latent_part * scale_latent
        latent = (normed_latent * gain_latent).astype(BF16)
        key_rope = (
            latent_raw[:, KVR : KVR + ROPE] * cos_wide + latent_raw[:, KVR + ROPE :] * sin_wide
        ).astype(BF16)
        both = lax.all_gather(
            jnp.concatenate([latent, key_rope, key_rope], axis=1), "ctx", axis=0, tiled=True
        )
        latent_all, rope_all = both[:, :KVR], both[:, KVR:]
        query_heads = query_full.reshape(width, head_count, NOPE + ROPE)
        query_wide = jnp.concatenate(
            [query_heads, turned(query_heads[..., NOPE:])], axis=-1
        ).reshape(width, head_count * HEAD)
        query_in = (
            dot(normed_in, query_wide).reshape(row_count, head_count, HEAD) * table[:, None]
        ).astype(BF16).reshape(row_count, head_count * HEAD)
        key_value = dot(latent_all, up_full).astype(BF16)
        place = jnp.stack([row_offset, prefix_len]).astype(jnp.int32)
        block_rows = min(256, row_count)
        attended, log_totals = attend(place, query_in, key_value, rope_all, block_rows)

        def tp_scatter(partial):
            parts = partial.astype(BF16).reshape(row_count, tp_n, quarter).transpose(1, 0, 2)
            return lax.psum_scatter(parts, TP, scatter_dimension=0, tiled=True)[0].astype(F32)

        def tp_gather(part_rows):
            got = lax.all_gather(part_rows, TP, axis=0)
            return got.transpose(1, 0, 2).reshape(row_count, width)

        residual = columns(tokens).astype(F32) + tp_scatter(dot(attended, out_full))
        scale_two = lax.rsqrt(
            lax.psum(jnp.sum(residual * residual, axis=-1, keepdims=True), TP) / width + EPSILON
        )
        normed_two = residual * scale_two
        gain_two_part = columns(gain_two[None])
        mid_part = (normed_two * gain_two_part).astype(BF16)

        slot_rows = dispatch(mid_part, 1)
        normed_mid = tp_gather(mid_part)

        logits = dot(normed_mid, router_full)
        router_prob = jax.nn.softmax(logits, axis=-1)
        slot_prob = jax.nn.softmax(dot(slot_rows, router_full), axis=-1)
        slot_gate = lax.dynamic_slice_in_dim(slot_prob, own_expert, 1, 1)

        gate_pre = dot(normed_mid, shared_gate_full)
        up_pre = dot(normed_mid, shared_up_full)
        shared_dact = dot_nt(out_grad, shared_down_full)
        shared_silu, shared_slope = silu_parts(gate_pre)
        shared_act = (shared_silu * up_pre).astype(BF16)
        shared_dgate = (shared_dact * up_pre * shared_slope).astype(BF16)
        shared_dup = (shared_dact * shared_silu).astype(BF16)
        mid_shared = tp_scatter(
            dot_nt(shared_dgate, shared_gate_full) + dot_nt(shared_dup, shared_up_full)
        )
        out_shared = tp_scatter(dot(shared_act, shared_down_full))

        expert_dact_raw = dot_nt(slot_grads, down_weight)
        expert_gpre = dot_nt(slot_rows, gate_full)
        expert_upre = dot_nt(slot_rows, expert_up_full)
        expert_silu, expert_slope = silu_parts(expert_gpre)
        expert_act_wide = expert_silu * expert_upre
        expert_act = expert_act_wide.astype(BF16)
        slot_gate_grad = jnp.sum(expert_act.astype(F32) * expert_dact_raw, axis=-1)
        expert_dact = expert_dact_raw * slot_gate
        expert_dgate = (expert_dact * expert_upre * expert_slope).astype(BF16)
        expert_dup = (expert_dact * expert_silu).astype(BF16)
        slot_drows = dot(expert_dgate, gate_full) + dot(expert_dup, expert_up_full)
        mid_routed = give_back(slot_drows.astype(BF16), 2)
        gate_back = lax.all_gather(
            slot_gate_grad.reshape(z_part, ctx_n, capacity), CHIPS + ("tpc",), axis=0
        ).reshape(expert_count, fi_n, ctx_n, capacity)
        gate_back = lax.dynamic_index_in_dim(gate_back, lax.axis_index("fi"), 1, keepdims=False)
        gate_back = lax.dynamic_index_in_dim(gate_back, lax.axis_index("ctx"), 1, keepdims=False)
        prob_grad = jnp.sum(
            jnp.where(own_slots[:, None, :] == slot_ids[None, :, None], gate_back[:, :, None], 0.0),
            axis=1,
        ).T
        logit_grad = (
            router_prob * (prob_grad - jnp.sum(router_prob * prob_grad, axis=-1, keepdims=True))
        ).astype(BF16)

        slot_dout = (slot_grads.astype(F32) * slot_gate).astype(BF16)
        routed_grads = split_expert_grads(
            (
                dot_tn(expert_dgate, slot_rows),
                dot_tn(expert_dup, slot_rows),
                dot_tn(expert_act, slot_dout),
            )
        )
        sdown_grad = dot_tn(shared_act, out_grad)
        sgate_grad = dot_tn(normed_mid, shared_dgate)
        sup_grad = dot_tn(normed_mid, shared_dup)

        mid_total = mid_shared + mid_routed + dot_nt(logit_grad, columns(router_full.T).T)
        gain_two_grad = jnp.sum(mid_total * normed_two, axis=0)
        dn_two = mid_total * gain_two_part
        dot_two = lax.psum(jnp.sum(dn_two * normed_two, axis=-1, keepdims=True), TP) / width
        residual_grad = columns(out_grad).astype(F32) + scale_two * (dn_two - normed_two * dot_two)
        attn_dout = tp_gather(residual_grad.astype(BF16))

        out_weight_grad = dot_tn(attended, attn_dout)
        attended_grad = dot_nt(attn_dout, out_full).astype(BF16)
        attended_grad, routed_grads = lax.optimization_barrier((attended_grad, routed_grads))
        egate_grad, eup_grad, edown_grad = own_expert_grads(routed_grads)
        query_grad, kv_grad, rope_grad = attend_back(
            place, query_in, key_value, rope_all, attended_grad, log_totals, table,
            min(512, row_count),
        )
        late_act, query_grad = lax.optimization_barrier((expert_act, query_grad))
        expert_out = (dot(late_act, down_weight) * slot_gate).astype(BF16)
        output = residual + out_shared + give_back(expert_out, 3)
        up_grad = dot_tn(latent_all, kv_grad)
        latent_grad = dot_nt(kv_grad, up_full)
        query_wide_grad = dot_tn(normed_in, query_grad).reshape(width, head_count, HEAD)
        query_weight_grad = jnp.concatenate(
            [
                query_wide_grad[..., :NOPE],
                query_wide_grad[..., NOPE : NOPE + ROPE] - turned(query_wide_grad[..., NOPE + ROPE :]),
            ],
            axis=-1,
        ).reshape(width, head_count * (NOPE + ROPE))
        input_part = tp_scatter(dot_nt(query_grad, query_wide))
        both_grad = lax.psum_scatter(
            jnp.concatenate([latent_grad, rope_grad], axis=1).astype(BF16),
            "ctx",
            scatter_dimension=0,
            tiled=True,
        )
        both_grad = lax.psum(both_grad, TP).astype(F32)
        latent_own = both_grad[:, :KVR]
        rope_own = both_grad[:, KVR : KVR + ROPE] + both_grad[:, KVR + ROPE :]
        gain_latent_grad = jnp.sum(latent_own * normed_latent, axis=0)
        latent_raw_grad = norm_back(latent_own * gain_latent, normed_latent, scale_latent)
        down_out_grad = jnp.concatenate(
            [latent_raw_grad, rotate(rope_own, cos_table, -sin_table)], axis=-1
        ).astype(BF16)
        down_grad = dot_tn(normed_in, down_out_grad)
        input_total = input_part + dot_nt(
            down_out_grad, lax.dynamic_slice_in_dim(down_full, tp_index * quarter, quarter, 0)
        )
        normed_one_part = columns(normed_one)
        gain_one_grad = jnp.sum(input_total * normed_one_part, axis=0)
        dn_one = input_total * columns(gain_one[None])
        dot_one = lax.psum(jnp.sum(dn_one * normed_one_part, axis=-1, keepdims=True), TP) / width
        token_grad = residual_grad + scale_one * (dn_one - normed_one_part * dot_one)
        router_grad = dot_tn(normed_mid, logit_grad)
        pack_grad = jnp.concatenate([down_grad, router_grad], axis=1)
        pack_used = pack_grad.shape[1]
        pack_grad = jnp.pad(pack_grad, ((0, 0), (0, -pack_used % 128)))
        gains = jnp.stack([gain_one_grad, gain_two_grad])
        gains = lax.dynamic_update_slice_in_dim(
            jnp.zeros((2, width), F32), gains, tp_index * quarter, 1
        )
        latent_rows = jnp.pad(
            gain_latent_grad.reshape(row_shards, -1),
            ((0, 0), (0, depth - latent_gain.shape[0])),
        ).reshape(1, width)
        gains = jnp.concatenate([gains, latent_rows * (tp_index == 0).astype(F32)], axis=0)
        gains = jnp.pad(
            gains.reshape(3, row_shards, depth).transpose(1, 0, 2), ((0, 0), (0, 13), (0, 0))
        ).reshape(row_shards * 16, depth)
        kinds = ("share", "sum", "row", "row", "col", "row", "row", "col")
        partials = (
            pack_grad,
            gains,
            query_weight_grad,
            up_grad,
            out_weight_grad,
            sgate_grad,
            sup_grad,
            sdown_grad,
        )
        done = finish(
            sizes,
            kinds,
            [fo_sum(part.astype(BF16), kind) for part, kind in zip(partials, kinds)],
            [output.astype(BF16), token_grad.astype(BF16)],
            6,
        )
        pack_own = done[0].reshape(depth, -1).astype(F32)
        gains_own = done[1].astype(F32)
        query_weight_grad, up_grad, out_weight_grad, sgate_grad, sup_grad, sdown_grad = (
            part.astype(F32) for part in done[2:8]
        )
        output, token_grad = done[8], done[9].astype(F32)
        return (
            output,
            token_grad,
            gains_own[0],
            query_weight_grad,
            pack_own[:, :down_width],
            gains_own[2, : latent_gain.shape[0]],
            up_grad,
            out_weight_grad,
            gains_own[1],
            pack_own[:, down_width:pack_used],
            sgate_grad,
            sup_grad,
            sdown_grad,
            egate_grad,
            eup_grad,
            edown_grad,
        )

    return shards


EXPERTS = 16


def solution(mesh):
    ctx_n, tp_n = mesh.shape["ctx"], mesh.shape["tp"]
    tpc_n = 2
    tpx_n = tp_n // tpc_n
    fi_n = EXPERTS // (ctx_n * tpx_n)
    sizes = {
        "fo": mesh.shape["fsdp"] // fi_n,
        "fi": fi_n,
        "ctx": ctx_n,
        "tpx": tpx_n,
        "tpc": tpc_n,
    }
    fine = Mesh(mesh.devices.reshape(tuple(sizes.values())), tuple(sizes))
    rows = P(ROWS)
    rows_two = P(ROWS, None)
    rows_tp = P(ROWS, TP)
    tp_rows = P(TP, ROWS)
    wide_in = P(None, ROWS, TP)
    wide_out = P(None, TP, ROWS)
    weights = (
        rows,
        rows_tp,
        rows_two,
        rows,
        rows_tp,
        tp_rows,
        rows,
        rows_two,
        rows_tp,
        rows_tp,
        tp_rows,
        wide_in,
        wide_in,
        wide_out,
    )
    return jax.shard_map(
        build(sizes),
        mesh=fine,
        in_specs=(rows_two, rows_two, rows_two, rows_two, P()) + weights,
        out_specs=(rows_two, rows_two) + weights,
        check_vma=False,
    )
```

```python
import functools
import math

import jax
import jax.numpy as jnp
from jax import lax
from jax.experimental import pallas as pl
from jax.experimental.pallas import tpu as pltpu
from jax.sharding import Mesh
from jax.sharding import PartitionSpec as P

NOPE = 128
ROPE = 64
KVR = 512
VDIM = 128
HEAD = 256

EPSILON = 1e-06
THETA_BASE = 10000.0
F32 = jnp.float32
BF16 = jnp.bfloat16
MESH_ID = pl.DeviceIdType.MESH

ROWS = ("fo", "fi", "ctx")
TP = ("tpx", "tpc")
PLANE = ("ctx", "tpx", "tpc")
CHIPS = ("fi", "ctx", "tpx")


def rotation_tables(positions, half_width):
    freq_table = jnp.exp(jnp.arange(half_width, dtype=F32) * (-math.log(THETA_BASE) / half_width))
    angle_table = positions.astype(F32)[:, None] * freq_table[None, :]
    return (jnp.cos(angle_table), jnp.sin(angle_table))


def rotate(values, cos_table, sin_table):
    half_width = values.shape[-1] // 2
    first_half = values[..., :half_width]
    second_half = values[..., half_width:]
    return jnp.concatenate(
        [
            first_half * cos_table - second_half * sin_table,
            second_half * cos_table + first_half * sin_table,
        ],
        axis=-1,
    )


def silu_parts(values):
    sigma = jax.nn.sigmoid(values)
    return (values * sigma, sigma * (1.0 + values * (1.0 - sigma)))


def rms_scale(values):
    return lax.rsqrt(jnp.mean(values * values, axis=-1, keepdims=True) + EPSILON)


def norm_back(grad_normed, normed, scale_rows):
    return scale_rows * (
        grad_normed - normed * jnp.mean(grad_normed * normed, axis=-1, keepdims=True)
    )


def dot(left, right):
    return jnp.dot(left, right, preferred_element_type=F32)


def dot_nt(left, right):
    return lax.dot_general(left, right, (((1,), (1,)), ((), ())), preferred_element_type=F32)


def dot_tn(left, right):
    return lax.dot_general(left, right, (((0,), (0,)), ((), ())), preferred_element_type=F32)


def ein(spec, left, right):
    return jnp.einsum(spec, left, right, preferred_element_type=F32)


def plane_place(sizes):
    tpx_n, tpc_n = sizes["tpx"], sizes["tpc"]
    fo, z, y, x, c = (lax.axis_index(name) for name in ("fo", "fi", "ctx", "tpx", "tpc"))
    own = (y * tpx_n + x) * tpc_n + c

    def device(index, z_at=None):
        return (
            fo,
            z if z_at is None else z_at,
            index // (tpx_n * tpc_n),
            lax.rem(index // tpc_n, tpx_n),
            lax.rem(index, tpc_n),
        )

    return z, y, x, c, own, device


def greet_plane(sizes, z, own, device):
    fi_n = sizes["fi"]
    plane_n = sizes["ctx"] * sizes["tpx"] * sizes["tpc"]
    barrier = pltpu.get_barrier_semaphore()
    for step in range(1, plane_n):
        pl.semaphore_signal(
            barrier,
            inc=1,
            device_id=device(lax.rem(own + step, plane_n)),
            device_id_type=MESH_ID,
        )
    for near in (-1, 1):

        @pl.when((z + near >= 0) & (z + near < fi_n))
        def _():
            pl.semaphore_signal(
                barrier, inc=1, device_id=device(own, z + near), device_id_type=MESH_ID
            )

    sides = (z > 0).astype(jnp.int32) + (z < fi_n - 1).astype(jnp.int32)
    pl.semaphore_wait(barrier, plane_n - 1 + sides)


def dispatch_body(
    sizes,
    slots_ref,
    rows_ref,
    out_ref,
    held,
    picked,
    own_sem,
    line_send,
    line_recv,
    plane_send,
    plane_recv,
):
    fi_n, tpx_n, tpc_n = sizes["fi"], sizes["tpx"], sizes["tpc"]
    plane_n = sizes["ctx"] * tpx_n * tpc_n
    chips = sizes["ctx"] * tpx_n
    z_part = fi_n // tpc_n
    capacity, quarter = picked.shape[2:]
    tokens = held.shape[1]
    z, y, x, c, own, device = plane_place(sizes)
    greet_plane(sizes, z, own, device)
    columns = pl.ds(pl.multiple_of((x * tpc_n + c) * quarter, quarter), quarter)

    load = pltpu.make_async_copy(rows_ref, held.at[z], own_sem)
    load.start()
    load.wait()

    def line(side, step):
        block = z - step if side == 0 else z + step
        to = z + 1 if side == 0 else z - 1
        return block, to, pltpu.make_async_remote_copy(
            src_ref=held.at[block],
            dst_ref=held.at[block],
            send_sem=line_send.at[side, step],
            recv_sem=line_recv.at[side, step],
            device_id=device(own, to),
            device_id_type=MESH_ID,
        )

    def sends(side, step):
        block = z - step if side == 0 else z + step
        to = z + 1 if side == 0 else z - 1
        return (block >= 0) & (block < fi_n) & (to >= 0) & (to < fi_n)

    def plane_copy(block, chip):
        target = chip * tpc_n + block // z_part
        at = lax.rem(block, z_part)
        return pltpu.make_async_remote_copy(
            src_ref=picked.at[block, chip],
            dst_ref=out_ref.at[at, y, :, columns],
            send_sem=plane_send.at[block, chip],
            recv_sem=plane_recv.at[own, at],
            device_id=device(target),
            device_id_type=MESH_ID,
        )

    def keep_copy(block, chip):
        return pltpu.make_async_copy(
            picked.at[block, chip],
            out_ref.at[lax.rem(block, z_part), y, :, columns],
            plane_send.at[block, chip],
        )

    def at_home(block, chip):
        return chip * tpc_n + block // z_part == own

    def pick(block):
        def one(chip, carry):
            wanted = slots_ref[block, pl.ds(chip, 1), :]
            rank = lax.broadcasted_iota(jnp.int32, (capacity, tokens), 0)
            hits = jnp.where(rank == wanted, 1.0, 0.0).astype(BF16)
            picked[block, chip] = jnp.dot(
                hits, held[block], preferred_element_type=F32
            ).astype(BF16)

            @pl.when(at_home(block, chip))
            def _():
                keep_copy(block, chip).start()

            @pl.when(jnp.logical_not(at_home(block, chip)))
            def _():
                plane_copy(block, chip).start()

            return carry

        lax.fori_loop(0, chips, one, 0)

    for step in range(fi_n):
        for side in (0, 1):
            if step < fi_n - 1:

                @pl.when(sends(side, step))
                def _():
                    line(side, step)[2].start()

        if step == 0:
            pick(z)
        else:
            for side in (0, 1):
                block = z - step if side == 0 else z + step

                @pl.when((block >= 0) & (block < fi_n))
                def _():
                    pick(block)

        if step < fi_n - 1:
            for side in (0, 1):
                block = z - 1 - step if side == 0 else z + 1 + step

                @pl.when((block >= 0) & (block < fi_n))
                def _():
                    pltpu.make_async_remote_copy(
                        src_ref=held.at[block],
                        dst_ref=held.at[block],
                        send_sem=line_send.at[side, step],
                        recv_sem=line_recv.at[side, step],
                        device_id=device(own, z),
                        device_id_type=MESH_ID,
                    ).wait_recv()

    for step in range(fi_n - 1):
        for side in (0, 1):

            @pl.when(sends(side, step))
            def _():
                line(side, step)[2].wait_send()

    def settle(index, carry):
        block, chip = index // chips, lax.rem(index, chips)

        @pl.when(at_home(block, chip))
        def _():
            keep_copy(block, chip).wait()

        @pl.when(jnp.logical_not(at_home(block, chip)))
        def _():
            plane_copy(block, chip).wait_send()

        return carry

    lax.fori_loop(0, fi_n * chips, settle, 0)

    def arrive(index, carry):
        source, at = index // z_part, lax.rem(index, z_part)

        @pl.when(source != own)
        def _():
            pltpu.make_async_remote_copy(
                src_ref=picked.at[0, 0],
                dst_ref=out_ref.at[at, y, :, columns],
                send_sem=plane_send.at[0, 0],
                recv_sem=plane_recv.at[source, at],
                device_id=device(own),
                device_id_type=MESH_ID,
            ).wait_recv()

        return carry

    lax.fori_loop(0, plane_n * z_part, arrive, 0)


def dispatch_rows(sizes, part_rows, plane_slots, capacity, collective_id):
    tokens, quarter = part_rows.shape
    fi_n, ctx_n, tpx_n, tpc_n = (sizes[n] for n in ("fi", "ctx", "tpx", "tpc"))
    z_part, plane_n, chips = fi_n // tpc_n, ctx_n * tpx_n * tpc_n, ctx_n * tpx_n
    return pl.pallas_call(
        functools.partial(dispatch_body, sizes),
        out_shape=jax.ShapeDtypeStruct(
            (z_part, ctx_n, capacity, quarter * tpx_n * tpc_n), BF16
        ),
        in_specs=[
            pl.BlockSpec(memory_space=pltpu.VMEM),
            pl.BlockSpec(memory_space=pl.ANY),
        ],
        out_specs=pl.BlockSpec(memory_space=pl.ANY),
        scratch_shapes=[
            pltpu.VMEM((fi_n, tokens, quarter), BF16),
            pltpu.VMEM((fi_n, chips, capacity, quarter), BF16),
            pltpu.SemaphoreType.DMA,
            pltpu.SemaphoreType.DMA((2, fi_n)),
            pltpu.SemaphoreType.DMA((2, fi_n)),
            pltpu.SemaphoreType.DMA((fi_n, chips)),
            pltpu.SemaphoreType.DMA((plane_n, z_part)),
        ],
        compiler_params=pltpu.CompilerParams(
            collective_id=collective_id, has_side_effects=True, vmem_limit_bytes=40 << 20
        ),
        cost_estimate=pl.CostEstimate(
            flops=2 * fi_n * chips * capacity * tokens * quarter,
            bytes_accessed=100_000_000,
            transcendentals=0,
        ),
        name="dispatch",
    )(plane_slots, part_rows)


def give_back_body(sizes, gated, *refs):
    fi_n, tpx_n, tpc_n = sizes["fi"], sizes["tpx"], sizes["tpc"]
    plane_n = sizes["ctx"] * tpx_n * tpc_n
    chips = sizes["ctx"] * tpx_n
    z_part = fi_n // tpc_n
    slots_ref, rows_ref, refs = refs[0], refs[1], refs[2:]
    if gated:
        gates_ref, refs = refs[0], refs[1:]
    out_ref, refs = refs[0], refs[1:]
    if gated:
        gate_out, refs = refs[0], refs[1:]
    got, total, going, coming, plane_send, plane_recv, line_send, line_recv = refs[:8]
    if gated:
        gates_got, gate_total, gate_going, gate_coming = refs[8:12]
        gate_send, gate_recv, gate_line_send, gate_line_recv = refs[12:]
    capacity, quarter = got.shape[2:]
    tokens = total.shape[0]
    z, y, x, c, own, device = plane_place(sizes)
    greet_plane(sizes, z, own, device)
    tile = min(256, tokens)

    def piece(target, at):
        side = lax.rem(target, tpx_n * tpc_n)
        return rows_ref.at[
            at,
            target // (tpx_n * tpc_n),
            :,
            pl.ds(pl.multiple_of(side * quarter, quarter), quarter),
        ]

    def plane_copies(target, at):
        made = [
            pltpu.make_async_remote_copy(
                src_ref=piece(target, at),
                dst_ref=got.at[c * z_part + at, own // tpc_n],
                send_sem=plane_send.at[target, at],
                recv_sem=plane_recv.at[own, at],
                device_id=device(target),
                device_id_type=MESH_ID,
            )
        ]
        if gated:
            made.append(
                pltpu.make_async_remote_copy(
                    src_ref=gates_ref.at[at, target // (tpx_n * tpc_n)],
                    dst_ref=gates_got.at[c * z_part + at, own // tpc_n],
                    send_sem=gate_send.at[target, at],
                    recv_sem=gate_recv.at[own, at],
                    device_id=device(target),
                    device_id_type=MESH_ID,
                )
            )
        return made

    def keep_copies(at):
        made = [
            pltpu.make_async_copy(
                piece(own, at), got.at[c * z_part + at, own // tpc_n], plane_recv.at[own, at]
            )
        ]
        if gated:
            made.append(
                pltpu.make_async_copy(
                    gates_ref.at[at, y],
                    gates_got.at[c * z_part + at, own // tpc_n],
                    gate_recv.at[own, at],
                )
            )
        return made

    far_first = z < fi_n // 2
    for turn in range(z_part):
        at = jnp.where(far_first, z_part - 1 - turn, turn)

        def one(step, carry):
            for copy in plane_copies(lax.rem(own + step, plane_n), at):
                copy.start()
            return carry

        for copy in keep_copies(at):
            copy.start()
        lax.fori_loop(1, plane_n, one, 0)

    def gathered(block):
        def one(chip, carry):
            source, at = chip * tpc_n + block // z_part, lax.rem(block, z_part)

            @pl.when(source == own)
            def _():
                for copy in keep_copies(at):
                    copy.wait()

            @pl.when(source != own)
            def _():
                pltpu.make_async_remote_copy(
                    src_ref=got.at[block, chip],
                    dst_ref=got.at[block, chip],
                    send_sem=plane_send.at[own, at],
                    recv_sem=plane_recv.at[source, at],
                    device_id=device(own),
                    device_id_type=MESH_ID,
                ).wait_recv()
                if gated:
                    pltpu.make_async_remote_copy(
                        src_ref=gates_got.at[block, chip],
                        dst_ref=gates_got.at[block, chip],
                        send_sem=gate_send.at[own, at],
                        recv_sem=gate_recv.at[source, at],
                        device_id=device(own),
                        device_id_type=MESH_ID,
                    ).wait_recv()

            return carry

        lax.fori_loop(0, chips, one, 0)

        def rows(step, carry):
            first = pl.multiple_of(step * tile, tile)
            spots = slots_ref[block, pl.ds(first, tile), :]
            rank = lax.broadcasted_iota(jnp.int32, (tile, capacity), 1)
            summed = jnp.zeros((tile, quarter), F32)
            if gated:
                experts = gate_total.shape[0]
                gates = jnp.zeros((experts, tile), F32)
                expert = lax.broadcasted_iota(jnp.int32, (experts, capacity), 0)
            for chip in range(chips):
                hits = jnp.where(rank == spots[:, chip : chip + 1], 1.0, 0.0).astype(BF16)
                summed = summed + jnp.dot(hits, got[block, chip], preferred_element_type=F32)
                if gated:
                    left = jnp.where(
                        expert == z * chips + chip, gates_got[block, chip, 0:1, :], 0.0
                    ).astype(BF16)
                    gates = gates + dot_nt(left, hits)
            total[pl.ds(first, tile), :] = summed
            if gated:
                gate_total[:, pl.ds(first, tile)] = gates
            return carry

        lax.fori_loop(0, tokens // tile, rows, 0)

    def lines(side, target, to):
        made = [
            pltpu.make_async_remote_copy(
                src_ref=going.at[target],
                dst_ref=coming.at[side, target],
                send_sem=line_send.at[side, target],
                recv_sem=line_recv.at[side, target],
                device_id=device(own, to),
                device_id_type=MESH_ID,
            )
        ]
        if gated:
            made.append(
                pltpu.make_async_remote_copy(
                    src_ref=gate_going.at[target],
                    dst_ref=gate_coming.at[side, target],
                    send_sem=gate_line_send.at[side, target],
                    recv_sem=gate_line_recv.at[side, target],
                    device_id=device(own, to),
                    device_id_type=MESH_ID,
                )
            )
        return made

    for step in range(fi_n - 1):
        for side in (0, 1):
            target = fi_n - 1 - step if side == 0 else step
            passes = (z < target) if side == 0 else (z > target)
            inner = (z > 0) if side == 0 else (z < fi_n - 1)

            @pl.when(passes)
            def _():
                gathered(target)

                @pl.when(inner)
                def _():
                    for copy in lines(side, target, z):
                        copy.wait_recv()
                    going[target] = (total[...] + coming[side, target].astype(F32)).astype(BF16)
                    if gated:
                        gate_going[target] = gate_total[...] + gate_coming[side, target]

                @pl.when(jnp.logical_not(inner))
                def _():
                    going[target] = total[...].astype(BF16)
                    if gated:
                        gate_going[target] = gate_total[...]

                for copy in lines(side, target, z + 1 if side == 0 else z - 1):
                    copy.start()

    gathered(z)
    for side in (0, 1):

        @pl.when((z > 0) if side == 0 else (z < fi_n - 1))
        def _():
            for copy in lines(side, z, z):
                copy.wait_recv()
            total[...] += coming[side, z].astype(F32)
            if gated:
                gate_total[...] += gate_coming[side, z]

    out_ref[...] = total[...]
    if gated:
        gate_out[...] = gate_total[...]

    for target in range(fi_n):
        for side in (0, 1):

            @pl.when((z < target) if side == 0 else (z > target))
            def _():
                for copy in lines(side, target, z + 1 if side == 0 else z - 1):
                    copy.wait_send()

    def settle(index, carry):
        target, at = index // z_part, lax.rem(index, z_part)

        @pl.when(target != own)
        def _():
            for copy in plane_copies(target, at):
                copy.wait_send()

        return carry

    lax.fori_loop(0, plane_n * z_part, settle, 0)


def give_back_rows(sizes, rows, token_slots, gates, collective_id):
    fi_n, ctx_n, tpx_n, tpc_n = (sizes[n] for n in ("fi", "ctx", "tpx", "tpc"))
    z_part, plane_n, chips = fi_n // tpc_n, ctx_n * tpx_n * tpc_n, ctx_n * tpx_n
    capacity, width = rows.shape[2:]
    quarter = width // (tpx_n * tpc_n)
    tokens = token_slots.shape[1]
    experts = fi_n * chips
    gated = gates is not None
    hbm, vmem = pl.BlockSpec(memory_space=pl.ANY), pl.BlockSpec(memory_space=pltpu.VMEM)
    shapes = [jax.ShapeDtypeStruct((tokens, quarter), F32)]
    scratch = [
        pltpu.VMEM((fi_n, chips, capacity, quarter), BF16),
        pltpu.VMEM((tokens, quarter), F32),
        pltpu.VMEM((fi_n, tokens, quarter), BF16),
        pltpu.VMEM((2, fi_n, tokens, quarter), BF16),
        pltpu.SemaphoreType.DMA((plane_n, z_part)),
        pltpu.SemaphoreType.DMA((plane_n, z_part)),
        pltpu.SemaphoreType.DMA((2, fi_n)),
        pltpu.SemaphoreType.DMA((2, fi_n)),
    ]
    args = [token_slots, rows]
    if gated:
        args.append(gates)
        shapes.append(jax.ShapeDtypeStruct((experts, tokens), F32))
        scratch += [
            pltpu.VMEM((fi_n, chips, 8, capacity), F32),
            pltpu.VMEM((experts, tokens), F32),
            pltpu.VMEM((fi_n, experts, tokens), F32),
            pltpu.VMEM((2, fi_n, experts, tokens), F32),
            pltpu.SemaphoreType.DMA((plane_n, z_part)),
            pltpu.SemaphoreType.DMA((plane_n, z_part)),
            pltpu.SemaphoreType.DMA((2, fi_n)),
            pltpu.SemaphoreType.DMA((2, fi_n)),
        ]
    return pl.pallas_call(
        functools.partial(give_back_body, sizes, gated),
        out_shape=tuple(shapes),
        in_specs=[vmem] + [hbm] * (len(args) - 1),
        out_specs=tuple([vmem] * len(shapes)),
        scratch_shapes=scratch,
        compiler_params=pltpu.CompilerParams(
            collective_id=collective_id, has_side_effects=True, vmem_limit_bytes=48 << 20
        ),
        cost_estimate=pl.CostEstimate(
            flops=2 * fi_n * chips * capacity * tokens * quarter,
            bytes_accessed=100_000_000,
            transcendentals=0,
        ),
        name="give_back",
    )(*args)


def collect_body(sizes, kinds, routed, *refs):
    fo_n, fi_n, ctx_n, tpx_n, tpc_n = (sizes[n] for n in ("fo", "fi", "ctx", "tpx", "tpc"))
    tp_n = tpx_n * tpc_n
    chip_n = fi_n * ctx_n * tpx_n
    count = len(kinds)
    shards, refs = refs[:count], refs[count:]
    if routed:
        local, refs = refs[0], refs[1:]
    outs, refs = refs[:count], refs[count:]
    if routed:
        experts, refs = refs[:3], refs[3:]
    own_sem, line_send, line_recv, col_send, col_recv, tp_send, tp_recv = refs[:7]
    fo, z, y, x, c = (lax.axis_index(n) for n in ("fo", "fi", "ctx", "tpx", "tpc"))
    q = x * tpc_n + c
    barrier = pltpu.get_barrier_semaphore()

    def hello(device):
        pl.semaphore_signal(barrier, inc=1, device_id=device, device_id_type=MESH_ID)

    for near in (-1, 1):

        @pl.when((z + near >= 0) & (z + near < fi_n))
        def _():
            hello((fo, z + near, y, x, c))

    for dy in range(1, ctx_n):
        hello((fo, z, lax.rem(y + dy, ctx_n), x, c))
    for step in range(1, tp_n):
        other = lax.rem(q + step, tp_n)
        hello((fo, z, y, other // tpc_n, lax.rem(other, tpc_n)))
    expected = ctx_n - 1 + tp_n - 1
    expected = expected + (z > 0).astype(jnp.int32) + (z < fi_n - 1).astype(jnp.int32)
    pl.semaphore_wait(barrier, expected)

    items = [(i, f) for f in range(fo_n) for i in range(count)]

    def source(n):
        i, f = items[n]
        if kinds[i] == "share":
            a = shards[i].shape[1] // tp_n
            return shards[i].at[f, pl.ds(pl.multiple_of(q * a, a), a), :]
        return shards[i].at[f]

    def place(n, zb, yb):
        i, f = items[n]
        a, b = shards[i].shape[1:]
        block = (f * fi_n + zb) * ctx_n + yb
        if kinds[i] == "col":
            return outs[i].at[:, pl.ds(pl.multiple_of(block * b, b), b)]
        if kinds[i] == "share":
            part = a // tp_n
            return outs[i].at[pl.ds(pl.multiple_of(block * a + q * part, part), part), :]
        return outs[i].at[pl.ds(pl.multiple_of(block * a, a), a), :]

    def line(n, side, step, first):
        block = z - step if side == 0 else z + step
        to = z + 1 if side == 0 else z - 1
        return pltpu.make_async_remote_copy(
            src_ref=source(n) if first else place(n, block, y),
            dst_ref=place(n, block, y),
            send_sem=line_send.at[n, side, step],
            recv_sem=line_recv.at[n, side, step],
            device_id=(fo, to, y, x, c),
            device_id_type=MESH_ID,
        )

    def sends(side, step):
        block = z - step if side == 0 else z + step
        to = z + 1 if side == 0 else z - 1
        return (block >= 0) & (block < fi_n) & (to >= 0) & (to < fi_n)

    def across(n, zb, dy, first=False):
        return pltpu.make_async_remote_copy(
            src_ref=source(n) if first else place(n, zb, y),
            dst_ref=place(n, zb, y),
            send_sem=col_send.at[n, zb, dy],
            recv_sem=col_recv.at[n, zb, dy],
            device_id=(fo, z, lax.rem(y + dy, ctx_n), x, c),
            device_id_type=MESH_ID,
        )

    def keep(n):
        return pltpu.make_async_copy(source(n), place(n, z, y), own_sem.at[n])

    for n in range(len(items)):
        for side in (0, 1):

            @pl.when(sends(side, 0))
            def _():
                line(n, side, 0, True).start()

        for dy in range(1, ctx_n):
            across(n, z, dy, True).start()
        keep(n).start()

    if routed:
        keep_sem, pair_send, pair_recv = refs[7:]

        def spot(k, f, chip, core):
            rows, depth = local.shape[3:]
            block = f * fi_n * ctx_n + chip // tpx_n
            return experts[k].at[
                pl.ds(
                    pl.multiple_of((lax.rem(chip, tpx_n) * tpc_n + core) * rows, rows), rows
                ),
                pl.ds(pl.multiple_of(block * depth, depth), depth),
            ]

        def expert_keep(f, k, chip):
            return pltpu.make_async_copy(
                local.at[f, chip, k], spot(k, f, chip, c), keep_sem.at[f, k, chip]
            )

        def pair_copy(f, k, chip, dc):
            return pltpu.make_async_remote_copy(
                src_ref=local.at[f, chip, k],
                dst_ref=spot(k, f, chip, c),
                send_sem=pair_send.at[f, k, chip, dc],
                recv_sem=pair_recv.at[f, k, chip, dc],
                device_id=(fo, z, y, x, lax.rem(c + dc, tpc_n)),
                device_id_type=MESH_ID,
            )

        def launch(step, carry):
            f, chip = step // chip_n, lax.rem(step, chip_n)
            for k in range(3):
                expert_keep(f, k, chip).start()
                for dc in range(1, tpc_n):
                    pair_copy(f, k, chip, dc).start()
            return carry

        lax.fori_loop(0, fo_n * chip_n, launch, 0)

    for step in range(fi_n - 1):
        for n in range(len(items)):
            for side in (0, 1):
                block = z - 1 - step if side == 0 else z + 1 + step

                @pl.when((block >= 0) & (block < fi_n))
                def _():
                    pltpu.make_async_remote_copy(
                        src_ref=place(n, block, y),
                        dst_ref=place(n, block, y),
                        send_sem=line_send.at[n, side, step],
                        recv_sem=line_recv.at[n, side, step],
                        device_id=(fo, z, y, x, c),
                        device_id_type=MESH_ID,
                    ).wait_recv()
                    for dy in range(1, ctx_n):
                        across(n, block, dy).start()

                if step < fi_n - 2:

                    @pl.when(sends(side, step + 1))
                    def _():
                        line(n, side, step + 1, False).start()

    for n in range(len(items)):
        keep(n).wait()
        for dy in range(1, ctx_n):
            for zb in range(fi_n):
                pltpu.make_async_remote_copy(
                    src_ref=place(n, zb, y),
                    dst_ref=place(n, zb, lax.rem(y + ctx_n - dy, ctx_n)),
                    send_sem=col_send.at[n, zb, dy],
                    recv_sem=col_recv.at[n, zb, dy],
                    device_id=(fo, z, y, x, c),
                    device_id_type=MESH_ID,
                ).wait_recv()
        i, f = items[n]
        if kinds[i] == "share":
            a = shards[i].shape[1]
            part = a // tp_n

            def spread(block, step, n=n, i=i, f=f, a=a, part=part):
                other = lax.rem(q + step, tp_n)
                at = (f * fi_n * ctx_n + block) * a + q * part
                return pltpu.make_async_remote_copy(
                    src_ref=outs[i].at[pl.ds(pl.multiple_of(at, part), part), :],
                    dst_ref=outs[i].at[pl.ds(pl.multiple_of(at, part), part), :],
                    send_sem=tp_send.at[n, block, step],
                    recv_sem=tp_recv.at[n, block, step],
                    device_id=(fo, z, y, other // tpc_n, lax.rem(other, tpc_n)),
                    device_id_type=MESH_ID,
                )

            def spread_all(block, carry):
                for step in range(1, tp_n):
                    spread(block, step).start()
                return carry

            lax.fori_loop(0, fi_n * ctx_n, spread_all, 0)

    for n in range(len(items)):
        i, f = items[n]
        if kinds[i] == "share":
            a = shards[i].shape[1]
            part = a // tp_n

            def landed(block, carry, n=n, i=i, f=f, a=a, part=part):
                for step in range(1, tp_n):
                    origin = lax.rem(q + tp_n - step, tp_n)
                    at = (f * fi_n * ctx_n + block) * a
                    mine = pl.ds(pl.multiple_of(at + q * part, part), part)
                    theirs = pl.ds(pl.multiple_of(at + origin * part, part), part)
                    copy = pltpu.make_async_remote_copy(
                        src_ref=outs[i].at[mine, :],
                        dst_ref=outs[i].at[theirs, :],
                        send_sem=tp_send.at[n, block, step],
                        recv_sem=tp_recv.at[n, block, step],
                        device_id=(fo, z, y, x, c),
                        device_id_type=MESH_ID,
                    )
                    copy.wait_send()
                    copy.wait_recv()
                return carry

            lax.fori_loop(0, fi_n * ctx_n, landed, 0)
        for side in (0, 1):
            for step in range(fi_n - 1):

                @pl.when(sends(side, step))
                def _():
                    line(n, side, step, step == 0).wait_send()

        for dy in range(1, ctx_n):
            for zb in range(fi_n):
                across(n, zb, dy).wait_send()

    if routed:

        def settle(step, carry):
            f, chip = step // chip_n, lax.rem(step, chip_n)
            for k in range(3):
                expert_keep(f, k, chip).wait()
                for dc in range(1, tpc_n):
                    pair_copy(f, k, chip, dc).wait_send()
                    pltpu.make_async_remote_copy(
                        src_ref=local.at[f, chip, k],
                        dst_ref=spot(k, f, chip, lax.rem(c + tpc_n - dc, tpc_n)),
                        send_sem=pair_send.at[f, k, chip, dc],
                        recv_sem=pair_recv.at[f, k, chip, dc],
                        device_id=(fo, z, y, x, c),
                        device_id_type=MESH_ID,
                    ).wait_recv()
            return carry

        lax.fori_loop(0, fo_n * chip_n, settle, 0)


def collect(sizes, kinds, shards, local, collective_id):
    fo_n, fi_n, ctx_n, tpx_n, tpc_n = (sizes[n] for n in ("fo", "fi", "ctx", "tpx", "tpc"))
    tp_n = tpx_n * tpc_n
    blocks = fo_n * fi_n * ctx_n
    shapes = []
    for kind, shard in zip(kinds, shards):
        _, a, b = shard.shape
        shapes.append((a, blocks * b) if kind == "col" else (blocks * a, b))
    types = [shard.dtype for shard in shards]
    n = len(kinds) * fo_n
    scratch = [
        pltpu.SemaphoreType.DMA((n,)),
        pltpu.SemaphoreType.DMA((n, 2, fi_n)),
        pltpu.SemaphoreType.DMA((n, 2, fi_n)),
        pltpu.SemaphoreType.DMA((n, fi_n, ctx_n)),
        pltpu.SemaphoreType.DMA((n, fi_n, ctx_n)),
        pltpu.SemaphoreType.DMA((n, fi_n * ctx_n, tp_n)),
        pltpu.SemaphoreType.DMA((n, fi_n * ctx_n, tp_n)),
    ]
    args = list(shards)
    routed = local is not None
    if routed:
        args.append(local)
        chip_n = fi_n * ctx_n * tpx_n
        rows, depth = local.shape[3:]
        shapes += [(rows * tp_n, depth * blocks)] * 3
        types += [BF16] * 3
        scratch += [pltpu.SemaphoreType.DMA((fo_n, 3, chip_n))]
        scratch += [pltpu.SemaphoreType.DMA((fo_n, 3, chip_n, tpc_n))] * 2
    return pl.pallas_call(
        functools.partial(collect_body, sizes, tuple(kinds), routed),
        out_shape=tuple(jax.ShapeDtypeStruct(shape, kind) for shape, kind in zip(shapes, types)),
        in_specs=[pl.BlockSpec(memory_space=pl.ANY)] * len(args),
        out_specs=tuple(pl.BlockSpec(memory_space=pl.ANY) for _ in shapes),
        scratch_shapes=scratch,
        compiler_params=pltpu.CompilerParams(
            collective_id=collective_id, has_side_effects=True
        ),
        cost_estimate=pl.CostEstimate(flops=0, bytes_accessed=100_000_000, transcendentals=0),
        name="collect",
    )(*args)


def pair_body(sizes, fo_n, *refs):
    fi_n, ctx_n, tpx_n, tpc_n = (sizes[n] for n in ("fi", "ctx", "tpx", "tpc"))
    grads, (out_ref, mine, theirs, load_sem, store_sem, send_sem, recv_sem) = refs[:3], refs[3:]
    chip_n = fi_n * ctx_n * tpx_n
    rows, depth = mine.shape[2:]
    fo, z, y, x, c = (lax.axis_index(n) for n in ("fo", "fi", "ctx", "tpx", "tpc"))
    sibling = (fo, z, y, x, 1 - c)
    barrier = pltpu.get_barrier_semaphore()
    pl.semaphore_signal(barrier, inc=1, device_id=sibling, device_id_type=MESH_ID)
    pl.semaphore_wait(barrier, 1)

    def spot(k, at, core):
        block, side = at // tpx_n, lax.rem(at, tpx_n)
        return grads[k].at[
            pl.ds(pl.multiple_of((side * tpc_n + core) * rows, rows), rows),
            pl.ds(pl.multiple_of(block * depth, depth), depth),
        ]

    def load(k, at):
        return pltpu.make_async_copy(spot(k, at, c), mine.at[at, k], load_sem.at[at, k])

    def store(k, at):
        return pltpu.make_async_copy(mine.at[at, k], out_ref.at[at, k], store_sem.at[at, k])

    def give(k, at):
        return pltpu.make_async_remote_copy(
            src_ref=spot(k, at, 1 - c),
            dst_ref=theirs.at[at, k],
            send_sem=send_sem.at[at, k],
            recv_sem=recv_sem.at[at, k],
            device_id=sibling,
            device_id_type=MESH_ID,
        )

    def launch(at, carry):
        for k in range(3):
            give(k, at).start()
            load(k, at).start()
        return carry

    def add(at, carry):
        for k in range(3):
            load(k, at).wait()
            give(k, at).wait_recv()
            mine[at, k] = (mine[at, k].astype(F32) + theirs[at, k].astype(F32)).astype(BF16)
            store(k, at).start()
        return carry

    def settle(at, carry):
        for k in range(3):
            give(k, at).wait_send()
            store(k, at).wait()
        return carry

    total = fo_n * chip_n
    lax.fori_loop(0, total, launch, 0)
    lax.fori_loop(0, total, add, 0)
    lax.fori_loop(0, total, settle, 0)


def pair_sum(sizes, grads, collective_id):
    fo_n, fi_n, ctx_n, tpx_n, tpc_n = (sizes[n] for n in ("fo", "fi", "ctx", "tpx", "tpc"))
    rows = grads[0].shape[0] // (tpx_n * tpc_n)
    depth = grads[0].shape[1] // (fo_n * fi_n * ctx_n)
    total = fo_n * fi_n * ctx_n * tpx_n
    shape = (total, 3, rows, depth)
    hbm = pl.BlockSpec(memory_space=pl.ANY)
    return pl.pallas_call(
        functools.partial(pair_body, sizes, fo_n),
        out_shape=jax.ShapeDtypeStruct(shape, BF16),
        in_specs=[hbm] * 3,
        out_specs=hbm,
        scratch_shapes=[pltpu.VMEM(shape, BF16)] * 2 + [pltpu.SemaphoreType.DMA((total, 3))] * 4,
        compiler_params=pltpu.CompilerParams(
            collective_id=collective_id, has_side_effects=True, vmem_limit_bytes=32 << 20
        ),
        cost_estimate=pl.CostEstimate(flops=0, bytes_accessed=60_000_000, transcendentals=0),
        name="pair_sum",
    )(*grads)


def finish_body(sizes, kinds, extra, *refs):
    fi_n, ctx_n, tpx_n, tpc_n = (sizes[n] for n in ("fi", "ctx", "tpx", "tpc"))
    tp_n = tpx_n * tpc_n
    count = len(kinds)
    parts, refs = refs[:count], refs[count:]
    quarters, refs = refs[:extra], refs[extra:]
    outs, refs = refs[:count], refs[count:]
    wholes, refs = refs[:extra], refs[extra:]
    mine, refs = refs[:count], refs[count:]
    other, refs = refs[:count], refs[count:]
    coming, refs = refs[:count], refs[count:]
    tiny, refs = refs[0], refs[1:]
    load_sem, col_send, col_recv, line_send, line_recv, tp_send, tp_recv = refs[:7]
    keep_sem, x_send, x_recv, c_send, c_recv = refs[7:]
    fo, z, y, x, c = (lax.axis_index(n) for n in ("fo", "fi", "ctx", "tpx", "tpc"))
    q = x * tpc_n + c
    barrier = pltpu.get_barrier_semaphore()

    def hello(device):
        pl.semaphore_signal(barrier, inc=1, device_id=device, device_id_type=MESH_ID)

    for near in (-1, 1):

        @pl.when((z + near >= 0) & (z + near < fi_n))
        def _():
            hello((fo, z + near, y, x, c))

    for dy in range(1, ctx_n):
        hello((fo, z, lax.rem(y + dy, ctx_n), x, c))
    for step in range(1, tp_n):
        peer = lax.rem(q + step, tp_n)
        hello((fo, z, y, peer // tpc_n, lax.rem(peer, tpc_n)))
    sides = (z > 0).astype(jnp.int32) + (z < fi_n - 1).astype(jnp.int32)
    pl.semaphore_wait(barrier, ctx_n - 1 + tp_n - 1 + sides)

    def slab(j, owner):
        wide = quarters[j].shape[1]
        return wholes[j].at[:, pl.ds(pl.multiple_of(owner * wide, wide), wide)]

    def keep(j):
        return pltpu.make_async_copy(quarters[j], slab(j, q), keep_sem.at[j])

    def to_chip(j, dx):
        return pltpu.make_async_remote_copy(
            src_ref=quarters[j],
            dst_ref=slab(j, q),
            send_sem=x_send.at[j, dx],
            recv_sem=x_recv.at[j, dx],
            device_id=(fo, z, y, lax.rem(x + dx, tpx_n), c),
            device_id_type=MESH_ID,
        )

    def to_core(j, dx, dc):
        owner = lax.rem(x + tpx_n - dx, tpx_n) * tpc_n + c
        return pltpu.make_async_remote_copy(
            src_ref=quarters[j] if dx == 0 else slab(j, owner),
            dst_ref=slab(j, owner),
            send_sem=c_send.at[j, dx, dc],
            recv_sem=c_recv.at[j, dx, dc],
            device_id=(fo, z, y, x, lax.rem(c + dc, tpc_n)),
            device_id_type=MESH_ID,
        )

    for j in range(extra):
        for dx in range(1, tpx_n):
            to_chip(j, dx).start()
        for dc in range(1, tpc_n):
            to_core(j, 0, dc).start()
        keep(j).start()

    def view(n, zb, yb):
        a, b = mine[n].shape[1:]
        block = zb * ctx_n + yb
        if kinds[n] == "col":
            return parts[n].at[:, pl.ds(pl.multiple_of(block * b, b), b)]
        if kinds[n] == "share":
            return parts[n].at[pl.ds(pl.multiple_of(block * a * tp_n + q * a, a), a), :]
        return parts[n].at[pl.ds(pl.multiple_of(block * a, a), a), :]

    def across(n, zb, dy):
        to = lax.rem(y + dy, ctx_n)
        return pltpu.make_async_remote_copy(
            src_ref=view(n, zb, to),
            dst_ref=other[n].at[dy - 1, zb],
            send_sem=col_send.at[n, zb, dy],
            recv_sem=col_recv.at[n, zb, dy],
            device_id=(fo, z, to, x, c),
            device_id_type=MESH_ID,
        )

    def load(n, zb):
        return pltpu.make_async_copy(view(n, zb, y), mine[n].at[zb], load_sem.at[n, zb])

    order = [fi_n - 1 - k // 2 if k % 2 == 0 else k // 2 for k in range(fi_n)]
    for zb in order:
        for n in range(count):
            for dy in range(1, ctx_n):
                across(n, zb, dy).start()
            load(n, zb).start()

    def line(n, side, target):
        at = jnp.where(target == (z + 1 if side == 0 else z - 1), fi_n, target) if side == 1 else target
        return pltpu.make_async_remote_copy(
            src_ref=mine[n].at[target],
            dst_ref=coming[n].at[at],
            send_sem=line_send.at[n, side, target],
            recv_sem=line_recv.at[n, side, target],
            device_id=(fo, z + 1 if side == 0 else z - 1, y, x, c),
            device_id_type=MESH_ID,
        )

    def came(n, side, target, at):
        pltpu.make_async_remote_copy(
            src_ref=mine[n].at[target],
            dst_ref=coming[n].at[at],
            send_sem=line_send.at[n, side, target],
            recv_sem=line_recv.at[n, side, target],
            device_id=(fo, z, y, x, c),
            device_id_type=MESH_ID,
        ).wait_recv()

    def ready(n, target):
        load(n, target).wait()
        for dy in range(1, ctx_n):
            across(n, target, dy).wait_recv()

    def add(n, target, use, store):
        a = mine[n].shape[1]
        tile = math.gcd(a, 64)

        def rows(step, carry):
            at = pl.ds(pl.multiple_of(step * tile, tile), tile)
            summed = mine[n][target, at, :].astype(F32)
            for dy in range(1, ctx_n):
                summed = summed + other[n][dy - 1, target, at, :].astype(F32)
            for slot in use:
                summed = summed + coming[n][slot, at, :].astype(F32)
            store(at, summed.astype(BF16))
            return carry

        lax.fori_loop(0, a // tile, rows, 0)

    for step in range(fi_n - 1):
        for n in range(count):
            for side in (0, 1):
                target = fi_n - 1 - step if side == 0 else step
                passes = (z < target) if side == 0 else (z > target)
                inner = (z > 0) if side == 0 else (z < fi_n - 1)

                def back(at, values, n=n, target=target):
                    mine[n][target, at, :] = values

                @pl.when(passes & inner)
                def _():
                    ready(n, target)
                    came(n, side, target, target)
                    add(n, target, (target,), back)
                    line(n, side, target).start()

                @pl.when(passes & jnp.logical_not(inner))
                def _():
                    ready(n, target)
                    add(n, target, (), back)
                    line(n, side, target).start()

    for n in range(count):
        ready(n, z)

        def out(at, values, n=n):
            if kinds[n] == "share":
                a = mine[n].shape[1]
                outs[n][q, at, :] = values
            elif kinds[n] == "sum":
                tiny[q, at, :] = values
            else:
                outs[n][at, :] = values

        @pl.when(z > 0)
        def _():
            came(n, 0, z, z)

        @pl.when(z < fi_n - 1)
        def _():
            came(n, 1, z, fi_n)

        @pl.when((z > 0) & (z < fi_n - 1))
        def _():
            add(n, z, (z, fi_n), out)

        @pl.when((z == 0) & (z < fi_n - 1))
        def _():
            add(n, z, (fi_n,), out)

        @pl.when((z > 0) & (z == fi_n - 1))
        def _():
            add(n, z, (z,), out)

        @pl.when((z == 0) & (z == fi_n - 1))
        def _():
            add(n, z, (), out)

        if kinds[n] in ("share", "sum"):
            held = outs[n] if kinds[n] == "share" else tiny
            for step in range(1, tp_n):
                peer = lax.rem(q + step, tp_n)
                pltpu.make_async_remote_copy(
                    src_ref=held.at[q],
                    dst_ref=held.at[q],
                    send_sem=tp_send.at[n, step],
                    recv_sem=tp_recv.at[n, step],
                    device_id=(fo, z, y, peer // tpc_n, lax.rem(peer, tpc_n)),
                    device_id_type=MESH_ID,
                ).start()

    for j in range(extra):
        for dx in range(1, tpx_n):
            owner = lax.rem(x + tpx_n - dx, tpx_n) * tpc_n + c
            pltpu.make_async_remote_copy(
                src_ref=quarters[j],
                dst_ref=slab(j, owner),
                send_sem=x_send.at[j, dx],
                recv_sem=x_recv.at[j, dx],
                device_id=(fo, z, y, x, c),
                device_id_type=MESH_ID,
            ).wait_recv()
            for dc in range(1, tpc_n):
                to_core(j, dx, dc).start()

    for n in range(count):
        if kinds[n] in ("share", "sum"):
            held = outs[n] if kinds[n] == "share" else tiny
            for step in range(1, tp_n):
                origin = lax.rem(q + tp_n - step, tp_n)
                copy = pltpu.make_async_remote_copy(
                    src_ref=held.at[q],
                    dst_ref=held.at[origin],
                    send_sem=tp_send.at[n, step],
                    recv_sem=tp_recv.at[n, step],
                    device_id=(fo, z, y, x, c),
                    device_id_type=MESH_ID,
                )
                copy.wait_send()
                copy.wait_recv()
            if kinds[n] == "sum":
                summed = tiny[0].astype(F32)
                for k in range(1, tp_n):
                    summed = summed + tiny[k].astype(F32)
                outs[n][...] = summed.astype(BF16)
        for target in range(fi_n):
            for dy in range(1, ctx_n):
                across(n, target, dy).wait_send()
            for side in (0, 1):

                @pl.when((z < target) if side == 0 else (z > target))
                def _():
                    line(n, side, target).wait_send()

    for j in range(extra):
        keep(j).wait()
        for dx in range(tpx_n):
            if dx > 0:
                to_chip(j, dx).wait_send()
            for dc in range(1, tpc_n):
                to_core(j, dx, dc).wait_send()
                owner = lax.rem(x + tpx_n - dx, tpx_n) * tpc_n + lax.rem(c + tpc_n - dc, tpc_n)
                pltpu.make_async_remote_copy(
                    src_ref=quarters[j],
                    dst_ref=slab(j, owner),
                    send_sem=c_send.at[j, dx, dc],
                    recv_sem=c_recv.at[j, dx, dc],
                    device_id=(fo, z, y, x, c),
                    device_id_type=MESH_ID,
                ).wait_recv()


def finish(sizes, kinds, parts, quarters, collective_id):
    fi_n, ctx_n, tpx_n, tpc_n = (sizes[n] for n in ("fi", "ctx", "tpx", "tpc"))
    tp_n = tpx_n * tpc_n
    blocks = fi_n * ctx_n
    count, extra = len(kinds), len(quarters)
    own, shapes = [], []
    sum_shape = (16, 256)
    for kind, part in zip(kinds, parts):
        a, b = part.shape
        if kind == "col":
            own.append((a, b // blocks))
            shapes.append(own[-1])
        elif kind == "share":
            own.append((a // (blocks * tp_n), b))
            shapes.append((tp_n,) + own[-1])
        else:
            own.append((a // blocks, b))
            shapes.append(own[-1])
        if kind == "sum":
            sum_shape = own[-1]
    wide = [(v.shape[0], v.shape[1] * tp_n) for v in quarters]
    hbm = pl.BlockSpec(memory_space=pl.ANY)
    vmem = pl.BlockSpec(memory_space=pltpu.VMEM)
    some = max(extra, 1)
    return pl.pallas_call(
        functools.partial(finish_body, sizes, tuple(kinds), extra),
        out_shape=tuple(jax.ShapeDtypeStruct(s, BF16) for s in shapes + wide),
        in_specs=[hbm] * (count + extra),
        out_specs=tuple([vmem] * count + [hbm] * extra),
        scratch_shapes=[pltpu.VMEM((fi_n,) + s, BF16) for s in own]
        + [pltpu.VMEM((max(ctx_n - 1, 1), fi_n) + s, BF16) for s in own]
        + [pltpu.VMEM((fi_n + 1,) + s, BF16) for s in own]
        + [
            pltpu.VMEM((tp_n,) + sum_shape, BF16),
            pltpu.SemaphoreType.DMA((count, fi_n)),
            pltpu.SemaphoreType.DMA((count, fi_n, ctx_n)),
            pltpu.SemaphoreType.DMA((count, fi_n, ctx_n)),
            pltpu.SemaphoreType.DMA((count, 2, fi_n)),
            pltpu.SemaphoreType.DMA((count, 2, fi_n)),
            pltpu.SemaphoreType.DMA((count, tp_n)),
            pltpu.SemaphoreType.DMA((count, tp_n)),
            pltpu.SemaphoreType.DMA((some,)),
            pltpu.SemaphoreType.DMA((some, tpx_n)),
            pltpu.SemaphoreType.DMA((some, tpx_n)),
            pltpu.SemaphoreType.DMA((some, tpx_n, tpc_n)),
            pltpu.SemaphoreType.DMA((some, tpx_n, tpc_n)),
        ],
        compiler_params=pltpu.CompilerParams(
            collective_id=collective_id, has_side_effects=True, vmem_limit_bytes=48 << 20
        ),
        cost_estimate=pl.CostEstimate(flops=0, bytes_accessed=100_000_000, transcendentals=0),
        name="finish",
    )(*parts, *quarters)


def attend_body(place_ref, q_ref, kv_ref, rope_ref, out_ref, log_ref):
    block_rows, key_count = q_ref.shape[0], kv_ref.shape[0]
    first = place_ref[0] + pl.program_id(1) * block_rows
    keys = jnp.concatenate([kv_ref[:, :NOPE], rope_ref[...]], axis=1)
    scores = dot_nt(q_ref[...], keys)
    row = first + lax.broadcasted_iota(jnp.int32, (block_rows, 1), 0)
    limit = jnp.maximum(row, place_ref[1] - 1)
    key = lax.broadcasted_iota(jnp.int32, (block_rows, key_count), 1)
    scores = jnp.where(key <= limit, scores, -1e30)
    top = jnp.max(scores, axis=1, keepdims=True)
    exponent = jnp.exp(scores - top)
    row_total = jnp.sum(exponent, axis=1, keepdims=True)
    summed = jnp.dot(exponent.astype(BF16), kv_ref[:, NOPE:], preferred_element_type=F32)
    out_ref[...] = (summed / row_total).astype(BF16)
    log_total = jnp.broadcast_to(top + jnp.log(row_total), (block_rows, 128))
    log_ref[0] = log_total.T[:1]

def attend(place, query, key_value, rope, block_rows):
    rows, key_count = query.shape[0], key_value.shape[0]
    heads = query.shape[1] // HEAD
    return pl.pallas_call(
        attend_body,
        out_shape=(jax.ShapeDtypeStruct((rows, heads * VDIM), BF16), jax.ShapeDtypeStruct((heads, 1, rows), F32)),
        grid_spec=pltpu.PrefetchScalarGridSpec(
            num_scalar_prefetch=1,
            grid=(heads, rows // block_rows),
            in_specs=[
                pl.BlockSpec((block_rows, HEAD), lambda h, i, s: (i, h)),
                pl.BlockSpec((key_count, HEAD), lambda h, i, s: (0, h)),
                pl.BlockSpec((key_count, NOPE), lambda h, i, s: (0, 0)),
            ],
            out_specs=[
                pl.BlockSpec((block_rows, VDIM), lambda h, i, s: (i, h)),
                pl.BlockSpec((1, 1, block_rows), lambda h, i, s: (h, 0, i)),
            ],
        ),
        compiler_params=pltpu.CompilerParams(vmem_limit_bytes=48 << 20),
        cost_estimate=pl.CostEstimate(flops=4 * rows * key_count * heads * HEAD, bytes_accessed=20_000_000, transcendentals=rows * key_count * heads),
        name="attend",
    )(place, query, key_value, rope)

def attend_back_body(place_ref, q_ref, kv_ref, rope_ref, dout_ref, log_ref, table_ref, dq_ref, dkv_ref, drope_ref, keys_acc, values_acc):
    block_rows, key_count = q_ref.shape[0], kv_ref.shape[0]
    head, step = pl.program_id(0), pl.program_id(1)
    first = place_ref[0] + step * block_rows
    keys = jnp.concatenate([kv_ref[:, :NOPE], rope_ref[...]], axis=1)
    scores = dot_nt(keys, q_ref[...])
    row = first + lax.broadcasted_iota(jnp.int32, (1, block_rows), 1)
    limit = jnp.maximum(row, place_ref[1] - 1)
    key = lax.broadcasted_iota(jnp.int32, (key_count, block_rows), 0)
    soft = jnp.exp(jnp.where(key <= limit, scores, -1e30) - log_ref[0])
    soft_grad = dot_nt(kv_ref[:, NOPE:], dout_ref[...])
    mean = jnp.sum(soft * soft_grad, axis=0, keepdims=True)
    score_grad = (soft * (soft_grad - mean)).astype(BF16)
    values = jnp.dot(soft.astype(BF16), dout_ref[...], preferred_element_type=F32)
    keys_grad = jnp.dot(score_grad, q_ref[...], preferred_element_type=F32)
    dq_ref[...] = (dot_tn(score_grad, keys) * table_ref[...]).astype(BF16)

    @pl.when(step == 0)
    def _():
        keys_acc[...] = keys_grad
        values_acc[...] = values

    @pl.when(step > 0)
    def _():
        keys_acc[...] += keys_grad
        values_acc[...] += values

    @pl.when(step == pl.num_programs(1) - 1)
    def _():
        dkv_ref[...] = jnp.concatenate([keys_acc[:, :NOPE], values_acc[...]], axis=1).astype(BF16)

        @pl.when(head == 0)
        def _():
            drope_ref[...] = keys_acc[:, NOPE:]

        @pl.when(head > 0)
        def _():
            drope_ref[...] += keys_acc[:, NOPE:]

def attend_back(place, query, key_value, rope, dout, log_total, table, block_rows):
    rows, key_count = query.shape[0], key_value.shape[0]
    heads = query.shape[1] // HEAD
    return pl.pallas_call(
        attend_back_body,
        out_shape=(jax.ShapeDtypeStruct((rows, heads * HEAD), BF16), jax.ShapeDtypeStruct((key_count, heads * HEAD), BF16), jax.ShapeDtypeStruct((key_count, NOPE), F32)),
        grid_spec=pltpu.PrefetchScalarGridSpec(
            num_scalar_prefetch=1,
            grid=(heads, rows // block_rows),
            in_specs=[
                pl.BlockSpec((block_rows, HEAD), lambda h, i, s: (i, h)),
                pl.BlockSpec((key_count, HEAD), lambda h, i, s: (0, h)),
                pl.BlockSpec((key_count, NOPE), lambda h, i, s: (0, 0)),
                pl.BlockSpec((block_rows, VDIM), lambda h, i, s: (i, h)),
                pl.BlockSpec((1, 1, block_rows), lambda h, i, s: (h, 0, i)),
                pl.BlockSpec((block_rows, HEAD), lambda h, i, s: (i, 0)),
            ],
            out_specs=[
                pl.BlockSpec((block_rows, HEAD), lambda h, i, s: (i, h)),
                pl.BlockSpec((key_count, HEAD), lambda h, i, s: (0, h)),
                pl.BlockSpec((key_count, NOPE), lambda h, i, s: (0, 0)),
            ],
            scratch_shapes=[pltpu.VMEM((key_count, HEAD), F32), pltpu.VMEM((key_count, VDIM), F32)],
        ),
        compiler_params=pltpu.CompilerParams(vmem_limit_bytes=56 << 20),
        cost_estimate=pl.CostEstimate(flops=10 * rows * key_count * heads * HEAD, bytes_accessed=40_000_000, transcendentals=rows * key_count * heads),
        name="attend_back",
    )(place, query, key_value, rope, dout, log_total, table)


def build(sizes):
    fo_n, fi_n, ctx_n, tpx_n, tpc_n = (sizes[name] for name in ("fo", "fi", "ctx", "tpx", "tpc"))
    tp_n = tpx_n * tpc_n
    row_shards = fo_n * fi_n * ctx_n
    plane_experts = ctx_n * tpx_n
    z_part = fi_n // tpc_n

    def expert_weights(gate, up, down):
        local = jnp.stack([gate.transpose(0, 2, 1), up.transpose(0, 2, 1), down], axis=1)
        return lax.all_gather(local, "fo", axis=0) if fo_n > 1 else local[None]

    def shard_of(weight):
        return lax.all_gather(weight, "fo", axis=0) if fo_n > 1 else weight[None]

    def fo_sum(part, kind):
        if fo_n == 1:
            return part
        if kind == "col":
            a = part.shape[0]
            part = part.reshape(a, fo_n, -1)
            return lax.psum_scatter(part, "fo", scatter_dimension=1, tiled=True).reshape(a, -1)
        return lax.psum_scatter(part, "fo", scatter_dimension=0, tiled=True)

    def own_expert_grads(mine):
        mine = mine.reshape((fo_n, -1) + mine.shape[1:])
        got = lax.all_to_all(mine, CHIPS, split_axis=1, concat_axis=1, tiled=True)
        if fo_n > 1:
            got = lax.psum_scatter(got, "fo", scatter_dimension=0, tiled=True)
        got = got[0].astype(F32)
        return (got[:, 0].transpose(0, 2, 1), got[:, 1].transpose(0, 2, 1), got[:, 2])

    def shards(
        tokens,
        out_grad,
        routes,
        slot_index,
        prefix,
        attn_gain,
        query_weight,
        latent_down,
        latent_gain,
        latent_up,
        out_weight,
        moe_gain,
        router_weight,
        shared_gate,
        shared_up,
        shared_down,
        expert_gate,
        expert_up,
        expert_down,
    ):
        row_count, width = tokens.shape
        expert_count = expert_gate.shape[0]
        capacity = row_count * routes.shape[1] // expert_count
        quarter = width // tp_n
        tp_index = lax.axis_index(TP)
        own_expert = lax.axis_index(CHIPS)
        plane_base = lax.axis_index("fi") * plane_experts

        def columns(values):
            return lax.dynamic_slice_in_dim(values, tp_index * quarter, quarter, values.ndim - 1)

        depth = latent_down.shape[0]
        down_width = latent_down.shape[1]

        def turned(weight):
            half = weight.shape[-1] // 2
            return jnp.concatenate([-weight[..., half:], weight[..., :half]], axis=-1)

        small = jnp.concatenate(
            [
                latent_down,
                turned(latent_down[:, KVR:]),
                attn_gain[:, None],
                moe_gain[:, None],
                jnp.pad(latent_gain, (0, depth - latent_gain.shape[0]))[:, None],
                router_weight,
            ],
            axis=1,
        )
        used = small.shape[1]
        small = jnp.pad(small, ((0, 0), (0, -used % 128)))
        keys = jnp.where(slot_index < capacity, routes * capacity + slot_index, -1).T
        keys = jnp.pad(keys, ((0, 8 - keys.shape[0]), (0, 0)), constant_values=-1)
        small, query_full, up_full, out_full, keys_all = collect(
            sizes,
            ("share", "row", "row", "col", "row"),
            [shard_of(w) for w in (small, query_weight, latent_up, out_weight, keys)],
            None,
            4,
        )
        local_weights, small = lax.optimization_barrier(
            (expert_weights(expert_gate, expert_up, expert_down), small)
        )
        routed_weights = lax.all_to_all(
            local_weights, CHIPS, split_axis=1, concat_axis=1, tiled=True
        )
        wide_down = small[:, : down_width + ROPE]
        down_full = small[:, :down_width]
        gain_at = down_width + ROPE
        gain_one = small[:, gain_at].astype(F32)
        gain_two = small[:, gain_at + 1].astype(F32)
        gain_latent = (
            small[:, gain_at + 2]
            .reshape(row_shards, depth)[:, : latent_gain.shape[0]]
            .reshape(-1)
            .astype(F32)
        )
        router_full = small[:, gain_at + 3 : used]

        keys_all = lax.dynamic_slice_in_dim(
            keys_all, lax.axis_index("fo") * (fi_n * ctx_n * 8), fi_n * ctx_n * 8, 0
        ).reshape(fi_n, ctx_n, 8, row_count)
        keys_column = lax.dynamic_index_in_dim(keys_all, lax.axis_index("ctx"), 1, keepdims=False)
        first_keys = (plane_base + jnp.arange(plane_experts, dtype=jnp.int32)) * capacity
        rel = keys_column[:, None] - first_keys[:, None, None]
        plane_slots = jnp.max(jnp.where((rel >= 0) & (rel < capacity), rel, -1), axis=2)
        token_slots = plane_slots.transpose(0, 2, 1)

        def dispatch(part_rows, collective_id):
            got = dispatch_rows(sizes, part_rows, plane_slots, capacity, collective_id)
            return got.reshape(-1, width)

        def give_back(rows, gates, collective_id):
            rows = rows.reshape(z_part, ctx_n, capacity, width)
            return give_back_rows(sizes, rows, token_slots, gates, collective_id)

        slot_grads = dispatch(columns(out_grad), 0)
        (
            shared_gate_full,
            shared_up_full,
            shared_down_full,
            gate_full,
            expert_up_full,
            down_weight,
        ) = collect(
            sizes,
            ("row", "row", "col"),
            [shard_of(w) for w in (shared_gate, shared_up, shared_down)],
            routed_weights,
            5,
        )

        head_count = query_full.shape[1] // (NOPE + ROPE)
        hidden = tokens.astype(F32)
        scale_one = rms_scale(hidden)
        normed_one = hidden * scale_one
        normed_in = (normed_one * gain_one).astype(BF16)
        seq_index = lax.axis_index(("fo", "fi"))
        prefix_len = lax.dynamic_index_in_dim(prefix, seq_index, keepdims=False)
        row_offset = lax.axis_index("ctx") * row_count
        query_pos = row_offset + jnp.arange(row_count, dtype=jnp.int32)
        cos_table, sin_table = rotation_tables(query_pos, ROPE // 2)
        score_scale = (NOPE + ROPE) ** (-0.5)
        cos_wide = jnp.concatenate([cos_table, cos_table], axis=1)
        sin_wide = jnp.concatenate([sin_table, sin_table], axis=1)
        table = score_scale * jnp.concatenate(
            [jnp.ones((row_count, NOPE), F32), cos_wide, sin_wide], axis=1
        )

        latent_raw = dot(normed_in, wide_down)
        latent_part = latent_raw[:, :KVR]
        scale_latent = rms_scale(latent_part)
        normed_latent = latent_part * scale_latent
        latent = (normed_latent * gain_latent).astype(BF16)
        key_rope = (
            latent_raw[:, KVR : KVR + ROPE] * cos_wide + latent_raw[:, KVR + ROPE :] * sin_wide
        ).astype(BF16)
        both = lax.all_gather(
            jnp.concatenate([latent, key_rope, key_rope], axis=1), "ctx", axis=0, tiled=True
        )
        latent_all, rope_all = both[:, :KVR], both[:, KVR:]
        query_heads = query_full.reshape(width, head_count, NOPE + ROPE)
        query_wide = jnp.concatenate(
            [query_heads, turned(query_heads[..., NOPE:])], axis=-1
        ).reshape(width, head_count * HEAD)
        query_in = (
            dot(normed_in, query_wide).reshape(row_count, head_count, HEAD) * table[:, None]
        ).astype(BF16).reshape(row_count, head_count * HEAD)
        key_value = dot(latent_all, up_full).astype(BF16)
        place = jnp.stack([row_offset, prefix_len]).astype(jnp.int32)
        block_rows = min(256, row_count)
        attended, log_totals = attend(place, query_in, key_value, rope_all, block_rows)

        def tp_scatter(partial):
            parts = partial.astype(BF16).reshape(row_count, tp_n, quarter).transpose(1, 0, 2)
            return lax.psum_scatter(parts, TP, scatter_dimension=0, tiled=True)[0].astype(F32)

        def tp_gather(part_rows):
            got = lax.all_gather(part_rows, TP, axis=0)
            return got.transpose(1, 0, 2).reshape(row_count, width)

        residual = columns(tokens).astype(F32) + tp_scatter(dot(attended, out_full))
        scale_two = lax.rsqrt(
            lax.psum(jnp.sum(residual * residual, axis=-1, keepdims=True), TP) / width + EPSILON
        )
        normed_two = residual * scale_two
        gain_two_part = columns(gain_two[None])
        mid_part = (normed_two * gain_two_part).astype(BF16)

        slot_rows = dispatch(mid_part, 1)
        normed_mid = tp_gather(mid_part)

        logits = dot(normed_mid, router_full)
        router_prob = jax.nn.softmax(logits, axis=-1)
        slot_prob = jax.nn.softmax(dot(slot_rows, router_full), axis=-1)
        slot_gate = lax.dynamic_slice_in_dim(slot_prob, own_expert, 1, 1)

        gate_pre = dot(normed_mid, shared_gate_full)
        up_pre = dot(normed_mid, shared_up_full)
        shared_dact = dot_nt(out_grad, shared_down_full)
        shared_silu, shared_slope = silu_parts(gate_pre)
        shared_act = (shared_silu * up_pre).astype(BF16)
        shared_dgate = (shared_dact * up_pre * shared_slope).astype(BF16)
        shared_dup = (shared_dact * shared_silu).astype(BF16)
        mid_shared = tp_scatter(
            dot_nt(shared_dgate, shared_gate_full) + dot_nt(shared_dup, shared_up_full)
        )
        out_shared = tp_scatter(dot(shared_act, shared_down_full))

        expert_dact_raw = dot_nt(slot_grads, down_weight)
        expert_gpre = dot_nt(slot_rows, gate_full)
        expert_upre = dot_nt(slot_rows, expert_up_full)
        expert_silu, expert_slope = silu_parts(expert_gpre)
        expert_act_wide = expert_silu * expert_upre
        expert_act = expert_act_wide.astype(BF16)
        slot_gate_grad = jnp.sum(expert_act.astype(F32) * expert_dact_raw, axis=-1)
        expert_dact = expert_dact_raw * slot_gate
        expert_dgate = (expert_dact * expert_upre * expert_slope).astype(BF16)
        expert_dup = (expert_dact * expert_silu).astype(BF16)
        slot_drows = dot(expert_dgate, gate_full) + dot(expert_dup, expert_up_full)
        gate_rows = jnp.broadcast_to(
            slot_gate_grad.reshape(z_part, ctx_n, 1, capacity), (z_part, ctx_n, 8, capacity)
        )
        mid_routed, prob_grad = give_back(slot_drows.astype(BF16), gate_rows, 2)
        prob_grad = prob_grad.T
        logit_grad = (
            router_prob * (prob_grad - jnp.sum(router_prob * prob_grad, axis=-1, keepdims=True))
        ).astype(BF16)

        slot_dout = (slot_grads.astype(F32) * slot_gate).astype(BF16)
        routed_grads = pair_sum(
            sizes,
            [
                dot_tn(expert_dgate, slot_rows).astype(BF16),
                dot_tn(expert_dup, slot_rows).astype(BF16),
                dot_tn(expert_act, slot_dout).astype(BF16),
            ],
            7,
        )
        sdown_grad = dot_tn(shared_act, out_grad)
        sgate_grad = dot_tn(normed_mid, shared_dgate)
        sup_grad = dot_tn(normed_mid, shared_dup)

        mid_total = mid_shared + mid_routed + dot_nt(logit_grad, columns(router_full.T).T)
        gain_two_grad = jnp.sum(mid_total * normed_two, axis=0)
        dn_two = mid_total * gain_two_part
        dot_two = lax.psum(jnp.sum(dn_two * normed_two, axis=-1, keepdims=True), TP) / width
        residual_grad = columns(out_grad).astype(F32) + scale_two * (dn_two - normed_two * dot_two)
        attn_dout = tp_gather(residual_grad.astype(BF16))

        out_weight_grad = dot_tn(attended, attn_dout)
        attended_grad = dot_nt(attn_dout, out_full).astype(BF16)
        attended_grad, routed_grads = lax.optimization_barrier((attended_grad, routed_grads))
        egate_grad, eup_grad, edown_grad = own_expert_grads(routed_grads)
        query_grad, kv_grad, rope_grad = attend_back(
            place, query_in, key_value, rope_all, attended_grad, log_totals, table,
            min(512, row_count),
        )
        late_act, query_grad, egate_grad, eup_grad, edown_grad = lax.optimization_barrier(
            (expert_act, query_grad, egate_grad, eup_grad, edown_grad)
        )
        expert_out = (dot(late_act, down_weight) * slot_gate).astype(BF16)
        output = residual + out_shared + give_back(expert_out, None, 3)[0]
        up_grad = dot_tn(latent_all, kv_grad)
        latent_grad = dot_nt(kv_grad, up_full)
        query_wide_grad = dot_tn(normed_in, query_grad).reshape(width, head_count, HEAD)
        query_weight_grad = jnp.concatenate(
            [
                query_wide_grad[..., :NOPE],
                query_wide_grad[..., NOPE : NOPE + ROPE] - turned(query_wide_grad[..., NOPE + ROPE :]),
            ],
            axis=-1,
        ).reshape(width, head_count * (NOPE + ROPE))
        input_part = tp_scatter(dot_nt(query_grad, query_wide))
        both_grad = lax.psum_scatter(
            jnp.concatenate([latent_grad, rope_grad], axis=1).astype(BF16),
            "ctx",
            scatter_dimension=0,
            tiled=True,
        )
        both_grad = lax.psum(both_grad, TP).astype(F32)
        latent_own = both_grad[:, :KVR]
        rope_own = both_grad[:, KVR : KVR + ROPE] + both_grad[:, KVR + ROPE :]
        gain_latent_grad = jnp.sum(latent_own * normed_latent, axis=0)
        latent_raw_grad = norm_back(latent_own * gain_latent, normed_latent, scale_latent)
        down_out_grad = jnp.concatenate(
            [latent_raw_grad, rotate(rope_own, cos_table, -sin_table)], axis=-1
        ).astype(BF16)
        down_grad = dot_tn(normed_in, down_out_grad)
        input_total = input_part + dot_nt(
            down_out_grad, lax.dynamic_slice_in_dim(down_full, tp_index * quarter, quarter, 0)
        )
        normed_one_part = columns(normed_one)
        gain_one_grad = jnp.sum(input_total * normed_one_part, axis=0)
        dn_one = input_total * columns(gain_one[None])
        dot_one = lax.psum(jnp.sum(dn_one * normed_one_part, axis=-1, keepdims=True), TP) / width
        token_grad = residual_grad + scale_one * (dn_one - normed_one_part * dot_one)
        router_grad = dot_tn(normed_mid, logit_grad)
        pack_grad = jnp.concatenate([down_grad, router_grad], axis=1)
        pack_used = pack_grad.shape[1]
        pack_grad = jnp.pad(pack_grad, ((0, 0), (0, -pack_used % 128)))
        gains = jnp.stack([gain_one_grad, gain_two_grad])
        gains = lax.dynamic_update_slice_in_dim(
            jnp.zeros((2, width), F32), gains, tp_index * quarter, 1
        )
        latent_rows = jnp.pad(
            gain_latent_grad.reshape(row_shards, -1),
            ((0, 0), (0, depth - latent_gain.shape[0])),
        ).reshape(1, width)
        gains = jnp.concatenate([gains, latent_rows * (tp_index == 0).astype(F32)], axis=0)
        gains = jnp.pad(
            gains.reshape(3, row_shards, depth).transpose(1, 0, 2), ((0, 0), (0, 13), (0, 0))
        ).reshape(row_shards * 16, depth)
        kinds = ("share", "sum", "row", "row", "col", "row", "row", "col")
        partials = (
            pack_grad,
            gains,
            query_weight_grad,
            up_grad,
            out_weight_grad,
            sgate_grad,
            sup_grad,
            sdown_grad,
        )
        done = finish(
            sizes,
            kinds,
            [fo_sum(part.astype(BF16), kind) for part, kind in zip(partials, kinds)],
            [output.astype(BF16), token_grad.astype(BF16)],
            6,
        )
        pack_own = done[0].reshape(depth, -1).astype(F32)
        gains_own = done[1].astype(F32)
        query_weight_grad, up_grad, out_weight_grad, sgate_grad, sup_grad, sdown_grad = (
            part.astype(F32) for part in done[2:8]
        )
        output, token_grad = done[8], done[9].astype(F32)
        return (
            output,
            token_grad,
            gains_own[0],
            query_weight_grad,
            pack_own[:, :down_width],
            gains_own[2, : latent_gain.shape[0]],
            up_grad,
            out_weight_grad,
            gains_own[1],
            pack_own[:, down_width:pack_used],
            sgate_grad,
            sup_grad,
            sdown_grad,
            egate_grad,
            eup_grad,
            edown_grad,
        )

    return shards


EXPERTS = 16


def solution(mesh):
    ctx_n, tp_n = mesh.shape["ctx"], mesh.shape["tp"]
    tpc_n = 2
    tpx_n = tp_n // tpc_n
    fi_n = EXPERTS // (ctx_n * tpx_n)
    sizes = {
        "fo": mesh.shape["fsdp"] // fi_n,
        "fi": fi_n,
        "ctx": ctx_n,
        "tpx": tpx_n,
        "tpc": tpc_n,
    }
    fine = Mesh(mesh.devices.reshape(tuple(sizes.values())), tuple(sizes))
    rows = P(ROWS)
    rows_two = P(ROWS, None)
    rows_tp = P(ROWS, TP)
    tp_rows = P(TP, ROWS)
    wide_in = P(None, ROWS, TP)
    wide_out = P(None, TP, ROWS)
    weights = (
        rows,
        rows_tp,
        rows_two,
        rows,
        rows_tp,
        tp_rows,
        rows,
        rows_two,
        rows_tp,
        rows_tp,
        tp_rows,
        wide_in,
        wide_in,
        wide_out,
    )
    return jax.shard_map(
        build(sizes),
        mesh=fine,
        in_specs=(rows_two, rows_two, rows_two, rows_two, P()) + weights,
        out_specs=(rows_two, rows_two) + weights,
        check_vma=False,
    )
```

```python
import functools
import math

import jax
import jax.numpy as jnp
from jax import lax
from jax.experimental import pallas as pl
from jax.experimental.pallas import tpu as pltpu
from jax.sharding import Mesh
from jax.sharding import PartitionSpec as P

NOPE = 128
ROPE = 64
KVR = 512
VDIM = 128
HEAD = 256

EPSILON = 1e-06
THETA_BASE = 10000.0
F32 = jnp.float32
BF16 = jnp.bfloat16
MESH_ID = pl.DeviceIdType.MESH

ROWS = ("fo", "fi", "ctx")
TP = ("tpx", "tpc")
PLANE = ("ctx", "tpx", "tpc")
CHIPS = ("fi", "ctx", "tpx")


def rotation_tables(positions, half_width):
    freq_table = jnp.exp(jnp.arange(half_width, dtype=F32) * (-math.log(THETA_BASE) / half_width))
    angle_table = positions.astype(F32)[:, None] * freq_table[None, :]
    return (jnp.cos(angle_table), jnp.sin(angle_table))


def rotate(values, cos_table, sin_table):
    half_width = values.shape[-1] // 2
    first_half = values[..., :half_width]
    second_half = values[..., half_width:]
    return jnp.concatenate(
        [
            first_half * cos_table - second_half * sin_table,
            second_half * cos_table + first_half * sin_table,
        ],
        axis=-1,
    )


def silu_parts(values):
    sigma = jax.nn.sigmoid(values)
    return (values * sigma, sigma * (1.0 + values * (1.0 - sigma)))


def rms_scale(values):
    return lax.rsqrt(jnp.mean(values * values, axis=-1, keepdims=True) + EPSILON)


def norm_back(grad_normed, normed, scale_rows):
    return scale_rows * (
        grad_normed - normed * jnp.mean(grad_normed * normed, axis=-1, keepdims=True)
    )


def dot(left, right):
    return jnp.dot(left, right, preferred_element_type=F32)


def dot_nt(left, right):
    return lax.dot_general(left, right, (((1,), (1,)), ((), ())), preferred_element_type=F32)


def dot_tn(left, right):
    return lax.dot_general(left, right, (((0,), (0,)), ((), ())), preferred_element_type=F32)


def ein(spec, left, right):
    return jnp.einsum(spec, left, right, preferred_element_type=F32)


def plane_place(sizes):
    tpx_n, tpc_n = sizes["tpx"], sizes["tpc"]
    fo, z, y, x, c = (lax.axis_index(name) for name in ("fo", "fi", "ctx", "tpx", "tpc"))
    own = (y * tpx_n + x) * tpc_n + c

    def device(index, z_at=None):
        return (
            fo,
            z if z_at is None else z_at,
            index // (tpx_n * tpc_n),
            lax.rem(index // tpc_n, tpx_n),
            lax.rem(index, tpc_n),
        )

    return z, y, x, c, own, device


def greet_plane(sizes):
    fi_n = sizes["fi"]
    plane_n = sizes["ctx"] * sizes["tpx"] * sizes["tpc"]
    z, y, x, c, own, device = plane_place(sizes)
    barrier = pltpu.get_barrier_semaphore()
    for step in range(1, plane_n):
        pl.semaphore_signal(
            barrier,
            inc=1,
            device_id=device(lax.rem(own + step, plane_n)),
            device_id_type=MESH_ID,
        )
    for near in (-1, 1):

        @pl.when((z + near >= 0) & (z + near < fi_n))
        def _():
            pl.semaphore_signal(
                barrier, inc=1, device_id=device(own, z + near), device_id_type=MESH_ID
            )

    sides = (z > 0).astype(jnp.int32) + (z < fi_n - 1).astype(jnp.int32)
    pl.semaphore_wait(barrier, plane_n - 1 + sides)


HBM_SPEC = pl.BlockSpec(memory_space=pl.ANY)
VMEM_SPEC = pl.BlockSpec(memory_space=pltpu.VMEM)


def exchange(sizes, jobs, collective_id, name, flops=0, vmem=56):
    counts = [(len(job["args"]), len(job["outs"]), len(job["scratch"])) for job in jobs]

    def body(*refs):
        at = [0, sum(n[0] for n in counts), sum(n[0] + n[1] for n in counts)]
        running = []
        for job, count in zip(jobs, counts):
            given = [refs[at[k] : at[k] + count[k]] for k in range(3)]
            at = [at[k] + count[k] for k in range(3)]
            running.append(job["run"](sizes, *given))
        greet_plane(sizes)
        while running:
            running = [run for run in running if next(run, "ended") != "ended"]

    results = pl.pallas_call(
        body,
        out_shape=tuple(shape for job in jobs for shape, _ in job["outs"]),
        in_specs=[spec for job in jobs for _, spec in job["args"]],
        out_specs=tuple(spec for job in jobs for _, spec in job["outs"]),
        scratch_shapes=[shape for job in jobs for shape in job["scratch"]],
        compiler_params=pltpu.CompilerParams(
            collective_id=collective_id, has_side_effects=True, vmem_limit_bytes=vmem << 20
        ),
        cost_estimate=pl.CostEstimate(
            flops=flops, bytes_accessed=200_000_000, transcendentals=0
        ),
        name=name,
    )(*[arg for job in jobs for arg, _ in job["args"]])
    grouped, at = [], 0
    for _, count, _ in counts:
        grouped.append(results[at : at + count])
        at += count
    return grouped


def tp_spread(sizes, source, held, whole, sems):
    tpx_n, tpc_n = sizes["tpx"], sizes["tpc"]
    keep_sem, x_send, x_recv, c_send, c_recv = sems
    fo, z, y, x, c = (lax.axis_index(n) for n in ("fo", "fi", "ctx", "tpx", "tpc"))
    wide = source.shape[1]

    def slab(side, core):
        at = (side * tpc_n + core) * wide
        return whole.at[:, pl.ds(pl.multiple_of(at, wide), wide)]

    def origin(dx):
        return lax.rem(x + tpx_n - dx, tpx_n)

    keep = pltpu.make_async_copy(held, slab(x, c), keep_sem)

    def to_chip(dx, side):
        return pltpu.make_async_remote_copy(
            src_ref=source,
            dst_ref=slab(side, c),
            send_sem=x_send.at[dx],
            recv_sem=x_recv.at[dx],
            device_id=(fo, z, y, lax.rem(x + dx, tpx_n), c),
            device_id_type=MESH_ID,
        )

    def to_core(dx, dc, core):
        return pltpu.make_async_remote_copy(
            src_ref=source if dx == 0 else slab(origin(dx), c),
            dst_ref=slab(origin(dx), core),
            send_sem=c_send.at[dx, dc],
            recv_sem=c_recv.at[dx, dc],
            device_id=(fo, z, y, x, lax.rem(c + dc, tpc_n)),
            device_id_type=MESH_ID,
        )

    def start():
        for dx in range(1, tpx_n):
            to_chip(dx, x).start()
        for dc in range(1, tpc_n):
            to_core(0, dc, c).start()

    def relay():
        for dx in range(1, tpx_n):
            to_chip(dx, origin(dx)).wait_recv()
            for dc in range(1, tpc_n):
                to_core(dx, dc, c).start()

    def settle():
        keep.wait()
        for dx in range(tpx_n):
            if dx > 0:
                to_chip(dx, x).wait_send()
            for dc in range(1, tpc_n):
                to_core(dx, dc, c).wait_send()
                to_core(dx, dc, lax.rem(c + tpc_n - dc, tpc_n)).wait_recv()

    return start, keep, relay, settle


def tp_spread_sems(sizes):
    tpx_n, tpc_n = sizes["tpx"], sizes["tpc"]
    return [
        pltpu.SemaphoreType.DMA,
        pltpu.SemaphoreType.DMA((tpx_n,)),
        pltpu.SemaphoreType.DMA((tpx_n,)),
        pltpu.SemaphoreType.DMA((tpx_n, tpc_n)),
        pltpu.SemaphoreType.DMA((tpx_n, tpc_n)),
    ]


def dispatch_job(sizes, part_rows, plane_slots, capacity):
    tokens, quarter = part_rows.shape
    fi_n, ctx_n, tpx_n, tpc_n = (sizes[n] for n in ("fi", "ctx", "tpx", "tpc"))
    z_part, plane_n, chips = fi_n // tpc_n, ctx_n * tpx_n * tpc_n, ctx_n * tpx_n
    shape = (z_part, ctx_n, capacity, quarter * tpx_n * tpc_n)
    return {
        "args": [(plane_slots, VMEM_SPEC), (part_rows, HBM_SPEC)],
        "outs": [(jax.ShapeDtypeStruct(shape, BF16), HBM_SPEC)],
        "scratch": [
            pltpu.VMEM((fi_n, tokens, quarter), BF16),
            pltpu.VMEM((fi_n, chips, capacity, quarter), BF16),
            pltpu.SemaphoreType.DMA,
            pltpu.SemaphoreType.DMA((2, fi_n)),
            pltpu.SemaphoreType.DMA((2, fi_n)),
            pltpu.SemaphoreType.DMA((fi_n, chips)),
            pltpu.SemaphoreType.DMA((plane_n, z_part)),
        ],
        "run": dispatch_run,
    }


def dispatch_run(sizes, args, outs, scratch):
    slots_ref, rows_ref = args
    (out_ref,) = outs
    held, picked, own_sem, line_send, line_recv, plane_send, plane_recv = scratch
    fi_n, tpx_n, tpc_n = sizes["fi"], sizes["tpx"], sizes["tpc"]
    plane_n = sizes["ctx"] * tpx_n * tpc_n
    chips = sizes["ctx"] * tpx_n
    z_part = fi_n // tpc_n
    capacity, quarter = picked.shape[2:]
    tokens = held.shape[1]
    z, y, x, c, own, device = plane_place(sizes)
    columns = pl.ds(pl.multiple_of((x * tpc_n + c) * quarter, quarter), quarter)
    load = pltpu.make_async_copy(rows_ref, held.at[z], own_sem)

    def line(side, step):
        block = z - step if side == 0 else z + step
        to = z + 1 if side == 0 else z - 1
        return pltpu.make_async_remote_copy(
            src_ref=held.at[block],
            dst_ref=held.at[block],
            send_sem=line_send.at[side, step],
            recv_sem=line_recv.at[side, step],
            device_id=device(own, to),
            device_id_type=MESH_ID,
        )

    def sends(side, step):
        block = z - step if side == 0 else z + step
        to = z + 1 if side == 0 else z - 1
        return (block >= 0) & (block < fi_n) & (to >= 0) & (to < fi_n)

    def plane_copy(block, chip):
        at = lax.rem(block, z_part)
        return pltpu.make_async_remote_copy(
            src_ref=picked.at[block, chip],
            dst_ref=out_ref.at[at, y, :, columns],
            send_sem=plane_send.at[block, chip],
            recv_sem=plane_recv.at[own, at],
            device_id=device(chip * tpc_n + block // z_part),
            device_id_type=MESH_ID,
        )

    def keep_copy(block, chip):
        return pltpu.make_async_copy(
            picked.at[block, chip],
            out_ref.at[lax.rem(block, z_part), y, :, columns],
            plane_send.at[block, chip],
        )

    def at_home(block, chip):
        return chip * tpc_n + block // z_part == own

    def pick(block):
        def one(chip, carry):
            wanted = slots_ref[block, pl.ds(chip, 1), :]
            rank = lax.broadcasted_iota(jnp.int32, (capacity, tokens), 0)
            hits = jnp.where(rank == wanted, 1.0, 0.0).astype(BF16)
            picked[block, chip] = jnp.dot(
                hits, held[block], preferred_element_type=F32
            ).astype(BF16)

            @pl.when(at_home(block, chip))
            def _():
                keep_copy(block, chip).start()

            @pl.when(jnp.logical_not(at_home(block, chip)))
            def _():
                plane_copy(block, chip).start()

            return carry

        lax.fori_loop(0, chips, one, 0)

    load.start()
    load.wait()
    for side in (0, 1):

        @pl.when(sends(side, 0))
        def _():
            line(side, 0).start()

    yield
    pick(z)
    for step in range(fi_n - 1):
        for side in (0, 1):
            block = z - 1 - step if side == 0 else z + 1 + step

            @pl.when((block >= 0) & (block < fi_n))
            def _():
                pltpu.make_async_remote_copy(
                    src_ref=held.at[block],
                    dst_ref=held.at[block],
                    send_sem=line_send.at[side, step],
                    recv_sem=line_recv.at[side, step],
                    device_id=device(own, z),
                    device_id_type=MESH_ID,
                ).wait_recv()

            if step < fi_n - 2:

                @pl.when(sends(side, step + 1))
                def _():
                    line(side, step + 1).start()

        for side in (0, 1):
            block = z - 1 - step if side == 0 else z + 1 + step

            @pl.when((block >= 0) & (block < fi_n))
            def _():
                pick(block)

        yield

    for step in range(fi_n - 1):
        for side in (0, 1):

            @pl.when(sends(side, step))
            def _():
                line(side, step).wait_send()

    def settle(index, carry):
        block, chip = index // chips, lax.rem(index, chips)

        @pl.when(at_home(block, chip))
        def _():
            keep_copy(block, chip).wait()

        @pl.when(jnp.logical_not(at_home(block, chip)))
        def _():
            plane_copy(block, chip).wait_send()

        return carry

    lax.fori_loop(0, fi_n * chips, settle, 0)

    def arrive(index, carry):
        source, at = index // z_part, lax.rem(index, z_part)

        @pl.when(source != own)
        def _():
            pltpu.make_async_remote_copy(
                src_ref=picked.at[0, 0],
                dst_ref=out_ref.at[at, y, :, columns],
                send_sem=plane_send.at[0, 0],
                recv_sem=plane_recv.at[source, at],
                device_id=device(own),
                device_id_type=MESH_ID,
            ).wait_recv()

        return carry

    lax.fori_loop(0, plane_n * z_part, arrive, 0)


def give_back_run(sizes, args, outs, scratch):
    fi_n, tpx_n, tpc_n = sizes["fi"], sizes["tpx"], sizes["tpc"]
    plane_n = sizes["ctx"] * tpx_n * tpc_n
    chips = sizes["ctx"] * tpx_n
    z_part = fi_n // tpc_n
    ends, gated = len(args) > 3, len(args) == 3
    slots_ref, rows_ref = args[:2]
    out_ref = outs[0]
    got, total, going, coming, plane_send, plane_recv, line_send, line_recv = scratch[:8]
    if gated:
        gates_ref, gate_out = args[2], outs[1]
        gates_got, gate_total, gate_going, gate_coming = scratch[8:12]
        gate_send, gate_recv, gate_line_send, gate_line_recv = scratch[12:]
    if ends:
        held = scratch[8]
        start, keep, relay, spread_settle = tp_spread(sizes, held, held, out_ref, scratch[9:])
    capacity, quarter = got.shape[2:]
    tokens = total.shape[0]
    z, y, x, c, own, device = plane_place(sizes)
    tile = min(256, tokens)

    def piece(target, at):
        side = lax.rem(target, tpx_n * tpc_n)
        return rows_ref.at[
            at,
            target // (tpx_n * tpc_n),
            :,
            pl.ds(pl.multiple_of(side * quarter, quarter), quarter),
        ]

    def plane_copies(target, at):
        made = [
            pltpu.make_async_remote_copy(
                src_ref=piece(target, at),
                dst_ref=got.at[c * z_part + at, own // tpc_n],
                send_sem=plane_send.at[target, at],
                recv_sem=plane_recv.at[own, at],
                device_id=device(target),
                device_id_type=MESH_ID,
            )
        ]
        if gated:
            made.append(
                pltpu.make_async_remote_copy(
                    src_ref=gates_ref.at[at, target // (tpx_n * tpc_n)],
                    dst_ref=gates_got.at[c * z_part + at, own // tpc_n],
                    send_sem=gate_send.at[target, at],
                    recv_sem=gate_recv.at[own, at],
                    device_id=device(target),
                    device_id_type=MESH_ID,
                )
            )
        return made

    def keep_copies(at):
        made = [
            pltpu.make_async_copy(
                piece(own, at), got.at[c * z_part + at, own // tpc_n], plane_recv.at[own, at]
            )
        ]
        if gated:
            made.append(
                pltpu.make_async_copy(
                    gates_ref.at[at, y],
                    gates_got.at[c * z_part + at, own // tpc_n],
                    gate_recv.at[own, at],
                )
            )
        return made

    far_first = z < fi_n // 2
    for turn in range(z_part):
        at = jnp.where(far_first, z_part - 1 - turn, turn)

        def one(step, carry):
            for copy in plane_copies(lax.rem(own + step, plane_n), at):
                copy.start()
            return carry

        for copy in keep_copies(at):
            copy.start()
        lax.fori_loop(1, plane_n, one, 0)

    yield

    def gathered(block):
        def one(chip, carry):
            source, at = chip * tpc_n + block // z_part, lax.rem(block, z_part)

            @pl.when(source == own)
            def _():
                for copy in keep_copies(at):
                    copy.wait()

            @pl.when(source != own)
            def _():
                pltpu.make_async_remote_copy(
                    src_ref=got.at[block, chip],
                    dst_ref=got.at[block, chip],
                    send_sem=plane_send.at[own, at],
                    recv_sem=plane_recv.at[source, at],
                    device_id=device(own),
                    device_id_type=MESH_ID,
                ).wait_recv()
                if gated:
                    pltpu.make_async_remote_copy(
                        src_ref=gates_got.at[block, chip],
                        dst_ref=gates_got.at[block, chip],
                        send_sem=gate_send.at[own, at],
                        recv_sem=gate_recv.at[source, at],
                        device_id=device(own),
                        device_id_type=MESH_ID,
                    ).wait_recv()

            return carry

        lax.fori_loop(0, chips, one, 0)

        def rows(step, carry):
            first = pl.multiple_of(step * tile, tile)
            spots = slots_ref[block, pl.ds(first, tile), :]
            rank = lax.broadcasted_iota(jnp.int32, (tile, capacity), 1)
            summed = jnp.zeros((tile, quarter), F32)
            if gated:
                experts = gate_total.shape[0]
                gates = jnp.zeros((experts, tile), F32)
                expert = lax.broadcasted_iota(jnp.int32, (experts, capacity), 0)
            for chip in range(chips):
                hits = jnp.where(rank == spots[:, chip : chip + 1], 1.0, 0.0).astype(BF16)
                summed = summed + jnp.dot(hits, got[block, chip], preferred_element_type=F32)
                if gated:
                    left = jnp.where(
                        expert == z * chips + chip, gates_got[block, chip, 0:1, :], 0.0
                    ).astype(BF16)
                    gates = gates + dot_nt(left, hits)
            total[pl.ds(first, tile), :] = summed
            if gated:
                gate_total[:, pl.ds(first, tile)] = gates
            return carry

        lax.fori_loop(0, tokens // tile, rows, 0)

    def lines(side, target, to):
        made = [
            pltpu.make_async_remote_copy(
                src_ref=going.at[target],
                dst_ref=coming.at[side, target],
                send_sem=line_send.at[side, target],
                recv_sem=line_recv.at[side, target],
                device_id=device(own, to),
                device_id_type=MESH_ID,
            )
        ]
        if gated:
            made.append(
                pltpu.make_async_remote_copy(
                    src_ref=gate_going.at[target],
                    dst_ref=gate_coming.at[side, target],
                    send_sem=gate_line_send.at[side, target],
                    recv_sem=gate_line_recv.at[side, target],
                    device_id=device(own, to),
                    device_id_type=MESH_ID,
                )
            )
        return made

    for step in range(fi_n - 1):
        for side in (0, 1):
            target = fi_n - 1 - step if side == 0 else step
            passes = (z < target) if side == 0 else (z > target)
            inner = (z > 0) if side == 0 else (z < fi_n - 1)

            @pl.when(passes)
            def _():
                gathered(target)

                @pl.when(inner)
                def _():
                    for copy in lines(side, target, z):
                        copy.wait_recv()
                    going[target] = (total[...] + coming[side, target].astype(F32)).astype(BF16)
                    if gated:
                        gate_going[target] = gate_total[...] + gate_coming[side, target]

                @pl.when(jnp.logical_not(inner))
                def _():
                    going[target] = total[...].astype(BF16)
                    if gated:
                        gate_going[target] = gate_total[...]

                for copy in lines(side, target, z + 1 if side == 0 else z - 1):
                    copy.start()

        yield

    gathered(z)
    for side in (0, 1):

        @pl.when((z > 0) if side == 0 else (z < fi_n - 1))
        def _():
            for copy in lines(side, z, z):
                copy.wait_recv()
            total[...] += coming[side, z].astype(F32)
            if gated:
                gate_total[...] += gate_coming[side, z]

    if ends:
        held[...] = (total[...] + args[2][...] + args[3][...]).astype(BF16)
        start()
        keep.start()
    else:
        out_ref[...] = total[...]
    if gated:
        gate_out[...] = gate_total[...]
    yield
    if ends:
        relay()


    for target in range(fi_n):
        for side in (0, 1):

            @pl.when((z < target) if side == 0 else (z > target))
            def _():
                for copy in lines(side, target, z + 1 if side == 0 else z - 1):
                    copy.wait_send()

    def settle(index, carry):
        target, at = index // z_part, lax.rem(index, z_part)

        @pl.when(target != own)
        def _():
            for copy in plane_copies(target, at):
                copy.wait_send()

        return carry

    lax.fori_loop(0, plane_n * z_part, settle, 0)
    yield
    if ends:
        spread_settle()


def give_back_job(sizes, rows, token_slots, gates, bases=None):
    fi_n, ctx_n, tpx_n, tpc_n = (sizes[n] for n in ("fi", "ctx", "tpx", "tpc"))
    z_part, plane_n, chips = fi_n // tpc_n, ctx_n * tpx_n * tpc_n, ctx_n * tpx_n
    capacity, width = rows.shape[2:]
    quarter = width // (tpx_n * tpc_n)
    tokens = token_slots.shape[1]
    experts = fi_n * chips
    gated = gates is not None
    shapes = [jax.ShapeDtypeStruct((tokens, quarter), F32)]
    scratch = [
        pltpu.VMEM((fi_n, chips, capacity, quarter), BF16),
        pltpu.VMEM((tokens, quarter), F32),
        pltpu.VMEM((fi_n, tokens, quarter), BF16),
        pltpu.VMEM((2, fi_n, tokens, quarter), BF16),
        pltpu.SemaphoreType.DMA((plane_n, z_part)),
        pltpu.SemaphoreType.DMA((plane_n, z_part)),
        pltpu.SemaphoreType.DMA((2, fi_n)),
        pltpu.SemaphoreType.DMA((2, fi_n)),
    ]
    args = [token_slots, rows]
    if gated:
        args.append(gates)
        shapes.append(jax.ShapeDtypeStruct((experts, tokens), F32))
        scratch += [
            pltpu.VMEM((fi_n, chips, 8, capacity), F32),
            pltpu.VMEM((experts, tokens), F32),
            pltpu.VMEM((fi_n, experts, tokens), F32),
            pltpu.VMEM((2, fi_n, experts, tokens), F32),
            pltpu.SemaphoreType.DMA((plane_n, z_part)),
            pltpu.SemaphoreType.DMA((plane_n, z_part)),
            pltpu.SemaphoreType.DMA((2, fi_n)),
            pltpu.SemaphoreType.DMA((2, fi_n)),
        ]
    specs = [VMEM_SPEC] + [HBM_SPEC] * (len(args) - 1)
    if bases is not None:
        args += list(bases)
        specs += [VMEM_SPEC] * 2
        shapes = [jax.ShapeDtypeStruct((tokens, width), BF16)]
        scratch += [pltpu.VMEM((tokens, quarter), BF16)] + tp_spread_sems(sizes)
    return {
        "args": list(zip(args, specs)),
        "outs": [(shape, HBM_SPEC if bases is not None else VMEM_SPEC) for shape in shapes],
        "scratch": scratch,
        "run": give_back_run,
    }


def collect_run(kinds, sizes, args, outs, scratch):
    fo_n, fi_n, ctx_n, tpx_n, tpc_n = (sizes[n] for n in ("fo", "fi", "ctx", "tpx", "tpc"))
    tp_n = tpx_n * tpc_n
    count = len(kinds)
    shards = args
    own_sem, line_send, line_recv, col_send, col_recv, tp_send, tp_recv = scratch[:7]
    staged = scratch[7:]
    fo, z, y, x, c = (lax.axis_index(n) for n in ("fo", "fi", "ctx", "tpx", "tpc"))
    q = x * tpc_n + c

    items = [(i, f) for f in range(fo_n) for i in range(count)]

    def source(n):
        i, f = items[n]
        if kinds[i] == "share":
            a = shards[i].shape[1] // tp_n
            return shards[i].at[f, pl.ds(pl.multiple_of(q * a, a), a), :]
        return shards[i].at[f]

    def place(n, zb, yb):
        i, f = items[n]
        a, b = shards[i].shape[1:]
        block = (f * fi_n + zb) * ctx_n + yb
        if kinds[i] == "col":
            return outs[i].at[:, pl.ds(pl.multiple_of(block * b, b), b)]
        if kinds[i] == "share":
            part = a // tp_n
            return outs[i].at[pl.ds(pl.multiple_of(block * a + q * part, part), part), :]
        return outs[i].at[pl.ds(pl.multiple_of(block * a, a), a), :]

    def line(n, side, step, first):
        block = z - step if side == 0 else z + step
        to = z + 1 if side == 0 else z - 1
        return pltpu.make_async_remote_copy(
            src_ref=source(n) if first else place(n, block, y),
            dst_ref=place(n, block, y),
            send_sem=line_send.at[n, side, step],
            recv_sem=line_recv.at[n, side, step],
            device_id=(fo, to, y, x, c),
            device_id_type=MESH_ID,
        )

    def sends(side, step):
        block = z - step if side == 0 else z + step
        to = z + 1 if side == 0 else z - 1
        return (block >= 0) & (block < fi_n) & (to >= 0) & (to < fi_n)

    def across(n, zb, dy, first=False):
        return pltpu.make_async_remote_copy(
            src_ref=source(n) if first else place(n, zb, y),
            dst_ref=place(n, zb, y),
            send_sem=col_send.at[n, zb, dy],
            recv_sem=col_recv.at[n, zb, dy],
            device_id=(fo, z, lax.rem(y + dy, ctx_n), x, c),
            device_id_type=MESH_ID,
        )

    def stage(n):
        return pltpu.make_async_copy(source(n), staged[n], own_sem.at[n, 0])

    def keep(n):
        return pltpu.make_async_copy(staged[n], place(n, z, y), own_sem.at[n, 1])

    for n in range(len(items)):
        for side in (0, 1):

            @pl.when(sends(side, 0))
            def _():
                line(n, side, 0, True).start()

        for dy in range(1, ctx_n):
            across(n, z, dy, True).start()
        stage(n).start()

    yield
    for n in range(len(items)):
        stage(n).wait()
        keep(n).start()

    for step in range(fi_n - 1):
        for n in range(len(items)):
            for side in (0, 1):
                block = z - 1 - step if side == 0 else z + 1 + step

                @pl.when((block >= 0) & (block < fi_n))
                def _():
                    pltpu.make_async_remote_copy(
                        src_ref=place(n, block, y),
                        dst_ref=place(n, block, y),
                        send_sem=line_send.at[n, side, step],
                        recv_sem=line_recv.at[n, side, step],
                        device_id=(fo, z, y, x, c),
                        device_id_type=MESH_ID,
                    ).wait_recv()
                    for dy in range(1, ctx_n):
                        across(n, block, dy).start()

                if step < fi_n - 2:

                    @pl.when(sends(side, step + 1))
                    def _():
                        line(n, side, step + 1, False).start()

        yield

    for n in range(len(items)):
        keep(n).wait()
        for dy in range(1, ctx_n):
            for zb in range(fi_n):
                pltpu.make_async_remote_copy(
                    src_ref=place(n, zb, y),
                    dst_ref=place(n, zb, lax.rem(y + ctx_n - dy, ctx_n)),
                    send_sem=col_send.at[n, zb, dy],
                    recv_sem=col_recv.at[n, zb, dy],
                    device_id=(fo, z, y, x, c),
                    device_id_type=MESH_ID,
                ).wait_recv()
        i, f = items[n]
        if kinds[i] == "share":
            a = shards[i].shape[1]
            part = a // tp_n

            def spread(block, step, n=n, i=i, f=f, a=a, part=part):
                other = lax.rem(q + step, tp_n)
                at = (f * fi_n * ctx_n + block) * a + q * part
                return pltpu.make_async_remote_copy(
                    src_ref=outs[i].at[pl.ds(pl.multiple_of(at, part), part), :],
                    dst_ref=outs[i].at[pl.ds(pl.multiple_of(at, part), part), :],
                    send_sem=tp_send.at[n, block, step],
                    recv_sem=tp_recv.at[n, block, step],
                    device_id=(fo, z, y, other // tpc_n, lax.rem(other, tpc_n)),
                    device_id_type=MESH_ID,
                )

            def spread_all(block, carry):
                for step in range(1, tp_n):
                    spread(block, step).start()
                return carry

            lax.fori_loop(0, fi_n * ctx_n, spread_all, 0)

    yield

    for n in range(len(items)):
        i, f = items[n]
        if kinds[i] == "share":
            a = shards[i].shape[1]
            part = a // tp_n

            def landed(block, carry, n=n, i=i, f=f, a=a, part=part):
                for step in range(1, tp_n):
                    origin = lax.rem(q + tp_n - step, tp_n)
                    at = (f * fi_n * ctx_n + block) * a
                    mine = pl.ds(pl.multiple_of(at + q * part, part), part)
                    theirs = pl.ds(pl.multiple_of(at + origin * part, part), part)
                    copy = pltpu.make_async_remote_copy(
                        src_ref=outs[i].at[mine, :],
                        dst_ref=outs[i].at[theirs, :],
                        send_sem=tp_send.at[n, block, step],
                        recv_sem=tp_recv.at[n, block, step],
                        device_id=(fo, z, y, x, c),
                        device_id_type=MESH_ID,
                    )
                    copy.wait_send()
                    copy.wait_recv()
                return carry

            lax.fori_loop(0, fi_n * ctx_n, landed, 0)
        for side in (0, 1):
            for step in range(fi_n - 1):

                @pl.when(sends(side, step))
                def _():
                    line(n, side, step, step == 0).wait_send()

        for dy in range(1, ctx_n):
            for zb in range(fi_n):
                across(n, zb, dy).wait_send()


def collect_job(sizes, kinds, shards):
    fo_n, fi_n, ctx_n, tpx_n, tpc_n = (sizes[n] for n in ("fo", "fi", "ctx", "tpx", "tpc"))
    tp_n = tpx_n * tpc_n
    blocks = fo_n * fi_n * ctx_n
    outs, staged = [], []
    for kind, shard in zip(kinds, shards):
        _, a, b = shard.shape
        shape = (a, blocks * b) if kind == "col" else (blocks * a, b)
        outs.append((jax.ShapeDtypeStruct(shape, shard.dtype), HBM_SPEC))
        staged.append(pltpu.VMEM((a // tp_n if kind == "share" else a, b), shard.dtype))
    n = len(kinds) * fo_n
    return {
        "args": [(shard, HBM_SPEC) for shard in shards],
        "outs": outs,
        "scratch": [
            pltpu.SemaphoreType.DMA((n, 2)),
            pltpu.SemaphoreType.DMA((n, 2, fi_n)),
            pltpu.SemaphoreType.DMA((n, 2, fi_n)),
            pltpu.SemaphoreType.DMA((n, fi_n, ctx_n)),
            pltpu.SemaphoreType.DMA((n, fi_n, ctx_n)),
            pltpu.SemaphoreType.DMA((n, fi_n * ctx_n, tp_n)),
            pltpu.SemaphoreType.DMA((n, fi_n * ctx_n, tp_n)),
        ]
        + staged * fo_n,
        "run": functools.partial(collect_run, tuple(kinds)),
    }


def place_job(sizes, local):
    fo_n, fi_n, ctx_n, tpx_n, tpc_n = (sizes[n] for n in ("fo", "fi", "ctx", "tpx", "tpc"))
    chip_n = fi_n * ctx_n * tpx_n
    rows, depth = local.shape[3:]
    shape = (rows * tpx_n * tpc_n, depth * fo_n * fi_n * ctx_n)
    return {
        "args": [(local, HBM_SPEC)],
        "outs": [(jax.ShapeDtypeStruct(shape, BF16), HBM_SPEC)] * 3,
        "scratch": [pltpu.VMEM(local.shape, BF16)]
        + [pltpu.SemaphoreType.DMA((fo_n, 3, chip_n))] * 2
        + [pltpu.SemaphoreType.DMA((fo_n, 3, chip_n, tpc_n))] * 2,
        "run": place_run,
    }


def place_run(sizes, args, outs, scratch):
    fo_n, fi_n, ctx_n, tpx_n, tpc_n = (sizes[n] for n in ("fo", "fi", "ctx", "tpx", "tpc"))
    (local,) = args
    staged, load_sem, keep_sem, pair_send, pair_recv = scratch
    chip_n = fi_n * ctx_n * tpx_n
    rows, depth = local.shape[3:]
    fo, z, y, x, c = (lax.axis_index(n) for n in ("fo", "fi", "ctx", "tpx", "tpc"))

    def spot(k, f, chip, core):
        block = f * fi_n * ctx_n + chip // tpx_n
        return outs[k].at[
            pl.ds(pl.multiple_of((lax.rem(chip, tpx_n) * tpc_n + core) * rows, rows), rows),
            pl.ds(pl.multiple_of(block * depth, depth), depth),
        ]

    def load(f, k, chip):
        return pltpu.make_async_copy(
            local.at[f, chip, k], staged.at[f, chip, k], load_sem.at[f, k, chip]
        )

    def keep(f, k, chip):
        return pltpu.make_async_copy(
            staged.at[f, chip, k], spot(k, f, chip, c), keep_sem.at[f, k, chip]
        )

    def pair_copy(f, k, chip, dc, core):
        return pltpu.make_async_remote_copy(
            src_ref=local.at[f, chip, k],
            dst_ref=spot(k, f, chip, core),
            send_sem=pair_send.at[f, k, chip, dc],
            recv_sem=pair_recv.at[f, k, chip, dc],
            device_id=(fo, z, y, x, lax.rem(c + dc, tpc_n)),
            device_id_type=MESH_ID,
        )

    def launch(step, carry):
        f, chip = step // chip_n, lax.rem(step, chip_n)
        for k in range(3):
            load(f, k, chip).start()
            for dc in range(1, tpc_n):
                pair_copy(f, k, chip, dc, c).start()
        return carry

    def store(step, carry):
        f, chip = step // chip_n, lax.rem(step, chip_n)
        for k in range(3):
            load(f, k, chip).wait()
            keep(f, k, chip).start()
        return carry

    def settle(step, carry):
        f, chip = step // chip_n, lax.rem(step, chip_n)
        for k in range(3):
            keep(f, k, chip).wait()
            for dc in range(1, tpc_n):
                pair_copy(f, k, chip, dc, c).wait_send()
                pair_copy(f, k, chip, dc, lax.rem(c + tpc_n - dc, tpc_n)).wait_recv()
        return carry

    lax.fori_loop(0, fo_n * chip_n, launch, 0)
    yield
    lax.fori_loop(0, fo_n * chip_n, store, 0)
    yield
    lax.fori_loop(0, fo_n * chip_n, settle, 0)


def pair_body(sizes, fo_n, *refs):
    fi_n, ctx_n, tpx_n, tpc_n = (sizes[n] for n in ("fi", "ctx", "tpx", "tpc"))
    grads, (out_ref, mine, theirs, load_sem, store_sem, send_sem, recv_sem) = refs[:3], refs[3:]
    chip_n = fi_n * ctx_n * tpx_n
    rows, depth = mine.shape[2:]
    fo, z, y, x, c = (lax.axis_index(n) for n in ("fo", "fi", "ctx", "tpx", "tpc"))
    sibling = (fo, z, y, x, 1 - c)
    barrier = pltpu.get_barrier_semaphore()
    pl.semaphore_signal(barrier, inc=1, device_id=sibling, device_id_type=MESH_ID)
    pl.semaphore_wait(barrier, 1)

    def spot(k, at, core):
        block, side = at // tpx_n, lax.rem(at, tpx_n)
        return grads[k].at[
            pl.ds(pl.multiple_of((side * tpc_n + core) * rows, rows), rows),
            pl.ds(pl.multiple_of(block * depth, depth), depth),
        ]

    def load(k, at):
        return pltpu.make_async_copy(spot(k, at, c), mine.at[at, k], load_sem.at[at, k])

    def store(k, at):
        return pltpu.make_async_copy(mine.at[at, k], out_ref.at[at, k], store_sem.at[at, k])

    def give(k, at):
        return pltpu.make_async_remote_copy(
            src_ref=spot(k, at, 1 - c),
            dst_ref=theirs.at[at, k],
            send_sem=send_sem.at[at, k],
            recv_sem=recv_sem.at[at, k],
            device_id=sibling,
            device_id_type=MESH_ID,
        )

    def launch(at, carry):
        for k in range(3):
            give(k, at).start()
            load(k, at).start()
        return carry

    def add(at, carry):
        for k in range(3):
            load(k, at).wait()
            give(k, at).wait_recv()
            mine[at, k] = (mine[at, k].astype(F32) + theirs[at, k].astype(F32)).astype(BF16)
            store(k, at).start()
        return carry

    def settle(at, carry):
        for k in range(3):
            give(k, at).wait_send()
            store(k, at).wait()
        return carry

    total = fo_n * chip_n
    lax.fori_loop(0, total, launch, 0)
    lax.fori_loop(0, total, add, 0)
    lax.fori_loop(0, total, settle, 0)


def pair_sum(sizes, grads, collective_id):
    fo_n, fi_n, ctx_n, tpx_n, tpc_n = (sizes[n] for n in ("fo", "fi", "ctx", "tpx", "tpc"))
    rows = grads[0].shape[0] // (tpx_n * tpc_n)
    depth = grads[0].shape[1] // (fo_n * fi_n * ctx_n)
    total = fo_n * fi_n * ctx_n * tpx_n
    shape = (total, 3, rows, depth)
    hbm = pl.BlockSpec(memory_space=pl.ANY)
    return pl.pallas_call(
        functools.partial(pair_body, sizes, fo_n),
        out_shape=jax.ShapeDtypeStruct(shape, BF16),
        in_specs=[hbm] * 3,
        out_specs=hbm,
        scratch_shapes=[pltpu.VMEM(shape, BF16)] * 2 + [pltpu.SemaphoreType.DMA((total, 3))] * 4,
        compiler_params=pltpu.CompilerParams(
            collective_id=collective_id, has_side_effects=True, vmem_limit_bytes=32 << 20
        ),
        cost_estimate=pl.CostEstimate(flops=0, bytes_accessed=60_000_000, transcendentals=0),
        name="pair_sum",
    )(*grads)


def finish_run(kinds, sizes, args, outs, scratch):
    fi_n, ctx_n, tpx_n, tpc_n = (sizes[n] for n in ("fi", "ctx", "tpx", "tpc"))
    tp_n = tpx_n * tpc_n
    count = len(kinds)
    extra = len(args) - count
    parts, quarters = args[:count], args[count:]
    outs, wholes = outs[:count], outs[count:]
    mine, other, coming = (scratch[k * count : (k + 1) * count] for k in range(3))
    staged, (tiny, *sems) = scratch[3 * count : 3 * count + extra], scratch[3 * count + extra :]
    load_sem, col_send, col_recv, line_send, line_recv, tp_send, tp_recv = sems[:7]
    fo, z, y, x, c = (lax.axis_index(n) for n in ("fo", "fi", "ctx", "tpx", "tpc"))
    q = x * tpc_n + c

    spreads = [
        tp_spread(sizes, quarters[j], staged[j], wholes[j], sems[8 + 5 * j : 13 + 5 * j])
        for j in range(extra)
    ]

    def stage(j):
        return pltpu.make_async_copy(quarters[j], staged[j], sems[7].at[j])

    for j in range(extra):
        spreads[j][0]()
        stage(j).start()

    def view(n, zb, yb):
        a, b = mine[n].shape[1:]
        block = zb * ctx_n + yb
        if kinds[n] == "col":
            return parts[n].at[:, pl.ds(pl.multiple_of(block * b, b), b)]
        if kinds[n] == "share":
            return parts[n].at[pl.ds(pl.multiple_of(block * a * tp_n + q * a, a), a), :]
        return parts[n].at[pl.ds(pl.multiple_of(block * a, a), a), :]

    def across(n, zb, dy):
        to = lax.rem(y + dy, ctx_n)
        return pltpu.make_async_remote_copy(
            src_ref=view(n, zb, to),
            dst_ref=other[n].at[dy - 1, zb],
            send_sem=col_send.at[n, zb, dy],
            recv_sem=col_recv.at[n, zb, dy],
            device_id=(fo, z, to, x, c),
            device_id_type=MESH_ID,
        )

    def load(n, zb):
        return pltpu.make_async_copy(view(n, zb, y), mine[n].at[zb], load_sem.at[n, zb])

    order = [fi_n - 1 - k // 2 if k % 2 == 0 else k // 2 for k in range(fi_n)]
    for zb in order:
        for n in range(count):
            for dy in range(1, ctx_n):
                across(n, zb, dy).start()
            load(n, zb).start()

    yield
    for j in range(extra):
        stage(j).wait()
        spreads[j][1].start()

    def line(n, side, target):
        at = jnp.where(target == (z + 1 if side == 0 else z - 1), fi_n, target) if side == 1 else target
        return pltpu.make_async_remote_copy(
            src_ref=mine[n].at[target],
            dst_ref=coming[n].at[at],
            send_sem=line_send.at[n, side, target],
            recv_sem=line_recv.at[n, side, target],
            device_id=(fo, z + 1 if side == 0 else z - 1, y, x, c),
            device_id_type=MESH_ID,
        )

    def came(n, side, target, at):
        pltpu.make_async_remote_copy(
            src_ref=mine[n].at[target],
            dst_ref=coming[n].at[at],
            send_sem=line_send.at[n, side, target],
            recv_sem=line_recv.at[n, side, target],
            device_id=(fo, z, y, x, c),
            device_id_type=MESH_ID,
        ).wait_recv()

    def ready(n, target):
        load(n, target).wait()
        for dy in range(1, ctx_n):
            across(n, target, dy).wait_recv()

    def add(n, target, use, store):
        a = mine[n].shape[1]
        tile = math.gcd(a, 64)

        def rows(step, carry):
            at = pl.ds(pl.multiple_of(step * tile, tile), tile)
            summed = mine[n][target, at, :].astype(F32)
            for dy in range(1, ctx_n):
                summed = summed + other[n][dy - 1, target, at, :].astype(F32)
            for slot in use:
                summed = summed + coming[n][slot, at, :].astype(F32)
            store(at, summed.astype(BF16))
            return carry

        lax.fori_loop(0, a // tile, rows, 0)

    for step in range(fi_n - 1):
        for n in range(count):
            for side in (0, 1):
                target = fi_n - 1 - step if side == 0 else step
                passes = (z < target) if side == 0 else (z > target)
                inner = (z > 0) if side == 0 else (z < fi_n - 1)

                def back(at, values, n=n, target=target):
                    mine[n][target, at, :] = values

                @pl.when(passes & inner)
                def _():
                    ready(n, target)
                    came(n, side, target, target)
                    add(n, target, (target,), back)
                    line(n, side, target).start()

                @pl.when(passes & jnp.logical_not(inner))
                def _():
                    ready(n, target)
                    add(n, target, (), back)
                    line(n, side, target).start()

        yield

    for n in range(count):
        ready(n, z)

        def out(at, values, n=n):
            if kinds[n] == "share":
                a = mine[n].shape[1]
                outs[n][q, at, :] = values
            elif kinds[n] == "sum":
                tiny[q, at, :] = values
            else:
                outs[n][at, :] = values

        @pl.when(z > 0)
        def _():
            came(n, 0, z, z)

        @pl.when(z < fi_n - 1)
        def _():
            came(n, 1, z, fi_n)

        @pl.when((z > 0) & (z < fi_n - 1))
        def _():
            add(n, z, (z, fi_n), out)

        @pl.when((z == 0) & (z < fi_n - 1))
        def _():
            add(n, z, (fi_n,), out)

        @pl.when((z > 0) & (z == fi_n - 1))
        def _():
            add(n, z, (z,), out)

        @pl.when((z == 0) & (z == fi_n - 1))
        def _():
            add(n, z, (), out)

        if kinds[n] in ("share", "sum"):
            held = outs[n] if kinds[n] == "share" else tiny
            for step in range(1, tp_n):
                peer = lax.rem(q + step, tp_n)
                pltpu.make_async_remote_copy(
                    src_ref=held.at[q],
                    dst_ref=held.at[q],
                    send_sem=tp_send.at[n, step],
                    recv_sem=tp_recv.at[n, step],
                    device_id=(fo, z, y, peer // tpc_n, lax.rem(peer, tpc_n)),
                    device_id_type=MESH_ID,
                ).start()

    yield
    for j in range(extra):
        spreads[j][2]()

    for n in range(count):
        if kinds[n] in ("share", "sum"):
            held = outs[n] if kinds[n] == "share" else tiny
            for step in range(1, tp_n):
                origin = lax.rem(q + tp_n - step, tp_n)
                copy = pltpu.make_async_remote_copy(
                    src_ref=held.at[q],
                    dst_ref=held.at[origin],
                    send_sem=tp_send.at[n, step],
                    recv_sem=tp_recv.at[n, step],
                    device_id=(fo, z, y, x, c),
                    device_id_type=MESH_ID,
                )
                copy.wait_send()
                copy.wait_recv()
            if kinds[n] == "sum":
                summed = tiny[0].astype(F32)
                for k in range(1, tp_n):
                    summed = summed + tiny[k].astype(F32)
                outs[n][...] = summed.astype(BF16)
        for target in range(fi_n):
            for dy in range(1, ctx_n):
                across(n, target, dy).wait_send()
            for side in (0, 1):

                @pl.when((z < target) if side == 0 else (z > target))
                def _():
                    line(n, side, target).wait_send()

    for j in range(extra):
        spreads[j][3]()


def finish_job(sizes, kinds, parts, quarters):
    fi_n, ctx_n, tpx_n, tpc_n = (sizes[n] for n in ("fi", "ctx", "tpx", "tpc"))
    tp_n = tpx_n * tpc_n
    blocks = fi_n * ctx_n
    count, extra = len(kinds), len(quarters)
    own, shapes = [], []
    sum_shape = (16, 256)
    for kind, part in zip(kinds, parts):
        a, b = part.shape
        if kind == "col":
            own.append((a, b // blocks))
            shapes.append(own[-1])
        elif kind == "share":
            own.append((a // (blocks * tp_n), b))
            shapes.append((tp_n,) + own[-1])
        else:
            own.append((a // blocks, b))
            shapes.append(own[-1])
        if kind == "sum":
            sum_shape = own[-1]
    wide = [(v.shape[0], v.shape[1] * tp_n) for v in quarters]
    some = max(extra, 1)
    shapes = [jax.ShapeDtypeStruct(shape, BF16) for shape in shapes + wide]
    return {
        "args": [(arg, HBM_SPEC) for arg in (*parts, *quarters)],
        "outs": list(zip(shapes, [VMEM_SPEC] * count + [HBM_SPEC] * extra)),
        "scratch": [pltpu.VMEM((fi_n,) + s, BF16) for s in own]
        + [pltpu.VMEM((max(ctx_n - 1, 1), fi_n) + s, BF16) for s in own]
        + [pltpu.VMEM((fi_n + 1,) + s, BF16) for s in own]
        + [pltpu.VMEM(v.shape, BF16) for v in quarters]
        + [
            pltpu.VMEM((tp_n,) + sum_shape, BF16),
            pltpu.SemaphoreType.DMA((count, fi_n)),
            pltpu.SemaphoreType.DMA((count, fi_n, ctx_n)),
            pltpu.SemaphoreType.DMA((count, fi_n, ctx_n)),
            pltpu.SemaphoreType.DMA((count, 2, fi_n)),
            pltpu.SemaphoreType.DMA((count, 2, fi_n)),
            pltpu.SemaphoreType.DMA((count, tp_n)),
            pltpu.SemaphoreType.DMA((count, tp_n)),
            pltpu.SemaphoreType.DMA((some,)),
            *(tp_spread_sems(sizes) * extra),
        ],
        "run": functools.partial(finish_run, tuple(kinds)),
    }


def attend_body(place_ref, q_ref, kv_ref, rope_ref, out_ref, log_ref):
    block_rows, key_count = q_ref.shape[0], kv_ref.shape[0]
    first = place_ref[0] + pl.program_id(1) * block_rows
    keys = jnp.concatenate([kv_ref[:, :NOPE], rope_ref[...]], axis=1)
    scores = dot_nt(q_ref[...], keys)
    row = first + lax.broadcasted_iota(jnp.int32, (block_rows, 1), 0)
    limit = jnp.maximum(row, place_ref[1] - 1)
    key = lax.broadcasted_iota(jnp.int32, (block_rows, key_count), 1)
    scores = jnp.where(key <= limit, scores, -1e30)
    top = jnp.max(scores, axis=1, keepdims=True)
    exponent = jnp.exp(scores - top)
    row_total = jnp.sum(exponent, axis=1, keepdims=True)
    summed = jnp.dot(exponent.astype(BF16), kv_ref[:, NOPE:], preferred_element_type=F32)
    out_ref[...] = (summed / row_total).astype(BF16)
    log_total = jnp.broadcast_to(top + jnp.log(row_total), (block_rows, 128))
    log_ref[0] = log_total.T[:1]

def attend(place, query, key_value, rope, block_rows):
    rows, key_count = query.shape[0], key_value.shape[0]
    heads = query.shape[1] // HEAD
    return pl.pallas_call(
        attend_body,
        out_shape=(jax.ShapeDtypeStruct((rows, heads * VDIM), BF16), jax.ShapeDtypeStruct((heads, 1, rows), F32)),
        grid_spec=pltpu.PrefetchScalarGridSpec(
            num_scalar_prefetch=1,
            grid=(heads, rows // block_rows),
            in_specs=[
                pl.BlockSpec((block_rows, HEAD), lambda h, i, s: (i, h)),
                pl.BlockSpec((key_count, HEAD), lambda h, i, s: (0, h)),
                pl.BlockSpec((key_count, NOPE), lambda h, i, s: (0, 0)),
            ],
            out_specs=[
                pl.BlockSpec((block_rows, VDIM), lambda h, i, s: (i, h)),
                pl.BlockSpec((1, 1, block_rows), lambda h, i, s: (h, 0, i)),
            ],
        ),
        compiler_params=pltpu.CompilerParams(vmem_limit_bytes=48 << 20),
        cost_estimate=pl.CostEstimate(flops=4 * rows * key_count * heads * HEAD, bytes_accessed=20_000_000, transcendentals=rows * key_count * heads),
        name="attend",
    )(place, query, key_value, rope)

def attend_back_body(place_ref, q_ref, kv_ref, rope_ref, dout_ref, log_ref, table_ref, dq_ref, dkv_ref, drope_ref, keys_acc, values_acc):
    block_rows, key_count = q_ref.shape[0], kv_ref.shape[0]
    head, step = pl.program_id(0), pl.program_id(1)
    first = place_ref[0] + step * block_rows
    keys = jnp.concatenate([kv_ref[:, :NOPE], rope_ref[...]], axis=1)
    scores = dot_nt(keys, q_ref[...])
    row = first + lax.broadcasted_iota(jnp.int32, (1, block_rows), 1)
    limit = jnp.maximum(row, place_ref[1] - 1)
    key = lax.broadcasted_iota(jnp.int32, (key_count, block_rows), 0)
    soft = jnp.exp(jnp.where(key <= limit, scores, -1e30) - log_ref[0])
    soft_grad = dot_nt(kv_ref[:, NOPE:], dout_ref[...])
    mean = jnp.sum(soft * soft_grad, axis=0, keepdims=True)
    score_grad = (soft * (soft_grad - mean)).astype(BF16)
    values = jnp.dot(soft.astype(BF16), dout_ref[...], preferred_element_type=F32)
    keys_grad = jnp.dot(score_grad, q_ref[...], preferred_element_type=F32)
    dq_ref[...] = (dot_tn(score_grad, keys) * table_ref[...]).astype(BF16)

    @pl.when(step == 0)
    def _():
        keys_acc[...] = keys_grad
        values_acc[...] = values

    @pl.when(step > 0)
    def _():
        keys_acc[...] += keys_grad
        values_acc[...] += values

    @pl.when(step == pl.num_programs(1) - 1)
    def _():
        dkv_ref[...] = jnp.concatenate([keys_acc[:, :NOPE], values_acc[...]], axis=1).astype(BF16)

        @pl.when(head == 0)
        def _():
            drope_ref[...] = keys_acc[:, NOPE:]

        @pl.when(head > 0)
        def _():
            drope_ref[...] += keys_acc[:, NOPE:]

def attend_back(place, query, key_value, rope, dout, log_total, table, block_rows):
    rows, key_count = query.shape[0], key_value.shape[0]
    heads = query.shape[1] // HEAD
    return pl.pallas_call(
        attend_back_body,
        out_shape=(jax.ShapeDtypeStruct((rows, heads * HEAD), BF16), jax.ShapeDtypeStruct((key_count, heads * HEAD), BF16), jax.ShapeDtypeStruct((key_count, NOPE), F32)),
        grid_spec=pltpu.PrefetchScalarGridSpec(
            num_scalar_prefetch=1,
            grid=(heads, rows // block_rows),
            in_specs=[
                pl.BlockSpec((block_rows, HEAD), lambda h, i, s: (i, h)),
                pl.BlockSpec((key_count, HEAD), lambda h, i, s: (0, h)),
                pl.BlockSpec((key_count, NOPE), lambda h, i, s: (0, 0)),
                pl.BlockSpec((block_rows, VDIM), lambda h, i, s: (i, h)),
                pl.BlockSpec((1, 1, block_rows), lambda h, i, s: (h, 0, i)),
                pl.BlockSpec((block_rows, HEAD), lambda h, i, s: (i, 0)),
            ],
            out_specs=[
                pl.BlockSpec((block_rows, HEAD), lambda h, i, s: (i, h)),
                pl.BlockSpec((key_count, HEAD), lambda h, i, s: (0, h)),
                pl.BlockSpec((key_count, NOPE), lambda h, i, s: (0, 0)),
            ],
            scratch_shapes=[pltpu.VMEM((key_count, HEAD), F32), pltpu.VMEM((key_count, VDIM), F32)],
        ),
        compiler_params=pltpu.CompilerParams(vmem_limit_bytes=56 << 20),
        cost_estimate=pl.CostEstimate(flops=10 * rows * key_count * heads * HEAD, bytes_accessed=40_000_000, transcendentals=rows * key_count * heads),
        name="attend_back",
    )(place, query, key_value, rope, dout, log_total, table)


def build(sizes):
    fo_n, fi_n, ctx_n, tpx_n, tpc_n = (sizes[name] for name in ("fo", "fi", "ctx", "tpx", "tpc"))
    tp_n = tpx_n * tpc_n
    row_shards = fo_n * fi_n * ctx_n
    plane_experts = ctx_n * tpx_n
    z_part = fi_n // tpc_n

    def expert_weights(gate, up, down):
        local = jnp.stack([gate.transpose(0, 2, 1), up.transpose(0, 2, 1), down], axis=1)
        return lax.all_gather(local, "fo", axis=0) if fo_n > 1 else local[None]

    def shard_of(weight):
        return lax.all_gather(weight, "fo", axis=0) if fo_n > 1 else weight[None]

    def fo_sum(part, kind):
        if fo_n == 1:
            return part
        if kind == "col":
            a = part.shape[0]
            part = part.reshape(a, fo_n, -1)
            return lax.psum_scatter(part, "fo", scatter_dimension=1, tiled=True).reshape(a, -1)
        return lax.psum_scatter(part, "fo", scatter_dimension=0, tiled=True)

    def own_expert_grads(mine):
        mine = mine.reshape((fo_n, -1) + mine.shape[1:])
        got = lax.all_to_all(mine, CHIPS, split_axis=1, concat_axis=1, tiled=True)
        if fo_n > 1:
            got = lax.psum_scatter(got, "fo", scatter_dimension=0, tiled=True)
        got = got[0].astype(F32)
        return (got[:, 0].transpose(0, 2, 1), got[:, 1].transpose(0, 2, 1), got[:, 2])

    def shards(
        tokens,
        out_grad,
        routes,
        slot_index,
        prefix,
        attn_gain,
        query_weight,
        latent_down,
        latent_gain,
        latent_up,
        out_weight,
        moe_gain,
        router_weight,
        shared_gate,
        shared_up,
        shared_down,
        expert_gate,
        expert_up,
        expert_down,
    ):
        row_count, width = tokens.shape
        expert_count = expert_gate.shape[0]
        capacity = row_count * routes.shape[1] // expert_count
        quarter = width // tp_n
        tp_index = lax.axis_index(TP)
        own_expert = lax.axis_index(CHIPS)
        plane_base = lax.axis_index("fi") * plane_experts

        def columns(values):
            return lax.dynamic_slice_in_dim(values, tp_index * quarter, quarter, values.ndim - 1)

        depth = latent_down.shape[0]
        down_width = latent_down.shape[1]

        def turned(weight):
            half = weight.shape[-1] // 2
            return jnp.concatenate([-weight[..., half:], weight[..., :half]], axis=-1)

        small = jnp.concatenate(
            [
                latent_down,
                turned(latent_down[:, KVR:]),
                attn_gain[:, None],
                moe_gain[:, None],
                jnp.pad(latent_gain, (0, depth - latent_gain.shape[0]))[:, None],
                router_weight,
            ],
            axis=1,
        )
        used = small.shape[1]
        small = jnp.pad(small, ((0, 0), (0, -used % 128)))
        keys = jnp.where(slot_index < capacity, routes * capacity + slot_index, -1).T
        keys = jnp.pad(keys, ((0, 8 - keys.shape[0]), (0, 0)), constant_values=-1)
        (small, query_full, up_full, out_full, keys_all), *_ = exchange(
            sizes,
            [
                collect_job(
                    sizes,
                    ("share", "row", "row", "col", "row"),
                    [shard_of(w) for w in (small, query_weight, latent_up, out_weight, keys)],
                )
            ],
            4,
            "collect_attention",
        )
        local_weights, small = lax.optimization_barrier(
            (expert_weights(expert_gate, expert_up, expert_down), small)
        )
        routed_weights = lax.all_to_all(
            local_weights, CHIPS, split_axis=1, concat_axis=1, tiled=True
        )
        wide_down = small[:, : down_width + ROPE]
        down_full = small[:, :down_width]
        gain_at = down_width + ROPE
        gain_one = small[:, gain_at].astype(F32)
        gain_two = small[:, gain_at + 1].astype(F32)
        gain_latent = (
            small[:, gain_at + 2]
            .reshape(row_shards, depth)[:, : latent_gain.shape[0]]
            .reshape(-1)
            .astype(F32)
        )
        router_full = small[:, gain_at + 3 : used]

        keys_all = lax.dynamic_slice_in_dim(
            keys_all, lax.axis_index("fo") * (fi_n * ctx_n * 8), fi_n * ctx_n * 8, 0
        ).reshape(fi_n, ctx_n, 8, row_count)
        keys_column = lax.dynamic_index_in_dim(keys_all, lax.axis_index("ctx"), 1, keepdims=False)
        first_keys = (plane_base + jnp.arange(plane_experts, dtype=jnp.int32)) * capacity
        rel = keys_column[:, None] - first_keys[:, None, None]
        plane_slots = jnp.max(jnp.where((rel >= 0) & (rel < capacity), rel, -1), axis=2)
        token_slots = plane_slots.transpose(0, 2, 1)

        def give_back(rows, gates, bases=None):
            rows = rows.reshape(z_part, ctx_n, capacity, width)
            return give_back_job(sizes, rows, token_slots, gates, bases)

        (slot_grads,), (shared_gate_full, shared_up_full, shared_down_full) = exchange(
            sizes,
            [
                dispatch_job(sizes, columns(out_grad), plane_slots, capacity),
                collect_job(
                    sizes,
                    ("row", "row", "col"),
                    [shard_of(w) for w in (shared_gate, shared_up, shared_down)],
                ),
            ],
            0,
            "dispatch_grads",
        )
        slot_grads = slot_grads.reshape(-1, width)
        ((gate_full, expert_up_full, down_weight),) = exchange(
            sizes, [place_job(sizes, routed_weights)], 5, "place_experts"
        )

        head_count = query_full.shape[1] // (NOPE + ROPE)
        hidden = tokens.astype(F32)
        scale_one = rms_scale(hidden)
        normed_one = hidden * scale_one
        normed_in = (normed_one * gain_one).astype(BF16)
        seq_index = lax.axis_index(("fo", "fi"))
        prefix_len = lax.dynamic_index_in_dim(prefix, seq_index, keepdims=False)
        row_offset = lax.axis_index("ctx") * row_count
        query_pos = row_offset + jnp.arange(row_count, dtype=jnp.int32)
        cos_table, sin_table = rotation_tables(query_pos, ROPE // 2)
        score_scale = (NOPE + ROPE) ** (-0.5)
        cos_wide = jnp.concatenate([cos_table, cos_table], axis=1)
        sin_wide = jnp.concatenate([sin_table, sin_table], axis=1)
        table = score_scale * jnp.concatenate(
            [jnp.ones((row_count, NOPE), F32), cos_wide, sin_wide], axis=1
        )

        latent_raw = dot(normed_in, wide_down)
        latent_part = latent_raw[:, :KVR]
        scale_latent = rms_scale(latent_part)
        normed_latent = latent_part * scale_latent
        latent = (normed_latent * gain_latent).astype(BF16)
        key_rope = (
            latent_raw[:, KVR : KVR + ROPE] * cos_wide + latent_raw[:, KVR + ROPE :] * sin_wide
        ).astype(BF16)
        both = lax.all_gather(
            jnp.concatenate([latent, key_rope, key_rope], axis=1), "ctx", axis=0, tiled=True
        )
        latent_all, rope_all = both[:, :KVR], both[:, KVR:]
        query_heads = query_full.reshape(width, head_count, NOPE + ROPE)
        query_wide = jnp.concatenate(
            [query_heads, turned(query_heads[..., NOPE:])], axis=-1
        ).reshape(width, head_count * HEAD)
        query_in = (
            dot(normed_in, query_wide).reshape(row_count, head_count, HEAD) * table[:, None]
        ).astype(BF16).reshape(row_count, head_count * HEAD)
        key_value = dot(latent_all, up_full).astype(BF16)
        place = jnp.stack([row_offset, prefix_len]).astype(jnp.int32)
        block_rows = min(256, row_count)
        attended, log_totals = attend(place, query_in, key_value, rope_all, block_rows)

        def tp_scatter(partial):
            parts = partial.astype(BF16).reshape(row_count, tp_n, quarter).transpose(1, 0, 2)
            return lax.psum_scatter(parts, TP, scatter_dimension=0, tiled=True)[0].astype(F32)

        def tp_gather(part_rows):
            got = lax.all_gather(part_rows, TP, axis=0)
            return got.transpose(1, 0, 2).reshape(row_count, width)

        residual = columns(tokens).astype(F32) + tp_scatter(dot(attended, out_full))
        scale_two = lax.rsqrt(
            lax.psum(jnp.sum(residual * residual, axis=-1, keepdims=True), TP) / width + EPSILON
        )
        normed_two = residual * scale_two
        gain_two_part = columns(gain_two[None])
        mid_part = (normed_two * gain_two_part).astype(BF16)

        ((slot_rows,),) = exchange(
            sizes, [dispatch_job(sizes, mid_part, plane_slots, capacity)], 1, "dispatch_rows"
        )
        slot_rows = slot_rows.reshape(-1, width)
        normed_mid = tp_gather(mid_part)

        logits = dot(normed_mid, router_full)
        router_prob = jax.nn.softmax(logits, axis=-1)
        slot_prob = jax.nn.softmax(dot(slot_rows, router_full), axis=-1)
        slot_gate = lax.dynamic_slice_in_dim(slot_prob, own_expert, 1, 1)

        gate_pre = dot(normed_mid, shared_gate_full)
        up_pre = dot(normed_mid, shared_up_full)
        shared_dact = dot_nt(out_grad, shared_down_full)
        shared_silu, shared_slope = silu_parts(gate_pre)
        shared_act = (shared_silu * up_pre).astype(BF16)
        shared_dgate = (shared_dact * up_pre * shared_slope).astype(BF16)
        shared_dup = (shared_dact * shared_silu).astype(BF16)
        mid_shared = tp_scatter(
            dot_nt(shared_dgate, shared_gate_full) + dot_nt(shared_dup, shared_up_full)
        )
        out_shared = tp_scatter(dot(shared_act, shared_down_full))

        expert_dact_raw = dot_nt(slot_grads, down_weight)
        expert_gpre = dot_nt(slot_rows, gate_full)
        expert_upre = dot_nt(slot_rows, expert_up_full)
        expert_silu, expert_slope = silu_parts(expert_gpre)
        expert_act_wide = expert_silu * expert_upre
        expert_act = expert_act_wide.astype(BF16)
        slot_gate_grad = jnp.sum(expert_act.astype(F32) * expert_dact_raw, axis=-1)
        expert_dact = expert_dact_raw * slot_gate
        expert_dgate = (expert_dact * expert_upre * expert_slope).astype(BF16)
        expert_dup = (expert_dact * expert_silu).astype(BF16)
        slot_drows = dot(expert_dgate, gate_full) + dot(expert_dup, expert_up_full)
        gate_rows = jnp.broadcast_to(
            slot_gate_grad.reshape(z_part, ctx_n, 1, capacity), (z_part, ctx_n, 8, capacity)
        )
        sdown_grad = dot_tn(shared_act, out_grad)
        sgate_grad = dot_tn(normed_mid, shared_dgate)
        sup_grad = dot_tn(normed_mid, shared_dup)
        shared_kinds = ("row", "row", "col")
        shared_parts = [
            fo_sum(part.astype(BF16), kind)
            for part, kind in zip((sgate_grad, sup_grad, sdown_grad), shared_kinds)
        ]
        (mid_routed, prob_grad), shared_own = exchange(
            sizes,
            [
                give_back(slot_drows.astype(BF16), gate_rows),
                finish_job(sizes, shared_kinds, shared_parts, []),
            ],
            2,
            "give_back_rows",
        )
        sgate_grad, sup_grad, sdown_grad = (part.astype(F32) for part in shared_own)
        prob_grad = prob_grad.T
        logit_grad = (
            router_prob * (prob_grad - jnp.sum(router_prob * prob_grad, axis=-1, keepdims=True))
        ).astype(BF16)

        slot_dout = (slot_grads.astype(F32) * slot_gate).astype(BF16)
        routed_grads = pair_sum(
            sizes,
            [
                dot_tn(expert_dgate, slot_rows).astype(BF16),
                dot_tn(expert_dup, slot_rows).astype(BF16),
                dot_tn(expert_act, slot_dout).astype(BF16),
            ],
            7,
        )
        mid_total = mid_shared + mid_routed + dot_nt(logit_grad, columns(router_full.T).T)
        gain_two_grad = jnp.sum(mid_total * normed_two, axis=0)
        dn_two = mid_total * gain_two_part
        dot_two = lax.psum(jnp.sum(dn_two * normed_two, axis=-1, keepdims=True), TP) / width
        residual_grad = columns(out_grad).astype(F32) + scale_two * (dn_two - normed_two * dot_two)
        attn_dout = tp_gather(residual_grad.astype(BF16))

        out_weight_grad = dot_tn(attended, attn_dout)
        attended_grad = dot_nt(attn_dout, out_full).astype(BF16)
        attended_grad, routed_grads = lax.optimization_barrier((attended_grad, routed_grads))
        egate_grad, eup_grad, edown_grad = own_expert_grads(routed_grads)
        query_grad, kv_grad, rope_grad = attend_back(
            place, query_in, key_value, rope_all, attended_grad, log_totals, table,
            min(512, row_count),
        )
        late_act, query_grad, egate_grad, eup_grad, edown_grad = lax.optimization_barrier(
            (expert_act, query_grad, egate_grad, eup_grad, edown_grad)
        )
        expert_out = (dot(late_act, down_weight) * slot_gate).astype(BF16)
        up_grad = dot_tn(latent_all, kv_grad)
        latent_grad = dot_nt(kv_grad, up_full)
        query_wide_grad = dot_tn(normed_in, query_grad).reshape(width, head_count, HEAD)
        query_weight_grad = jnp.concatenate(
            [
                query_wide_grad[..., :NOPE],
                query_wide_grad[..., NOPE : NOPE + ROPE] - turned(query_wide_grad[..., NOPE + ROPE :]),
            ],
            axis=-1,
        ).reshape(width, head_count * (NOPE + ROPE))
        input_part = tp_scatter(dot_nt(query_grad, query_wide))
        both_grad = lax.psum_scatter(
            jnp.concatenate([latent_grad, rope_grad], axis=1).astype(BF16),
            "ctx",
            scatter_dimension=0,
            tiled=True,
        )
        both_grad = lax.psum(both_grad, TP).astype(F32)
        latent_own = both_grad[:, :KVR]
        rope_own = both_grad[:, KVR : KVR + ROPE] + both_grad[:, KVR + ROPE :]
        gain_latent_grad = jnp.sum(latent_own * normed_latent, axis=0)
        latent_raw_grad = norm_back(latent_own * gain_latent, normed_latent, scale_latent)
        down_out_grad = jnp.concatenate(
            [latent_raw_grad, rotate(rope_own, cos_table, -sin_table)], axis=-1
        ).astype(BF16)
        down_grad = dot_tn(normed_in, down_out_grad)
        input_total = input_part + dot_nt(
            down_out_grad, lax.dynamic_slice_in_dim(down_full, tp_index * quarter, quarter, 0)
        )
        normed_one_part = columns(normed_one)
        gain_one_grad = jnp.sum(input_total * normed_one_part, axis=0)
        dn_one = input_total * columns(gain_one[None])
        dot_one = lax.psum(jnp.sum(dn_one * normed_one_part, axis=-1, keepdims=True), TP) / width
        token_grad = residual_grad + scale_one * (dn_one - normed_one_part * dot_one)
        router_grad = dot_tn(normed_mid, logit_grad)
        pack_grad = jnp.concatenate([down_grad, router_grad], axis=1)
        pack_used = pack_grad.shape[1]
        pack_grad = jnp.pad(pack_grad, ((0, 0), (0, -pack_used % 128)))
        gains = jnp.stack([gain_one_grad, gain_two_grad])
        gains = lax.dynamic_update_slice_in_dim(
            jnp.zeros((2, width), F32), gains, tp_index * quarter, 1
        )
        latent_rows = jnp.pad(
            gain_latent_grad.reshape(row_shards, -1),
            ((0, 0), (0, depth - latent_gain.shape[0])),
        ).reshape(1, width)
        gains = jnp.concatenate([gains, latent_rows * (tp_index == 0).astype(F32)], axis=0)
        gains = jnp.pad(
            gains.reshape(3, row_shards, depth).transpose(1, 0, 2), ((0, 0), (0, 13), (0, 0))
        ).reshape(row_shards * 16, depth)
        kinds = ("share", "sum", "row", "row", "col")
        partials = (pack_grad, gains, query_weight_grad, up_grad, out_weight_grad)
        (output,), done = exchange(
            sizes,
            [
                give_back(expert_out, None, (residual, out_shared)),
                finish_job(
                    sizes,
                    kinds,
                    [fo_sum(part.astype(BF16), kind) for part, kind in zip(partials, kinds)],
                    [token_grad.astype(BF16)],
                ),
            ],
            3,
            "finish_attention",
        )
        pack_own = done[0].reshape(depth, -1).astype(F32)
        gains_own = done[1].astype(F32)
        query_weight_grad, up_grad, out_weight_grad = (part.astype(F32) for part in done[2:5])
        token_grad = done[5].astype(F32)
        return (
            output,
            token_grad,
            gains_own[0],
            query_weight_grad,
            pack_own[:, :down_width],
            gains_own[2, : latent_gain.shape[0]],
            up_grad,
            out_weight_grad,
            gains_own[1],
            pack_own[:, down_width:pack_used],
            sgate_grad,
            sup_grad,
            sdown_grad,
            egate_grad,
            eup_grad,
            edown_grad,
        )

    return shards


EXPERTS = 16


def solution(mesh):
    ctx_n, tp_n = mesh.shape["ctx"], mesh.shape["tp"]
    tpc_n = 2
    tpx_n = tp_n // tpc_n
    fi_n = EXPERTS // (ctx_n * tpx_n)
    sizes = {
        "fo": mesh.shape["fsdp"] // fi_n,
        "fi": fi_n,
        "ctx": ctx_n,
        "tpx": tpx_n,
        "tpc": tpc_n,
    }
    fine = Mesh(mesh.devices.reshape(tuple(sizes.values())), tuple(sizes))
    rows = P(ROWS)
    rows_two = P(ROWS, None)
    rows_tp = P(ROWS, TP)
    tp_rows = P(TP, ROWS)
    wide_in = P(None, ROWS, TP)
    wide_out = P(None, TP, ROWS)
    weights = (
        rows,
        rows_tp,
        rows_two,
        rows,
        rows_tp,
        tp_rows,
        rows,
        rows_two,
        rows_tp,
        rows_tp,
        tp_rows,
        wide_in,
        wide_in,
        wide_out,
    )
    return jax.shard_map(
        build(sizes),
        mesh=fine,
        in_specs=(rows_two, rows_two, rows_two, rows_two, P()) + weights,
        out_specs=(rows_two, rows_two) + weights,
        check_vma=False,
    )
```

```python
import functools
import math

import jax
import jax.numpy as jnp
from jax import lax
from jax.experimental import pallas as pl
from jax.experimental.pallas import tpu as pltpu
from jax.sharding import Mesh
from jax.sharding import PartitionSpec as P

NOPE = 128
ROPE = 64
KVR = 512
VDIM = 128
HEAD = 256

EPSILON = 1e-06
THETA_BASE = 10000.0
F32 = jnp.float32
BF16 = jnp.bfloat16
MESH_ID = pl.DeviceIdType.MESH

ROWS = ("fo", "fi", "ctx")
TP = ("tpx", "tpc")
PLANE = ("ctx", "tpx", "tpc")
CHIPS = ("fi", "ctx", "tpx")


def rotation_tables(positions, half_width):
    freq_table = jnp.exp(jnp.arange(half_width, dtype=F32) * (-math.log(THETA_BASE) / half_width))
    angle_table = positions.astype(F32)[:, None] * freq_table[None, :]
    return (jnp.cos(angle_table), jnp.sin(angle_table))


def rotate(values, cos_table, sin_table):
    half_width = values.shape[-1] // 2
    first_half = values[..., :half_width]
    second_half = values[..., half_width:]
    return jnp.concatenate(
        [
            first_half * cos_table - second_half * sin_table,
            second_half * cos_table + first_half * sin_table,
        ],
        axis=-1,
    )


def silu_parts(values):
    sigma = jax.nn.sigmoid(values)
    return (values * sigma, sigma * (1.0 + values * (1.0 - sigma)))


def rms_scale(values):
    return lax.rsqrt(jnp.mean(values * values, axis=-1, keepdims=True) + EPSILON)


def norm_back(grad_normed, normed, scale_rows):
    return scale_rows * (
        grad_normed - normed * jnp.mean(grad_normed * normed, axis=-1, keepdims=True)
    )


def dot(left, right):
    return jnp.dot(left, right, preferred_element_type=F32)


def dot_nt(left, right):
    return lax.dot_general(left, right, (((1,), (1,)), ((), ())), preferred_element_type=F32)


def dot_tn(left, right):
    return lax.dot_general(left, right, (((0,), (0,)), ((), ())), preferred_element_type=F32)


def ein(spec, left, right):
    return jnp.einsum(spec, left, right, preferred_element_type=F32)


def plane_place(sizes):
    tpx_n, tpc_n = sizes["tpx"], sizes["tpc"]
    fo, z, y, x, c = (lax.axis_index(name) for name in ("fo", "fi", "ctx", "tpx", "tpc"))
    own = (y * tpx_n + x) * tpc_n + c

    def device(index, z_at=None):
        return (
            fo,
            z if z_at is None else z_at,
            index // (tpx_n * tpc_n),
            lax.rem(index // tpc_n, tpx_n),
            lax.rem(index, tpc_n),
        )

    return z, y, x, c, own, device


def greet_plane(sizes):
    fi_n = sizes["fi"]
    plane_n = sizes["ctx"] * sizes["tpx"] * sizes["tpc"]
    z, y, x, c, own, device = plane_place(sizes)
    barrier = pltpu.get_barrier_semaphore()
    for step in range(1, plane_n):
        pl.semaphore_signal(
            barrier,
            inc=1,
            device_id=device(lax.rem(own + step, plane_n)),
            device_id_type=MESH_ID,
        )
    for near in (-1, 1):

        @pl.when((z + near >= 0) & (z + near < fi_n))
        def _():
            pl.semaphore_signal(
                barrier, inc=1, device_id=device(own, z + near), device_id_type=MESH_ID
            )

    sides = (z > 0).astype(jnp.int32) + (z < fi_n - 1).astype(jnp.int32)
    pl.semaphore_wait(barrier, plane_n - 1 + sides)


HBM_SPEC = pl.BlockSpec(memory_space=pl.ANY)
VMEM_SPEC = pl.BlockSpec(memory_space=pltpu.VMEM)


def exchange(sizes, jobs, collective_id, name, flops=0, vmem=56):
    counts = [(len(job["args"]), len(job["outs"]), len(job["scratch"])) for job in jobs]

    def body(*refs):
        at = [0, sum(n[0] for n in counts), sum(n[0] + n[1] for n in counts)]
        running = []
        for job, count in zip(jobs, counts):
            given = [refs[at[k] : at[k] + count[k]] for k in range(3)]
            at = [at[k] + count[k] for k in range(3)]
            running.append(job["run"](sizes, *given))
        greet_plane(sizes)
        while running:
            running = [run for run in running if next(run, "ended") != "ended"]

    results = pl.pallas_call(
        body,
        out_shape=tuple(shape for job in jobs for shape, _ in job["outs"]),
        in_specs=[spec for job in jobs for _, spec in job["args"]],
        out_specs=tuple(spec for job in jobs for _, spec in job["outs"]),
        scratch_shapes=[shape for job in jobs for shape in job["scratch"]],
        compiler_params=pltpu.CompilerParams(
            collective_id=collective_id, has_side_effects=True, vmem_limit_bytes=vmem << 20
        ),
        cost_estimate=pl.CostEstimate(
            flops=flops, bytes_accessed=200_000_000, transcendentals=0
        ),
        name=name,
    )(*[arg for job in jobs for arg, _ in job["args"]])
    grouped, at = [], 0
    for _, count, _ in counts:
        grouped.append(results[at : at + count])
        at += count
    return grouped


def tp_spread(sizes, source, held, whole, sems):
    tpx_n, tpc_n = sizes["tpx"], sizes["tpc"]
    keep_sem, x_send, x_recv, c_send, c_recv = sems
    fo, z, y, x, c = (lax.axis_index(n) for n in ("fo", "fi", "ctx", "tpx", "tpc"))
    wide = source.shape[1]

    def slab(side, core):
        at = (side * tpc_n + core) * wide
        return whole.at[:, pl.ds(pl.multiple_of(at, wide), wide)]

    def origin(dx):
        return lax.rem(x + tpx_n - dx, tpx_n)

    keep = pltpu.make_async_copy(held, slab(x, c), keep_sem)

    def to_chip(dx, side):
        return pltpu.make_async_remote_copy(
            src_ref=source,
            dst_ref=slab(side, c),
            send_sem=x_send.at[dx],
            recv_sem=x_recv.at[dx],
            device_id=(fo, z, y, lax.rem(x + dx, tpx_n), c),
            device_id_type=MESH_ID,
        )

    def to_core(dx, dc, core):
        return pltpu.make_async_remote_copy(
            src_ref=source if dx == 0 else slab(origin(dx), c),
            dst_ref=slab(origin(dx), core),
            send_sem=c_send.at[dx, dc],
            recv_sem=c_recv.at[dx, dc],
            device_id=(fo, z, y, x, lax.rem(c + dc, tpc_n)),
            device_id_type=MESH_ID,
        )

    def start():
        for dx in range(1, tpx_n):
            to_chip(dx, x).start()
        for dc in range(1, tpc_n):
            to_core(0, dc, c).start()

    def relay():
        for dx in range(1, tpx_n):
            to_chip(dx, origin(dx)).wait_recv()
            for dc in range(1, tpc_n):
                to_core(dx, dc, c).start()

    def settle():
        keep.wait()
        for dx in range(tpx_n):
            if dx > 0:
                to_chip(dx, x).wait_send()
            for dc in range(1, tpc_n):
                to_core(dx, dc, c).wait_send()
                to_core(dx, dc, lax.rem(c + tpc_n - dc, tpc_n)).wait_recv()

    return start, keep, relay, settle


def tp_spread_sems(sizes):
    tpx_n, tpc_n = sizes["tpx"], sizes["tpc"]
    return [
        pltpu.SemaphoreType.DMA,
        pltpu.SemaphoreType.DMA((tpx_n,)),
        pltpu.SemaphoreType.DMA((tpx_n,)),
        pltpu.SemaphoreType.DMA((tpx_n, tpc_n)),
        pltpu.SemaphoreType.DMA((tpx_n, tpc_n)),
    ]


def dispatch_job(sizes, part_rows, plane_slots, capacity):
    tokens, quarter = part_rows.shape
    fi_n, ctx_n, tpx_n, tpc_n = (sizes[n] for n in ("fi", "ctx", "tpx", "tpc"))
    z_part, plane_n, chips = fi_n // tpc_n, ctx_n * tpx_n * tpc_n, ctx_n * tpx_n
    shape = (z_part, ctx_n, capacity, quarter * tpx_n * tpc_n)
    return {
        "args": [(plane_slots, VMEM_SPEC), (part_rows, HBM_SPEC)],
        "outs": [(jax.ShapeDtypeStruct(shape, BF16), HBM_SPEC)],
        "scratch": [
            pltpu.VMEM((fi_n, tokens, quarter), BF16),
            pltpu.VMEM((fi_n, chips, capacity, quarter), BF16),
            pltpu.SemaphoreType.DMA,
            pltpu.SemaphoreType.DMA((2, fi_n)),
            pltpu.SemaphoreType.DMA((2, fi_n)),
            pltpu.SemaphoreType.DMA((fi_n, chips)),
            pltpu.SemaphoreType.DMA((plane_n, z_part)),
        ],
        "run": dispatch_run,
    }


def dispatch_run(sizes, args, outs, scratch):
    slots_ref, rows_ref = args
    (out_ref,) = outs
    held, picked, own_sem, line_send, line_recv, plane_send, plane_recv = scratch
    fi_n, tpx_n, tpc_n = sizes["fi"], sizes["tpx"], sizes["tpc"]
    plane_n = sizes["ctx"] * tpx_n * tpc_n
    chips = sizes["ctx"] * tpx_n
    z_part = fi_n // tpc_n
    capacity, quarter = picked.shape[2:]
    tokens = held.shape[1]
    z, y, x, c, own, device = plane_place(sizes)
    columns = pl.ds(pl.multiple_of((x * tpc_n + c) * quarter, quarter), quarter)
    load = pltpu.make_async_copy(rows_ref, held.at[z], own_sem)

    def line(side, step):
        block = z - step if side == 0 else z + step
        to = z + 1 if side == 0 else z - 1
        return pltpu.make_async_remote_copy(
            src_ref=held.at[block],
            dst_ref=held.at[block],
            send_sem=line_send.at[side, step],
            recv_sem=line_recv.at[side, step],
            device_id=device(own, to),
            device_id_type=MESH_ID,
        )

    def sends(side, step):
        block = z - step if side == 0 else z + step
        to = z + 1 if side == 0 else z - 1
        return (block >= 0) & (block < fi_n) & (to >= 0) & (to < fi_n)

    def plane_copy(block, chip):
        at = lax.rem(block, z_part)
        return pltpu.make_async_remote_copy(
            src_ref=picked.at[block, chip],
            dst_ref=out_ref.at[at, y, :, columns],
            send_sem=plane_send.at[block, chip],
            recv_sem=plane_recv.at[own, at],
            device_id=device(chip * tpc_n + block // z_part),
            device_id_type=MESH_ID,
        )

    def keep_copy(block, chip):
        return pltpu.make_async_copy(
            picked.at[block, chip],
            out_ref.at[lax.rem(block, z_part), y, :, columns],
            plane_send.at[block, chip],
        )

    def at_home(block, chip):
        return chip * tpc_n + block // z_part == own

    def pick(block):
        def one(chip, carry):
            wanted = slots_ref[block, pl.ds(chip, 1), :]
            rank = lax.broadcasted_iota(jnp.int32, (capacity, tokens), 0)
            hits = jnp.where(rank == wanted, 1.0, 0.0).astype(BF16)
            picked[block, chip] = jnp.dot(
                hits, held[block], preferred_element_type=F32
            ).astype(BF16)

            @pl.when(at_home(block, chip))
            def _():
                keep_copy(block, chip).start()

            @pl.when(jnp.logical_not(at_home(block, chip)))
            def _():
                plane_copy(block, chip).start()

            return carry

        lax.fori_loop(0, chips, one, 0)

    load.start()
    load.wait()
    for side in (0, 1):

        @pl.when(sends(side, 0))
        def _():
            line(side, 0).start()

    yield
    pick(z)
    for step in range(fi_n - 1):
        for side in (0, 1):
            block = z - 1 - step if side == 0 else z + 1 + step

            @pl.when((block >= 0) & (block < fi_n))
            def _():
                pltpu.make_async_remote_copy(
                    src_ref=held.at[block],
                    dst_ref=held.at[block],
                    send_sem=line_send.at[side, step],
                    recv_sem=line_recv.at[side, step],
                    device_id=device(own, z),
                    device_id_type=MESH_ID,
                ).wait_recv()

            if step < fi_n - 2:

                @pl.when(sends(side, step + 1))
                def _():
                    line(side, step + 1).start()

        for side in (0, 1):
            block = z - 1 - step if side == 0 else z + 1 + step

            @pl.when((block >= 0) & (block < fi_n))
            def _():
                pick(block)

        yield

    for step in range(fi_n - 1):
        for side in (0, 1):

            @pl.when(sends(side, step))
            def _():
                line(side, step).wait_send()

    def settle(index, carry):
        block, chip = index // chips, lax.rem(index, chips)

        @pl.when(at_home(block, chip))
        def _():
            keep_copy(block, chip).wait()

        @pl.when(jnp.logical_not(at_home(block, chip)))
        def _():
            plane_copy(block, chip).wait_send()

        return carry

    lax.fori_loop(0, fi_n * chips, settle, 0)

    def arrive(index, carry):
        source, at = index // z_part, lax.rem(index, z_part)

        @pl.when(source != own)
        def _():
            pltpu.make_async_remote_copy(
                src_ref=picked.at[0, 0],
                dst_ref=out_ref.at[at, y, :, columns],
                send_sem=plane_send.at[0, 0],
                recv_sem=plane_recv.at[source, at],
                device_id=device(own),
                device_id_type=MESH_ID,
            ).wait_recv()

        return carry

    lax.fori_loop(0, plane_n * z_part, arrive, 0)


def give_back_run(sizes, args, outs, scratch):
    fi_n, tpx_n, tpc_n = sizes["fi"], sizes["tpx"], sizes["tpc"]
    plane_n = sizes["ctx"] * tpx_n * tpc_n
    chips = sizes["ctx"] * tpx_n
    z_part = fi_n // tpc_n
    ends, gated = len(args) > 3, len(args) == 3
    slots_ref, rows_ref = args[:2]
    out_ref = outs[0]
    got, total, going, coming, plane_send, plane_recv, line_send, line_recv = scratch[:8]
    if gated:
        gates_ref, gate_out = args[2], outs[1]
        gates_got, gate_total, gate_going, gate_coming = scratch[8:12]
        gate_send, gate_recv, gate_line_send, gate_line_recv = scratch[12:]
    if ends:
        held = scratch[8]
        start, keep, relay, spread_settle = tp_spread(sizes, held, held, out_ref, scratch[9:])
    capacity, quarter = got.shape[2:]
    tokens = total.shape[0]
    z, y, x, c, own, device = plane_place(sizes)
    tile = min(256, tokens)

    def piece(target, at):
        side = lax.rem(target, tpx_n * tpc_n)
        return rows_ref.at[
            at,
            target // (tpx_n * tpc_n),
            :,
            pl.ds(pl.multiple_of(side * quarter, quarter), quarter),
        ]

    def plane_copies(target, at):
        made = [
            pltpu.make_async_remote_copy(
                src_ref=piece(target, at),
                dst_ref=got.at[c * z_part + at, own // tpc_n],
                send_sem=plane_send.at[target, at],
                recv_sem=plane_recv.at[own, at],
                device_id=device(target),
                device_id_type=MESH_ID,
            )
        ]
        if gated:
            made.append(
                pltpu.make_async_remote_copy(
                    src_ref=gates_ref.at[at, target // (tpx_n * tpc_n)],
                    dst_ref=gates_got.at[c * z_part + at, own // tpc_n],
                    send_sem=gate_send.at[target, at],
                    recv_sem=gate_recv.at[own, at],
                    device_id=device(target),
                    device_id_type=MESH_ID,
                )
            )
        return made

    def keep_copies(at):
        made = [
            pltpu.make_async_copy(
                piece(own, at), got.at[c * z_part + at, own // tpc_n], plane_recv.at[own, at]
            )
        ]
        if gated:
            made.append(
                pltpu.make_async_copy(
                    gates_ref.at[at, y],
                    gates_got.at[c * z_part + at, own // tpc_n],
                    gate_recv.at[own, at],
                )
            )
        return made

    far_first = z < fi_n // 2
    for turn in range(z_part):
        at = jnp.where(far_first, z_part - 1 - turn, turn)

        def one(step, carry):
            for copy in plane_copies(lax.rem(own + step, plane_n), at):
                copy.start()
            return carry

        for copy in keep_copies(at):
            copy.start()
        lax.fori_loop(1, plane_n, one, 0)

    yield

    def gathered(block):
        def one(chip, carry):
            source, at = chip * tpc_n + block // z_part, lax.rem(block, z_part)

            @pl.when(source == own)
            def _():
                for copy in keep_copies(at):
                    copy.wait()

            @pl.when(source != own)
            def _():
                pltpu.make_async_remote_copy(
                    src_ref=got.at[block, chip],
                    dst_ref=got.at[block, chip],
                    send_sem=plane_send.at[own, at],
                    recv_sem=plane_recv.at[source, at],
                    device_id=device(own),
                    device_id_type=MESH_ID,
                ).wait_recv()
                if gated:
                    pltpu.make_async_remote_copy(
                        src_ref=gates_got.at[block, chip],
                        dst_ref=gates_got.at[block, chip],
                        send_sem=gate_send.at[own, at],
                        recv_sem=gate_recv.at[source, at],
                        device_id=device(own),
                        device_id_type=MESH_ID,
                    ).wait_recv()

            return carry

        lax.fori_loop(0, chips, one, 0)

        def rows(step, carry):
            first = pl.multiple_of(step * tile, tile)
            spots = slots_ref[block, pl.ds(first, tile), :]
            rank = lax.broadcasted_iota(jnp.int32, (tile, capacity), 1)
            summed = jnp.zeros((tile, quarter), F32)
            if gated:
                experts = gate_total.shape[0]
                gates = jnp.zeros((experts, tile), F32)
                expert = lax.broadcasted_iota(jnp.int32, (experts, capacity), 0)
            for chip in range(chips):
                hits = jnp.where(rank == spots[:, chip : chip + 1], 1.0, 0.0).astype(BF16)
                summed = summed + jnp.dot(hits, got[block, chip], preferred_element_type=F32)
                if gated:
                    left = jnp.where(
                        expert == z * chips + chip, gates_got[block, chip, 0:1, :], 0.0
                    ).astype(BF16)
                    gates = gates + dot_nt(left, hits)
            total[pl.ds(first, tile), :] = summed
            if gated:
                gate_total[:, pl.ds(first, tile)] = gates
            return carry

        lax.fori_loop(0, tokens // tile, rows, 0)

    def lines(side, target, to):
        made = [
            pltpu.make_async_remote_copy(
                src_ref=going.at[target],
                dst_ref=coming.at[side, target],
                send_sem=line_send.at[side, target],
                recv_sem=line_recv.at[side, target],
                device_id=device(own, to),
                device_id_type=MESH_ID,
            )
        ]
        if gated:
            made.append(
                pltpu.make_async_remote_copy(
                    src_ref=gate_going.at[target],
                    dst_ref=gate_coming.at[side, target],
                    send_sem=gate_line_send.at[side, target],
                    recv_sem=gate_line_recv.at[side, target],
                    device_id=device(own, to),
                    device_id_type=MESH_ID,
                )
            )
        return made

    for step in range(fi_n - 1):
        for side in (0, 1):
            depth = z if side == 0 else fi_n - 1 - z
            target = fi_n - 1 - step + z if side == 0 else step - (fi_n - 1) + z
            passes, inner = depth <= step, depth > 0

            @pl.when(passes)
            def _():
                gathered(target)

                @pl.when(inner)
                def _():
                    for copy in lines(side, target, z):
                        copy.wait_recv()
                    going[target] = (total[...] + coming[side, target].astype(F32)).astype(BF16)
                    if gated:
                        gate_going[target] = gate_total[...] + gate_coming[side, target]

                @pl.when(jnp.logical_not(inner))
                def _():
                    going[target] = total[...].astype(BF16)
                    if gated:
                        gate_going[target] = gate_total[...]

                for copy in lines(side, target, z + 1 if side == 0 else z - 1):
                    copy.start()

        yield

    gathered(z)
    for side in (0, 1):

        @pl.when((z > 0) if side == 0 else (z < fi_n - 1))
        def _():
            for copy in lines(side, z, z):
                copy.wait_recv()
            total[...] += coming[side, z].astype(F32)
            if gated:
                gate_total[...] += gate_coming[side, z]

    if ends:
        held[...] = (total[...] + args[2][...] + args[3][...]).astype(BF16)
        start()
        keep.start()
    else:
        out_ref[...] = total[...]
    if gated:
        gate_out[...] = gate_total[...]
    yield
    if ends:
        relay()


    for target in range(fi_n):
        for side in (0, 1):

            @pl.when((z < target) if side == 0 else (z > target))
            def _():
                for copy in lines(side, target, z + 1 if side == 0 else z - 1):
                    copy.wait_send()

    def settle(index, carry):
        target, at = index // z_part, lax.rem(index, z_part)

        @pl.when(target != own)
        def _():
            for copy in plane_copies(target, at):
                copy.wait_send()

        return carry

    lax.fori_loop(0, plane_n * z_part, settle, 0)
    yield
    if ends:
        spread_settle()


def give_back_job(sizes, rows, token_slots, gates, bases=None):
    fi_n, ctx_n, tpx_n, tpc_n = (sizes[n] for n in ("fi", "ctx", "tpx", "tpc"))
    z_part, plane_n, chips = fi_n // tpc_n, ctx_n * tpx_n * tpc_n, ctx_n * tpx_n
    capacity, width = rows.shape[2:]
    quarter = width // (tpx_n * tpc_n)
    tokens = token_slots.shape[1]
    experts = fi_n * chips
    gated = gates is not None
    shapes = [jax.ShapeDtypeStruct((tokens, quarter), F32)]
    scratch = [
        pltpu.VMEM((fi_n, chips, capacity, quarter), BF16),
        pltpu.VMEM((tokens, quarter), F32),
        pltpu.VMEM((fi_n, tokens, quarter), BF16),
        pltpu.VMEM((2, fi_n, tokens, quarter), BF16),
        pltpu.SemaphoreType.DMA((plane_n, z_part)),
        pltpu.SemaphoreType.DMA((plane_n, z_part)),
        pltpu.SemaphoreType.DMA((2, fi_n)),
        pltpu.SemaphoreType.DMA((2, fi_n)),
    ]
    args = [token_slots, rows]
    if gated:
        args.append(gates)
        shapes.append(jax.ShapeDtypeStruct((experts, tokens), F32))
        scratch += [
            pltpu.VMEM((fi_n, chips, 8, capacity), F32),
            pltpu.VMEM((experts, tokens), F32),
            pltpu.VMEM((fi_n, experts, tokens), F32),
            pltpu.VMEM((2, fi_n, experts, tokens), F32),
            pltpu.SemaphoreType.DMA((plane_n, z_part)),
            pltpu.SemaphoreType.DMA((plane_n, z_part)),
            pltpu.SemaphoreType.DMA((2, fi_n)),
            pltpu.SemaphoreType.DMA((2, fi_n)),
        ]
    specs = [VMEM_SPEC] + [HBM_SPEC] * (len(args) - 1)
    if bases is not None:
        args += list(bases)
        specs += [VMEM_SPEC] * 2
        shapes = [jax.ShapeDtypeStruct((tokens, width), BF16)]
        scratch += [pltpu.VMEM((tokens, quarter), BF16)] + tp_spread_sems(sizes)
    return {
        "args": list(zip(args, specs)),
        "outs": [(shape, HBM_SPEC if bases is not None else VMEM_SPEC) for shape in shapes],
        "scratch": scratch,
        "run": give_back_run,
    }


def collect_run(kinds, sizes, args, outs, scratch):
    fo_n, fi_n, ctx_n, tpx_n, tpc_n = (sizes[n] for n in ("fo", "fi", "ctx", "tpx", "tpc"))
    tp_n = tpx_n * tpc_n
    count = len(kinds)
    shards = args
    own_sem, line_send, line_recv, col_send, col_recv, tp_send, tp_recv = scratch[:7]
    staged = scratch[7:]
    fo, z, y, x, c = (lax.axis_index(n) for n in ("fo", "fi", "ctx", "tpx", "tpc"))
    q = x * tpc_n + c

    items = [(i, f) for f in range(fo_n) for i in range(count)]

    def source(n):
        i, f = items[n]
        if kinds[i] == "share":
            a = shards[i].shape[1] // tp_n
            return shards[i].at[f, pl.ds(pl.multiple_of(q * a, a), a), :]
        return shards[i].at[f]

    def place(n, zb, yb):
        i, f = items[n]
        a, b = shards[i].shape[1:]
        block = (f * fi_n + zb) * ctx_n + yb
        if kinds[i] == "col":
            return outs[i].at[:, pl.ds(pl.multiple_of(block * b, b), b)]
        if kinds[i] == "share":
            part = a // tp_n
            return outs[i].at[pl.ds(pl.multiple_of(block * a + q * part, part), part), :]
        return outs[i].at[pl.ds(pl.multiple_of(block * a, a), a), :]

    def line(n, side, step, first):
        block = z - step if side == 0 else z + step
        to = z + 1 if side == 0 else z - 1
        return pltpu.make_async_remote_copy(
            src_ref=source(n) if first else place(n, block, y),
            dst_ref=place(n, block, y),
            send_sem=line_send.at[n, side, step],
            recv_sem=line_recv.at[n, side, step],
            device_id=(fo, to, y, x, c),
            device_id_type=MESH_ID,
        )

    def sends(side, step):
        block = z - step if side == 0 else z + step
        to = z + 1 if side == 0 else z - 1
        return (block >= 0) & (block < fi_n) & (to >= 0) & (to < fi_n)

    def across(n, zb, dy, first=False):
        return pltpu.make_async_remote_copy(
            src_ref=source(n) if first else place(n, zb, y),
            dst_ref=place(n, zb, y),
            send_sem=col_send.at[n, zb, dy],
            recv_sem=col_recv.at[n, zb, dy],
            device_id=(fo, z, lax.rem(y + dy, ctx_n), x, c),
            device_id_type=MESH_ID,
        )

    def stage(n):
        return pltpu.make_async_copy(source(n), staged[n], own_sem.at[n, 0])

    def keep(n):
        return pltpu.make_async_copy(staged[n], place(n, z, y), own_sem.at[n, 1])

    for n in range(len(items)):
        for side in (0, 1):

            @pl.when(sends(side, 0))
            def _():
                line(n, side, 0, True).start()

        for dy in range(1, ctx_n):
            across(n, z, dy, True).start()
        stage(n).start()

    yield
    for n in range(len(items)):
        stage(n).wait()
        keep(n).start()

    for step in range(fi_n - 1):
        for n in range(len(items)):
            for side in (0, 1):
                block = z - 1 - step if side == 0 else z + 1 + step

                @pl.when((block >= 0) & (block < fi_n))
                def _():
                    pltpu.make_async_remote_copy(
                        src_ref=place(n, block, y),
                        dst_ref=place(n, block, y),
                        send_sem=line_send.at[n, side, step],
                        recv_sem=line_recv.at[n, side, step],
                        device_id=(fo, z, y, x, c),
                        device_id_type=MESH_ID,
                    ).wait_recv()
                    for dy in range(1, ctx_n):
                        across(n, block, dy).start()

                if step < fi_n - 2:

                    @pl.when(sends(side, step + 1))
                    def _():
                        line(n, side, step + 1, False).start()

        yield

    for n in range(len(items)):
        keep(n).wait()
        for dy in range(1, ctx_n):
            for zb in range(fi_n):
                pltpu.make_async_remote_copy(
                    src_ref=place(n, zb, y),
                    dst_ref=place(n, zb, lax.rem(y + ctx_n - dy, ctx_n)),
                    send_sem=col_send.at[n, zb, dy],
                    recv_sem=col_recv.at[n, zb, dy],
                    device_id=(fo, z, y, x, c),
                    device_id_type=MESH_ID,
                ).wait_recv()
        i, f = items[n]
        if kinds[i] == "share":
            a = shards[i].shape[1]
            part = a // tp_n

            def spread(block, step, n=n, i=i, f=f, a=a, part=part):
                other = lax.rem(q + step, tp_n)
                at = (f * fi_n * ctx_n + block) * a + q * part
                return pltpu.make_async_remote_copy(
                    src_ref=outs[i].at[pl.ds(pl.multiple_of(at, part), part), :],
                    dst_ref=outs[i].at[pl.ds(pl.multiple_of(at, part), part), :],
                    send_sem=tp_send.at[n, block, step],
                    recv_sem=tp_recv.at[n, block, step],
                    device_id=(fo, z, y, other // tpc_n, lax.rem(other, tpc_n)),
                    device_id_type=MESH_ID,
                )

            def spread_all(block, carry):
                for step in range(1, tp_n):
                    spread(block, step).start()
                return carry

            lax.fori_loop(0, fi_n * ctx_n, spread_all, 0)

    yield

    for n in range(len(items)):
        i, f = items[n]
        if kinds[i] == "share":
            a = shards[i].shape[1]
            part = a // tp_n

            def landed(block, carry, n=n, i=i, f=f, a=a, part=part):
                for step in range(1, tp_n):
                    origin = lax.rem(q + tp_n - step, tp_n)
                    at = (f * fi_n * ctx_n + block) * a
                    mine = pl.ds(pl.multiple_of(at + q * part, part), part)
                    theirs = pl.ds(pl.multiple_of(at + origin * part, part), part)
                    copy = pltpu.make_async_remote_copy(
                        src_ref=outs[i].at[mine, :],
                        dst_ref=outs[i].at[theirs, :],
                        send_sem=tp_send.at[n, block, step],
                        recv_sem=tp_recv.at[n, block, step],
                        device_id=(fo, z, y, x, c),
                        device_id_type=MESH_ID,
                    )
                    copy.wait_send()
                    copy.wait_recv()
                return carry

            lax.fori_loop(0, fi_n * ctx_n, landed, 0)
        for side in (0, 1):
            for step in range(fi_n - 1):

                @pl.when(sends(side, step))
                def _():
                    line(n, side, step, step == 0).wait_send()

        for dy in range(1, ctx_n):
            for zb in range(fi_n):
                across(n, zb, dy).wait_send()


def collect_job(sizes, kinds, shards):
    fo_n, fi_n, ctx_n, tpx_n, tpc_n = (sizes[n] for n in ("fo", "fi", "ctx", "tpx", "tpc"))
    tp_n = tpx_n * tpc_n
    blocks = fo_n * fi_n * ctx_n
    outs, staged = [], []
    for kind, shard in zip(kinds, shards):
        _, a, b = shard.shape
        shape = (a, blocks * b) if kind == "col" else (blocks * a, b)
        outs.append((jax.ShapeDtypeStruct(shape, shard.dtype), HBM_SPEC))
        staged.append(pltpu.VMEM((a // tp_n if kind == "share" else a, b), shard.dtype))
    n = len(kinds) * fo_n
    return {
        "args": [(shard, HBM_SPEC) for shard in shards],
        "outs": outs,
        "scratch": [
            pltpu.SemaphoreType.DMA((n, 2)),
            pltpu.SemaphoreType.DMA((n, 2, fi_n)),
            pltpu.SemaphoreType.DMA((n, 2, fi_n)),
            pltpu.SemaphoreType.DMA((n, fi_n, ctx_n)),
            pltpu.SemaphoreType.DMA((n, fi_n, ctx_n)),
            pltpu.SemaphoreType.DMA((n, fi_n * ctx_n, tp_n)),
            pltpu.SemaphoreType.DMA((n, fi_n * ctx_n, tp_n)),
        ]
        + staged * fo_n,
        "run": functools.partial(collect_run, tuple(kinds)),
    }


def place_job(sizes, local):
    fo_n, fi_n, ctx_n, tpx_n, tpc_n = (sizes[n] for n in ("fo", "fi", "ctx", "tpx", "tpc"))
    chip_n = fi_n * ctx_n * tpx_n
    rows, depth = local.shape[3:]
    shape = (rows * tpx_n * tpc_n, depth * fo_n * fi_n * ctx_n)
    return {
        "args": [(local, HBM_SPEC)],
        "outs": [(jax.ShapeDtypeStruct(shape, BF16), HBM_SPEC)] * 3,
        "scratch": [pltpu.VMEM(local.shape, BF16)]
        + [pltpu.SemaphoreType.DMA((fo_n, 3, chip_n))] * 2
        + [pltpu.SemaphoreType.DMA((fo_n, 3, chip_n, tpc_n))] * 2,
        "run": place_run,
    }


def place_run(sizes, args, outs, scratch):
    fo_n, fi_n, ctx_n, tpx_n, tpc_n = (sizes[n] for n in ("fo", "fi", "ctx", "tpx", "tpc"))
    (local,) = args
    staged, load_sem, keep_sem, pair_send, pair_recv = scratch
    chip_n = fi_n * ctx_n * tpx_n
    rows, depth = local.shape[3:]
    fo, z, y, x, c = (lax.axis_index(n) for n in ("fo", "fi", "ctx", "tpx", "tpc"))

    def spot(k, f, chip, core):
        block = f * fi_n * ctx_n + chip // tpx_n
        return outs[k].at[
            pl.ds(pl.multiple_of((lax.rem(chip, tpx_n) * tpc_n + core) * rows, rows), rows),
            pl.ds(pl.multiple_of(block * depth, depth), depth),
        ]

    def load(f, k, chip):
        return pltpu.make_async_copy(
            local.at[f, chip, k], staged.at[f, chip, k], load_sem.at[f, k, chip]
        )

    def keep(f, k, chip):
        return pltpu.make_async_copy(
            staged.at[f, chip, k], spot(k, f, chip, c), keep_sem.at[f, k, chip]
        )

    def pair_copy(f, k, chip, dc, core):
        return pltpu.make_async_remote_copy(
            src_ref=local.at[f, chip, k],
            dst_ref=spot(k, f, chip, core),
            send_sem=pair_send.at[f, k, chip, dc],
            recv_sem=pair_recv.at[f, k, chip, dc],
            device_id=(fo, z, y, x, lax.rem(c + dc, tpc_n)),
            device_id_type=MESH_ID,
        )

    def launch(step, carry):
        f, chip = step // chip_n, lax.rem(step, chip_n)
        for k in range(3):
            load(f, k, chip).start()
            for dc in range(1, tpc_n):
                pair_copy(f, k, chip, dc, c).start()
        return carry

    def store(step, carry):
        f, chip = step // chip_n, lax.rem(step, chip_n)
        for k in range(3):
            load(f, k, chip).wait()
            keep(f, k, chip).start()
        return carry

    def settle(step, carry):
        f, chip = step // chip_n, lax.rem(step, chip_n)
        for k in range(3):
            keep(f, k, chip).wait()
            for dc in range(1, tpc_n):
                pair_copy(f, k, chip, dc, c).wait_send()
                pair_copy(f, k, chip, dc, lax.rem(c + tpc_n - dc, tpc_n)).wait_recv()
        return carry

    lax.fori_loop(0, fo_n * chip_n, launch, 0)
    yield
    lax.fori_loop(0, fo_n * chip_n, store, 0)
    yield
    lax.fori_loop(0, fo_n * chip_n, settle, 0)


def pair_body(sizes, fo_n, *refs):
    fi_n, ctx_n, tpx_n, tpc_n = (sizes[n] for n in ("fi", "ctx", "tpx", "tpc"))
    grads, (out_ref, mine, theirs, load_sem, store_sem, send_sem, recv_sem) = refs[:3], refs[3:]
    chip_n = fi_n * ctx_n * tpx_n
    rows, depth = mine.shape[2:]
    fo, z, y, x, c = (lax.axis_index(n) for n in ("fo", "fi", "ctx", "tpx", "tpc"))
    sibling = (fo, z, y, x, 1 - c)
    barrier = pltpu.get_barrier_semaphore()
    pl.semaphore_signal(barrier, inc=1, device_id=sibling, device_id_type=MESH_ID)
    pl.semaphore_wait(barrier, 1)

    def spot(k, at, core):
        block, side = at // tpx_n, lax.rem(at, tpx_n)
        return grads[k].at[
            pl.ds(pl.multiple_of((side * tpc_n + core) * rows, rows), rows),
            pl.ds(pl.multiple_of(block * depth, depth), depth),
        ]

    def load(k, at):
        return pltpu.make_async_copy(spot(k, at, c), mine.at[at, k], load_sem.at[at, k])

    def store(k, at):
        return pltpu.make_async_copy(mine.at[at, k], out_ref.at[at, k], store_sem.at[at, k])

    def give(k, at):
        return pltpu.make_async_remote_copy(
            src_ref=spot(k, at, 1 - c),
            dst_ref=theirs.at[at, k],
            send_sem=send_sem.at[at, k],
            recv_sem=recv_sem.at[at, k],
            device_id=sibling,
            device_id_type=MESH_ID,
        )

    def launch(at, carry):
        for k in range(3):
            give(k, at).start()
            load(k, at).start()
        return carry

    def add(at, carry):
        for k in range(3):
            load(k, at).wait()
            give(k, at).wait_recv()
            mine[at, k] = (mine[at, k].astype(F32) + theirs[at, k].astype(F32)).astype(BF16)
            store(k, at).start()
        return carry

    def settle(at, carry):
        for k in range(3):
            give(k, at).wait_send()
            store(k, at).wait()
        return carry

    total = fo_n * chip_n
    lax.fori_loop(0, total, launch, 0)
    lax.fori_loop(0, total, add, 0)
    lax.fori_loop(0, total, settle, 0)


def pair_sum(sizes, grads, collective_id):
    fo_n, fi_n, ctx_n, tpx_n, tpc_n = (sizes[n] for n in ("fo", "fi", "ctx", "tpx", "tpc"))
    rows = grads[0].shape[0] // (tpx_n * tpc_n)
    depth = grads[0].shape[1] // (fo_n * fi_n * ctx_n)
    total = fo_n * fi_n * ctx_n * tpx_n
    shape = (total, 3, rows, depth)
    hbm = pl.BlockSpec(memory_space=pl.ANY)
    return pl.pallas_call(
        functools.partial(pair_body, sizes, fo_n),
        out_shape=jax.ShapeDtypeStruct(shape, BF16),
        in_specs=[hbm] * 3,
        out_specs=hbm,
        scratch_shapes=[pltpu.VMEM(shape, BF16)] * 2 + [pltpu.SemaphoreType.DMA((total, 3))] * 4,
        compiler_params=pltpu.CompilerParams(
            collective_id=collective_id, has_side_effects=True, vmem_limit_bytes=32 << 20
        ),
        cost_estimate=pl.CostEstimate(flops=0, bytes_accessed=60_000_000, transcendentals=0),
        name="pair_sum",
    )(*grads)


def finish_run(kinds, sizes, args, outs, scratch):
    fi_n, ctx_n, tpx_n, tpc_n = (sizes[n] for n in ("fi", "ctx", "tpx", "tpc"))
    tp_n = tpx_n * tpc_n
    count = len(kinds)
    extra = len(args) - count
    parts, quarters = args[:count], args[count:]
    outs, wholes = outs[:count], outs[count:]
    mine, other, coming = (scratch[k * count : (k + 1) * count] for k in range(3))
    staged, (tiny, *sems) = scratch[3 * count : 3 * count + extra], scratch[3 * count + extra :]
    load_sem, col_send, col_recv, line_send, line_recv, tp_send, tp_recv = sems[:7]
    fo, z, y, x, c = (lax.axis_index(n) for n in ("fo", "fi", "ctx", "tpx", "tpc"))
    q = x * tpc_n + c

    spreads = [
        tp_spread(sizes, quarters[j], staged[j], wholes[j], sems[8 + 5 * j : 13 + 5 * j])
        for j in range(extra)
    ]

    def stage(j):
        return pltpu.make_async_copy(quarters[j], staged[j], sems[7].at[j])

    for j in range(extra):
        spreads[j][0]()
        stage(j).start()

    def view(n, zb, yb):
        a, b = mine[n].shape[1:]
        block = zb * ctx_n + yb
        if kinds[n] == "col":
            return parts[n].at[:, pl.ds(pl.multiple_of(block * b, b), b)]
        if kinds[n] == "share":
            return parts[n].at[pl.ds(pl.multiple_of(block * a * tp_n + q * a, a), a), :]
        return parts[n].at[pl.ds(pl.multiple_of(block * a, a), a), :]

    def across(n, zb, dy):
        to = lax.rem(y + dy, ctx_n)
        return pltpu.make_async_remote_copy(
            src_ref=view(n, zb, to),
            dst_ref=other[n].at[dy - 1, zb],
            send_sem=col_send.at[n, zb, dy],
            recv_sem=col_recv.at[n, zb, dy],
            device_id=(fo, z, to, x, c),
            device_id_type=MESH_ID,
        )

    def load(n, zb):
        return pltpu.make_async_copy(view(n, zb, y), mine[n].at[zb], load_sem.at[n, zb])

    for turn in range(fi_n):
        zb = jnp.where(z < fi_n // 2, fi_n - 1 - turn, turn)
        for n in range(count):
            for dy in range(1, ctx_n):
                across(n, zb, dy).start()
            load(n, zb).start()

    yield
    for j in range(extra):
        stage(j).wait()
        spreads[j][1].start()

    def line(n, side, target):
        at = jnp.where(target == (z + 1 if side == 0 else z - 1), fi_n, target) if side == 1 else target
        return pltpu.make_async_remote_copy(
            src_ref=mine[n].at[target],
            dst_ref=coming[n].at[at],
            send_sem=line_send.at[n, side, target],
            recv_sem=line_recv.at[n, side, target],
            device_id=(fo, z + 1 if side == 0 else z - 1, y, x, c),
            device_id_type=MESH_ID,
        )

    def came(n, side, target, at):
        pltpu.make_async_remote_copy(
            src_ref=mine[n].at[target],
            dst_ref=coming[n].at[at],
            send_sem=line_send.at[n, side, target],
            recv_sem=line_recv.at[n, side, target],
            device_id=(fo, z, y, x, c),
            device_id_type=MESH_ID,
        ).wait_recv()

    def ready(n, target):
        load(n, target).wait()
        for dy in range(1, ctx_n):
            across(n, target, dy).wait_recv()

    def add(n, target, use, store):
        a = mine[n].shape[1]
        tile = math.gcd(a, 64)

        def rows(step, carry):
            at = pl.ds(pl.multiple_of(step * tile, tile), tile)
            summed = mine[n][target, at, :].astype(F32)
            for dy in range(1, ctx_n):
                summed = summed + other[n][dy - 1, target, at, :].astype(F32)
            for slot in use:
                summed = summed + coming[n][slot, at, :].astype(F32)
            store(at, summed.astype(BF16))
            return carry

        lax.fori_loop(0, a // tile, rows, 0)

    for step in range(fi_n - 1):
        for n in range(count):
            for side in (0, 1):
                depth = z if side == 0 else fi_n - 1 - z
                target = fi_n - 1 - step + z if side == 0 else step - (fi_n - 1) + z
                passes, inner = depth <= step, depth > 0

                def back(at, values, n=n, target=target):
                    mine[n][target, at, :] = values

                @pl.when(passes & inner)
                def _():
                    ready(n, target)
                    came(n, side, target, target)
                    add(n, target, (target,), back)
                    line(n, side, target).start()

                @pl.when(passes & jnp.logical_not(inner))
                def _():
                    ready(n, target)
                    add(n, target, (), back)
                    line(n, side, target).start()

        yield

    for n in range(count):
        ready(n, z)

        def out(at, values, n=n):
            if kinds[n] == "share":
                a = mine[n].shape[1]
                outs[n][q, at, :] = values
            elif kinds[n] == "sum":
                tiny[q, at, :] = values
            else:
                outs[n][at, :] = values

        @pl.when(z > 0)
        def _():
            came(n, 0, z, z)

        @pl.when(z < fi_n - 1)
        def _():
            came(n, 1, z, fi_n)

        @pl.when((z > 0) & (z < fi_n - 1))
        def _():
            add(n, z, (z, fi_n), out)

        @pl.when((z == 0) & (z < fi_n - 1))
        def _():
            add(n, z, (fi_n,), out)

        @pl.when((z > 0) & (z == fi_n - 1))
        def _():
            add(n, z, (z,), out)

        @pl.when((z == 0) & (z == fi_n - 1))
        def _():
            add(n, z, (), out)

        if kinds[n] in ("share", "sum"):
            held = outs[n] if kinds[n] == "share" else tiny
            for step in range(1, tp_n):
                peer = lax.rem(q + step, tp_n)
                pltpu.make_async_remote_copy(
                    src_ref=held.at[q],
                    dst_ref=held.at[q],
                    send_sem=tp_send.at[n, step],
                    recv_sem=tp_recv.at[n, step],
                    device_id=(fo, z, y, peer // tpc_n, lax.rem(peer, tpc_n)),
                    device_id_type=MESH_ID,
                ).start()

    yield
    for j in range(extra):
        spreads[j][2]()

    for n in range(count):
        if kinds[n] in ("share", "sum"):
            held = outs[n] if kinds[n] == "share" else tiny
            for step in range(1, tp_n):
                origin = lax.rem(q + tp_n - step, tp_n)
                copy = pltpu.make_async_remote_copy(
                    src_ref=held.at[q],
                    dst_ref=held.at[origin],
                    send_sem=tp_send.at[n, step],
                    recv_sem=tp_recv.at[n, step],
                    device_id=(fo, z, y, x, c),
                    device_id_type=MESH_ID,
                )
                copy.wait_send()
                copy.wait_recv()
            if kinds[n] == "sum":
                summed = tiny[0].astype(F32)
                for k in range(1, tp_n):
                    summed = summed + tiny[k].astype(F32)
                outs[n][...] = summed.astype(BF16)
        for target in range(fi_n):
            for dy in range(1, ctx_n):
                across(n, target, dy).wait_send()
            for side in (0, 1):

                @pl.when((z < target) if side == 0 else (z > target))
                def _():
                    line(n, side, target).wait_send()

    for j in range(extra):
        spreads[j][3]()


def finish_job(sizes, kinds, parts, quarters):
    fi_n, ctx_n, tpx_n, tpc_n = (sizes[n] for n in ("fi", "ctx", "tpx", "tpc"))
    tp_n = tpx_n * tpc_n
    blocks = fi_n * ctx_n
    count, extra = len(kinds), len(quarters)
    own, shapes = [], []
    sum_shape = (16, 256)
    for kind, part in zip(kinds, parts):
        a, b = part.shape
        if kind == "col":
            own.append((a, b // blocks))
            shapes.append(own[-1])
        elif kind == "share":
            own.append((a // (blocks * tp_n), b))
            shapes.append((tp_n,) + own[-1])
        else:
            own.append((a // blocks, b))
            shapes.append(own[-1])
        if kind == "sum":
            sum_shape = own[-1]
    wide = [(v.shape[0], v.shape[1] * tp_n) for v in quarters]
    some = max(extra, 1)
    shapes = [jax.ShapeDtypeStruct(shape, BF16) for shape in shapes + wide]
    return {
        "args": [(arg, HBM_SPEC) for arg in (*parts, *quarters)],
        "outs": list(zip(shapes, [VMEM_SPEC] * count + [HBM_SPEC] * extra)),
        "scratch": [pltpu.VMEM((fi_n,) + s, BF16) for s in own]
        + [pltpu.VMEM((max(ctx_n - 1, 1), fi_n) + s, BF16) for s in own]
        + [pltpu.VMEM((fi_n + 1,) + s, BF16) for s in own]
        + [pltpu.VMEM(v.shape, BF16) for v in quarters]
        + [
            pltpu.VMEM((tp_n,) + sum_shape, BF16),
            pltpu.SemaphoreType.DMA((count, fi_n)),
            pltpu.SemaphoreType.DMA((count, fi_n, ctx_n)),
            pltpu.SemaphoreType.DMA((count, fi_n, ctx_n)),
            pltpu.SemaphoreType.DMA((count, 2, fi_n)),
            pltpu.SemaphoreType.DMA((count, 2, fi_n)),
            pltpu.SemaphoreType.DMA((count, tp_n)),
            pltpu.SemaphoreType.DMA((count, tp_n)),
            pltpu.SemaphoreType.DMA((some,)),
            *(tp_spread_sems(sizes) * extra),
        ],
        "run": functools.partial(finish_run, tuple(kinds)),
    }


def attend_body(place_ref, q_ref, kv_ref, rope_ref, out_ref, log_ref):
    block_rows, key_count = q_ref.shape[0], kv_ref.shape[0]
    first = place_ref[0] + pl.program_id(1) * block_rows
    keys = jnp.concatenate([kv_ref[:, :NOPE], rope_ref[...]], axis=1)
    scores = dot_nt(q_ref[...], keys)
    row = first + lax.broadcasted_iota(jnp.int32, (block_rows, 1), 0)
    limit = jnp.maximum(row, place_ref[1] - 1)
    key = lax.broadcasted_iota(jnp.int32, (block_rows, key_count), 1)
    scores = jnp.where(key <= limit, scores, -1e30)
    top = jnp.max(scores, axis=1, keepdims=True)
    exponent = jnp.exp(scores - top)
    row_total = jnp.sum(exponent, axis=1, keepdims=True)
    summed = jnp.dot(exponent.astype(BF16), kv_ref[:, NOPE:], preferred_element_type=F32)
    out_ref[...] = (summed / row_total).astype(BF16)
    log_total = jnp.broadcast_to(top + jnp.log(row_total), (block_rows, 128))
    log_ref[0] = log_total.T[:1]

def attend(place, query, key_value, rope, block_rows):
    rows, key_count = query.shape[0], key_value.shape[0]
    heads = query.shape[1] // HEAD
    return pl.pallas_call(
        attend_body,
        out_shape=(jax.ShapeDtypeStruct((rows, heads * VDIM), BF16), jax.ShapeDtypeStruct((heads, 1, rows), F32)),
        grid_spec=pltpu.PrefetchScalarGridSpec(
            num_scalar_prefetch=1,
            grid=(heads, rows // block_rows),
            in_specs=[
                pl.BlockSpec((block_rows, HEAD), lambda h, i, s: (i, h)),
                pl.BlockSpec((key_count, HEAD), lambda h, i, s: (0, h)),
                pl.BlockSpec((key_count, NOPE), lambda h, i, s: (0, 0)),
            ],
            out_specs=[
                pl.BlockSpec((block_rows, VDIM), lambda h, i, s: (i, h)),
                pl.BlockSpec((1, 1, block_rows), lambda h, i, s: (h, 0, i)),
            ],
        ),
        compiler_params=pltpu.CompilerParams(vmem_limit_bytes=48 << 20),
        cost_estimate=pl.CostEstimate(flops=4 * rows * key_count * heads * HEAD, bytes_accessed=20_000_000, transcendentals=rows * key_count * heads),
        name="attend",
    )(place, query, key_value, rope)

def attend_back_body(place_ref, q_ref, kv_ref, rope_ref, dout_ref, log_ref, table_ref, dq_ref, dkv_ref, drope_ref, keys_acc, values_acc):
    block_rows, key_count = q_ref.shape[0], kv_ref.shape[0]
    head, step = pl.program_id(0), pl.program_id(1)
    first = place_ref[0] + step * block_rows
    keys = jnp.concatenate([kv_ref[:, :NOPE], rope_ref[...]], axis=1)
    scores = dot_nt(keys, q_ref[...])
    row = first + lax.broadcasted_iota(jnp.int32, (1, block_rows), 1)
    limit = jnp.maximum(row, place_ref[1] - 1)
    key = lax.broadcasted_iota(jnp.int32, (key_count, block_rows), 0)
    soft = jnp.exp(jnp.where(key <= limit, scores, -1e30) - log_ref[0])
    soft_grad = dot_nt(kv_ref[:, NOPE:], dout_ref[...])
    mean = jnp.sum(soft * soft_grad, axis=0, keepdims=True)
    score_grad = (soft * (soft_grad - mean)).astype(BF16)
    values = jnp.dot(soft.astype(BF16), dout_ref[...], preferred_element_type=F32)
    keys_grad = jnp.dot(score_grad, q_ref[...], preferred_element_type=F32)
    dq_ref[...] = (dot_tn(score_grad, keys) * table_ref[...]).astype(BF16)

    @pl.when(step == 0)
    def _():
        keys_acc[...] = keys_grad
        values_acc[...] = values

    @pl.when(step > 0)
    def _():
        keys_acc[...] += keys_grad
        values_acc[...] += values

    @pl.when(step == pl.num_programs(1) - 1)
    def _():
        dkv_ref[...] = jnp.concatenate([keys_acc[:, :NOPE], values_acc[...]], axis=1).astype(BF16)

        @pl.when(head == 0)
        def _():
            drope_ref[...] = keys_acc[:, NOPE:]

        @pl.when(head > 0)
        def _():
            drope_ref[...] += keys_acc[:, NOPE:]

def attend_back(place, query, key_value, rope, dout, log_total, table, block_rows):
    rows, key_count = query.shape[0], key_value.shape[0]
    heads = query.shape[1] // HEAD
    return pl.pallas_call(
        attend_back_body,
        out_shape=(jax.ShapeDtypeStruct((rows, heads * HEAD), BF16), jax.ShapeDtypeStruct((key_count, heads * HEAD), BF16), jax.ShapeDtypeStruct((key_count, NOPE), F32)),
        grid_spec=pltpu.PrefetchScalarGridSpec(
            num_scalar_prefetch=1,
            grid=(heads, rows // block_rows),
            in_specs=[
                pl.BlockSpec((block_rows, HEAD), lambda h, i, s: (i, h)),
                pl.BlockSpec((key_count, HEAD), lambda h, i, s: (0, h)),
                pl.BlockSpec((key_count, NOPE), lambda h, i, s: (0, 0)),
                pl.BlockSpec((block_rows, VDIM), lambda h, i, s: (i, h)),
                pl.BlockSpec((1, 1, block_rows), lambda h, i, s: (h, 0, i)),
                pl.BlockSpec((block_rows, HEAD), lambda h, i, s: (i, 0)),
            ],
            out_specs=[
                pl.BlockSpec((block_rows, HEAD), lambda h, i, s: (i, h)),
                pl.BlockSpec((key_count, HEAD), lambda h, i, s: (0, h)),
                pl.BlockSpec((key_count, NOPE), lambda h, i, s: (0, 0)),
            ],
            scratch_shapes=[pltpu.VMEM((key_count, HEAD), F32), pltpu.VMEM((key_count, VDIM), F32)],
        ),
        compiler_params=pltpu.CompilerParams(vmem_limit_bytes=56 << 20),
        cost_estimate=pl.CostEstimate(
            flops=10 * rows * key_count * heads * HEAD,
            bytes_accessed=40_000_000,
            transcendentals=rows * key_count * heads,
        ),
        name="attend_back",
    )(place, query, key_value, rope, dout, log_total, table)


def build(sizes):
    fo_n, fi_n, ctx_n, tpx_n, tpc_n = (sizes[name] for name in ("fo", "fi", "ctx", "tpx", "tpc"))
    tp_n = tpx_n * tpc_n
    row_shards = fo_n * fi_n * ctx_n
    plane_experts = ctx_n * tpx_n
    z_part = fi_n // tpc_n

    def expert_weights(gate, up, down):
        local = jnp.stack([gate.transpose(0, 2, 1), up.transpose(0, 2, 1), down], axis=1)
        return lax.all_gather(local, "fo", axis=0) if fo_n > 1 else local[None]

    def shard_of(weight):
        return lax.all_gather(weight, "fo", axis=0) if fo_n > 1 else weight[None]

    def fo_sum(part, kind):
        if fo_n == 1:
            return part
        if kind == "col":
            a = part.shape[0]
            part = part.reshape(a, fo_n, -1)
            return lax.psum_scatter(part, "fo", scatter_dimension=1, tiled=True).reshape(a, -1)
        return lax.psum_scatter(part, "fo", scatter_dimension=0, tiled=True)

    def own_expert_grads(mine):
        mine = mine.reshape((fo_n, -1) + mine.shape[1:])
        got = lax.all_to_all(mine, CHIPS, split_axis=1, concat_axis=1, tiled=True)
        if fo_n > 1:
            got = lax.psum_scatter(got, "fo", scatter_dimension=0, tiled=True)
        got = got[0].astype(F32)
        return (got[:, 0].transpose(0, 2, 1), got[:, 1].transpose(0, 2, 1), got[:, 2])

    def shards(
        tokens,
        out_grad,
        routes,
        slot_index,
        prefix,
        attn_gain,
        query_weight,
        latent_down,
        latent_gain,
        latent_up,
        out_weight,
        moe_gain,
        router_weight,
        shared_gate,
        shared_up,
        shared_down,
        expert_gate,
        expert_up,
        expert_down,
    ):
        row_count, width = tokens.shape
        expert_count = expert_gate.shape[0]
        capacity = row_count * routes.shape[1] // expert_count
        quarter = width // tp_n
        tp_index = lax.axis_index(TP)
        own_expert = lax.axis_index(CHIPS)
        plane_base = lax.axis_index("fi") * plane_experts

        def columns(values):
            return lax.dynamic_slice_in_dim(values, tp_index * quarter, quarter, values.ndim - 1)

        depth = latent_down.shape[0]
        down_width = latent_down.shape[1]

        def turned(weight):
            half = weight.shape[-1] // 2
            return jnp.concatenate([-weight[..., half:], weight[..., :half]], axis=-1)

        small = jnp.concatenate(
            [
                latent_down,
                turned(latent_down[:, KVR:]),
                attn_gain[:, None],
                moe_gain[:, None],
                jnp.pad(latent_gain, (0, depth - latent_gain.shape[0]))[:, None],
                router_weight,
            ],
            axis=1,
        )
        used = small.shape[1]
        small = jnp.pad(small, ((0, 0), (0, -used % 128)))
        keys = jnp.where(slot_index < capacity, routes * capacity + slot_index, -1).T
        keys = jnp.pad(keys, ((0, 8 - keys.shape[0]), (0, 0)), constant_values=-1)
        (small, query_full, up_full, out_full, keys_all), *_ = exchange(
            sizes,
            [
                collect_job(
                    sizes,
                    ("share", "row", "row", "col", "row"),
                    [shard_of(w) for w in (small, query_weight, latent_up, out_weight, keys)],
                )
            ],
            4,
            "collect_attention",
        )
        local_weights, small = lax.optimization_barrier(
            (expert_weights(expert_gate, expert_up, expert_down), small)
        )
        routed_weights = lax.all_to_all(
            local_weights, CHIPS, split_axis=1, concat_axis=1, tiled=True
        )
        wide_down = small[:, : down_width + ROPE]
        down_full = small[:, :down_width]
        gain_at = down_width + ROPE
        gain_one = small[:, gain_at].astype(F32)
        gain_two = small[:, gain_at + 1].astype(F32)
        gain_latent = (
            small[:, gain_at + 2]
            .reshape(row_shards, depth)[:, : latent_gain.shape[0]]
            .reshape(-1)
            .astype(F32)
        )
        router_full = small[:, gain_at + 3 : used]

        keys_all = lax.dynamic_slice_in_dim(
            keys_all, lax.axis_index("fo") * (fi_n * ctx_n * 8), fi_n * ctx_n * 8, 0
        ).reshape(fi_n, ctx_n, 8, row_count)
        keys_column = lax.dynamic_index_in_dim(keys_all, lax.axis_index("ctx"), 1, keepdims=False)
        first_keys = (plane_base + jnp.arange(plane_experts, dtype=jnp.int32)) * capacity
        rel = keys_column[:, None] - first_keys[:, None, None]
        plane_slots = jnp.max(jnp.where((rel >= 0) & (rel < capacity), rel, -1), axis=2)
        token_slots = plane_slots.transpose(0, 2, 1)

        def give_back(rows, gates, bases=None):
            rows = rows.reshape(z_part, ctx_n, capacity, width)
            return give_back_job(sizes, rows, token_slots, gates, bases)

        (slot_grads,), (shared_gate_full, shared_up_full, shared_down_full) = exchange(
            sizes,
            [
                dispatch_job(sizes, columns(out_grad), plane_slots, capacity),
                collect_job(
                    sizes,
                    ("row", "row", "col"),
                    [shard_of(w) for w in (shared_gate, shared_up, shared_down)],
                ),
            ],
            0,
            "dispatch_grads",
        )
        slot_grads = slot_grads.reshape(-1, width)
        ((gate_full, expert_up_full, down_weight),) = exchange(
            sizes, [place_job(sizes, routed_weights)], 5, "place_experts"
        )

        head_count = query_full.shape[1] // (NOPE + ROPE)
        hidden = tokens.astype(F32)
        scale_one = rms_scale(hidden)
        normed_one = hidden * scale_one
        normed_in = (normed_one * gain_one).astype(BF16)
        seq_index = lax.axis_index(("fo", "fi"))
        prefix_len = lax.dynamic_index_in_dim(prefix, seq_index, keepdims=False)
        row_offset = lax.axis_index("ctx") * row_count
        query_pos = row_offset + jnp.arange(row_count, dtype=jnp.int32)
        cos_table, sin_table = rotation_tables(query_pos, ROPE // 2)
        score_scale = (NOPE + ROPE) ** (-0.5)
        cos_wide = jnp.concatenate([cos_table, cos_table], axis=1)
        sin_wide = jnp.concatenate([sin_table, sin_table], axis=1)
        table = score_scale * jnp.concatenate(
            [jnp.ones((row_count, NOPE), F32), cos_wide, sin_wide], axis=1
        )

        latent_raw = dot(normed_in, wide_down)
        latent_part = latent_raw[:, :KVR]
        scale_latent = rms_scale(latent_part)
        normed_latent = latent_part * scale_latent
        latent = (normed_latent * gain_latent).astype(BF16)
        key_rope = (
            latent_raw[:, KVR : KVR + ROPE] * cos_wide + latent_raw[:, KVR + ROPE :] * sin_wide
        ).astype(BF16)
        both = lax.all_gather(
            jnp.concatenate([latent, key_rope, key_rope], axis=1), "ctx", axis=0, tiled=True
        )
        latent_all, rope_all = both[:, :KVR], both[:, KVR:]
        query_heads = query_full.reshape(width, head_count, NOPE + ROPE)
        query_wide = jnp.concatenate(
            [query_heads, turned(query_heads[..., NOPE:])], axis=-1
        ).reshape(width, head_count * HEAD)
        query_in = (
            dot(normed_in, query_wide).reshape(row_count, head_count, HEAD) * table[:, None]
        ).astype(BF16).reshape(row_count, head_count * HEAD)
        key_value = dot(latent_all, up_full).astype(BF16)
        place = jnp.stack([row_offset, prefix_len]).astype(jnp.int32)
        block_rows = min(256, row_count)
        attended, log_totals = attend(place, query_in, key_value, rope_all, block_rows)

        def tp_scatter(parts):
            parts = jnp.stack([part.astype(BF16) for part in parts])
            return lax.psum_scatter(parts, TP, scatter_dimension=0, tiled=True)[0].astype(F32)

        def quarters(weight, axis):
            return jnp.split(weight, tp_n, axis=axis)

        def tp_gather(part_rows):
            got = lax.all_gather(part_rows, TP, axis=0)
            return got.transpose(1, 0, 2).reshape(row_count, width)

        attn_out = tp_scatter([dot(attended, part) for part in quarters(out_full, 1)])
        attn_out, slot_grads = lax.optimization_barrier((attn_out, slot_grads))
        residual = columns(tokens).astype(F32) + attn_out
        scale_two = lax.rsqrt(
            lax.psum(jnp.sum(residual * residual, axis=-1, keepdims=True), TP) / width + EPSILON
        )
        normed_two = residual * scale_two
        gain_two_part = columns(gain_two[None])
        mid_part = (normed_two * gain_two_part).astype(BF16)

        ((slot_rows,),) = exchange(
            sizes, [dispatch_job(sizes, mid_part, plane_slots, capacity)], 1, "dispatch_rows"
        )
        slot_rows = slot_rows.reshape(-1, width)
        normed_mid = tp_gather(mid_part)

        logits = dot(normed_mid, router_full)
        router_prob = jax.nn.softmax(logits, axis=-1)
        slot_prob = jax.nn.softmax(dot(slot_rows, router_full), axis=-1)
        slot_gate = lax.dynamic_slice_in_dim(slot_prob, own_expert, 1, 1)

        gate_pre = dot(normed_mid, shared_gate_full)
        up_pre = dot(normed_mid, shared_up_full)
        shared_dact = dot_nt(out_grad, shared_down_full)
        shared_silu, shared_slope = silu_parts(gate_pre)
        shared_act = (shared_silu * up_pre).astype(BF16)
        shared_dgate = (shared_dact * up_pre * shared_slope).astype(BF16)
        shared_dup = (shared_dact * shared_silu).astype(BF16)
        mid_shared = tp_scatter(
            [
                dot_nt(shared_dgate, gate_part) + dot_nt(shared_dup, up_part)
                for gate_part, up_part in zip(
                    quarters(shared_gate_full, 0), quarters(shared_up_full, 0)
                )
            ]
        )
        out_shared = tp_scatter([dot(shared_act, part) for part in quarters(shared_down_full, 1)])

        expert_dact_raw = dot_nt(slot_grads, down_weight)
        expert_gpre = dot_nt(slot_rows, gate_full)
        expert_upre = dot_nt(slot_rows, expert_up_full)
        expert_silu, expert_slope = silu_parts(expert_gpre)
        expert_act_wide = expert_silu * expert_upre
        expert_act = expert_act_wide.astype(BF16)
        slot_gate_grad = jnp.sum(expert_act.astype(F32) * expert_dact_raw, axis=-1)
        expert_dact = expert_dact_raw * slot_gate
        expert_dgate = (expert_dact * expert_upre * expert_slope).astype(BF16)
        expert_dup = (expert_dact * expert_silu).astype(BF16)
        slot_drows = dot(expert_dgate, gate_full) + dot(expert_dup, expert_up_full)
        gate_rows = jnp.broadcast_to(
            slot_gate_grad.reshape(z_part, ctx_n, 1, capacity), (z_part, ctx_n, 8, capacity)
        )
        sdown_grad = dot_tn(shared_act, out_grad)
        sgate_grad = dot_tn(normed_mid, shared_dgate)
        sup_grad = dot_tn(normed_mid, shared_dup)
        shared_kinds = ("row", "row", "col")
        shared_parts = [
            fo_sum(part.astype(BF16), kind)
            for part, kind in zip((sgate_grad, sup_grad, sdown_grad), shared_kinds)
        ]
        (mid_routed, prob_grad), shared_own = exchange(
            sizes,
            [
                give_back(slot_drows.astype(BF16), gate_rows),
                finish_job(sizes, shared_kinds, shared_parts, []),
            ],
            2,
            "give_back_rows",
        )
        sgate_grad, sup_grad, sdown_grad = (part.astype(F32) for part in shared_own)
        prob_grad = prob_grad.T
        logit_grad = (
            router_prob * (prob_grad - jnp.sum(router_prob * prob_grad, axis=-1, keepdims=True))
        ).astype(BF16)

        slot_dout = (slot_grads.astype(F32) * slot_gate).astype(BF16)
        routed_grads = pair_sum(
            sizes,
            [
                dot_tn(expert_dgate, slot_rows).astype(BF16),
                dot_tn(expert_dup, slot_rows).astype(BF16),
                dot_tn(expert_act, slot_dout).astype(BF16),
            ],
            7,
        )
        mid_total = mid_shared + mid_routed + dot_nt(logit_grad, columns(router_full.T).T)
        gain_two_grad = jnp.sum(mid_total * normed_two, axis=0)
        dn_two = mid_total * gain_two_part
        dot_two = lax.psum(jnp.sum(dn_two * normed_two, axis=-1, keepdims=True), TP) / width
        residual_grad = columns(out_grad).astype(F32) + scale_two * (dn_two - normed_two * dot_two)
        attn_dout = tp_gather(residual_grad.astype(BF16))

        out_weight_grad = dot_tn(attended, attn_dout)
        attended_grad = dot_nt(attn_dout, out_full).astype(BF16)
        attended_grad, routed_grads = lax.optimization_barrier((attended_grad, routed_grads))
        egate_grad, eup_grad, edown_grad = own_expert_grads(routed_grads)
        query_grad, kv_grad, rope_grad = attend_back(
            place, query_in, key_value, rope_all, attended_grad, log_totals, table,
            min(512, row_count),
        )
        late_act, query_grad = lax.optimization_barrier((expert_act, query_grad))
        expert_out = (dot(late_act, down_weight) * slot_gate).astype(BF16)
        up_grad = dot_tn(latent_all, kv_grad)
        latent_grad = dot_nt(kv_grad, up_full)
        query_wide_grad = dot_tn(normed_in, query_grad).reshape(width, head_count, HEAD)
        query_weight_grad = jnp.concatenate(
            [
                query_wide_grad[..., :NOPE],
                query_wide_grad[..., NOPE : NOPE + ROPE] - turned(query_wide_grad[..., NOPE + ROPE :]),
            ],
            axis=-1,
        ).reshape(width, head_count * (NOPE + ROPE))
        input_part = tp_scatter([dot_nt(query_grad, part) for part in quarters(query_wide, 0)])
        both_grad = lax.psum_scatter(
            jnp.concatenate([latent_grad, rope_grad], axis=1).astype(BF16),
            "ctx",
            scatter_dimension=0,
            tiled=True,
        )
        both_grad = lax.psum(both_grad, TP).astype(F32)
        latent_own = both_grad[:, :KVR]
        rope_own = both_grad[:, KVR : KVR + ROPE] + both_grad[:, KVR + ROPE :]
        gain_latent_grad = jnp.sum(latent_own * normed_latent, axis=0)
        latent_raw_grad = norm_back(latent_own * gain_latent, normed_latent, scale_latent)
        down_out_grad = jnp.concatenate(
            [latent_raw_grad, rotate(rope_own, cos_table, -sin_table)], axis=-1
        ).astype(BF16)
        down_grad = dot_tn(normed_in, down_out_grad)
        input_total = input_part + dot_nt(
            down_out_grad, lax.dynamic_slice_in_dim(down_full, tp_index * quarter, quarter, 0)
        )
        normed_one_part = columns(normed_one)
        gain_one_grad = jnp.sum(input_total * normed_one_part, axis=0)
        dn_one = input_total * columns(gain_one[None])
        dot_one = lax.psum(jnp.sum(dn_one * normed_one_part, axis=-1, keepdims=True), TP) / width
        token_grad = residual_grad + scale_one * (dn_one - normed_one_part * dot_one)
        token_grad, egate_grad, eup_grad, edown_grad = lax.optimization_barrier(
            (token_grad, egate_grad, eup_grad, edown_grad)
        )
        router_grad = dot_tn(normed_mid, logit_grad)
        pack_grad = jnp.concatenate([down_grad, router_grad], axis=1)
        pack_used = pack_grad.shape[1]
        pack_grad = jnp.pad(pack_grad, ((0, 0), (0, -pack_used % 128)))
        gains = jnp.stack([gain_one_grad, gain_two_grad])
        gains = lax.dynamic_update_slice_in_dim(
            jnp.zeros((2, width), F32), gains, tp_index * quarter, 1
        )
        latent_rows = jnp.pad(
            gain_latent_grad.reshape(row_shards, -1),
            ((0, 0), (0, depth - latent_gain.shape[0])),
        ).reshape(1, width)
        gains = jnp.concatenate([gains, latent_rows * (tp_index == 0).astype(F32)], axis=0)
        gains = jnp.pad(
            gains.reshape(3, row_shards, depth).transpose(1, 0, 2), ((0, 0), (0, 13), (0, 0))
        ).reshape(row_shards * 16, depth)
        kinds = ("share", "sum", "row", "row", "col")
        partials = (pack_grad, gains, query_weight_grad, up_grad, out_weight_grad)
        (output,), done = exchange(
            sizes,
            [
                give_back(expert_out, None, (residual, out_shared)),
                finish_job(
                    sizes,
                    kinds,
                    [fo_sum(part.astype(BF16), kind) for part, kind in zip(partials, kinds)],
                    [token_grad.astype(BF16)],
                ),
            ],
            3,
            "finish_attention",
        )
        pack_own = done[0].reshape(depth, -1).astype(F32)
        gains_own = done[1].astype(F32)
        query_weight_grad, up_grad, out_weight_grad = (part.astype(F32) for part in done[2:5])
        token_grad = done[5].astype(F32)
        return (
            output,
            token_grad,
            gains_own[0],
            query_weight_grad,
            pack_own[:, :down_width],
            gains_own[2, : latent_gain.shape[0]],
            up_grad,
            out_weight_grad,
            gains_own[1],
            pack_own[:, down_width:pack_used],
            sgate_grad,
            sup_grad,
            sdown_grad,
            egate_grad,
            eup_grad,
            edown_grad,
        )

    return shards


EXPERTS = 16


def solution(mesh):
    ctx_n, tp_n = mesh.shape["ctx"], mesh.shape["tp"]
    tpc_n = 2
    tpx_n = tp_n // tpc_n
    fi_n = EXPERTS // (ctx_n * tpx_n)
    sizes = {
        "fo": mesh.shape["fsdp"] // fi_n,
        "fi": fi_n,
        "ctx": ctx_n,
        "tpx": tpx_n,
        "tpc": tpc_n,
    }
    fine = Mesh(mesh.devices.reshape(tuple(sizes.values())), tuple(sizes))
    rows = P(ROWS)
    rows_two = P(ROWS, None)
    rows_tp = P(ROWS, TP)
    tp_rows = P(TP, ROWS)
    wide_in = P(None, ROWS, TP)
    wide_out = P(None, TP, ROWS)
    weights = (
        rows,
        rows_tp,
        rows_two,
        rows,
        rows_tp,
        tp_rows,
        rows,
        rows_two,
        rows_tp,
        rows_tp,
        tp_rows,
        wide_in,
        wide_in,
        wide_out,
    )
    return jax.shard_map(
        build(sizes),
        mesh=fine,
        in_specs=(rows_two, rows_two, rows_two, rows_two, P()) + weights,
        out_specs=(rows_two, rows_two) + weights,
        check_vma=False,
    )
```

```python
import functools
import math

import jax
import jax.numpy as jnp
from jax import lax
from jax.experimental import pallas as pl
from jax.experimental.pallas import tpu as pltpu
from jax.sharding import Mesh
from jax.sharding import PartitionSpec as P

NOPE = 128
ROPE = 64
KVR = 512
VDIM = 128
HEAD = 256

EPSILON = 1e-06
THETA_BASE = 10000.0
F32 = jnp.float32
BF16 = jnp.bfloat16
MESH_ID = pl.DeviceIdType.MESH

ROWS = ("fo", "fi", "ctx")
TP = ("tpx", "tpc")
PLANE = ("ctx", "tpx", "tpc")
CHIPS = ("fi", "ctx", "tpx")


def rotation_tables(positions, half_width):
    freq_table = jnp.exp(jnp.arange(half_width, dtype=F32) * (-math.log(THETA_BASE) / half_width))
    angle_table = positions.astype(F32)[:, None] * freq_table[None, :]
    return (jnp.cos(angle_table), jnp.sin(angle_table))


def rotate(values, cos_table, sin_table):
    half_width = values.shape[-1] // 2
    first_half = values[..., :half_width]
    second_half = values[..., half_width:]
    return jnp.concatenate(
        [
            first_half * cos_table - second_half * sin_table,
            second_half * cos_table + first_half * sin_table,
        ],
        axis=-1,
    )


def silu_parts(values):
    sigma = jax.nn.sigmoid(values)
    return (values * sigma, sigma * (1.0 + values * (1.0 - sigma)))


def rms_scale(values):
    return lax.rsqrt(jnp.mean(values * values, axis=-1, keepdims=True) + EPSILON)


def norm_back(grad_normed, normed, scale_rows):
    return scale_rows * (
        grad_normed - normed * jnp.mean(grad_normed * normed, axis=-1, keepdims=True)
    )


def dot(left, right):
    return jnp.dot(left, right, preferred_element_type=F32)


def dot_nt(left, right):
    return lax.dot_general(left, right, (((1,), (1,)), ((), ())), preferred_element_type=F32)


def dot_tn(left, right):
    return lax.dot_general(left, right, (((0,), (0,)), ((), ())), preferred_element_type=F32)


def ein(spec, left, right):
    return jnp.einsum(spec, left, right, preferred_element_type=F32)


def plane_place(sizes):
    tpx_n, tpc_n = sizes["tpx"], sizes["tpc"]
    fo, z, y, x, c = (lax.axis_index(name) for name in ("fo", "fi", "ctx", "tpx", "tpc"))
    own = (y * tpx_n + x) * tpc_n + c

    def device(index, z_at=None):
        return (
            fo,
            z if z_at is None else z_at,
            index // (tpx_n * tpc_n),
            lax.rem(index // tpc_n, tpx_n),
            lax.rem(index, tpc_n),
        )

    return z, y, x, c, own, device


def greet_plane(sizes):
    fi_n = sizes["fi"]
    plane_n = sizes["ctx"] * sizes["tpx"] * sizes["tpc"]
    z, y, x, c, own, device = plane_place(sizes)
    barrier = pltpu.get_barrier_semaphore()
    for step in range(1, plane_n):
        pl.semaphore_signal(
            barrier,
            inc=1,
            device_id=device(lax.rem(own + step, plane_n)),
            device_id_type=MESH_ID,
        )
    for near in (-1, 1):

        @pl.when((z + near >= 0) & (z + near < fi_n))
        def _():
            pl.semaphore_signal(
                barrier, inc=1, device_id=device(own, z + near), device_id_type=MESH_ID
            )

    sides = (z > 0).astype(jnp.int32) + (z < fi_n - 1).astype(jnp.int32)
    pl.semaphore_wait(barrier, plane_n - 1 + sides)


HBM_SPEC = pl.BlockSpec(memory_space=pl.ANY)
VMEM_SPEC = pl.BlockSpec(memory_space=pltpu.VMEM)


def exchange(sizes, jobs, collective_id, name, vmem=56):
    counts = [(len(job["args"]), len(job["outs"]), len(job["scratch"])) for job in jobs]

    def body(*refs):
        at = [0, sum(n[0] for n in counts), sum(n[0] + n[1] for n in counts)]
        running = []
        for job, count in zip(jobs, counts):
            given = [refs[at[k] : at[k] + count[k]] for k in range(3)]
            at = [at[k] + count[k] for k in range(3)]
            running.append(job["run"](sizes, *given))
        greet_plane(sizes)
        while running:
            running = [run for run in running if next(run, "ended") != "ended"]

    results = pl.pallas_call(
        body,
        out_shape=tuple(shape for job in jobs for shape, _ in job["outs"]),
        in_specs=[spec for job in jobs for _, spec in job["args"]],
        out_specs=tuple(spec for job in jobs for _, spec in job["outs"]),
        scratch_shapes=[shape for job in jobs for shape in job["scratch"]],
        compiler_params=pltpu.CompilerParams(
            collective_id=collective_id, has_side_effects=True, vmem_limit_bytes=vmem << 20
        ),
        cost_estimate=pl.CostEstimate(
            flops=0, bytes_accessed=20_000_000, transcendentals=0
        ),
        name=name,
    )(*[arg for job in jobs for arg, _ in job["args"]])
    grouped, at = [], 0
    for _, count, _ in counts:
        grouped.append(results[at : at + count])
        at += count
    return grouped


def tp_spread(sizes, source, held, whole, sems):
    tpx_n, tpc_n = sizes["tpx"], sizes["tpc"]
    keep_sem, x_send, x_recv, c_send, c_recv = sems
    fo, z, y, x, c = (lax.axis_index(n) for n in ("fo", "fi", "ctx", "tpx", "tpc"))
    wide = source.shape[1]

    def slab(side, core):
        at = (side * tpc_n + core) * wide
        return whole.at[:, pl.ds(pl.multiple_of(at, wide), wide)]

    def origin(dx):
        return lax.rem(x + tpx_n - dx, tpx_n)

    keep = pltpu.make_async_copy(held, slab(x, c), keep_sem)

    def to_chip(dx, side):
        return pltpu.make_async_remote_copy(
            src_ref=source,
            dst_ref=slab(side, c),
            send_sem=x_send.at[dx],
            recv_sem=x_recv.at[dx],
            device_id=(fo, z, y, lax.rem(x + dx, tpx_n), c),
            device_id_type=MESH_ID,
        )

    def to_core(dx, dc, core):
        return pltpu.make_async_remote_copy(
            src_ref=source if dx == 0 else slab(origin(dx), c),
            dst_ref=slab(origin(dx), core),
            send_sem=c_send.at[dx, dc],
            recv_sem=c_recv.at[dx, dc],
            device_id=(fo, z, y, x, lax.rem(c + dc, tpc_n)),
            device_id_type=MESH_ID,
        )

    def start():
        for dx in range(1, tpx_n):
            to_chip(dx, x).start()
        for dc in range(1, tpc_n):
            to_core(0, dc, c).start()

    def relay():
        for dx in range(1, tpx_n):
            to_chip(dx, origin(dx)).wait_recv()
            for dc in range(1, tpc_n):
                to_core(dx, dc, c).start()

    def settle():
        keep.wait()
        for dx in range(tpx_n):
            if dx > 0:
                to_chip(dx, x).wait_send()
            for dc in range(1, tpc_n):
                to_core(dx, dc, c).wait_send()
                to_core(dx, dc, lax.rem(c + tpc_n - dc, tpc_n)).wait_recv()

    return start, keep, relay, settle


def tp_spread_sems(sizes):
    tpx_n, tpc_n = sizes["tpx"], sizes["tpc"]
    return [
        pltpu.SemaphoreType.DMA,
        pltpu.SemaphoreType.DMA((tpx_n,)),
        pltpu.SemaphoreType.DMA((tpx_n,)),
        pltpu.SemaphoreType.DMA((tpx_n, tpc_n)),
        pltpu.SemaphoreType.DMA((tpx_n, tpc_n)),
    ]


def dispatch_job(sizes, part_rows, plane_slots, capacity):
    tokens, quarter = part_rows.shape
    fi_n, ctx_n, tpx_n, tpc_n = (sizes[n] for n in ("fi", "ctx", "tpx", "tpc"))
    z_part, plane_n, chips = fi_n // tpc_n, ctx_n * tpx_n * tpc_n, ctx_n * tpx_n
    shape = (z_part, ctx_n, capacity, quarter * tpx_n * tpc_n)
    return {
        "args": [(plane_slots, VMEM_SPEC), (part_rows, HBM_SPEC)],
        "outs": [(jax.ShapeDtypeStruct(shape, BF16), HBM_SPEC)],
        "scratch": [
            pltpu.VMEM((fi_n, tokens, quarter), BF16),
            pltpu.VMEM((fi_n, chips, capacity, quarter), BF16),
            pltpu.SemaphoreType.DMA,
            pltpu.SemaphoreType.DMA((2, fi_n)),
            pltpu.SemaphoreType.DMA((2, fi_n)),
            pltpu.SemaphoreType.DMA((fi_n, chips)),
            pltpu.SemaphoreType.DMA((plane_n, z_part)),
        ],
        "run": dispatch_run,
    }


def dispatch_run(sizes, args, outs, scratch):
    slots_ref, rows_ref = args
    (out_ref,) = outs
    held, picked, own_sem, line_send, line_recv, plane_send, plane_recv = scratch
    fi_n, tpx_n, tpc_n = sizes["fi"], sizes["tpx"], sizes["tpc"]
    plane_n = sizes["ctx"] * tpx_n * tpc_n
    chips = sizes["ctx"] * tpx_n
    z_part = fi_n // tpc_n
    capacity, quarter = picked.shape[2:]
    tokens = held.shape[1]
    z, y, x, c, own, device = plane_place(sizes)
    columns = pl.ds(pl.multiple_of((x * tpc_n + c) * quarter, quarter), quarter)
    load = pltpu.make_async_copy(rows_ref, held.at[z], own_sem)

    def line(side, step):
        block = z - step if side == 0 else z + step
        to = z + 1 if side == 0 else z - 1
        return pltpu.make_async_remote_copy(
            src_ref=held.at[block],
            dst_ref=held.at[block],
            send_sem=line_send.at[side, step],
            recv_sem=line_recv.at[side, step],
            device_id=device(own, to),
            device_id_type=MESH_ID,
        )

    def sends(side, step):
        block = z - step if side == 0 else z + step
        to = z + 1 if side == 0 else z - 1
        return (block >= 0) & (block < fi_n) & (to >= 0) & (to < fi_n)

    def plane_copy(block, chip):
        at = lax.rem(block, z_part)
        return pltpu.make_async_remote_copy(
            src_ref=picked.at[block, chip],
            dst_ref=out_ref.at[at, y, :, columns],
            send_sem=plane_send.at[block, chip],
            recv_sem=plane_recv.at[own, at],
            device_id=device(chip * tpc_n + block // z_part),
            device_id_type=MESH_ID,
        )

    def keep_copy(block, chip):
        return pltpu.make_async_copy(
            picked.at[block, chip],
            out_ref.at[lax.rem(block, z_part), y, :, columns],
            plane_send.at[block, chip],
        )

    def at_home(block, chip):
        return chip * tpc_n + block // z_part == own

    def pick(block):
        def one(chip, carry):
            wanted = slots_ref[block, pl.ds(chip, 1), :]
            rank = lax.broadcasted_iota(jnp.int32, (capacity, tokens), 0)
            hits = jnp.where(rank == wanted, 1.0, 0.0).astype(BF16)
            picked[block, chip] = jnp.dot(
                hits, held[block], preferred_element_type=F32
            ).astype(BF16)

            @pl.when(at_home(block, chip))
            def _():
                keep_copy(block, chip).start()

            @pl.when(jnp.logical_not(at_home(block, chip)))
            def _():
                plane_copy(block, chip).start()

            return carry

        lax.fori_loop(0, chips, one, 0)

    load.start()
    load.wait()
    for side in (0, 1):

        @pl.when(sends(side, 0))
        def _():
            line(side, 0).start()

    yield
    pick(z)
    for step in range(fi_n - 1):
        for side in (0, 1):
            block = z - 1 - step if side == 0 else z + 1 + step

            @pl.when((block >= 0) & (block < fi_n))
            def _():
                pltpu.make_async_remote_copy(
                    src_ref=held.at[block],
                    dst_ref=held.at[block],
                    send_sem=line_send.at[side, step],
                    recv_sem=line_recv.at[side, step],
                    device_id=device(own, z),
                    device_id_type=MESH_ID,
                ).wait_recv()

            if step < fi_n - 2:

                @pl.when(sends(side, step + 1))
                def _():
                    line(side, step + 1).start()

        for side in (0, 1):
            block = z - 1 - step if side == 0 else z + 1 + step

            @pl.when((block >= 0) & (block < fi_n))
            def _():
                pick(block)

        yield

    for step in range(fi_n - 1):
        for side in (0, 1):

            @pl.when(sends(side, step))
            def _():
                line(side, step).wait_send()

    def settle(index, carry):
        block, chip = index // chips, lax.rem(index, chips)

        @pl.when(at_home(block, chip))
        def _():
            keep_copy(block, chip).wait()

        @pl.when(jnp.logical_not(at_home(block, chip)))
        def _():
            plane_copy(block, chip).wait_send()

        return carry

    lax.fori_loop(0, fi_n * chips, settle, 0)

    def arrive(index, carry):
        source, at = index // z_part, lax.rem(index, z_part)

        @pl.when(source != own)
        def _():
            pltpu.make_async_remote_copy(
                src_ref=picked.at[0, 0],
                dst_ref=out_ref.at[at, y, :, columns],
                send_sem=plane_send.at[0, 0],
                recv_sem=plane_recv.at[source, at],
                device_id=device(own),
                device_id_type=MESH_ID,
            ).wait_recv()

        return carry

    lax.fori_loop(0, plane_n * z_part, arrive, 0)


def give_back_run(sizes, args, outs, scratch):
    fi_n, tpx_n, tpc_n = sizes["fi"], sizes["tpx"], sizes["tpc"]
    plane_n = sizes["ctx"] * tpx_n * tpc_n
    chips = sizes["ctx"] * tpx_n
    z_part = fi_n // tpc_n
    ends, gated = len(args) > 3, len(args) == 3
    slots_ref, rows_ref = args[:2]
    out_ref = outs[0]
    got, total, going, coming, plane_send, plane_recv, line_send, line_recv = scratch[:8]
    if gated:
        gates_ref, gate_out = args[2], outs[1]
        gates_got, gate_total, gate_going, gate_coming = scratch[8:12]
        gate_send, gate_recv, gate_line_send, gate_line_recv = scratch[12:]
    if ends:
        held = scratch[8]
        start, keep, relay, spread_settle = tp_spread(sizes, held, held, out_ref, scratch[9:])
    capacity, quarter = got.shape[2:]
    tokens = total.shape[0]
    z, y, x, c, own, device = plane_place(sizes)
    tile = min(256, tokens)

    def piece(target, at):
        side = lax.rem(target, tpx_n * tpc_n)
        return rows_ref.at[
            at,
            target // (tpx_n * tpc_n),
            :,
            pl.ds(pl.multiple_of(side * quarter, quarter), quarter),
        ]

    def plane_copies(target, at):
        made = [
            pltpu.make_async_remote_copy(
                src_ref=piece(target, at),
                dst_ref=got.at[c * z_part + at, own // tpc_n],
                send_sem=plane_send.at[target, at],
                recv_sem=plane_recv.at[own, at],
                device_id=device(target),
                device_id_type=MESH_ID,
            )
        ]
        if gated:
            made.append(
                pltpu.make_async_remote_copy(
                    src_ref=gates_ref.at[at, target // (tpx_n * tpc_n)],
                    dst_ref=gates_got.at[c * z_part + at, own // tpc_n],
                    send_sem=gate_send.at[target, at],
                    recv_sem=gate_recv.at[own, at],
                    device_id=device(target),
                    device_id_type=MESH_ID,
                )
            )
        return made

    def keep_copies(at):
        made = [
            pltpu.make_async_copy(
                piece(own, at), got.at[c * z_part + at, own // tpc_n], plane_recv.at[own, at]
            )
        ]
        if gated:
            made.append(
                pltpu.make_async_copy(
                    gates_ref.at[at, y],
                    gates_got.at[c * z_part + at, own // tpc_n],
                    gate_recv.at[own, at],
                )
            )
        return made

    high_first = z < fi_n // 2
    early = c == jnp.where(high_first, tpc_n - 1, 0)

    def at_turn(turn):
        far = jnp.where(high_first, z_part - 1 - turn, turn)
        return jnp.where(early, far, lax.rem(z + 1 + turn, z_part))

    def send_turn(turn):
        at = at_turn(turn)

        def one(step, carry):
            for copy in plane_copies(lax.rem(own + step, plane_n), at):
                copy.start()
            return carry

        for copy in keep_copies(at):
            copy.start()
        lax.fori_loop(1, plane_n, one, 0)

    def sent_turn(turn):
        def one(step, carry):
            for copy in plane_copies(lax.rem(own + step, plane_n), at_turn(turn)):
                copy.wait_send()
            return carry

        lax.fori_loop(1, plane_n, one, 0)

    @pl.when(early)
    def _():
        for turn in range(z_part):
            send_turn(turn)
            if turn < z_part - 1:
                sent_turn(turn)

    yield

    def gathered(block):
        def one(chip, carry):
            source, at = chip * tpc_n + block // z_part, lax.rem(block, z_part)

            @pl.when(source == own)
            def _():
                for copy in keep_copies(at):
                    copy.wait()

            @pl.when(source != own)
            def _():
                pltpu.make_async_remote_copy(
                    src_ref=got.at[block, chip],
                    dst_ref=got.at[block, chip],
                    send_sem=plane_send.at[own, at],
                    recv_sem=plane_recv.at[source, at],
                    device_id=device(own),
                    device_id_type=MESH_ID,
                ).wait_recv()
                if gated:
                    pltpu.make_async_remote_copy(
                        src_ref=gates_got.at[block, chip],
                        dst_ref=gates_got.at[block, chip],
                        send_sem=gate_send.at[own, at],
                        recv_sem=gate_recv.at[source, at],
                        device_id=device(own),
                        device_id_type=MESH_ID,
                    ).wait_recv()

            return carry

        lax.fori_loop(0, chips, one, 0)

        def rows(step, carry):
            first = pl.multiple_of(step * tile, tile)
            spots = slots_ref[block, pl.ds(first, tile), :]
            rank = lax.broadcasted_iota(jnp.int32, (tile, capacity), 1)
            summed = jnp.zeros((tile, quarter), F32)
            if gated:
                experts = gate_total.shape[0]
                gates = jnp.zeros((experts, tile), F32)
                expert = lax.broadcasted_iota(jnp.int32, (experts, capacity), 0)
            for chip in range(chips):
                hits = jnp.where(rank == spots[:, chip : chip + 1], 1.0, 0.0).astype(BF16)
                summed = summed + jnp.dot(hits, got[block, chip], preferred_element_type=F32)
                if gated:
                    left = jnp.where(
                        expert == z * chips + chip, gates_got[block, chip, 0:1, :], 0.0
                    ).astype(BF16)
                    gates = gates + dot_nt(left, hits)
            total[pl.ds(first, tile), :] = summed
            if gated:
                gate_total[:, pl.ds(first, tile)] = gates
            return carry

        lax.fori_loop(0, tokens // tile, rows, 0)

    def lines(side, target, to):
        made = [
            pltpu.make_async_remote_copy(
                src_ref=going.at[target],
                dst_ref=coming.at[side, target],
                send_sem=line_send.at[side, target],
                recv_sem=line_recv.at[side, target],
                device_id=device(own, to),
                device_id_type=MESH_ID,
            )
        ]
        if gated:
            made.append(
                pltpu.make_async_remote_copy(
                    src_ref=gate_going.at[target],
                    dst_ref=gate_coming.at[side, target],
                    send_sem=gate_line_send.at[side, target],
                    recv_sem=gate_line_recv.at[side, target],
                    device_id=device(own, to),
                    device_id_type=MESH_ID,
                )
            )
        return made

    for step in range(fi_n - 1):
        for side in (0, 1):
            depth = z if side == 0 else fi_n - 1 - z
            target = fi_n - 1 - step + z if side == 0 else step - (fi_n - 1) + z
            passes, inner = depth <= step, depth > 0

            @pl.when(passes)
            def _():
                gathered(target)

                @pl.when(inner)
                def _():
                    for copy in lines(side, target, z):
                        copy.wait_recv()
                    going[target] = (total[...] + coming[side, target].astype(F32)).astype(BF16)
                    if gated:
                        gate_going[target] = gate_total[...] + gate_coming[side, target]

                @pl.when(jnp.logical_not(inner))
                def _():
                    going[target] = total[...].astype(BF16)
                    if gated:
                        gate_going[target] = gate_total[...]

                for copy in lines(side, target, z + 1 if side == 0 else z - 1):
                    copy.start()

        for turn in range(z_part):
            if min(turn, fi_n - 2) == step:

                @pl.when(jnp.logical_not(early))
                def _():
                    send_turn(turn)

        yield

    gathered(z)
    for side in (0, 1):

        @pl.when((z > 0) if side == 0 else (z < fi_n - 1))
        def _():
            for copy in lines(side, z, z):
                copy.wait_recv()
            total[...] += coming[side, z].astype(F32)
            if gated:
                gate_total[...] += gate_coming[side, z]

    if ends:
        held[...] = (total[...] + args[2][...] + args[3][...]).astype(BF16)
        start()
        keep.start()
    else:
        out_ref[...] = total[...]
    if gated:
        gate_out[...] = gate_total[...]
    yield
    if ends:
        relay()


    for target in range(fi_n):
        for side in (0, 1):

            @pl.when((z < target) if side == 0 else (z > target))
            def _():
                for copy in lines(side, target, z + 1 if side == 0 else z - 1):
                    copy.wait_send()

    for turn in range(z_part):

        @pl.when(jnp.logical_not(early) | (turn == z_part - 1))
        def _():
            sent_turn(turn)

    yield
    if ends:
        spread_settle()


def give_back_job(sizes, rows, token_slots, gates, bases=None):
    fi_n, ctx_n, tpx_n, tpc_n = (sizes[n] for n in ("fi", "ctx", "tpx", "tpc"))
    z_part, plane_n, chips = fi_n // tpc_n, ctx_n * tpx_n * tpc_n, ctx_n * tpx_n
    capacity, width = rows.shape[2:]
    quarter = width // (tpx_n * tpc_n)
    tokens = token_slots.shape[1]
    experts = fi_n * chips
    gated = gates is not None
    shapes = [jax.ShapeDtypeStruct((tokens, quarter), F32)]
    scratch = [
        pltpu.VMEM((fi_n, chips, capacity, quarter), BF16),
        pltpu.VMEM((tokens, quarter), F32),
        pltpu.VMEM((fi_n, tokens, quarter), BF16),
        pltpu.VMEM((2, fi_n, tokens, quarter), BF16),
        pltpu.SemaphoreType.DMA((plane_n, z_part)),
        pltpu.SemaphoreType.DMA((plane_n, z_part)),
        pltpu.SemaphoreType.DMA((2, fi_n)),
        pltpu.SemaphoreType.DMA((2, fi_n)),
    ]
    args = [token_slots, rows]
    if gated:
        args.append(gates)
        shapes.append(jax.ShapeDtypeStruct((experts, tokens), F32))
        scratch += [
            pltpu.VMEM((fi_n, chips, 8, capacity), F32),
            pltpu.VMEM((experts, tokens), F32),
            pltpu.VMEM((fi_n, experts, tokens), F32),
            pltpu.VMEM((2, fi_n, experts, tokens), F32),
            pltpu.SemaphoreType.DMA((plane_n, z_part)),
            pltpu.SemaphoreType.DMA((plane_n, z_part)),
            pltpu.SemaphoreType.DMA((2, fi_n)),
            pltpu.SemaphoreType.DMA((2, fi_n)),
        ]
    specs = [VMEM_SPEC] + [HBM_SPEC] * (len(args) - 1)
    if bases is not None:
        args += list(bases)
        specs += [VMEM_SPEC] * 2
        shapes = [jax.ShapeDtypeStruct((tokens, width), BF16)]
        scratch += [pltpu.VMEM((tokens, quarter), BF16)] + tp_spread_sems(sizes)
    return {
        "args": list(zip(args, specs)),
        "outs": [(shape, HBM_SPEC if bases is not None else VMEM_SPEC) for shape in shapes],
        "scratch": scratch,
        "run": give_back_run,
    }


def collect_run(kinds, sizes, args, outs, scratch):
    fo_n, fi_n, ctx_n, tpx_n, tpc_n = (sizes[n] for n in ("fo", "fi", "ctx", "tpx", "tpc"))
    tp_n = tpx_n * tpc_n
    count = len(kinds)
    shards = args
    own_sem, line_send, line_recv, col_send, col_recv, tp_send, tp_recv = scratch[:7]
    staged = scratch[7:]
    fo, z, y, x, c = (lax.axis_index(n) for n in ("fo", "fi", "ctx", "tpx", "tpc"))
    q = x * tpc_n + c

    items = [(i, f) for f in range(fo_n) for i in range(count)]

    def source(n):
        i, f = items[n]
        if kinds[i] == "share":
            a = shards[i].shape[1] // tp_n
            return shards[i].at[f, pl.ds(pl.multiple_of(q * a, a), a), :]
        return shards[i].at[f]

    def place(n, zb, yb):
        i, f = items[n]
        a, b = shards[i].shape[1:]
        block = (f * fi_n + zb) * ctx_n + yb
        if kinds[i] == "col":
            return outs[i].at[:, pl.ds(pl.multiple_of(block * b, b), b)]
        if kinds[i] == "share":
            part = a // tp_n
            return outs[i].at[pl.ds(pl.multiple_of(block * a + q * part, part), part), :]
        return outs[i].at[pl.ds(pl.multiple_of(block * a, a), a), :]

    def line(n, side, step, first):
        block = z - step if side == 0 else z + step
        to = z + 1 if side == 0 else z - 1
        return pltpu.make_async_remote_copy(
            src_ref=source(n) if first else place(n, block, y),
            dst_ref=place(n, block, y),
            send_sem=line_send.at[n, side, step],
            recv_sem=line_recv.at[n, side, step],
            device_id=(fo, to, y, x, c),
            device_id_type=MESH_ID,
        )

    def sends(side, step):
        block = z - step if side == 0 else z + step
        to = z + 1 if side == 0 else z - 1
        return (block >= 0) & (block < fi_n) & (to >= 0) & (to < fi_n)

    def across(n, zb, dy, first=False):
        return pltpu.make_async_remote_copy(
            src_ref=source(n) if first else place(n, zb, y),
            dst_ref=place(n, zb, y),
            send_sem=col_send.at[n, zb, dy],
            recv_sem=col_recv.at[n, zb, dy],
            device_id=(fo, z, lax.rem(y + dy, ctx_n), x, c),
            device_id_type=MESH_ID,
        )

    def stage(n):
        return pltpu.make_async_copy(source(n), staged[n], own_sem.at[n, 0])

    def keep(n):
        return pltpu.make_async_copy(staged[n], place(n, z, y), own_sem.at[n, 1])

    for n in range(len(items)):
        for side in (0, 1):

            @pl.when(sends(side, 0))
            def _():
                line(n, side, 0, True).start()

        for dy in range(1, ctx_n):
            across(n, z, dy, True).start()
        stage(n).start()

    yield
    for n in range(len(items)):
        stage(n).wait()
        keep(n).start()

    for step in range(fi_n - 1):
        for n in range(len(items)):
            for side in (0, 1):
                block = z - 1 - step if side == 0 else z + 1 + step

                @pl.when((block >= 0) & (block < fi_n))
                def _():
                    pltpu.make_async_remote_copy(
                        src_ref=place(n, block, y),
                        dst_ref=place(n, block, y),
                        send_sem=line_send.at[n, side, step],
                        recv_sem=line_recv.at[n, side, step],
                        device_id=(fo, z, y, x, c),
                        device_id_type=MESH_ID,
                    ).wait_recv()
                    for dy in range(1, ctx_n):
                        across(n, block, dy).start()

                if step < fi_n - 2:

                    @pl.when(sends(side, step + 1))
                    def _():
                        line(n, side, step + 1, False).start()

        yield

    for n in range(len(items)):
        keep(n).wait()
        for dy in range(1, ctx_n):
            for zb in range(fi_n):
                pltpu.make_async_remote_copy(
                    src_ref=place(n, zb, y),
                    dst_ref=place(n, zb, lax.rem(y + ctx_n - dy, ctx_n)),
                    send_sem=col_send.at[n, zb, dy],
                    recv_sem=col_recv.at[n, zb, dy],
                    device_id=(fo, z, y, x, c),
                    device_id_type=MESH_ID,
                ).wait_recv()
        i, f = items[n]
        if kinds[i] == "share":
            a = shards[i].shape[1]
            part = a // tp_n

            def spread(block, step, n=n, i=i, f=f, a=a, part=part):
                other = lax.rem(q + step, tp_n)
                at = (f * fi_n * ctx_n + block) * a + q * part
                return pltpu.make_async_remote_copy(
                    src_ref=outs[i].at[pl.ds(pl.multiple_of(at, part), part), :],
                    dst_ref=outs[i].at[pl.ds(pl.multiple_of(at, part), part), :],
                    send_sem=tp_send.at[n, block, step],
                    recv_sem=tp_recv.at[n, block, step],
                    device_id=(fo, z, y, other // tpc_n, lax.rem(other, tpc_n)),
                    device_id_type=MESH_ID,
                )

            def spread_all(block, carry):
                for step in range(1, tp_n):
                    spread(block, step).start()
                return carry

            lax.fori_loop(0, fi_n * ctx_n, spread_all, 0)

    yield

    for n in range(len(items)):
        i, f = items[n]
        if kinds[i] == "share":
            a = shards[i].shape[1]
            part = a // tp_n

            def landed(block, carry, n=n, i=i, f=f, a=a, part=part):
                for step in range(1, tp_n):
                    origin = lax.rem(q + tp_n - step, tp_n)
                    at = (f * fi_n * ctx_n + block) * a
                    mine = pl.ds(pl.multiple_of(at + q * part, part), part)
                    theirs = pl.ds(pl.multiple_of(at + origin * part, part), part)
                    copy = pltpu.make_async_remote_copy(
                        src_ref=outs[i].at[mine, :],
                        dst_ref=outs[i].at[theirs, :],
                        send_sem=tp_send.at[n, block, step],
                        recv_sem=tp_recv.at[n, block, step],
                        device_id=(fo, z, y, x, c),
                        device_id_type=MESH_ID,
                    )
                    copy.wait_send()
                    copy.wait_recv()
                return carry

            lax.fori_loop(0, fi_n * ctx_n, landed, 0)
        for side in (0, 1):
            for step in range(fi_n - 1):

                @pl.when(sends(side, step))
                def _():
                    line(n, side, step, step == 0).wait_send()

        for dy in range(1, ctx_n):
            for zb in range(fi_n):
                across(n, zb, dy).wait_send()


def collect_job(sizes, kinds, shards):
    fo_n, fi_n, ctx_n, tpx_n, tpc_n = (sizes[n] for n in ("fo", "fi", "ctx", "tpx", "tpc"))
    tp_n = tpx_n * tpc_n
    blocks = fo_n * fi_n * ctx_n
    outs, staged = [], []
    for kind, shard in zip(kinds, shards):
        _, a, b = shard.shape
        shape = (a, blocks * b) if kind == "col" else (blocks * a, b)
        outs.append((jax.ShapeDtypeStruct(shape, shard.dtype), HBM_SPEC))
        staged.append(pltpu.VMEM((a // tp_n if kind == "share" else a, b), shard.dtype))
    n = len(kinds) * fo_n
    return {
        "args": [(shard, HBM_SPEC) for shard in shards],
        "outs": outs,
        "scratch": [
            pltpu.SemaphoreType.DMA((n, 2)),
            pltpu.SemaphoreType.DMA((n, 2, fi_n)),
            pltpu.SemaphoreType.DMA((n, 2, fi_n)),
            pltpu.SemaphoreType.DMA((n, fi_n, ctx_n)),
            pltpu.SemaphoreType.DMA((n, fi_n, ctx_n)),
            pltpu.SemaphoreType.DMA((n, fi_n * ctx_n, tp_n)),
            pltpu.SemaphoreType.DMA((n, fi_n * ctx_n, tp_n)),
        ]
        + staged * fo_n,
        "run": functools.partial(collect_run, tuple(kinds)),
    }


def place_job(sizes, local):
    fo_n, fi_n, ctx_n, tpx_n, tpc_n = (sizes[n] for n in ("fo", "fi", "ctx", "tpx", "tpc"))
    chip_n = fi_n * ctx_n * tpx_n
    rows, depth = local.shape[3:]
    shape = (rows * tpx_n * tpc_n, depth * fo_n * fi_n * ctx_n)
    return {
        "args": [(local, HBM_SPEC)],
        "outs": [(jax.ShapeDtypeStruct(shape, BF16), HBM_SPEC)] * 3,
        "scratch": [pltpu.VMEM(local.shape, BF16)]
        + [pltpu.SemaphoreType.DMA((fo_n, 3, chip_n))] * 2
        + [pltpu.SemaphoreType.DMA((fo_n, 3, chip_n, tpc_n))] * 2,
        "run": place_run,
    }


def place_run(sizes, args, outs, scratch):
    fo_n, fi_n, ctx_n, tpx_n, tpc_n = (sizes[n] for n in ("fo", "fi", "ctx", "tpx", "tpc"))
    (local,) = args
    staged, load_sem, keep_sem, pair_send, pair_recv = scratch
    chip_n = fi_n * ctx_n * tpx_n
    rows, depth = local.shape[3:]
    fo, z, y, x, c = (lax.axis_index(n) for n in ("fo", "fi", "ctx", "tpx", "tpc"))

    def spot(k, f, chip, core):
        block = f * fi_n * ctx_n + chip // tpx_n
        return outs[k].at[
            pl.ds(pl.multiple_of((lax.rem(chip, tpx_n) * tpc_n + core) * rows, rows), rows),
            pl.ds(pl.multiple_of(block * depth, depth), depth),
        ]

    def load(f, k, chip):
        return pltpu.make_async_copy(
            local.at[f, chip, k], staged.at[f, chip, k], load_sem.at[f, k, chip]
        )

    def keep(f, k, chip):
        return pltpu.make_async_copy(
            staged.at[f, chip, k], spot(k, f, chip, c), keep_sem.at[f, k, chip]
        )

    def pair_copy(f, k, chip, dc, core):
        return pltpu.make_async_remote_copy(
            src_ref=local.at[f, chip, k],
            dst_ref=spot(k, f, chip, core),
            send_sem=pair_send.at[f, k, chip, dc],
            recv_sem=pair_recv.at[f, k, chip, dc],
            device_id=(fo, z, y, x, lax.rem(c + dc, tpc_n)),
            device_id_type=MESH_ID,
        )

    def launch(step, carry):
        f, chip = step // chip_n, lax.rem(step, chip_n)
        for k in range(3):
            load(f, k, chip).start()
            for dc in range(1, tpc_n):
                pair_copy(f, k, chip, dc, c).start()
        return carry

    def store(step, carry):
        f, chip = step // chip_n, lax.rem(step, chip_n)
        for k in range(3):
            load(f, k, chip).wait()
            keep(f, k, chip).start()
        return carry

    def settle(step, carry):
        f, chip = step // chip_n, lax.rem(step, chip_n)
        for k in range(3):
            keep(f, k, chip).wait()
            for dc in range(1, tpc_n):
                pair_copy(f, k, chip, dc, c).wait_send()
                pair_copy(f, k, chip, dc, lax.rem(c + tpc_n - dc, tpc_n)).wait_recv()
        return carry

    lax.fori_loop(0, fo_n * chip_n, launch, 0)
    yield
    lax.fori_loop(0, fo_n * chip_n, store, 0)
    yield
    lax.fori_loop(0, fo_n * chip_n, settle, 0)


def pair_body(sizes, fo_n, *refs):
    fi_n, ctx_n, tpx_n, tpc_n = (sizes[n] for n in ("fi", "ctx", "tpx", "tpc"))
    grads, (out_ref, mine, theirs, load_sem, store_sem, send_sem, recv_sem) = refs[:3], refs[3:]
    chip_n = fi_n * ctx_n * tpx_n
    rows, depth = mine.shape[2:]
    fo, z, y, x, c = (lax.axis_index(n) for n in ("fo", "fi", "ctx", "tpx", "tpc"))
    sibling = (fo, z, y, x, 1 - c)
    barrier = pltpu.get_barrier_semaphore()
    pl.semaphore_signal(barrier, inc=1, device_id=sibling, device_id_type=MESH_ID)
    pl.semaphore_wait(barrier, 1)

    def spot(k, at, core):
        block, side = at // tpx_n, lax.rem(at, tpx_n)
        return grads[k].at[
            pl.ds(pl.multiple_of((side * tpc_n + core) * rows, rows), rows),
            pl.ds(pl.multiple_of(block * depth, depth), depth),
        ]

    def load(k, at):
        return pltpu.make_async_copy(spot(k, at, c), mine.at[at, k], load_sem.at[at, k])

    def store(k, at):
        return pltpu.make_async_copy(mine.at[at, k], out_ref.at[at, k], store_sem.at[at, k])

    def give(k, at):
        return pltpu.make_async_remote_copy(
            src_ref=spot(k, at, 1 - c),
            dst_ref=theirs.at[at, k],
            send_sem=send_sem.at[at, k],
            recv_sem=recv_sem.at[at, k],
            device_id=sibling,
            device_id_type=MESH_ID,
        )

    def launch(at, carry):
        for k in range(3):
            give(k, at).start()
            load(k, at).start()
        return carry

    def add(at, carry):
        for k in range(3):
            load(k, at).wait()
            give(k, at).wait_recv()
            mine[at, k] = (mine[at, k].astype(F32) + theirs[at, k].astype(F32)).astype(BF16)
            store(k, at).start()
        return carry

    def settle(at, carry):
        for k in range(3):
            give(k, at).wait_send()
            store(k, at).wait()
        return carry

    total = fo_n * chip_n
    lax.fori_loop(0, total, launch, 0)
    lax.fori_loop(0, total, add, 0)
    lax.fori_loop(0, total, settle, 0)


def pair_sum(sizes, grads, collective_id):
    fo_n, fi_n, ctx_n, tpx_n, tpc_n = (sizes[n] for n in ("fo", "fi", "ctx", "tpx", "tpc"))
    rows = grads[0].shape[0] // (tpx_n * tpc_n)
    depth = grads[0].shape[1] // (fo_n * fi_n * ctx_n)
    total = fo_n * fi_n * ctx_n * tpx_n
    shape = (total, 3, rows, depth)
    hbm = pl.BlockSpec(memory_space=pl.ANY)
    return pl.pallas_call(
        functools.partial(pair_body, sizes, fo_n),
        out_shape=jax.ShapeDtypeStruct(shape, BF16),
        in_specs=[hbm] * 3,
        out_specs=hbm,
        scratch_shapes=[pltpu.VMEM(shape, BF16)] * 2 + [pltpu.SemaphoreType.DMA((total, 3))] * 4,
        compiler_params=pltpu.CompilerParams(
            collective_id=collective_id, has_side_effects=True, vmem_limit_bytes=32 << 20
        ),
        cost_estimate=pl.CostEstimate(flops=0, bytes_accessed=60_000_000, transcendentals=0),
        name="pair_sum",
    )(*grads)


def finish_run(kinds, sizes, args, outs, scratch):
    fi_n, ctx_n, tpx_n, tpc_n = (sizes[n] for n in ("fi", "ctx", "tpx", "tpc"))
    tp_n = tpx_n * tpc_n
    count = len(kinds)
    extra = len(args) - count
    parts, quarters = args[:count], args[count:]
    outs, wholes = outs[:count], outs[count:]
    mine, other, coming = (scratch[k * count : (k + 1) * count] for k in range(3))
    staged, (tiny, *sems) = scratch[3 * count : 3 * count + extra], scratch[3 * count + extra :]
    load_sem, col_send, col_recv, line_send, line_recv, tp_send, tp_recv = sems[:7]
    fo, z, y, x, c = (lax.axis_index(n) for n in ("fo", "fi", "ctx", "tpx", "tpc"))
    q = x * tpc_n + c

    spreads = [
        tp_spread(sizes, quarters[j], staged[j], wholes[j], sems[8 + 5 * j : 13 + 5 * j])
        for j in range(extra)
    ]

    def stage(j):
        return pltpu.make_async_copy(quarters[j], staged[j], sems[7].at[j])

    for j in range(extra):
        spreads[j][0]()
        stage(j).start()

    def view(n, zb, yb):
        a, b = mine[n].shape[1:]
        block = zb * ctx_n + yb
        if kinds[n] == "col":
            return parts[n].at[:, pl.ds(pl.multiple_of(block * b, b), b)]
        if kinds[n] == "share":
            return parts[n].at[pl.ds(pl.multiple_of(block * a * tp_n + q * a, a), a), :]
        return parts[n].at[pl.ds(pl.multiple_of(block * a, a), a), :]

    def across(n, zb, dy):
        to = lax.rem(y + dy, ctx_n)
        return pltpu.make_async_remote_copy(
            src_ref=view(n, zb, to),
            dst_ref=other[n].at[dy - 1, zb],
            send_sem=col_send.at[n, zb, dy],
            recv_sem=col_recv.at[n, zb, dy],
            device_id=(fo, z, to, x, c),
            device_id_type=MESH_ID,
        )

    def load(n, zb):
        return pltpu.make_async_copy(view(n, zb, y), mine[n].at[zb], load_sem.at[n, zb])

    def block_turn(turn):
        high_first = z < fi_n // 2
        place = jnp.where(high_first, fi_n - 1 - z, z)
        at = turn + (place <= turn).astype(jnp.int32)
        far = jnp.where(high_first, fi_n - 1 - at, at)
        return z if turn == fi_n - 1 else far

    def send_turn(turn):
        zb = block_turn(turn)
        for n in range(count):
            for dy in range(1, ctx_n):
                across(n, zb, dy).start()
            load(n, zb).start()

    def sent_turn(turn):
        for n in range(count):
            for dy in range(1, ctx_n):
                across(n, block_turn(turn), dy).wait_send()

    send_turn(0)
    yield
    send_turn(1)
    for j in range(extra):
        stage(j).wait()
        spreads[j][1].start()

    def line(n, side, target):
        at = jnp.where(target == (z + 1 if side == 0 else z - 1), fi_n, target) if side == 1 else target
        return pltpu.make_async_remote_copy(
            src_ref=mine[n].at[target],
            dst_ref=coming[n].at[at],
            send_sem=line_send.at[n, side, target],
            recv_sem=line_recv.at[n, side, target],
            device_id=(fo, z + 1 if side == 0 else z - 1, y, x, c),
            device_id_type=MESH_ID,
        )

    def came(n, side, target, at):
        pltpu.make_async_remote_copy(
            src_ref=mine[n].at[target],
            dst_ref=coming[n].at[at],
            send_sem=line_send.at[n, side, target],
            recv_sem=line_recv.at[n, side, target],
            device_id=(fo, z, y, x, c),
            device_id_type=MESH_ID,
        ).wait_recv()

    def ready(n, target):
        load(n, target).wait()
        for dy in range(1, ctx_n):
            across(n, target, dy).wait_recv()

    def add(n, target, use, store):
        a = mine[n].shape[1]
        tile = math.gcd(a, 64)

        def rows(step, carry):
            at = pl.ds(pl.multiple_of(step * tile, tile), tile)
            summed = mine[n][target, at, :].astype(F32)
            for dy in range(1, ctx_n):
                summed = summed + other[n][dy - 1, target, at, :].astype(F32)
            for slot in use:
                summed = summed + coming[n][slot, at, :].astype(F32)
            store(at, summed.astype(BF16))
            return carry

        lax.fori_loop(0, a // tile, rows, 0)

    for step in range(fi_n - 1):
        for n in range(count):
            for side in (0, 1):
                depth = z if side == 0 else fi_n - 1 - z
                target = fi_n - 1 - step + z if side == 0 else step - (fi_n - 1) + z
                passes, inner = depth <= step, depth > 0

                def back(at, values, n=n, target=target):
                    mine[n][target, at, :] = values

                @pl.when(passes & inner)
                def _():
                    ready(n, target)
                    came(n, side, target, target)
                    add(n, target, (target,), back)
                    line(n, side, target).start()

                @pl.when(passes & jnp.logical_not(inner))
                def _():
                    ready(n, target)
                    add(n, target, (), back)
                    line(n, side, target).start()

        if step + 2 < fi_n:
            sent_turn(step)
            send_turn(step + 2)
        yield

    for n in range(count):
        ready(n, z)

        def out(at, values, n=n):
            if kinds[n] == "share":
                a = mine[n].shape[1]
                outs[n][q, at, :] = values
            elif kinds[n] == "sum":
                tiny[q, at, :] = values
            else:
                outs[n][at, :] = values

        @pl.when(z > 0)
        def _():
            came(n, 0, z, z)

        @pl.when(z < fi_n - 1)
        def _():
            came(n, 1, z, fi_n)

        @pl.when((z > 0) & (z < fi_n - 1))
        def _():
            add(n, z, (z, fi_n), out)

        @pl.when((z == 0) & (z < fi_n - 1))
        def _():
            add(n, z, (fi_n,), out)

        @pl.when((z > 0) & (z == fi_n - 1))
        def _():
            add(n, z, (z,), out)

        @pl.when((z == 0) & (z == fi_n - 1))
        def _():
            add(n, z, (), out)

        if kinds[n] in ("share", "sum"):
            held = outs[n] if kinds[n] == "share" else tiny
            for step in range(1, tp_n):
                peer = lax.rem(q + step, tp_n)
                pltpu.make_async_remote_copy(
                    src_ref=held.at[q],
                    dst_ref=held.at[q],
                    send_sem=tp_send.at[n, step],
                    recv_sem=tp_recv.at[n, step],
                    device_id=(fo, z, y, peer // tpc_n, lax.rem(peer, tpc_n)),
                    device_id_type=MESH_ID,
                ).start()

    yield
    for j in range(extra):
        spreads[j][2]()

    for n in range(count):
        if kinds[n] in ("share", "sum"):
            held = outs[n] if kinds[n] == "share" else tiny
            for step in range(1, tp_n):
                origin = lax.rem(q + tp_n - step, tp_n)
                copy = pltpu.make_async_remote_copy(
                    src_ref=held.at[q],
                    dst_ref=held.at[origin],
                    send_sem=tp_send.at[n, step],
                    recv_sem=tp_recv.at[n, step],
                    device_id=(fo, z, y, x, c),
                    device_id_type=MESH_ID,
                )
                copy.wait_send()
                copy.wait_recv()
            if kinds[n] == "sum":
                summed = tiny[0].astype(F32)
                for k in range(1, tp_n):
                    summed = summed + tiny[k].astype(F32)
                outs[n][...] = summed.astype(BF16)
        for target in range(fi_n):
            for side in (0, 1):

                @pl.when((z < target) if side == 0 else (z > target))
                def _():
                    line(n, side, target).wait_send()

    for turn in range(fi_n - 2, fi_n):
        sent_turn(turn)
    for j in range(extra):
        spreads[j][3]()


def finish_job(sizes, kinds, parts, quarters):
    fi_n, ctx_n, tpx_n, tpc_n = (sizes[n] for n in ("fi", "ctx", "tpx", "tpc"))
    tp_n = tpx_n * tpc_n
    blocks = fi_n * ctx_n
    count, extra = len(kinds), len(quarters)
    own, shapes = [], []
    sum_shape = (16, 256)
    for kind, part in zip(kinds, parts):
        a, b = part.shape
        if kind == "col":
            own.append((a, b // blocks))
            shapes.append(own[-1])
        elif kind == "share":
            own.append((a // (blocks * tp_n), b))
            shapes.append((tp_n,) + own[-1])
        else:
            own.append((a // blocks, b))
            shapes.append(own[-1])
        if kind == "sum":
            sum_shape = own[-1]
    wide = [(v.shape[0], v.shape[1] * tp_n) for v in quarters]
    some = max(extra, 1)
    shapes = [jax.ShapeDtypeStruct(shape, BF16) for shape in shapes + wide]
    return {
        "args": [(arg, HBM_SPEC) for arg in (*parts, *quarters)],
        "outs": list(zip(shapes, [VMEM_SPEC] * count + [HBM_SPEC] * extra)),
        "scratch": [pltpu.VMEM((fi_n,) + s, BF16) for s in own]
        + [pltpu.VMEM((max(ctx_n - 1, 1), fi_n) + s, BF16) for s in own]
        + [pltpu.VMEM((fi_n + 1,) + s, BF16) for s in own]
        + [pltpu.VMEM(v.shape, BF16) for v in quarters]
        + [
            pltpu.VMEM((tp_n,) + sum_shape, BF16),
            pltpu.SemaphoreType.DMA((count, fi_n)),
            pltpu.SemaphoreType.DMA((count, fi_n, ctx_n)),
            pltpu.SemaphoreType.DMA((count, fi_n, ctx_n)),
            pltpu.SemaphoreType.DMA((count, 2, fi_n)),
            pltpu.SemaphoreType.DMA((count, 2, fi_n)),
            pltpu.SemaphoreType.DMA((count, tp_n)),
            pltpu.SemaphoreType.DMA((count, tp_n)),
            pltpu.SemaphoreType.DMA((some,)),
            *(tp_spread_sems(sizes) * extra),
        ],
        "run": functools.partial(finish_run, tuple(kinds)),
    }


def reduce_job(sizes, both, parts):
    ctx_n, tpx_n, tpc_n = (sizes[n] for n in ("ctx", "tpx", "tpc"))
    tp_n = tpx_n * tpc_n
    tokens, quarter = parts.shape[1:]
    wide = both.shape[1]
    piece = (ctx_n, tokens // tp_n, wide)
    return {
        "args": [(both.reshape(ctx_n, tokens, wide), HBM_SPEC), (parts, HBM_SPEC)],
        "outs": [
            (jax.ShapeDtypeStruct((tokens, wide), BF16), VMEM_SPEC),
            (jax.ShapeDtypeStruct((tokens, quarter), F32), VMEM_SPEC),
        ],
        "scratch": [
            pltpu.VMEM((3, tpx_n) + piece, BF16),
            pltpu.VMEM((3, tpx_n, tokens, quarter), BF16),
            pltpu.VMEM((ctx_n,) + piece[1:], BF16),
            pltpu.SemaphoreType.DMA((2, tpx_n)),
            pltpu.SemaphoreType.DMA((2, tpx_n)),
            pltpu.SemaphoreType.DMA((2, tpx_n)),
            pltpu.SemaphoreType.DMA((2, tpx_n)),
            pltpu.SemaphoreType.DMA((2, tpx_n)),
            pltpu.SemaphoreType.DMA((2, ctx_n)),
            pltpu.SemaphoreType.DMA((2, tp_n)),
        ],
        "run": reduce_run,
    }


def reduce_run(sizes, args, outs, scratch):
    ctx_n, tpx_n, tpc_n = (sizes[n] for n in ("ctx", "tpx", "tpc"))
    tp_n = tpx_n * tpc_n
    both_ref, parts_ref = args
    both_out, parts_out = outs
    both_buf, parts_buf, halves = scratch[:3]
    load_sem, core_send, core_recv, x_send, x_recv, y_sem, tp_sem = scratch[3:]
    rows = halves.shape[1]
    fo, z, y, x, c = (lax.axis_index(n) for n in ("fo", "fi", "ctx", "tpx", "tpc"))
    q = x * tpc_n + c
    bufs = (both_buf, parts_buf)

    def view(kind, side, core):
        to = side * tpc_n + core
        if kind == 0:
            return both_ref.at[:, pl.ds(pl.multiple_of(to * rows, rows), rows), :]
        return parts_ref.at[to]

    def load(kind, side):
        return pltpu.make_async_copy(
            view(kind, side, c), bufs[kind].at[0, side], load_sem.at[kind, side]
        )

    def to_core(kind, side):
        return pltpu.make_async_remote_copy(
            src_ref=view(kind, side, 1 - c),
            dst_ref=bufs[kind].at[1, side],
            send_sem=core_send.at[kind, side],
            recv_sem=core_recv.at[kind, side],
            device_id=(fo, z, y, x, 1 - c),
            device_id_type=MESH_ID,
        )

    def to_chip(kind, side, slot):
        return pltpu.make_async_remote_copy(
            src_ref=bufs[kind].at[0, side],
            dst_ref=bufs[kind].at[2, slot],
            send_sem=x_send.at[kind, side],
            recv_sem=x_recv.at[kind, slot],
            device_id=(fo, z, y, side, c),
            device_id_type=MESH_ID,
        )

    def side_of(dx):
        return lax.rem(x + dx, tpx_n)

    def add(kind, side):
        count = bufs[kind].shape[2] if kind == 1 else bufs[kind].shape[3]
        tile = math.gcd(count, 64)

        def one(step, carry):
            at = pl.ds(pl.multiple_of(step * tile, tile), tile)
            if kind == 1:
                mine, other = parts_buf[0, side, at, :], parts_buf[1, side, at, :]
                parts_buf[0, side, at, :] = (mine.astype(F32) + other.astype(F32)).astype(BF16)
            else:
                for half in range(ctx_n):
                    mine = both_buf[0, side, half, at, :]
                    other = both_buf[1, side, half, at, :]
                    both_buf[0, side, half, at, :] = (
                        mine.astype(F32) + other.astype(F32)
                    ).astype(BF16)
            return carry

        lax.fori_loop(0, count // tile, one, 0)

    order = list(range(1, tpx_n)) + [0]
    for kind in (0, 1):
        for dx in order:
            to_core(kind, side_of(dx)).start()
            load(kind, side_of(dx)).start()
    yield
    for kind in (0, 1):
        for dx in order:
            side = side_of(dx)
            load(kind, side).wait()
            to_core(kind, side).wait_recv()
            add(kind, side)
            if dx > 0:
                to_chip(kind, side, x).start()
    yield

    for dx in range(1, tpx_n):
        to_chip(0, side_of(dx), side_of(dx)).wait_recv()
    tile = math.gcd(rows, 64)

    def over_x(step, carry):
        at = pl.ds(pl.multiple_of(step * tile, tile), tile)
        for half in range(ctx_n):
            summed = both_buf[0, x, half, at, :].astype(F32)
            for dx in range(1, tpx_n):
                summed = summed + both_buf[2, side_of(dx), half, at, :].astype(F32)
            both_buf[0, x, half, at, :] = summed.astype(BF16)
        return carry

    lax.fori_loop(0, rows // tile, over_x, 0)

    def to_y(dy, half, slot):
        return pltpu.make_async_remote_copy(
            src_ref=both_buf.at[0, x, half],
            dst_ref=halves.at[slot],
            send_sem=y_sem.at[0, dy],
            recv_sem=y_sem.at[1, dy],
            device_id=(fo, z, half, x, c),
            device_id_type=MESH_ID,
        )

    for dy in range(1, ctx_n):
        to_y(dy, lax.rem(y + dy, ctx_n), y).start()
    yield
    for dy in range(1, ctx_n):
        source = lax.rem(y + ctx_n - dy, ctx_n)
        to_y(dy, y, source).wait_recv()

    def over_y(step, carry):
        at = pl.ds(pl.multiple_of(step * tile, tile), tile)
        summed = both_buf[0, x, y, at, :].astype(F32)
        for dy in range(1, ctx_n):
            summed = summed + halves[lax.rem(y + ctx_n - dy, ctx_n), at, :].astype(F32)
        both_out[pl.ds(pl.multiple_of(q * rows + step * tile, tile), tile), :] = summed.astype(BF16)
        return carry

    lax.fori_loop(0, rows // tile, over_y, 0)

    def to_tp(step, owner):
        peer = lax.rem(q + step, tp_n)
        held = both_out.at[pl.ds(pl.multiple_of(owner * rows, rows), rows), :]
        return pltpu.make_async_remote_copy(
            src_ref=both_out.at[pl.ds(pl.multiple_of(q * rows, rows), rows), :],
            dst_ref=held,
            send_sem=tp_sem.at[0, step],
            recv_sem=tp_sem.at[1, step],
            device_id=(fo, z, y, peer // tpc_n, lax.rem(peer, tpc_n)),
            device_id_type=MESH_ID,
        )

    for step in range(1, tp_n):
        to_tp(step, q).start()
    yield
    for dx in range(1, tpx_n):
        to_chip(1, side_of(dx), side_of(dx)).wait_recv()
    tall = math.gcd(parts_out.shape[0], 64)

    def last(step, carry):
        at = pl.ds(pl.multiple_of(step * tall, tall), tall)
        summed = parts_buf[0, x, at, :].astype(F32)
        for dx in range(1, tpx_n):
            summed = summed + parts_buf[2, side_of(dx), at, :].astype(F32)
        parts_out[at, :] = summed
        return carry

    lax.fori_loop(0, parts_out.shape[0] // tall, last, 0)
    for step in range(1, tp_n):
        to_tp(step, q).wait_send()
        to_tp(step, lax.rem(q + tp_n - step, tp_n)).wait_recv()
    for dy in range(1, ctx_n):
        to_y(dy, lax.rem(y + dy, ctx_n), y).wait_send()
    for kind in (0, 1):
        for dx in range(tpx_n):
            to_core(kind, side_of(dx)).wait_send()
            if dx > 0:
                to_chip(kind, side_of(dx), x).wait_send()


def attend_body(place_ref, q_ref, kv_ref, rope_ref, out_ref, log_ref):
    block_rows, key_count = q_ref.shape[0], kv_ref.shape[0]
    first = place_ref[0] + pl.program_id(1) * block_rows
    keys = jnp.concatenate([kv_ref[:, :NOPE], rope_ref[...]], axis=1)
    scores = dot_nt(q_ref[...], keys)
    row = first + lax.broadcasted_iota(jnp.int32, (block_rows, 1), 0)
    limit = jnp.maximum(row, place_ref[1] - 1)
    key = lax.broadcasted_iota(jnp.int32, (block_rows, key_count), 1)
    scores = jnp.where(key <= limit, scores, -1e30)
    top = jnp.max(scores, axis=1, keepdims=True)
    exponent = jnp.exp(scores - top)
    row_total = jnp.sum(exponent, axis=1, keepdims=True)
    summed = jnp.dot(exponent.astype(BF16), kv_ref[:, NOPE:], preferred_element_type=F32)
    out_ref[...] = (summed / row_total).astype(BF16)
    log_total = jnp.broadcast_to(top + jnp.log(row_total), (block_rows, 128))
    log_ref[0] = log_total.T[:1]

def attend(place, query, key_value, rope, block_rows):
    rows, key_count = query.shape[0], key_value.shape[0]
    heads = query.shape[1] // HEAD
    return pl.pallas_call(
        attend_body,
        out_shape=(jax.ShapeDtypeStruct((rows, heads * VDIM), BF16), jax.ShapeDtypeStruct((heads, 1, rows), F32)),
        grid_spec=pltpu.PrefetchScalarGridSpec(
            num_scalar_prefetch=1,
            grid=(heads, rows // block_rows),
            in_specs=[
                pl.BlockSpec((block_rows, HEAD), lambda h, i, s: (i, h)),
                pl.BlockSpec((key_count, HEAD), lambda h, i, s: (0, h)),
                pl.BlockSpec((key_count, NOPE), lambda h, i, s: (0, 0)),
            ],
            out_specs=[
                pl.BlockSpec((block_rows, VDIM), lambda h, i, s: (i, h)),
                pl.BlockSpec((1, 1, block_rows), lambda h, i, s: (h, 0, i)),
            ],
        ),
        compiler_params=pltpu.CompilerParams(vmem_limit_bytes=48 << 20),
        cost_estimate=pl.CostEstimate(flops=4 * rows * key_count * heads * HEAD, bytes_accessed=20_000_000, transcendentals=rows * key_count * heads),
        name="attend",
    )(place, query, key_value, rope)

def attend_back_body(place_ref, q_ref, kv_ref, rope_ref, dout_ref, log_ref, table_ref, dq_ref, dkv_ref, drope_ref, keys_acc, values_acc):
    block_rows, key_count = q_ref.shape[0], kv_ref.shape[0]
    head, step = pl.program_id(0), pl.program_id(1)
    first = place_ref[0] + step * block_rows
    keys = jnp.concatenate([kv_ref[:, :NOPE], rope_ref[...]], axis=1)
    scores = dot_nt(keys, q_ref[...])
    row = first + lax.broadcasted_iota(jnp.int32, (1, block_rows), 1)
    limit = jnp.maximum(row, place_ref[1] - 1)
    key = lax.broadcasted_iota(jnp.int32, (key_count, block_rows), 0)
    soft = jnp.exp(jnp.where(key <= limit, scores, -1e30) - log_ref[0])
    soft_grad = dot_nt(kv_ref[:, NOPE:], dout_ref[...])
    mean = jnp.sum(soft * soft_grad, axis=0, keepdims=True)
    score_grad = (soft * (soft_grad - mean)).astype(BF16)
    values = jnp.dot(soft.astype(BF16), dout_ref[...], preferred_element_type=F32)
    keys_grad = jnp.dot(score_grad, q_ref[...], preferred_element_type=F32)
    dq_ref[...] = (dot_tn(score_grad, keys) * table_ref[...]).astype(BF16)

    @pl.when(step == 0)
    def _():
        keys_acc[...] = keys_grad
        values_acc[...] = values

    @pl.when(step > 0)
    def _():
        keys_acc[...] += keys_grad
        values_acc[...] += values

    @pl.when(step == pl.num_programs(1) - 1)
    def _():
        dkv_ref[...] = jnp.concatenate([keys_acc[:, :NOPE], values_acc[...]], axis=1).astype(BF16)

        @pl.when(head == 0)
        def _():
            drope_ref[...] = keys_acc[:, NOPE:]

        @pl.when(head > 0)
        def _():
            drope_ref[...] += keys_acc[:, NOPE:]

def attend_back(place, query, key_value, rope, dout, log_total, table, block_rows):
    rows, key_count = query.shape[0], key_value.shape[0]
    heads = query.shape[1] // HEAD
    return pl.pallas_call(
        attend_back_body,
        out_shape=(jax.ShapeDtypeStruct((rows, heads * HEAD), BF16), jax.ShapeDtypeStruct((key_count, heads * HEAD), BF16), jax.ShapeDtypeStruct((key_count, NOPE), F32)),
        grid_spec=pltpu.PrefetchScalarGridSpec(
            num_scalar_prefetch=1,
            grid=(heads, rows // block_rows),
            in_specs=[
                pl.BlockSpec((block_rows, HEAD), lambda h, i, s: (i, h)),
                pl.BlockSpec((key_count, HEAD), lambda h, i, s: (0, h)),
                pl.BlockSpec((key_count, NOPE), lambda h, i, s: (0, 0)),
                pl.BlockSpec((block_rows, VDIM), lambda h, i, s: (i, h)),
                pl.BlockSpec((1, 1, block_rows), lambda h, i, s: (h, 0, i)),
                pl.BlockSpec((block_rows, HEAD), lambda h, i, s: (i, 0)),
            ],
            out_specs=[
                pl.BlockSpec((block_rows, HEAD), lambda h, i, s: (i, h)),
                pl.BlockSpec((key_count, HEAD), lambda h, i, s: (0, h)),
                pl.BlockSpec((key_count, NOPE), lambda h, i, s: (0, 0)),
            ],
            scratch_shapes=[pltpu.VMEM((key_count, HEAD), F32), pltpu.VMEM((key_count, VDIM), F32)],
        ),
        compiler_params=pltpu.CompilerParams(vmem_limit_bytes=56 << 20),
        cost_estimate=pl.CostEstimate(
            flops=10 * rows * key_count * heads * HEAD,
            bytes_accessed=40_000_000,
            transcendentals=rows * key_count * heads,
        ),
        name="attend_back",
    )(place, query, key_value, rope, dout, log_total, table)


def build(sizes):
    fo_n, fi_n, ctx_n, tpx_n, tpc_n = (sizes[name] for name in ("fo", "fi", "ctx", "tpx", "tpc"))
    tp_n = tpx_n * tpc_n
    row_shards = fo_n * fi_n * ctx_n
    plane_experts = ctx_n * tpx_n
    z_part = fi_n // tpc_n

    def expert_weights(gate, up, down):
        local = jnp.stack([gate.transpose(0, 2, 1), up.transpose(0, 2, 1), down], axis=1)
        return lax.all_gather(local, "fo", axis=0) if fo_n > 1 else local[None]

    def shard_of(weight):
        return lax.all_gather(weight, "fo", axis=0) if fo_n > 1 else weight[None]

    def fo_sum(part, kind):
        if fo_n == 1:
            return part
        if kind == "col":
            a = part.shape[0]
            part = part.reshape(a, fo_n, -1)
            return lax.psum_scatter(part, "fo", scatter_dimension=1, tiled=True).reshape(a, -1)
        return lax.psum_scatter(part, "fo", scatter_dimension=0, tiled=True)

    def own_expert_grads(mine):
        mine = mine.reshape((fo_n, -1) + mine.shape[1:])
        got = lax.all_to_all(mine, CHIPS, split_axis=1, concat_axis=1, tiled=True)
        if fo_n > 1:
            got = lax.psum_scatter(got, "fo", scatter_dimension=0, tiled=True)
        got = got[0].astype(F32)
        return (got[:, 0].transpose(0, 2, 1), got[:, 1].transpose(0, 2, 1), got[:, 2])

    def shards(
        tokens,
        out_grad,
        routes,
        slot_index,
        prefix,
        attn_gain,
        query_weight,
        latent_down,
        latent_gain,
        latent_up,
        out_weight,
        moe_gain,
        router_weight,
        shared_gate,
        shared_up,
        shared_down,
        expert_gate,
        expert_up,
        expert_down,
    ):
        row_count, width = tokens.shape
        expert_count = expert_gate.shape[0]
        capacity = row_count * routes.shape[1] // expert_count
        quarter = width // tp_n
        tp_index = lax.axis_index(TP)
        own_expert = lax.axis_index(CHIPS)
        plane_base = lax.axis_index("fi") * plane_experts

        def columns(values):
            return lax.dynamic_slice_in_dim(values, tp_index * quarter, quarter, values.ndim - 1)

        depth = latent_down.shape[0]
        down_width = latent_down.shape[1]

        def turned(weight):
            half = weight.shape[-1] // 2
            return jnp.concatenate([-weight[..., half:], weight[..., :half]], axis=-1)

        small = jnp.concatenate(
            [
                latent_down,
                turned(latent_down[:, KVR:]),
                attn_gain[:, None],
                moe_gain[:, None],
                jnp.pad(latent_gain, (0, depth - latent_gain.shape[0]))[:, None],
                router_weight,
            ],
            axis=1,
        )
        used = small.shape[1]
        small = jnp.pad(small, ((0, 0), (0, -used % 128)))
        keys = jnp.where(slot_index < capacity, routes * capacity + slot_index, -1).T
        keys = jnp.pad(keys, ((0, 8 - keys.shape[0]), (0, 0)), constant_values=-1)
        (small, query_full, up_full, out_full, keys_all), *_ = exchange(
            sizes,
            [
                collect_job(
                    sizes,
                    ("share", "row", "row", "col", "row"),
                    [shard_of(w) for w in (small, query_weight, latent_up, out_weight, keys)],
                )
            ],
            4,
            "collect_attention",
        )
        local_weights, small = lax.optimization_barrier(
            (expert_weights(expert_gate, expert_up, expert_down), small)
        )
        routed_weights = lax.all_to_all(
            local_weights, CHIPS, split_axis=1, concat_axis=1, tiled=True
        )
        wide_down = small[:, : down_width + ROPE]
        down_full = small[:, :down_width]
        gain_at = down_width + ROPE
        gain_one = small[:, gain_at].astype(F32)
        gain_two = small[:, gain_at + 1].astype(F32)
        gain_latent = (
            small[:, gain_at + 2]
            .reshape(row_shards, depth)[:, : latent_gain.shape[0]]
            .reshape(-1)
            .astype(F32)
        )
        router_full = small[:, gain_at + 3 : used]

        keys_all = lax.dynamic_slice_in_dim(
            keys_all, lax.axis_index("fo") * (fi_n * ctx_n * 8), fi_n * ctx_n * 8, 0
        ).reshape(fi_n, ctx_n, 8, row_count)
        keys_column = lax.dynamic_index_in_dim(keys_all, lax.axis_index("ctx"), 1, keepdims=False)
        first_keys = (plane_base + jnp.arange(plane_experts, dtype=jnp.int32)) * capacity
        rel = keys_column[:, None] - first_keys[:, None, None]
        plane_slots = jnp.max(jnp.where((rel >= 0) & (rel < capacity), rel, -1), axis=2)
        token_slots = plane_slots.transpose(0, 2, 1)

        def give_back(rows, gates, bases=None):
            rows = rows.reshape(z_part, ctx_n, capacity, width)
            return give_back_job(sizes, rows, token_slots, gates, bases)

        (slot_grads,), (shared_gate_full, shared_up_full, shared_down_full) = exchange(
            sizes,
            [
                dispatch_job(sizes, columns(out_grad), plane_slots, capacity),
                collect_job(
                    sizes,
                    ("row", "row", "col"),
                    [shard_of(w) for w in (shared_gate, shared_up, shared_down)],
                ),
            ],
            0,
            "dispatch_grads",
        )
        slot_grads = slot_grads.reshape(-1, width)

        head_count = query_full.shape[1] // (NOPE + ROPE)
        hidden = tokens.astype(F32)
        scale_one = rms_scale(hidden)
        normed_one = hidden * scale_one
        normed_in = (normed_one * gain_one).astype(BF16)
        seq_index = lax.axis_index(("fo", "fi"))
        prefix_len = lax.dynamic_index_in_dim(prefix, seq_index, keepdims=False)
        row_offset = lax.axis_index("ctx") * row_count
        query_pos = row_offset + jnp.arange(row_count, dtype=jnp.int32)
        cos_table, sin_table = rotation_tables(query_pos, ROPE // 2)
        score_scale = (NOPE + ROPE) ** (-0.5)
        cos_wide = jnp.concatenate([cos_table, cos_table], axis=1)
        sin_wide = jnp.concatenate([sin_table, sin_table], axis=1)
        table = score_scale * jnp.concatenate(
            [jnp.ones((row_count, NOPE), F32), cos_wide, sin_wide], axis=1
        )

        latent_raw = dot(normed_in, wide_down)
        latent_part = latent_raw[:, :KVR]
        scale_latent = rms_scale(latent_part)
        normed_latent = latent_part * scale_latent
        latent = (normed_latent * gain_latent).astype(BF16)
        key_rope = (
            latent_raw[:, KVR : KVR + ROPE] * cos_wide + latent_raw[:, KVR + ROPE :] * sin_wide
        ).astype(BF16)
        both = lax.all_gather(
            jnp.concatenate([latent, key_rope, key_rope], axis=1), "ctx", axis=0, tiled=True
        )
        latent_all, rope_all = both[:, :KVR], both[:, KVR:]
        query_heads = query_full.reshape(width, head_count, NOPE + ROPE)
        query_wide = jnp.concatenate(
            [query_heads, turned(query_heads[..., NOPE:])], axis=-1
        ).reshape(width, head_count * HEAD)
        query_in = (
            dot(normed_in, query_wide).reshape(row_count, head_count, HEAD) * table[:, None]
        ).astype(BF16).reshape(row_count, head_count * HEAD)
        key_value = dot(latent_all, up_full).astype(BF16)
        place = jnp.stack([row_offset, prefix_len]).astype(jnp.int32)
        block_rows = min(256, row_count)
        attended, log_totals = attend(place, query_in, key_value, rope_all, block_rows)

        def tp_scatter(parts):
            parts = jnp.stack([part.astype(BF16) for part in parts])
            return lax.psum_scatter(parts, TP, scatter_dimension=0, tiled=True)[0].astype(F32)

        def quarters(weight, axis):
            return jnp.split(weight, tp_n, axis=axis)

        def tp_gather(part_rows):
            got = lax.all_gather(part_rows, TP, axis=0)
            return got.transpose(1, 0, 2).reshape(row_count, width)

        attn_out = tp_scatter([dot(attended, part) for part in quarters(out_full, 1)])
        attn_out, slot_grads = lax.optimization_barrier((attn_out, slot_grads))
        residual = columns(tokens).astype(F32) + attn_out
        scale_two = lax.rsqrt(
            lax.psum(jnp.sum(residual * residual, axis=-1, keepdims=True), TP) / width + EPSILON
        )
        normed_two = residual * scale_two
        gain_two_part = columns(gain_two[None])
        mid_part = (normed_two * gain_two_part).astype(BF16)

        (slot_rows,), (gate_full, expert_up_full, down_weight) = exchange(
            sizes,
            [
                dispatch_job(sizes, mid_part, plane_slots, capacity),
                place_job(sizes, routed_weights),
            ],
            1,
            "dispatch_rows",
        )
        slot_rows = slot_rows.reshape(-1, width)
        normed_mid, slot_rows = lax.optimization_barrier((tp_gather(mid_part), slot_rows))

        logits = dot(normed_mid, router_full)
        router_prob = jax.nn.softmax(logits, axis=-1)
        slot_prob = jax.nn.softmax(dot(slot_rows, router_full), axis=-1)
        slot_gate = lax.dynamic_slice_in_dim(slot_prob, own_expert, 1, 1)

        gate_pre = dot(normed_mid, shared_gate_full)
        up_pre = dot(normed_mid, shared_up_full)
        shared_dact = dot_nt(out_grad, shared_down_full)
        shared_silu, shared_slope = silu_parts(gate_pre)
        shared_act = (shared_silu * up_pre).astype(BF16)
        shared_dgate = (shared_dact * up_pre * shared_slope).astype(BF16)
        shared_dup = (shared_dact * shared_silu).astype(BF16)
        mid_shared = tp_scatter(
            [
                dot_nt(shared_dgate, gate_part) + dot_nt(shared_dup, up_part)
                for gate_part, up_part in zip(
                    quarters(shared_gate_full, 0), quarters(shared_up_full, 0)
                )
            ]
        )
        out_shared = tp_scatter([dot(shared_act, part) for part in quarters(shared_down_full, 1)])

        expert_dact_raw = dot_nt(slot_grads, down_weight)
        expert_gpre = dot_nt(slot_rows, gate_full)
        expert_upre = dot_nt(slot_rows, expert_up_full)
        expert_silu, expert_slope = silu_parts(expert_gpre)
        expert_act_wide = expert_silu * expert_upre
        expert_act = expert_act_wide.astype(BF16)
        slot_gate_grad = jnp.sum(expert_act.astype(F32) * expert_dact_raw, axis=-1)
        expert_dact = expert_dact_raw * slot_gate
        expert_dgate = (expert_dact * expert_upre * expert_slope).astype(BF16)
        expert_dup = (expert_dact * expert_silu).astype(BF16)
        slot_drows = dot(expert_dgate, gate_full) + dot(expert_dup, expert_up_full)
        gate_rows = jnp.broadcast_to(
            slot_gate_grad.reshape(z_part, ctx_n, 1, capacity), (z_part, ctx_n, 8, capacity)
        )
        sdown_grad = dot_tn(shared_act, out_grad)
        sgate_grad = dot_tn(normed_mid, shared_dgate)
        sup_grad = dot_tn(normed_mid, shared_dup)
        shared_kinds = ("row", "row", "col")
        shared_parts = [
            fo_sum(part.astype(BF16), kind)
            for part, kind in zip((sgate_grad, sup_grad, sdown_grad), shared_kinds)
        ]
        shared_own, (mid_routed, prob_grad) = exchange(
            sizes,
            [
                finish_job(sizes, shared_kinds, shared_parts, []),
                give_back(slot_drows.astype(BF16), gate_rows),
            ],
            2,
            "give_back_rows",
        )
        sgate_grad, sup_grad, sdown_grad = (part.astype(F32) for part in shared_own)
        prob_grad = prob_grad.T
        logit_grad = (
            router_prob * (prob_grad - jnp.sum(router_prob * prob_grad, axis=-1, keepdims=True))
        ).astype(BF16)

        slot_dout = (slot_grads.astype(F32) * slot_gate).astype(BF16)
        routed_grads = pair_sum(
            sizes,
            [
                dot_tn(expert_dgate, slot_rows).astype(BF16),
                dot_tn(expert_dup, slot_rows).astype(BF16),
                dot_tn(expert_act, slot_dout).astype(BF16),
            ],
            7,
        )
        mid_routed, mid_shared, out_shared = lax.optimization_barrier(
            (mid_routed, mid_shared, out_shared)
        )
        mid_total = mid_shared + mid_routed + dot_nt(logit_grad, columns(router_full.T).T)
        gain_two_grad = jnp.sum(mid_total * normed_two, axis=0)
        dn_two = mid_total * gain_two_part
        dot_two = lax.psum(jnp.sum(dn_two * normed_two, axis=-1, keepdims=True), TP) / width
        residual_grad = columns(out_grad).astype(F32) + scale_two * (dn_two - normed_two * dot_two)
        attn_dout = tp_gather(residual_grad.astype(BF16))

        out_weight_grad = dot_tn(attended, attn_dout)
        attended_grad = dot_nt(attn_dout, out_full).astype(BF16)
        attended_grad, routed_grads = lax.optimization_barrier((attended_grad, routed_grads))
        egate_grad, eup_grad, edown_grad = own_expert_grads(routed_grads)
        query_grad, kv_grad, rope_grad = attend_back(
            place, query_in, key_value, rope_all, attended_grad, log_totals, table,
            min(512, row_count),
        )
        late_act, query_grad = lax.optimization_barrier((expert_act, query_grad))
        expert_out = (dot(late_act, down_weight) * slot_gate).astype(BF16)
        up_grad = dot_tn(latent_all, kv_grad)
        latent_grad = dot_nt(kv_grad, up_full)
        query_wide_grad = dot_tn(normed_in, query_grad).reshape(width, head_count, HEAD)
        query_weight_grad = jnp.concatenate(
            [
                query_wide_grad[..., :NOPE],
                query_wide_grad[..., NOPE : NOPE + ROPE] - turned(query_wide_grad[..., NOPE + ROPE :]),
            ],
            axis=-1,
        ).reshape(width, head_count * (NOPE + ROPE))
        input_parts = jnp.stack(
            [dot_nt(query_grad, part).astype(BF16) for part in quarters(query_wide, 0)]
        )
        ((both_grad, input_part),) = exchange(
            sizes,
            [
                reduce_job(
                    sizes,
                    jnp.concatenate([latent_grad, rope_grad], axis=1).astype(BF16),
                    input_parts,
                )
            ],
            6,
            "sum_inputs",
        )
        both_grad = both_grad.astype(F32)
        latent_own = both_grad[:, :KVR]
        rope_own = both_grad[:, KVR : KVR + ROPE] + both_grad[:, KVR + ROPE :]
        gain_latent_grad = jnp.sum(latent_own * normed_latent, axis=0)
        latent_raw_grad = norm_back(latent_own * gain_latent, normed_latent, scale_latent)
        down_out_grad = jnp.concatenate(
            [latent_raw_grad, rotate(rope_own, cos_table, -sin_table)], axis=-1
        ).astype(BF16)
        down_grad = dot_tn(normed_in, down_out_grad)
        input_total = input_part + dot_nt(
            down_out_grad, lax.dynamic_slice_in_dim(down_full, tp_index * quarter, quarter, 0)
        )
        normed_one_part = columns(normed_one)
        gain_one_grad = jnp.sum(input_total * normed_one_part, axis=0)
        dn_one = input_total * columns(gain_one[None])
        dot_one = lax.psum(jnp.sum(dn_one * normed_one_part, axis=-1, keepdims=True), TP) / width
        token_grad = residual_grad + scale_one * (dn_one - normed_one_part * dot_one)
        token_grad, egate_grad, eup_grad, edown_grad = lax.optimization_barrier(
            (token_grad, egate_grad, eup_grad, edown_grad)
        )
        router_grad = dot_tn(normed_mid, logit_grad)
        pack_grad = jnp.concatenate([down_grad, router_grad], axis=1)
        pack_used = pack_grad.shape[1]
        pack_grad = jnp.pad(pack_grad, ((0, 0), (0, -pack_used % 128)))
        gains = jnp.stack([gain_one_grad, gain_two_grad])
        gains = lax.dynamic_update_slice_in_dim(
            jnp.zeros((2, width), F32), gains, tp_index * quarter, 1
        )
        latent_rows = jnp.pad(
            gain_latent_grad.reshape(row_shards, -1),
            ((0, 0), (0, depth - latent_gain.shape[0])),
        ).reshape(1, width)
        gains = jnp.concatenate([gains, latent_rows * (tp_index == 0).astype(F32)], axis=0)
        gains = jnp.pad(
            gains.reshape(3, row_shards, depth).transpose(1, 0, 2), ((0, 0), (0, 13), (0, 0))
        ).reshape(row_shards * 16, depth)
        kinds = ("share", "sum", "row", "row", "col")
        partials = (pack_grad, gains, query_weight_grad, up_grad, out_weight_grad)
        done, (output,) = exchange(
            sizes,
            [
                finish_job(
                    sizes,
                    kinds,
                    [fo_sum(part.astype(BF16), kind) for part, kind in zip(partials, kinds)],
                    [token_grad.astype(BF16)],
                ),
                give_back(expert_out, None, (residual, out_shared)),
            ],
            3,
            "finish_attention",
        )
        pack_own = done[0].reshape(depth, -1).astype(F32)
        gains_own = done[1].astype(F32)
        query_weight_grad, up_grad, out_weight_grad = (part.astype(F32) for part in done[2:5])
        token_grad = done[5].astype(F32)
        return (
            output,
            token_grad,
            gains_own[0],
            query_weight_grad,
            pack_own[:, :down_width],
            gains_own[2, : latent_gain.shape[0]],
            up_grad,
            out_weight_grad,
            gains_own[1],
            pack_own[:, down_width:pack_used],
            sgate_grad,
            sup_grad,
            sdown_grad,
            egate_grad,
            eup_grad,
            edown_grad,
        )

    return shards


EXPERTS = 16


def solution(mesh):
    ctx_n, tp_n = mesh.shape["ctx"], mesh.shape["tp"]
    tpc_n = 2
    tpx_n = tp_n // tpc_n
    fi_n = EXPERTS // (ctx_n * tpx_n)
    sizes = {
        "fo": mesh.shape["fsdp"] // fi_n,
        "fi": fi_n,
        "ctx": ctx_n,
        "tpx": tpx_n,
        "tpc": tpc_n,
    }
    fine = Mesh(mesh.devices.reshape(tuple(sizes.values())), tuple(sizes))
    rows = P(ROWS)
    rows_two = P(ROWS, None)
    rows_tp = P(ROWS, TP)
    tp_rows = P(TP, ROWS)
    wide_in = P(None, ROWS, TP)
    wide_out = P(None, TP, ROWS)
    weights = (
        rows,
        rows_tp,
        rows_two,
        rows,
        rows_tp,
        tp_rows,
        rows,
        rows_two,
        rows_tp,
        rows_tp,
        tp_rows,
        wide_in,
        wide_in,
        wide_out,
    )
    return jax.shard_map(
        build(sizes),
        mesh=fine,
        in_specs=(rows_two, rows_two, rows_two, rows_two, P()) + weights,
        out_specs=(rows_two, rows_two) + weights,
        check_vma=False,
    )
```

```python
import functools
import math

import jax
import jax.numpy as jnp
from jax import lax
from jax.experimental import pallas as pl
from jax.experimental.pallas import tpu as pltpu
from jax.sharding import Mesh
from jax.sharding import PartitionSpec as P

NOPE = 128
ROPE = 64
KVR = 512
VDIM = 128
HEAD = 256

EPSILON = 1e-06
THETA_BASE = 10000.0
F32 = jnp.float32
BF16 = jnp.bfloat16
MESH_ID = pl.DeviceIdType.MESH

ROWS = ("fo", "fi", "ctx")
TP = ("tpx", "tpc")
PLANE = ("ctx", "tpx", "tpc")
CHIPS = ("fi", "ctx", "tpx")


def rotation_tables(positions, half_width):
    freq_table = jnp.exp(jnp.arange(half_width, dtype=F32) * (-math.log(THETA_BASE) / half_width))
    angle_table = positions.astype(F32)[:, None] * freq_table[None, :]
    return (jnp.cos(angle_table), jnp.sin(angle_table))


def rotate(values, cos_table, sin_table):
    half_width = values.shape[-1] // 2
    first_half = values[..., :half_width]
    second_half = values[..., half_width:]
    return jnp.concatenate(
        [
            first_half * cos_table - second_half * sin_table,
            second_half * cos_table + first_half * sin_table,
        ],
        axis=-1,
    )


def silu_parts(values):
    sigma = jax.nn.sigmoid(values)
    return (values * sigma, sigma * (1.0 + values * (1.0 - sigma)))


def rms_scale(values):
    return lax.rsqrt(jnp.mean(values * values, axis=-1, keepdims=True) + EPSILON)


def norm_back(grad_normed, normed, scale_rows):
    return scale_rows * (
        grad_normed - normed * jnp.mean(grad_normed * normed, axis=-1, keepdims=True)
    )


def dot(left, right):
    return jnp.dot(left, right, preferred_element_type=F32)


def dot_nt(left, right):
    return lax.dot_general(left, right, (((1,), (1,)), ((), ())), preferred_element_type=F32)


def dot_tn(left, right):
    return lax.dot_general(left, right, (((0,), (0,)), ((), ())), preferred_element_type=F32)


def ein(spec, left, right):
    return jnp.einsum(spec, left, right, preferred_element_type=F32)


def plane_place(sizes):
    tpx_n, tpc_n = sizes["tpx"], sizes["tpc"]
    fo, z, y, x, c = (lax.axis_index(name) for name in ("fo", "fi", "ctx", "tpx", "tpc"))
    own = (y * tpx_n + x) * tpc_n + c

    def device(index, z_at=None):
        return (
            fo,
            z if z_at is None else z_at,
            index // (tpx_n * tpc_n),
            lax.rem(index // tpc_n, tpx_n),
            lax.rem(index, tpc_n),
        )

    return z, y, x, c, own, device


def greet_plane(sizes):
    fi_n = sizes["fi"]
    plane_n = sizes["ctx"] * sizes["tpx"] * sizes["tpc"]
    z, y, x, c, own, device = plane_place(sizes)
    barrier = pltpu.get_barrier_semaphore()
    for step in range(1, plane_n):
        pl.semaphore_signal(
            barrier,
            inc=1,
            device_id=device(lax.rem(own + step, plane_n)),
            device_id_type=MESH_ID,
        )
    for near in (-1, 1):

        @pl.when((z + near >= 0) & (z + near < fi_n))
        def _():
            pl.semaphore_signal(
                barrier, inc=1, device_id=device(own, z + near), device_id_type=MESH_ID
            )

    sides = (z > 0).astype(jnp.int32) + (z < fi_n - 1).astype(jnp.int32)
    pl.semaphore_wait(barrier, plane_n - 1 + sides)


HBM_SPEC = pl.BlockSpec(memory_space=pl.ANY)
VMEM_SPEC = pl.BlockSpec(memory_space=pltpu.VMEM)


def exchange(sizes, jobs, collective_id, name, vmem=56):
    counts = [(len(job["args"]), len(job["outs"]), len(job["scratch"])) for job in jobs]

    def body(*refs):
        at = [0, sum(n[0] for n in counts), sum(n[0] + n[1] for n in counts)]
        running = []
        for job, count in zip(jobs, counts):
            given = [refs[at[k] : at[k] + count[k]] for k in range(3)]
            at = [at[k] + count[k] for k in range(3)]
            running.append(job["run"](sizes, *given))
        greet_plane(sizes)
        while running:
            running = [run for run in running if next(run, "ended") != "ended"]

    results = pl.pallas_call(
        body,
        out_shape=tuple(shape for job in jobs for shape, _ in job["outs"]),
        in_specs=[spec for job in jobs for _, spec in job["args"]],
        out_specs=tuple(spec for job in jobs for _, spec in job["outs"]),
        scratch_shapes=[shape for job in jobs for shape in job["scratch"]],
        compiler_params=pltpu.CompilerParams(
            collective_id=collective_id, has_side_effects=True, vmem_limit_bytes=vmem << 20
        ),
        cost_estimate=pl.CostEstimate(
            flops=0, bytes_accessed=20_000_000, transcendentals=0
        ),
        name=name,
    )(*[arg for job in jobs for arg, _ in job["args"]])
    grouped, at = [], 0
    for _, count, _ in counts:
        grouped.append(results[at : at + count])
        at += count
    return grouped


def columns_of(whole, wide):
    def slab(owner):
        return whole.at[:, pl.ds(pl.multiple_of(owner * wide, wide), wide)]

    return slab


def tp_spread(sizes, source, held, slab_of, sems):
    tpx_n, tpc_n = sizes["tpx"], sizes["tpc"]
    keep_sem, x_send, x_recv, c_send, c_recv = sems
    fo, z, y, x, c = (lax.axis_index(n) for n in ("fo", "fi", "ctx", "tpx", "tpc"))

    def slab(side, core):
        return slab_of(side * tpc_n + core)

    def origin(dx):
        return lax.rem(x + tpx_n - dx, tpx_n)

    keep = None if held is None else pltpu.make_async_copy(held, slab(x, c), keep_sem)

    def to_chip(dx, side):
        return pltpu.make_async_remote_copy(
            src_ref=source,
            dst_ref=slab(side, c),
            send_sem=x_send.at[dx],
            recv_sem=x_recv.at[dx],
            device_id=(fo, z, y, lax.rem(x + dx, tpx_n), c),
            device_id_type=MESH_ID,
        )

    def to_core(dx, dc, core):
        return pltpu.make_async_remote_copy(
            src_ref=source if dx == 0 else slab(origin(dx), c),
            dst_ref=slab(origin(dx), core),
            send_sem=c_send.at[dx, dc],
            recv_sem=c_recv.at[dx, dc],
            device_id=(fo, z, y, x, lax.rem(c + dc, tpc_n)),
            device_id_type=MESH_ID,
        )

    def start():
        for dx in range(1, tpx_n):
            to_chip(dx, x).start()
        for dc in range(1, tpc_n):
            to_core(0, dc, c).start()

    def relay():
        for dx in range(1, tpx_n):
            to_chip(dx, origin(dx)).wait_recv()
            for dc in range(1, tpc_n):
                to_core(dx, dc, c).start()

    def settle():
        if keep is not None:
            keep.wait()
        for dx in range(tpx_n):
            if dx > 0:
                to_chip(dx, x).wait_send()
            for dc in range(1, tpc_n):
                to_core(dx, dc, c).wait_send()
                to_core(dx, dc, lax.rem(c + tpc_n - dc, tpc_n)).wait_recv()

    return start, keep, relay, settle


def tp_spread_sems(sizes):
    tpx_n, tpc_n = sizes["tpx"], sizes["tpc"]
    return [
        pltpu.SemaphoreType.DMA,
        pltpu.SemaphoreType.DMA((tpx_n,)),
        pltpu.SemaphoreType.DMA((tpx_n,)),
        pltpu.SemaphoreType.DMA((tpx_n, tpc_n)),
        pltpu.SemaphoreType.DMA((tpx_n, tpc_n)),
    ]


def spread_job(sizes, part):
    tp_n = sizes["tpx"] * sizes["tpc"]
    shape = (part.shape[0], part.shape[1] * tp_n)
    return {
        "args": [(part, HBM_SPEC)],
        "outs": [(jax.ShapeDtypeStruct(shape, BF16), HBM_SPEC)],
        "scratch": [pltpu.VMEM(part.shape, BF16), pltpu.SemaphoreType.DMA]
        + tp_spread_sems(sizes),
        "run": spread_run,
    }


def spread_run(sizes, args, outs, scratch):
    held, load_sem = scratch[:2]
    start, keep, relay, settle = tp_spread(
        sizes, args[0], held, columns_of(outs[0], held.shape[1]), scratch[2:]
    )
    load = pltpu.make_async_copy(args[0], held, load_sem)
    load.start()
    start()
    yield
    load.wait()
    keep.start()
    relay()
    yield
    settle()


def dispatch_job(sizes, part_rows, plane_slots, capacity):
    tokens, quarter = part_rows.shape
    fi_n, ctx_n, tpx_n, tpc_n = (sizes[n] for n in ("fi", "ctx", "tpx", "tpc"))
    z_part, plane_n, chips = fi_n // tpc_n, ctx_n * tpx_n * tpc_n, ctx_n * tpx_n
    shape = (z_part, ctx_n, capacity, quarter * tpx_n * tpc_n)
    return {
        "args": [(plane_slots, VMEM_SPEC), (part_rows, HBM_SPEC)],
        "outs": [(jax.ShapeDtypeStruct(shape, BF16), HBM_SPEC)],
        "scratch": [
            pltpu.VMEM((fi_n, tokens, quarter), BF16),
            pltpu.VMEM((fi_n, chips, capacity, quarter), BF16),
            pltpu.SemaphoreType.DMA,
            pltpu.SemaphoreType.DMA((2, fi_n)),
            pltpu.SemaphoreType.DMA((2, fi_n)),
            pltpu.SemaphoreType.DMA((fi_n, chips)),
            pltpu.SemaphoreType.DMA((plane_n, z_part)),
        ],
        "run": dispatch_run,
    }


def dispatch_run(sizes, args, outs, scratch):
    slots_ref, rows_ref = args
    (out_ref,) = outs
    held, picked, own_sem, line_send, line_recv, plane_send, plane_recv = scratch
    fi_n, tpx_n, tpc_n = sizes["fi"], sizes["tpx"], sizes["tpc"]
    plane_n = sizes["ctx"] * tpx_n * tpc_n
    chips = sizes["ctx"] * tpx_n
    z_part = fi_n // tpc_n
    capacity, quarter = picked.shape[2:]
    tokens = held.shape[1]
    z, y, x, c, own, device = plane_place(sizes)
    columns = pl.ds(pl.multiple_of((x * tpc_n + c) * quarter, quarter), quarter)
    load = pltpu.make_async_copy(rows_ref, held.at[z], own_sem)

    def line(side, step):
        block = z - step if side == 0 else z + step
        to = z + 1 if side == 0 else z - 1
        return pltpu.make_async_remote_copy(
            src_ref=held.at[block],
            dst_ref=held.at[block],
            send_sem=line_send.at[side, step],
            recv_sem=line_recv.at[side, step],
            device_id=device(own, to),
            device_id_type=MESH_ID,
        )

    def sends(side, step):
        block = z - step if side == 0 else z + step
        to = z + 1 if side == 0 else z - 1
        return (block >= 0) & (block < fi_n) & (to >= 0) & (to < fi_n)

    def plane_copy(block, chip):
        at = lax.rem(block, z_part)
        return pltpu.make_async_remote_copy(
            src_ref=picked.at[block, chip],
            dst_ref=out_ref.at[at, y, :, columns],
            send_sem=plane_send.at[block, chip],
            recv_sem=plane_recv.at[own, at],
            device_id=device(chip * tpc_n + block // z_part),
            device_id_type=MESH_ID,
        )

    def keep_copy(block, chip):
        return pltpu.make_async_copy(
            picked.at[block, chip],
            out_ref.at[lax.rem(block, z_part), y, :, columns],
            plane_send.at[block, chip],
        )

    def at_home(block, chip):
        return chip * tpc_n + block // z_part == own

    def pick(block):
        def one(chip, carry):
            wanted = slots_ref[block, pl.ds(chip, 1), :]
            rank = lax.broadcasted_iota(jnp.int32, (capacity, tokens), 0)
            hits = jnp.where(rank == wanted, 1.0, 0.0).astype(BF16)
            picked[block, chip] = jnp.dot(
                hits, held[block], preferred_element_type=F32
            ).astype(BF16)

            @pl.when(at_home(block, chip))
            def _():
                keep_copy(block, chip).start()

            @pl.when(jnp.logical_not(at_home(block, chip)))
            def _():
                plane_copy(block, chip).start()

            return carry

        lax.fori_loop(0, chips, one, 0)

    load.start()
    load.wait()
    for side in (0, 1):

        @pl.when(sends(side, 0))
        def _():
            line(side, 0).start()

    yield
    pick(z)
    for step in range(fi_n - 1):
        for side in (0, 1):
            block = z - 1 - step if side == 0 else z + 1 + step

            @pl.when((block >= 0) & (block < fi_n))
            def _():
                pltpu.make_async_remote_copy(
                    src_ref=held.at[block],
                    dst_ref=held.at[block],
                    send_sem=line_send.at[side, step],
                    recv_sem=line_recv.at[side, step],
                    device_id=device(own, z),
                    device_id_type=MESH_ID,
                ).wait_recv()

            if step < fi_n - 2:

                @pl.when(sends(side, step + 1))
                def _():
                    line(side, step + 1).start()

        for side in (0, 1):
            block = z - 1 - step if side == 0 else z + 1 + step

            @pl.when((block >= 0) & (block < fi_n))
            def _():
                pick(block)

        yield

    for step in range(fi_n - 1):
        for side in (0, 1):

            @pl.when(sends(side, step))
            def _():
                line(side, step).wait_send()

    def settle(index, carry):
        block, chip = index // chips, lax.rem(index, chips)

        @pl.when(at_home(block, chip))
        def _():
            keep_copy(block, chip).wait()

        @pl.when(jnp.logical_not(at_home(block, chip)))
        def _():
            plane_copy(block, chip).wait_send()

        return carry

    lax.fori_loop(0, fi_n * chips, settle, 0)

    def arrive(index, carry):
        source, at = index // z_part, lax.rem(index, z_part)

        @pl.when(source != own)
        def _():
            pltpu.make_async_remote_copy(
                src_ref=picked.at[0, 0],
                dst_ref=out_ref.at[at, y, :, columns],
                send_sem=plane_send.at[0, 0],
                recv_sem=plane_recv.at[source, at],
                device_id=device(own),
                device_id_type=MESH_ID,
            ).wait_recv()

        return carry

    lax.fori_loop(0, plane_n * z_part, arrive, 0)


def give_back_run(sizes, args, outs, scratch):
    fi_n, tpx_n, tpc_n = sizes["fi"], sizes["tpx"], sizes["tpc"]
    plane_n = sizes["ctx"] * tpx_n * tpc_n
    chips = sizes["ctx"] * tpx_n
    z_part = fi_n // tpc_n
    ends, gated = len(args) > 3, len(args) == 3
    slots_ref, rows_ref = args[:2]
    out_ref = outs[0]
    got, total, going, coming, plane_send, plane_recv, line_send, line_recv = scratch[:8]
    if gated:
        gates_ref, gate_out = args[2], outs[1]
        gates_got, gate_total, gate_going, gate_coming = scratch[8:12]
        gate_send, gate_recv, gate_line_send, gate_line_recv = scratch[12:]
    if ends:
        held = scratch[8]
        start, keep, relay, spread_settle = tp_spread(
            sizes, held, held, columns_of(out_ref, held.shape[1]), scratch[9:]
        )
    capacity, quarter = got.shape[2:]
    tokens = total.shape[0]
    z, y, x, c, own, device = plane_place(sizes)
    tile = min(256, tokens)

    def piece(target, at):
        side = lax.rem(target, tpx_n * tpc_n)
        return rows_ref.at[
            at,
            target // (tpx_n * tpc_n),
            :,
            pl.ds(pl.multiple_of(side * quarter, quarter), quarter),
        ]

    def plane_copies(target, at):
        made = [
            pltpu.make_async_remote_copy(
                src_ref=piece(target, at),
                dst_ref=got.at[c * z_part + at, own // tpc_n],
                send_sem=plane_send.at[target, at],
                recv_sem=plane_recv.at[own, at],
                device_id=device(target),
                device_id_type=MESH_ID,
            )
        ]
        if gated:
            made.append(
                pltpu.make_async_remote_copy(
                    src_ref=gates_ref.at[at, target // (tpx_n * tpc_n)],
                    dst_ref=gates_got.at[c * z_part + at, own // tpc_n],
                    send_sem=gate_send.at[target, at],
                    recv_sem=gate_recv.at[own, at],
                    device_id=device(target),
                    device_id_type=MESH_ID,
                )
            )
        return made

    def keep_copies(at):
        made = [
            pltpu.make_async_copy(
                piece(own, at), got.at[c * z_part + at, own // tpc_n], plane_recv.at[own, at]
            )
        ]
        if gated:
            made.append(
                pltpu.make_async_copy(
                    gates_ref.at[at, y],
                    gates_got.at[c * z_part + at, own // tpc_n],
                    gate_recv.at[own, at],
                )
            )
        return made

    high_first = z < fi_n // 2
    early = c == jnp.where(high_first, tpc_n - 1, 0)

    def at_turn(turn):
        far = jnp.where(high_first, z_part - 1 - turn, turn)
        return jnp.where(early, far, lax.rem(z + 1 + turn, z_part))

    def send_turn(turn):
        at = at_turn(turn)

        def one(step, carry):
            for copy in plane_copies(lax.rem(own + step, plane_n), at):
                copy.start()
            return carry

        for copy in keep_copies(at):
            copy.start()
        lax.fori_loop(1, plane_n, one, 0)

    def sent_turn(turn):
        def one(step, carry):
            for copy in plane_copies(lax.rem(own + step, plane_n), at_turn(turn)):
                copy.wait_send()
            return carry

        lax.fori_loop(1, plane_n, one, 0)

    @pl.when(early)
    def _():
        for turn in range(z_part):
            send_turn(turn)
            if turn < z_part - 1:
                sent_turn(turn)

    yield

    def gathered(block):
        def one(chip, carry):
            source, at = chip * tpc_n + block // z_part, lax.rem(block, z_part)

            @pl.when(source == own)
            def _():
                for copy in keep_copies(at):
                    copy.wait()

            @pl.when(source != own)
            def _():
                pltpu.make_async_remote_copy(
                    src_ref=got.at[block, chip],
                    dst_ref=got.at[block, chip],
                    send_sem=plane_send.at[own, at],
                    recv_sem=plane_recv.at[source, at],
                    device_id=device(own),
                    device_id_type=MESH_ID,
                ).wait_recv()
                if gated:
                    pltpu.make_async_remote_copy(
                        src_ref=gates_got.at[block, chip],
                        dst_ref=gates_got.at[block, chip],
                        send_sem=gate_send.at[own, at],
                        recv_sem=gate_recv.at[source, at],
                        device_id=device(own),
                        device_id_type=MESH_ID,
                    ).wait_recv()

            return carry

        lax.fori_loop(0, chips, one, 0)

        def rows(step, carry):
            first = pl.multiple_of(step * tile, tile)
            spots = slots_ref[block, pl.ds(first, tile), :]
            rank = lax.broadcasted_iota(jnp.int32, (tile, capacity), 1)
            summed = jnp.zeros((tile, quarter), F32)
            if gated:
                experts = gate_total.shape[0]
                gates = jnp.zeros((experts, tile), F32)
                expert = lax.broadcasted_iota(jnp.int32, (experts, capacity), 0)
            for chip in range(chips):
                hits = jnp.where(rank == spots[:, chip : chip + 1], 1.0, 0.0).astype(BF16)
                summed = summed + jnp.dot(hits, got[block, chip], preferred_element_type=F32)
                if gated:
                    left = jnp.where(
                        expert == z * chips + chip, gates_got[block, chip, 0:1, :], 0.0
                    ).astype(BF16)
                    gates = gates + dot_nt(left, hits)
            total[pl.ds(first, tile), :] = summed
            if gated:
                gate_total[:, pl.ds(first, tile)] = gates
            return carry

        lax.fori_loop(0, tokens // tile, rows, 0)

    def onward(side, target):
        if side == 0:
            return z + 1, target
        return z - 1, jnp.where(target == z - 1, fi_n, target)

    def lines(side, target, to, slot):
        made = [
            pltpu.make_async_remote_copy(
                src_ref=going.at[target],
                dst_ref=coming.at[slot],
                send_sem=line_send.at[side, target],
                recv_sem=line_recv.at[side, target],
                device_id=device(own, to),
                device_id_type=MESH_ID,
            )
        ]
        if gated:
            made.append(
                pltpu.make_async_remote_copy(
                    src_ref=gate_going.at[target],
                    dst_ref=gate_coming.at[side, target],
                    send_sem=gate_line_send.at[side, target],
                    recv_sem=gate_line_recv.at[side, target],
                    device_id=device(own, to),
                    device_id_type=MESH_ID,
                )
            )
        return made

    for step in range(fi_n - 1):
        for side in (0, 1):
            depth = z if side == 0 else fi_n - 1 - z
            target = fi_n - 1 - step + z if side == 0 else step - (fi_n - 1) + z
            passes, inner = depth <= step, depth > 0

            @pl.when(passes)
            def _():
                gathered(target)

                @pl.when(inner)
                def _():
                    for copy in lines(side, target, z, target):
                        copy.wait_recv()
                    going[target] = (total[...] + coming[target].astype(F32)).astype(BF16)
                    if gated:
                        gate_going[target] = gate_total[...] + gate_coming[side, target]

                @pl.when(jnp.logical_not(inner))
                def _():
                    going[target] = total[...].astype(BF16)
                    if gated:
                        gate_going[target] = gate_total[...]

                for copy in lines(side, target, *onward(side, target)):
                    copy.start()

        for turn in range(z_part):
            if min(turn, fi_n - 2) == step:

                @pl.when(jnp.logical_not(early))
                def _():
                    send_turn(turn)

        yield

    gathered(z)
    for side in (0, 1):

        @pl.when((z > 0) if side == 0 else (z < fi_n - 1))
        def _():
            for copy in lines(side, z, z, fi_n if side == 1 else z):
                copy.wait_recv()
            total[...] += coming[fi_n if side == 1 else z].astype(F32)
            if gated:
                gate_total[...] += gate_coming[side, z]

    if ends:
        held[...] = (total[...] + args[2][...] + args[3][...]).astype(BF16)
        start()
        keep.start()
    else:
        out_ref[...] = total[...]
    if gated:
        gate_out[...] = gate_total[...]
    yield
    if ends:
        relay()


    for target in range(fi_n):
        for side in (0, 1):

            @pl.when((z < target) if side == 0 else (z > target))
            def _():
                for copy in lines(side, target, *onward(side, target)):
                    copy.wait_send()

    for turn in range(z_part):

        @pl.when(jnp.logical_not(early) | (turn == z_part - 1))
        def _():
            sent_turn(turn)

    yield
    if ends:
        spread_settle()


def give_back_job(sizes, rows, token_slots, gates, bases=None):
    fi_n, ctx_n, tpx_n, tpc_n = (sizes[n] for n in ("fi", "ctx", "tpx", "tpc"))
    z_part, plane_n, chips = fi_n // tpc_n, ctx_n * tpx_n * tpc_n, ctx_n * tpx_n
    capacity, width = rows.shape[2:]
    quarter = width // (tpx_n * tpc_n)
    tokens = token_slots.shape[1]
    experts = fi_n * chips
    gated = gates is not None
    shapes = [jax.ShapeDtypeStruct((tokens, quarter), F32)]
    scratch = [
        pltpu.VMEM((fi_n, chips, capacity, quarter), BF16),
        pltpu.VMEM((tokens, quarter), F32),
        pltpu.VMEM((fi_n, tokens, quarter), BF16),
        pltpu.VMEM((fi_n + 1, tokens, quarter), BF16),
        pltpu.SemaphoreType.DMA((plane_n, z_part)),
        pltpu.SemaphoreType.DMA((plane_n, z_part)),
        pltpu.SemaphoreType.DMA((2, fi_n)),
        pltpu.SemaphoreType.DMA((2, fi_n)),
    ]
    args = [token_slots, rows]
    if gated:
        args.append(gates)
        shapes.append(jax.ShapeDtypeStruct((experts, tokens), F32))
        scratch += [
            pltpu.VMEM((fi_n, chips, 8, capacity), F32),
            pltpu.VMEM((experts, tokens), F32),
            pltpu.VMEM((fi_n, experts, tokens), F32),
            pltpu.VMEM((2, fi_n, experts, tokens), F32),
            pltpu.SemaphoreType.DMA((plane_n, z_part)),
            pltpu.SemaphoreType.DMA((plane_n, z_part)),
            pltpu.SemaphoreType.DMA((2, fi_n)),
            pltpu.SemaphoreType.DMA((2, fi_n)),
        ]
    specs = [VMEM_SPEC] + [HBM_SPEC] * (len(args) - 1)
    if bases is not None:
        args += list(bases)
        specs += [VMEM_SPEC] * 2
        shapes = [jax.ShapeDtypeStruct((tokens, width), BF16)]
        scratch += [pltpu.VMEM((tokens, quarter), BF16)] + tp_spread_sems(sizes)
    return {
        "args": list(zip(args, specs)),
        "outs": [(shape, HBM_SPEC if bases is not None else VMEM_SPEC) for shape in shapes],
        "scratch": scratch,
        "run": give_back_run,
    }


def collect_run(kinds, sizes, args, outs, scratch):
    fo_n, fi_n, ctx_n, tpx_n, tpc_n = (sizes[n] for n in ("fo", "fi", "ctx", "tpx", "tpc"))
    tp_n = tpx_n * tpc_n
    count = len(kinds)
    shards = args
    own_sem, line_send, line_recv, col_send, col_recv = scratch[:5]
    staged, spread_sems = scratch[5 : 5 + count * fo_n], scratch[5 + count * fo_n :]
    fo, z, y, x, c = (lax.axis_index(n) for n in ("fo", "fi", "ctx", "tpx", "tpc"))
    q = x * tpc_n + c

    items = [(i, f) for f in range(fo_n) for i in range(count)]

    def source(n):
        i, f = items[n]
        if kinds[i] == "share":
            a = shards[i].shape[1] // tp_n
            return shards[i].at[f, pl.ds(pl.multiple_of(q * a, a), a), :]
        return shards[i].at[f]

    def place(n, zb, yb):
        i, f = items[n]
        a, b = shards[i].shape[1:]
        block = (f * fi_n + zb) * ctx_n + yb
        if kinds[i] == "col":
            return outs[i].at[:, pl.ds(pl.multiple_of(block * b, b), b)]
        if kinds[i] == "share":
            return outs[i].at[block, q]
        return outs[i].at[pl.ds(pl.multiple_of(block * a, a), a), :]

    def parts_of(n):
        i, f = items[n]
        blocks = pl.ds(f * fi_n * ctx_n, fi_n * ctx_n)
        return lambda owner: outs[i].at[blocks, owner]

    spreads = {}
    for n, (i, f) in enumerate(items):
        if kinds[i] == "share":
            at = 5 * len(spreads)
            spreads[n] = tp_spread(
                sizes, parts_of(n)(q), None, parts_of(n), spread_sems[at : at + 5]
            )

    def line(n, side, step, first):
        block = z - step if side == 0 else z + step
        to = z + 1 if side == 0 else z - 1
        return pltpu.make_async_remote_copy(
            src_ref=source(n) if first else place(n, block, y),
            dst_ref=place(n, block, y),
            send_sem=line_send.at[n, side, step],
            recv_sem=line_recv.at[n, side, step],
            device_id=(fo, to, y, x, c),
            device_id_type=MESH_ID,
        )

    def sends(side, step):
        block = z - step if side == 0 else z + step
        to = z + 1 if side == 0 else z - 1
        return (block >= 0) & (block < fi_n) & (to >= 0) & (to < fi_n)

    def across(n, zb, dy, first=False):
        return pltpu.make_async_remote_copy(
            src_ref=source(n) if first else place(n, zb, y),
            dst_ref=place(n, zb, y),
            send_sem=col_send.at[n, zb, dy],
            recv_sem=col_recv.at[n, zb, dy],
            device_id=(fo, z, lax.rem(y + dy, ctx_n), x, c),
            device_id_type=MESH_ID,
        )

    def stage(n):
        return pltpu.make_async_copy(source(n), staged[n], own_sem.at[n, 0])

    def keep(n):
        return pltpu.make_async_copy(staged[n], place(n, z, y), own_sem.at[n, 1])

    for n in range(len(items)):
        for side in (0, 1):

            @pl.when(sends(side, 0))
            def _():
                line(n, side, 0, True).start()

        for dy in range(1, ctx_n):
            across(n, z, dy, True).start()
        stage(n).start()

    yield
    for n in range(len(items)):
        stage(n).wait()
        keep(n).start()

    for step in range(fi_n - 1):
        for n in range(len(items)):
            for side in (0, 1):
                block = z - 1 - step if side == 0 else z + 1 + step

                @pl.when((block >= 0) & (block < fi_n))
                def _():
                    pltpu.make_async_remote_copy(
                        src_ref=place(n, block, y),
                        dst_ref=place(n, block, y),
                        send_sem=line_send.at[n, side, step],
                        recv_sem=line_recv.at[n, side, step],
                        device_id=(fo, z, y, x, c),
                        device_id_type=MESH_ID,
                    ).wait_recv()
                    for dy in range(1, ctx_n):
                        across(n, block, dy).start()

                if step < fi_n - 2:

                    @pl.when(sends(side, step + 1))
                    def _():
                        line(n, side, step + 1, False).start()

        yield

    for n in range(len(items)):
        keep(n).wait()
        for dy in range(1, ctx_n):
            for zb in range(fi_n):
                pltpu.make_async_remote_copy(
                    src_ref=place(n, zb, y),
                    dst_ref=place(n, zb, lax.rem(y + ctx_n - dy, ctx_n)),
                    send_sem=col_send.at[n, zb, dy],
                    recv_sem=col_recv.at[n, zb, dy],
                    device_id=(fo, z, y, x, c),
                    device_id_type=MESH_ID,
                ).wait_recv()
        if n in spreads:
            spreads[n][0]()

    yield

    for n in spreads:
        spreads[n][2]()

    for n in range(len(items)):
        if n in spreads:
            spreads[n][3]()
        for side in (0, 1):
            for step in range(fi_n - 1):

                @pl.when(sends(side, step))
                def _():
                    line(n, side, step, step == 0).wait_send()

        for dy in range(1, ctx_n):
            for zb in range(fi_n):
                across(n, zb, dy).wait_send()


def collect_job(sizes, kinds, shards):
    fo_n, fi_n, ctx_n, tpx_n, tpc_n = (sizes[n] for n in ("fo", "fi", "ctx", "tpx", "tpc"))
    tp_n = tpx_n * tpc_n
    blocks = fo_n * fi_n * ctx_n
    outs, staged = [], []
    for kind, shard in zip(kinds, shards):
        _, a, b = shard.shape
        shape = (a, blocks * b) if kind == "col" else (blocks * a, b)
        if kind == "share":
            shape = (blocks, tp_n, a // tp_n, b)
        outs.append((jax.ShapeDtypeStruct(shape, shard.dtype), HBM_SPEC))
        staged.append(pltpu.VMEM((a // tp_n if kind == "share" else a, b), shard.dtype))
    n = len(kinds) * fo_n
    return {
        "args": [(shard, HBM_SPEC) for shard in shards],
        "outs": outs,
        "scratch": [
            pltpu.SemaphoreType.DMA((n, 2)),
            pltpu.SemaphoreType.DMA((n, 2, fi_n)),
            pltpu.SemaphoreType.DMA((n, 2, fi_n)),
            pltpu.SemaphoreType.DMA((n, fi_n, ctx_n)),
            pltpu.SemaphoreType.DMA((n, fi_n, ctx_n)),
        ]
        + staged * fo_n
        + tp_spread_sems(sizes) * (kinds.count("share") * fo_n),
        "run": functools.partial(collect_run, tuple(kinds)),
    }


def place_job(sizes, local):
    fo_n, fi_n, ctx_n, tpx_n, tpc_n = (sizes[n] for n in ("fo", "fi", "ctx", "tpx", "tpc"))
    chip_n = fi_n * ctx_n * tpx_n
    rows, depth = local.shape[3:]
    shape = (rows * tpx_n * tpc_n, depth * fo_n * fi_n * ctx_n)
    return {
        "args": [(local, HBM_SPEC)],
        "outs": [(jax.ShapeDtypeStruct(shape, BF16), HBM_SPEC)] * 3,
        "scratch": [pltpu.VMEM(local.shape, BF16)]
        + [pltpu.SemaphoreType.DMA((fo_n, 3, chip_n))] * 2
        + [pltpu.SemaphoreType.DMA((fo_n, 3, chip_n, tpc_n))] * 2,
        "run": place_run,
    }


def place_run(sizes, args, outs, scratch):
    fo_n, fi_n, ctx_n, tpx_n, tpc_n = (sizes[n] for n in ("fo", "fi", "ctx", "tpx", "tpc"))
    (local,) = args
    staged, load_sem, keep_sem, pair_send, pair_recv = scratch
    chip_n = fi_n * ctx_n * tpx_n
    rows, depth = local.shape[3:]
    fo, z, y, x, c = (lax.axis_index(n) for n in ("fo", "fi", "ctx", "tpx", "tpc"))

    def spot(k, f, chip, core):
        block = f * fi_n * ctx_n + chip // tpx_n
        return outs[k].at[
            pl.ds(pl.multiple_of((lax.rem(chip, tpx_n) * tpc_n + core) * rows, rows), rows),
            pl.ds(pl.multiple_of(block * depth, depth), depth),
        ]

    def load(f, k, chip):
        return pltpu.make_async_copy(
            local.at[f, chip, k], staged.at[f, chip, k], load_sem.at[f, k, chip]
        )

    def keep(f, k, chip):
        return pltpu.make_async_copy(
            staged.at[f, chip, k], spot(k, f, chip, c), keep_sem.at[f, k, chip]
        )

    def pair_copy(f, k, chip, dc, core):
        return pltpu.make_async_remote_copy(
            src_ref=local.at[f, chip, k],
            dst_ref=spot(k, f, chip, core),
            send_sem=pair_send.at[f, k, chip, dc],
            recv_sem=pair_recv.at[f, k, chip, dc],
            device_id=(fo, z, y, x, lax.rem(c + dc, tpc_n)),
            device_id_type=MESH_ID,
        )

    def launch(step, carry):
        f, chip = step // chip_n, lax.rem(step, chip_n)
        for k in range(3):
            load(f, k, chip).start()
            for dc in range(1, tpc_n):
                pair_copy(f, k, chip, dc, c).start()
        return carry

    def store(step, carry):
        f, chip = step // chip_n, lax.rem(step, chip_n)
        for k in range(3):
            load(f, k, chip).wait()
            keep(f, k, chip).start()
        return carry

    def settle(step, carry):
        f, chip = step // chip_n, lax.rem(step, chip_n)
        for k in range(3):
            keep(f, k, chip).wait()
            for dc in range(1, tpc_n):
                pair_copy(f, k, chip, dc, c).wait_send()
                pair_copy(f, k, chip, dc, lax.rem(c + tpc_n - dc, tpc_n)).wait_recv()
        return carry

    lax.fori_loop(0, fo_n * chip_n, launch, 0)
    yield
    lax.fori_loop(0, fo_n * chip_n, store, 0)
    yield
    lax.fori_loop(0, fo_n * chip_n, settle, 0)


def pair_job(sizes, grads):
    fo_n, fi_n, ctx_n, tpx_n, tpc_n = (sizes[n] for n in ("fo", "fi", "ctx", "tpx", "tpc"))
    rows = grads[0].shape[0] // (tpx_n * tpc_n)
    depth = grads[0].shape[1] // (fo_n * fi_n * ctx_n)
    total = fo_n * fi_n * ctx_n * tpx_n
    shape = (total, 3, rows, depth)
    return {
        "args": [(grad, HBM_SPEC) for grad in grads],
        "outs": [(jax.ShapeDtypeStruct(shape, BF16), HBM_SPEC)],
        "scratch": [pltpu.VMEM(shape, BF16)] * 2 + [pltpu.SemaphoreType.DMA((total, 3))] * 4,
        "run": pair_run,
    }


def pair_run(sizes, grads, outs, scratch):
    tpx_n, tpc_n = sizes["tpx"], sizes["tpc"]
    (out_ref,) = outs
    mine, theirs, load_sem, store_sem, send_sem, recv_sem = scratch
    total, _, rows, depth = mine.shape
    fo, z, y, x, c = (lax.axis_index(n) for n in ("fo", "fi", "ctx", "tpx", "tpc"))
    sibling = (fo, z, y, x, 1 - c)

    def spot(k, at, core):
        block, side = at // tpx_n, lax.rem(at, tpx_n)
        return grads[k].at[
            pl.ds(pl.multiple_of((side * tpc_n + core) * rows, rows), rows),
            pl.ds(pl.multiple_of(block * depth, depth), depth),
        ]

    def load(k, at):
        return pltpu.make_async_copy(spot(k, at, c), mine.at[at, k], load_sem.at[at, k])

    def store(k, at):
        return pltpu.make_async_copy(mine.at[at, k], out_ref.at[at, k], store_sem.at[at, k])

    def give(k, at):
        return pltpu.make_async_remote_copy(
            src_ref=spot(k, at, 1 - c),
            dst_ref=theirs.at[at, k],
            send_sem=send_sem.at[at, k],
            recv_sem=recv_sem.at[at, k],
            device_id=sibling,
            device_id_type=MESH_ID,
        )

    def launch(at, carry):
        for k in range(3):
            give(k, at).start()
            load(k, at).start()
        return carry

    def add(at, carry):
        for k in range(3):
            load(k, at).wait()
            give(k, at).wait_recv()
            mine[at, k] = (mine[at, k].astype(F32) + theirs[at, k].astype(F32)).astype(BF16)
            store(k, at).start()
        return carry

    def settle(at, carry):
        for k in range(3):
            give(k, at).wait_send()
            store(k, at).wait()
        return carry

    lax.fori_loop(0, total, launch, 0)
    yield
    lax.fori_loop(0, total, add, 0)
    yield
    lax.fori_loop(0, total, settle, 0)


def finish_run(kinds, sizes, args, outs, scratch):
    fi_n, ctx_n, tpx_n, tpc_n = (sizes[n] for n in ("fi", "ctx", "tpx", "tpc"))
    tp_n = tpx_n * tpc_n
    count = len(kinds)
    extra = len(args) - count
    parts, quarters = args[:count], args[count:]
    outs, wholes = outs[:count], outs[count:]
    mine, other, coming = (scratch[k * count : (k + 1) * count] for k in range(3))
    staged, (tiny, *sems) = scratch[3 * count : 3 * count + extra], scratch[3 * count + extra :]
    load_sem, col_send, col_recv, line_send, line_recv, tp_send, tp_recv = sems[:7]
    fo, z, y, x, c = (lax.axis_index(n) for n in ("fo", "fi", "ctx", "tpx", "tpc"))
    q = x * tpc_n + c

    spreads = [
        tp_spread(
            sizes,
            quarters[j],
            staged[j],
            columns_of(wholes[j], quarters[j].shape[1]),
            sems[8 + 5 * j : 13 + 5 * j],
        )
        for j in range(extra)
    ]

    def stage(j):
        return pltpu.make_async_copy(quarters[j], staged[j], sems[7].at[j])

    for j in range(extra):
        spreads[j][0]()
        stage(j).start()

    def view(n, zb, yb):
        a, b = mine[n].shape[1:]
        block = zb * ctx_n + yb
        if kinds[n] == "col":
            return parts[n].at[:, pl.ds(pl.multiple_of(block * b, b), b)]
        if kinds[n] == "share":
            return parts[n].at[pl.ds(pl.multiple_of(block * a * tp_n + q * a, a), a), :]
        return parts[n].at[pl.ds(pl.multiple_of(block * a, a), a), :]

    def across(n, zb, dy):
        to = lax.rem(y + dy, ctx_n)
        return pltpu.make_async_remote_copy(
            src_ref=view(n, zb, to),
            dst_ref=other[n].at[dy - 1, zb],
            send_sem=col_send.at[n, zb, dy],
            recv_sem=col_recv.at[n, zb, dy],
            device_id=(fo, z, to, x, c),
            device_id_type=MESH_ID,
        )

    def load(n, zb):
        return pltpu.make_async_copy(view(n, zb, y), mine[n].at[zb], load_sem.at[n, zb])

    def block_turn(turn):
        high_first = z < fi_n // 2
        place = jnp.where(high_first, fi_n - 1 - z, z)
        at = turn + (place <= turn).astype(jnp.int32)
        far = jnp.where(high_first, fi_n - 1 - at, at)
        return z if turn == fi_n - 1 else far

    def send_turn(turn):
        zb = block_turn(turn)
        for n in range(count):
            for dy in range(1, ctx_n):
                across(n, zb, dy).start()
            load(n, zb).start()

    def sent_turn(turn):
        for n in range(count):
            for dy in range(1, ctx_n):
                across(n, block_turn(turn), dy).wait_send()

    send_turn(0)
    yield
    send_turn(1)
    for j in range(extra):
        stage(j).wait()
        spreads[j][1].start()

    def line(n, side, target):
        at = jnp.where(target == (z + 1 if side == 0 else z - 1), fi_n, target) if side == 1 else target
        return pltpu.make_async_remote_copy(
            src_ref=mine[n].at[target],
            dst_ref=coming[n].at[at],
            send_sem=line_send.at[n, side, target],
            recv_sem=line_recv.at[n, side, target],
            device_id=(fo, z + 1 if side == 0 else z - 1, y, x, c),
            device_id_type=MESH_ID,
        )

    def came(n, side, target, at):
        pltpu.make_async_remote_copy(
            src_ref=mine[n].at[target],
            dst_ref=coming[n].at[at],
            send_sem=line_send.at[n, side, target],
            recv_sem=line_recv.at[n, side, target],
            device_id=(fo, z, y, x, c),
            device_id_type=MESH_ID,
        ).wait_recv()

    def ready(n, target):
        load(n, target).wait()
        for dy in range(1, ctx_n):
            across(n, target, dy).wait_recv()

    def add(n, target, use, store):
        a = mine[n].shape[1]
        tile = math.gcd(a, 64)

        def rows(step, carry):
            at = pl.ds(pl.multiple_of(step * tile, tile), tile)
            summed = mine[n][target, at, :].astype(F32)
            for dy in range(1, ctx_n):
                summed = summed + other[n][dy - 1, target, at, :].astype(F32)
            for slot in use:
                summed = summed + coming[n][slot, at, :].astype(F32)
            store(at, summed.astype(BF16))
            return carry

        lax.fori_loop(0, a // tile, rows, 0)

    for step in range(fi_n - 1):
        for n in range(count):
            for side in (0, 1):
                depth = z if side == 0 else fi_n - 1 - z
                target = fi_n - 1 - step + z if side == 0 else step - (fi_n - 1) + z
                passes, inner = depth <= step, depth > 0

                def back(at, values, n=n, target=target):
                    mine[n][target, at, :] = values

                @pl.when(passes & inner)
                def _():
                    ready(n, target)
                    came(n, side, target, target)
                    add(n, target, (target,), back)
                    line(n, side, target).start()

                @pl.when(passes & jnp.logical_not(inner))
                def _():
                    ready(n, target)
                    add(n, target, (), back)
                    line(n, side, target).start()

        if step + 2 < fi_n:
            sent_turn(step)
            send_turn(step + 2)
        yield

    for n in range(count):
        ready(n, z)

        def out(at, values, n=n):
            if kinds[n] == "share":
                a = mine[n].shape[1]
                outs[n][q, at, :] = values
            elif kinds[n] == "sum":
                tiny[q, at, :] = values
            else:
                outs[n][at, :] = values

        @pl.when(z > 0)
        def _():
            came(n, 0, z, z)

        @pl.when(z < fi_n - 1)
        def _():
            came(n, 1, z, fi_n)

        @pl.when((z > 0) & (z < fi_n - 1))
        def _():
            add(n, z, (z, fi_n), out)

        @pl.when((z == 0) & (z < fi_n - 1))
        def _():
            add(n, z, (fi_n,), out)

        @pl.when((z > 0) & (z == fi_n - 1))
        def _():
            add(n, z, (z,), out)

        @pl.when((z == 0) & (z == fi_n - 1))
        def _():
            add(n, z, (), out)

        if kinds[n] in ("share", "sum"):
            held = outs[n] if kinds[n] == "share" else tiny
            for step in range(1, tp_n):
                peer = lax.rem(q + step, tp_n)
                pltpu.make_async_remote_copy(
                    src_ref=held.at[q],
                    dst_ref=held.at[q],
                    send_sem=tp_send.at[n, step],
                    recv_sem=tp_recv.at[n, step],
                    device_id=(fo, z, y, peer // tpc_n, lax.rem(peer, tpc_n)),
                    device_id_type=MESH_ID,
                ).start()

    yield
    for j in range(extra):
        spreads[j][2]()

    for n in range(count):
        if kinds[n] in ("share", "sum"):
            held = outs[n] if kinds[n] == "share" else tiny
            for step in range(1, tp_n):
                origin = lax.rem(q + tp_n - step, tp_n)
                copy = pltpu.make_async_remote_copy(
                    src_ref=held.at[q],
                    dst_ref=held.at[origin],
                    send_sem=tp_send.at[n, step],
                    recv_sem=tp_recv.at[n, step],
                    device_id=(fo, z, y, x, c),
                    device_id_type=MESH_ID,
                )
                copy.wait_send()
                copy.wait_recv()
            if kinds[n] == "sum":
                summed = tiny[0].astype(F32)
                for k in range(1, tp_n):
                    summed = summed + tiny[k].astype(F32)
                outs[n][...] = summed.astype(BF16)
        for target in range(fi_n):
            for side in (0, 1):

                @pl.when((z < target) if side == 0 else (z > target))
                def _():
                    line(n, side, target).wait_send()

    for turn in range(fi_n - 2, fi_n):
        sent_turn(turn)
    for j in range(extra):
        spreads[j][3]()


def finish_job(sizes, kinds, parts, quarters):
    fi_n, ctx_n, tpx_n, tpc_n = (sizes[n] for n in ("fi", "ctx", "tpx", "tpc"))
    tp_n = tpx_n * tpc_n
    blocks = fi_n * ctx_n
    count, extra = len(kinds), len(quarters)
    own, shapes = [], []
    sum_shape = (16, 256)
    for kind, part in zip(kinds, parts):
        a, b = part.shape
        if kind == "col":
            own.append((a, b // blocks))
            shapes.append(own[-1])
        elif kind == "share":
            own.append((a // (blocks * tp_n), b))
            shapes.append((tp_n,) + own[-1])
        else:
            own.append((a // blocks, b))
            shapes.append(own[-1])
        if kind == "sum":
            sum_shape = own[-1]
    wide = [(v.shape[0], v.shape[1] * tp_n) for v in quarters]
    some = max(extra, 1)
    shapes = [jax.ShapeDtypeStruct(shape, BF16) for shape in shapes + wide]
    return {
        "args": [(arg, HBM_SPEC) for arg in (*parts, *quarters)],
        "outs": list(zip(shapes, [VMEM_SPEC] * count + [HBM_SPEC] * extra)),
        "scratch": [pltpu.VMEM((fi_n,) + s, BF16) for s in own]
        + [pltpu.VMEM((max(ctx_n - 1, 1), fi_n) + s, BF16) for s in own]
        + [pltpu.VMEM((fi_n + 1,) + s, BF16) for s in own]
        + [pltpu.VMEM(v.shape, BF16) for v in quarters]
        + [
            pltpu.VMEM((tp_n,) + sum_shape, BF16),
            pltpu.SemaphoreType.DMA((count, fi_n)),
            pltpu.SemaphoreType.DMA((count, fi_n, ctx_n)),
            pltpu.SemaphoreType.DMA((count, fi_n, ctx_n)),
            pltpu.SemaphoreType.DMA((count, 2, fi_n)),
            pltpu.SemaphoreType.DMA((count, 2, fi_n)),
            pltpu.SemaphoreType.DMA((count, tp_n)),
            pltpu.SemaphoreType.DMA((count, tp_n)),
            pltpu.SemaphoreType.DMA((some,)),
            *(tp_spread_sems(sizes) * extra),
        ],
        "run": functools.partial(finish_run, tuple(kinds)),
    }


def products_job(sizes, lefts, rights, which):
    slots, hidden = lefts[0].shape
    width = rights[0].shape[1]
    tile = min(384, hidden)
    return {
        "args": [(arg, HBM_SPEC) for arg in (*lefts, *rights)],
        "outs": [(jax.ShapeDtypeStruct((hidden, width), BF16), HBM_SPEC)] * len(lefts),
        "scratch": [
            pltpu.VMEM((2, slots, tile), BF16),
            pltpu.VMEM((tile, slots), BF16),
            pltpu.VMEM((slots, width), BF16),
            pltpu.VMEM((2, tile, width), BF16),
            pltpu.SemaphoreType.DMA((2,)),
            pltpu.SemaphoreType.DMA,
            pltpu.SemaphoreType.DMA((2,)),
        ],
        "run": functools.partial(products_run, tuple(which), tile),
    }


def products_run(which, tile, sizes, args, outs, scratch):
    left_buf, turned, right_buf, out_buf, left_sem, right_sem, out_sem = scratch
    count = len(outs)
    lefts, rights = args[:count], args[count:]
    hidden = lefts[0].shape[1]
    width = right_buf.shape[1]
    cells = [(k, at, min(tile, hidden - at)) for k in range(count) for at in range(0, hidden, tile)]

    def load(n):
        k, at, size = cells[n]
        return pltpu.make_async_copy(
            lefts[k].at[:, pl.ds(at, size)],
            left_buf.at[n % 2, :, pl.ds(0, size)],
            left_sem.at[n % 2],
        )

    def fetch(k):
        return pltpu.make_async_copy(rights[which[k]], right_buf, right_sem)

    def store(n):
        k, at, size = cells[n]
        return pltpu.make_async_copy(
            out_buf.at[n % 2, pl.ds(0, size), :],
            outs[k].at[pl.ds(at, size), :],
            out_sem.at[n % 2],
        )

    columns = min(512, width)

    def products():
        for n, (k, at, size) in enumerate(cells):
            load(n).wait()
            if n + 1 < len(cells):
                load(n + 1).start()
            if at == 0 and (k == 0 or which[k] != which[k - 1]):
                if k > 0:
                    fetch(k).start()
                fetch(k).wait()
            if n >= 2:
                store(n - 2).wait()
            turned[pl.ds(0, size), :] = left_buf[n % 2, :, :size].T

            def one(step, carry, n=n, size=size):
                here = pl.ds(pl.multiple_of(step * columns, columns), columns)
                out_buf[n % 2, pl.ds(0, size), here] = jnp.dot(
                    turned[:size, :], right_buf[:, here], preferred_element_type=F32
                ).astype(BF16)
                return carry

            lax.fori_loop(0, width // columns, one, 0)
            store(n).start()
        for n in range(max(len(cells) - 2, 0), len(cells)):
            store(n).wait()

    fi_n = sizes["fi"]
    z = lax.axis_index("fi")
    inner = (z > 0) & (z < fi_n - 1)
    fetch(0).start()
    load(0).start()
    for phase in range(1, fi_n):
        yield
        if phase == 1:
            pl.when(inner)(products)
        if phase == fi_n - 1:
            pl.when(jnp.logical_not(inner))(products)


def reduce_job(sizes, both, parts):
    ctx_n, tpx_n, tpc_n = (sizes[n] for n in ("ctx", "tpx", "tpc"))
    tp_n = tpx_n * tpc_n
    tokens, quarter = parts.shape[1:]
    wide = both.shape[1]
    piece = (ctx_n, tokens // tp_n, wide)
    return {
        "args": [(both.reshape(ctx_n, tokens, wide), HBM_SPEC), (parts, HBM_SPEC)],
        "outs": [
            (jax.ShapeDtypeStruct((tokens, wide), BF16), VMEM_SPEC),
            (jax.ShapeDtypeStruct((tokens, quarter), F32), VMEM_SPEC),
        ],
        "scratch": [
            pltpu.VMEM((3, tpx_n) + piece, BF16),
            pltpu.VMEM((3, tpx_n, tokens, quarter), BF16),
            pltpu.VMEM((ctx_n,) + piece[1:], BF16),
            pltpu.SemaphoreType.DMA((2, tpx_n)),
            pltpu.SemaphoreType.DMA((2, tpx_n)),
            pltpu.SemaphoreType.DMA((2, tpx_n)),
            pltpu.SemaphoreType.DMA((2, tpx_n)),
            pltpu.SemaphoreType.DMA((2, tpx_n)),
            pltpu.SemaphoreType.DMA((2, ctx_n)),
            pltpu.SemaphoreType.DMA((2, tp_n)),
        ],
        "run": reduce_run,
    }


def reduce_run(sizes, args, outs, scratch):
    ctx_n, tpx_n, tpc_n = (sizes[n] for n in ("ctx", "tpx", "tpc"))
    tp_n = tpx_n * tpc_n
    both_ref, parts_ref = args
    both_out, parts_out = outs
    both_buf, parts_buf, halves = scratch[:3]
    load_sem, core_send, core_recv, x_send, x_recv, y_sem, tp_sem = scratch[3:]
    rows = halves.shape[1]
    fo, z, y, x, c = (lax.axis_index(n) for n in ("fo", "fi", "ctx", "tpx", "tpc"))
    q = x * tpc_n + c
    bufs = (both_buf, parts_buf)

    def view(kind, side, core):
        to = side * tpc_n + core
        if kind == 0:
            return both_ref.at[:, pl.ds(pl.multiple_of(to * rows, rows), rows), :]
        return parts_ref.at[to]

    def load(kind, side):
        return pltpu.make_async_copy(
            view(kind, side, c), bufs[kind].at[0, side], load_sem.at[kind, side]
        )

    def to_core(kind, side):
        return pltpu.make_async_remote_copy(
            src_ref=view(kind, side, 1 - c),
            dst_ref=bufs[kind].at[1, side],
            send_sem=core_send.at[kind, side],
            recv_sem=core_recv.at[kind, side],
            device_id=(fo, z, y, x, 1 - c),
            device_id_type=MESH_ID,
        )

    def to_chip(kind, side, slot):
        return pltpu.make_async_remote_copy(
            src_ref=bufs[kind].at[0, side],
            dst_ref=bufs[kind].at[2, slot],
            send_sem=x_send.at[kind, side],
            recv_sem=x_recv.at[kind, slot],
            device_id=(fo, z, y, side, c),
            device_id_type=MESH_ID,
        )

    def side_of(dx):
        return lax.rem(x + dx, tpx_n)

    def add(kind, side):
        count = bufs[kind].shape[2] if kind == 1 else bufs[kind].shape[3]
        tile = math.gcd(count, 64)

        def one(step, carry):
            at = pl.ds(pl.multiple_of(step * tile, tile), tile)
            if kind == 1:
                mine, other = parts_buf[0, side, at, :], parts_buf[1, side, at, :]
                parts_buf[0, side, at, :] = (mine.astype(F32) + other.astype(F32)).astype(BF16)
            else:
                for half in range(ctx_n):
                    mine = both_buf[0, side, half, at, :]
                    other = both_buf[1, side, half, at, :]
                    both_buf[0, side, half, at, :] = (
                        mine.astype(F32) + other.astype(F32)
                    ).astype(BF16)
            return carry

        lax.fori_loop(0, count // tile, one, 0)

    order = list(range(1, tpx_n)) + [0]
    for kind in (0, 1):
        for dx in order:
            to_core(kind, side_of(dx)).start()
            load(kind, side_of(dx)).start()
    yield
    for kind in (0, 1):
        for dx in order:
            side = side_of(dx)
            load(kind, side).wait()
            to_core(kind, side).wait_recv()
            add(kind, side)
            if dx > 0:
                to_chip(kind, side, x).start()
    yield

    for dx in range(1, tpx_n):
        to_chip(0, side_of(dx), side_of(dx)).wait_recv()
    tile = math.gcd(rows, 64)

    def over_x(step, carry):
        at = pl.ds(pl.multiple_of(step * tile, tile), tile)
        for half in range(ctx_n):
            summed = both_buf[0, x, half, at, :].astype(F32)
            for dx in range(1, tpx_n):
                summed = summed + both_buf[2, side_of(dx), half, at, :].astype(F32)
            both_buf[0, x, half, at, :] = summed.astype(BF16)
        return carry

    lax.fori_loop(0, rows // tile, over_x, 0)

    def to_y(dy, half, slot):
        return pltpu.make_async_remote_copy(
            src_ref=both_buf.at[0, x, half],
            dst_ref=halves.at[slot],
            send_sem=y_sem.at[0, dy],
            recv_sem=y_sem.at[1, dy],
            device_id=(fo, z, half, x, c),
            device_id_type=MESH_ID,
        )

    for dy in range(1, ctx_n):
        to_y(dy, lax.rem(y + dy, ctx_n), y).start()
    yield
    for dy in range(1, ctx_n):
        source = lax.rem(y + ctx_n - dy, ctx_n)
        to_y(dy, y, source).wait_recv()

    def over_y(step, carry):
        at = pl.ds(pl.multiple_of(step * tile, tile), tile)
        summed = both_buf[0, x, y, at, :].astype(F32)
        for dy in range(1, ctx_n):
            summed = summed + halves[lax.rem(y + ctx_n - dy, ctx_n), at, :].astype(F32)
        both_out[pl.ds(pl.multiple_of(q * rows + step * tile, tile), tile), :] = summed.astype(BF16)
        return carry

    lax.fori_loop(0, rows // tile, over_y, 0)

    def to_tp(step, owner):
        peer = lax.rem(q + step, tp_n)
        held = both_out.at[pl.ds(pl.multiple_of(owner * rows, rows), rows), :]
        return pltpu.make_async_remote_copy(
            src_ref=both_out.at[pl.ds(pl.multiple_of(q * rows, rows), rows), :],
            dst_ref=held,
            send_sem=tp_sem.at[0, step],
            recv_sem=tp_sem.at[1, step],
            device_id=(fo, z, y, peer // tpc_n, lax.rem(peer, tpc_n)),
            device_id_type=MESH_ID,
        )

    for step in range(1, tp_n):
        to_tp(step, q).start()
    yield
    for dx in range(1, tpx_n):
        to_chip(1, side_of(dx), side_of(dx)).wait_recv()
    tall = math.gcd(parts_out.shape[0], 64)

    def last(step, carry):
        at = pl.ds(pl.multiple_of(step * tall, tall), tall)
        summed = parts_buf[0, x, at, :].astype(F32)
        for dx in range(1, tpx_n):
            summed = summed + parts_buf[2, side_of(dx), at, :].astype(F32)
        parts_out[at, :] = summed
        return carry

    lax.fori_loop(0, parts_out.shape[0] // tall, last, 0)
    for step in range(1, tp_n):
        to_tp(step, q).wait_send()
        to_tp(step, lax.rem(q + tp_n - step, tp_n)).wait_recv()
    for dy in range(1, ctx_n):
        to_y(dy, lax.rem(y + dy, ctx_n), y).wait_send()
    for kind in (0, 1):
        for dx in range(tpx_n):
            to_core(kind, side_of(dx)).wait_send()
            if dx > 0:
                to_chip(kind, side_of(dx), x).wait_send()


def attend_body(place_ref, q_ref, kv_ref, rope_ref, out_ref, log_ref):
    block_rows, key_count = q_ref.shape[0], kv_ref.shape[0]
    first = place_ref[0] + pl.program_id(1) * block_rows
    keys = jnp.concatenate([kv_ref[:, :NOPE], rope_ref[...]], axis=1)
    scores = dot_nt(q_ref[...], keys)
    row = first + lax.broadcasted_iota(jnp.int32, (block_rows, 1), 0)
    limit = jnp.maximum(row, place_ref[1] - 1)
    key = lax.broadcasted_iota(jnp.int32, (block_rows, key_count), 1)
    scores = jnp.where(key <= limit, scores, -1e30)
    top = jnp.max(scores, axis=1, keepdims=True)
    exponent = jnp.exp(scores - top)
    row_total = jnp.sum(exponent, axis=1, keepdims=True)
    summed = jnp.dot(exponent.astype(BF16), kv_ref[:, NOPE:], preferred_element_type=F32)
    out_ref[...] = (summed / row_total).astype(BF16)
    log_total = jnp.broadcast_to(top + jnp.log(row_total), (block_rows, 128))
    log_ref[0] = log_total.T[:1]

def attend(place, query, key_value, rope, block_rows):
    rows, key_count = query.shape[0], key_value.shape[0]
    heads = query.shape[1] // HEAD
    return pl.pallas_call(
        attend_body,
        out_shape=(jax.ShapeDtypeStruct((rows, heads * VDIM), BF16), jax.ShapeDtypeStruct((heads, 1, rows), F32)),
        grid_spec=pltpu.PrefetchScalarGridSpec(
            num_scalar_prefetch=1,
            grid=(heads, rows // block_rows),
            in_specs=[
                pl.BlockSpec((block_rows, HEAD), lambda h, i, s: (i, h)),
                pl.BlockSpec((key_count, HEAD), lambda h, i, s: (0, h)),
                pl.BlockSpec((key_count, NOPE), lambda h, i, s: (0, 0)),
            ],
            out_specs=[
                pl.BlockSpec((block_rows, VDIM), lambda h, i, s: (i, h)),
                pl.BlockSpec((1, 1, block_rows), lambda h, i, s: (h, 0, i)),
            ],
        ),
        compiler_params=pltpu.CompilerParams(vmem_limit_bytes=48 << 20),
        cost_estimate=pl.CostEstimate(flops=4 * rows * key_count * heads * HEAD, bytes_accessed=20_000_000, transcendentals=rows * key_count * heads),
        name="attend",
    )(place, query, key_value, rope)

def attend_back_body(place_ref, q_ref, kv_ref, rope_ref, dout_ref, log_ref, table_ref, dq_ref, dkv_ref, drope_ref, keys_acc, values_acc):
    block_rows, key_count = q_ref.shape[0], kv_ref.shape[0]
    head, step = pl.program_id(0), pl.program_id(1)
    first = place_ref[0] + step * block_rows
    keys = jnp.concatenate([kv_ref[:, :NOPE], rope_ref[...]], axis=1)
    scores = dot_nt(keys, q_ref[...])
    row = first + lax.broadcasted_iota(jnp.int32, (1, block_rows), 1)
    limit = jnp.maximum(row, place_ref[1] - 1)
    key = lax.broadcasted_iota(jnp.int32, (key_count, block_rows), 0)
    soft = jnp.exp(jnp.where(key <= limit, scores, -1e30) - log_ref[0])
    soft_grad = dot_nt(kv_ref[:, NOPE:], dout_ref[...])
    mean = jnp.sum(soft * soft_grad, axis=0, keepdims=True)
    score_grad = (soft * (soft_grad - mean)).astype(BF16)
    values = jnp.dot(soft.astype(BF16), dout_ref[...], preferred_element_type=F32)
    keys_grad = jnp.dot(score_grad, q_ref[...], preferred_element_type=F32)
    dq_ref[...] = (dot_tn(score_grad, keys) * table_ref[...]).astype(BF16)

    @pl.when(step == 0)
    def _():
        keys_acc[...] = keys_grad
        values_acc[...] = values

    @pl.when(step > 0)
    def _():
        keys_acc[...] += keys_grad
        values_acc[...] += values

    @pl.when(step == pl.num_programs(1) - 1)
    def _():
        dkv_ref[...] = jnp.concatenate([keys_acc[:, :NOPE], values_acc[...]], axis=1).astype(BF16)

        @pl.when(head == 0)
        def _():
            drope_ref[...] = keys_acc[:, NOPE:]

        @pl.when(head > 0)
        def _():
            drope_ref[...] += keys_acc[:, NOPE:]

def attend_back(place, query, key_value, rope, dout, log_total, table, block_rows):
    rows, key_count = query.shape[0], key_value.shape[0]
    heads = query.shape[1] // HEAD
    return pl.pallas_call(
        attend_back_body,
        out_shape=(jax.ShapeDtypeStruct((rows, heads * HEAD), BF16), jax.ShapeDtypeStruct((key_count, heads * HEAD), BF16), jax.ShapeDtypeStruct((key_count, NOPE), F32)),
        grid_spec=pltpu.PrefetchScalarGridSpec(
            num_scalar_prefetch=1,
            grid=(heads, rows // block_rows),
            in_specs=[
                pl.BlockSpec((block_rows, HEAD), lambda h, i, s: (i, h)),
                pl.BlockSpec((key_count, HEAD), lambda h, i, s: (0, h)),
                pl.BlockSpec((key_count, NOPE), lambda h, i, s: (0, 0)),
                pl.BlockSpec((block_rows, VDIM), lambda h, i, s: (i, h)),
                pl.BlockSpec((1, 1, block_rows), lambda h, i, s: (h, 0, i)),
                pl.BlockSpec((block_rows, HEAD), lambda h, i, s: (i, 0)),
            ],
            out_specs=[
                pl.BlockSpec((block_rows, HEAD), lambda h, i, s: (i, h)),
                pl.BlockSpec((key_count, HEAD), lambda h, i, s: (0, h)),
                pl.BlockSpec((key_count, NOPE), lambda h, i, s: (0, 0)),
            ],
            scratch_shapes=[pltpu.VMEM((key_count, HEAD), F32), pltpu.VMEM((key_count, VDIM), F32)],
        ),
        compiler_params=pltpu.CompilerParams(vmem_limit_bytes=56 << 20),
        cost_estimate=pl.CostEstimate(
            flops=10 * rows * key_count * heads * HEAD,
            bytes_accessed=40_000_000,
            transcendentals=rows * key_count * heads,
        ),
        name="attend_back",
    )(place, query, key_value, rope, dout, log_total, table)


def build(sizes):
    fo_n, fi_n, ctx_n, tpx_n, tpc_n = (sizes[name] for name in ("fo", "fi", "ctx", "tpx", "tpc"))
    tp_n = tpx_n * tpc_n
    row_shards = fo_n * fi_n * ctx_n
    plane_experts = ctx_n * tpx_n
    z_part = fi_n // tpc_n

    def expert_weights(gate, up, down):
        local = jnp.stack([gate.transpose(0, 2, 1), up.transpose(0, 2, 1), down], axis=1)
        return lax.all_gather(local, "fo", axis=0) if fo_n > 1 else local[None]

    def shard_of(weight):
        return lax.all_gather(weight, "fo", axis=0) if fo_n > 1 else weight[None]

    def fo_sum(part, kind):
        if fo_n == 1:
            return part
        if kind == "col":
            a = part.shape[0]
            part = part.reshape(a, fo_n, -1)
            return lax.psum_scatter(part, "fo", scatter_dimension=1, tiled=True).reshape(a, -1)
        return lax.psum_scatter(part, "fo", scatter_dimension=0, tiled=True)

    def own_expert_grads(mine):
        mine = mine.reshape((fo_n, -1) + mine.shape[1:])
        got = lax.all_to_all(mine, CHIPS, split_axis=1, concat_axis=1, tiled=True)
        if fo_n > 1:
            got = lax.psum_scatter(got, "fo", scatter_dimension=0, tiled=True)
        got = got[0].astype(F32)
        return (got[:, 0].transpose(0, 2, 1), got[:, 1].transpose(0, 2, 1), got[:, 2])

    def shards(
        tokens,
        out_grad,
        routes,
        slot_index,
        prefix,
        attn_gain,
        query_weight,
        latent_down,
        latent_gain,
        latent_up,
        out_weight,
        moe_gain,
        router_weight,
        shared_gate,
        shared_up,
        shared_down,
        expert_gate,
        expert_up,
        expert_down,
    ):
        row_count, width = tokens.shape
        expert_count = expert_gate.shape[0]
        capacity = row_count * routes.shape[1] // expert_count
        quarter = width // tp_n
        tp_index = lax.axis_index(TP)
        own_expert = lax.axis_index(CHIPS)
        plane_base = lax.axis_index("fi") * plane_experts

        def columns(values):
            return lax.dynamic_slice_in_dim(values, tp_index * quarter, quarter, values.ndim - 1)

        depth = latent_down.shape[0]
        down_width = latent_down.shape[1]

        def turned(weight):
            half = weight.shape[-1] // 2
            return jnp.concatenate([-weight[..., half:], weight[..., :half]], axis=-1)

        small = jnp.concatenate(
            [
                latent_down,
                turned(latent_down[:, KVR:]),
                attn_gain[:, None],
                moe_gain[:, None],
                jnp.pad(latent_gain, (0, depth - latent_gain.shape[0]))[:, None],
                router_weight,
            ],
            axis=1,
        )
        used = small.shape[1]
        small = jnp.pad(small, ((0, 0), (0, -used % 128)))
        keys = jnp.where(slot_index < capacity, routes * capacity + slot_index, -1).T
        keys = jnp.pad(keys, ((0, 8 - keys.shape[0]), (0, 0)), constant_values=-1)
        (small, query_full, up_full, out_full, keys_all), *_ = exchange(
            sizes,
            [
                collect_job(
                    sizes,
                    ("share", "row", "row", "col", "row"),
                    [shard_of(w) for w in (small, query_weight, latent_up, out_weight, keys)],
                )
            ],
            4,
            "collect_attention",
        )
        local_weights = expert_weights(expert_gate, expert_up, expert_down)
        routed_weights = lax.all_to_all(
            local_weights, CHIPS, split_axis=1, concat_axis=1, tiled=True
        )
        small = small.reshape(row_shards * depth, -1)
        wide_down = small[:, : down_width + ROPE]
        down_full = small[:, :down_width]
        gain_at = down_width + ROPE
        gain_one = small[:, gain_at].astype(F32)
        gain_two = small[:, gain_at + 1].astype(F32)
        gain_latent = (
            small[:, gain_at + 2]
            .reshape(row_shards, depth)[:, : latent_gain.shape[0]]
            .reshape(-1)
            .astype(F32)
        )
        router_full = small[:, gain_at + 3 : used]

        keys_all = lax.dynamic_slice_in_dim(
            keys_all, lax.axis_index("fo") * (fi_n * ctx_n * 8), fi_n * ctx_n * 8, 0
        ).reshape(fi_n, ctx_n, 8, row_count)
        keys_column = lax.dynamic_index_in_dim(keys_all, lax.axis_index("ctx"), 1, keepdims=False)
        first_keys = (plane_base + jnp.arange(plane_experts, dtype=jnp.int32)) * capacity
        rel = keys_column[:, None] - first_keys[:, None, None]
        plane_slots = jnp.max(jnp.where((rel >= 0) & (rel < capacity), rel, -1), axis=2)
        token_slots = plane_slots.transpose(0, 2, 1)

        def give_back(rows, gates, bases=None):
            rows = rows.reshape(z_part, ctx_n, capacity, width)
            return give_back_job(sizes, rows, token_slots, gates, bases)

        (slot_grads,), (shared_gate_full, shared_up_full, shared_down_full) = exchange(
            sizes,
            [
                dispatch_job(sizes, columns(out_grad), plane_slots, capacity),
                collect_job(
                    sizes,
                    ("row", "row", "col"),
                    [shard_of(w) for w in (shared_gate, shared_up, shared_down)],
                ),
            ],
            0,
            "dispatch_grads",
        )
        slot_grads = slot_grads.reshape(-1, width)

        head_count = query_full.shape[1] // (NOPE + ROPE)
        hidden = tokens.astype(F32)
        scale_one = rms_scale(hidden)
        normed_one = hidden * scale_one
        normed_in = (normed_one * gain_one).astype(BF16)
        seq_index = lax.axis_index(("fo", "fi"))
        prefix_len = lax.dynamic_index_in_dim(prefix, seq_index, keepdims=False)
        row_offset = lax.axis_index("ctx") * row_count
        query_pos = row_offset + jnp.arange(row_count, dtype=jnp.int32)
        cos_table, sin_table = rotation_tables(query_pos, ROPE // 2)
        score_scale = (NOPE + ROPE) ** (-0.5)
        cos_wide = jnp.concatenate([cos_table, cos_table], axis=1)
        sin_wide = jnp.concatenate([sin_table, sin_table], axis=1)
        table = score_scale * jnp.concatenate(
            [jnp.ones((row_count, NOPE), F32), cos_wide, sin_wide], axis=1
        )

        latent_raw = dot(normed_in, wide_down)
        latent_part = latent_raw[:, :KVR]
        scale_latent = rms_scale(latent_part)
        normed_latent = latent_part * scale_latent
        latent = (normed_latent * gain_latent).astype(BF16)
        key_rope = (
            latent_raw[:, KVR : KVR + ROPE] * cos_wide + latent_raw[:, KVR + ROPE :] * sin_wide
        ).astype(BF16)
        both = lax.all_gather(
            jnp.concatenate([latent, key_rope, key_rope], axis=1), "ctx", axis=0, tiled=True
        )
        latent_all, rope_all = both[:, :KVR], both[:, KVR:]
        query_heads = query_full.reshape(width, head_count, NOPE + ROPE)
        query_wide = jnp.concatenate(
            [query_heads, turned(query_heads[..., NOPE:])], axis=-1
        ).reshape(width, head_count * HEAD)
        query_in = (
            dot(normed_in, query_wide).reshape(row_count, head_count, HEAD) * table[:, None]
        ).astype(BF16).reshape(row_count, head_count * HEAD)
        key_value = dot(latent_all, up_full).astype(BF16)
        place = jnp.stack([row_offset, prefix_len]).astype(jnp.int32)
        block_rows = min(256, row_count)
        attended, log_totals = attend(place, query_in, key_value, rope_all, block_rows)

        def tp_scatter(parts):
            parts = jnp.stack([part.astype(BF16) for part in parts])
            return lax.psum_scatter(parts, TP, scatter_dimension=0, tiled=True)[0].astype(F32)

        def quarters(weight, axis):
            return jnp.split(weight, tp_n, axis=axis)

        attn_out = tp_scatter([dot(attended, part) for part in quarters(out_full, 1)])
        attn_out, slot_grads = lax.optimization_barrier((attn_out, slot_grads))
        residual = columns(tokens).astype(F32) + attn_out
        scale_two = lax.rsqrt(
            lax.psum(jnp.sum(residual * residual, axis=-1, keepdims=True), TP) / width + EPSILON
        )
        normed_two = residual * scale_two
        gain_two_part = columns(gain_two[None])
        mid_part = (normed_two * gain_two_part).astype(BF16)

        (slot_rows,), (gate_full, expert_up_full, down_weight), (normed_mid,) = exchange(
            sizes,
            [
                dispatch_job(sizes, mid_part, plane_slots, capacity),
                place_job(sizes, routed_weights),
                spread_job(sizes, mid_part),
            ],
            1,
            "dispatch_rows",
        )
        slot_rows = slot_rows.reshape(-1, width)

        logits = dot(normed_mid, router_full)
        router_prob = jax.nn.softmax(logits, axis=-1)
        slot_prob = jax.nn.softmax(dot(slot_rows, router_full), axis=-1)
        slot_gate = lax.dynamic_slice_in_dim(slot_prob, own_expert, 1, 1)

        gate_pre = dot(normed_mid, shared_gate_full)
        up_pre = dot(normed_mid, shared_up_full)
        shared_dact = dot_nt(out_grad, shared_down_full)
        shared_silu, shared_slope = silu_parts(gate_pre)
        shared_act = (shared_silu * up_pre).astype(BF16)
        shared_dgate = (shared_dact * up_pre * shared_slope).astype(BF16)
        shared_dup = (shared_dact * shared_silu).astype(BF16)
        mid_shared = tp_scatter(
            [
                dot_nt(shared_dgate, gate_part) + dot_nt(shared_dup, up_part)
                for gate_part, up_part in zip(
                    quarters(shared_gate_full, 0), quarters(shared_up_full, 0)
                )
            ]
        )
        out_shared = tp_scatter([dot(shared_act, part) for part in quarters(shared_down_full, 1)])

        expert_dact_raw = dot_nt(slot_grads, down_weight)
        expert_gpre = dot_nt(slot_rows, gate_full)
        expert_upre = dot_nt(slot_rows, expert_up_full)
        expert_silu, expert_slope = silu_parts(expert_gpre)
        expert_act_wide = expert_silu * expert_upre
        expert_act = expert_act_wide.astype(BF16)
        slot_gate_grad = jnp.sum(expert_act.astype(F32) * expert_dact_raw, axis=-1)
        expert_dact = expert_dact_raw * slot_gate
        expert_dgate = (expert_dact * expert_upre * expert_slope).astype(BF16)
        expert_dup = (expert_dact * expert_silu).astype(BF16)
        slot_drows = dot(expert_dgate, gate_full) + dot(expert_dup, expert_up_full)
        gate_rows = jnp.broadcast_to(
            slot_gate_grad.reshape(z_part, ctx_n, 1, capacity), (z_part, ctx_n, 8, capacity)
        )
        sdown_grad = dot_tn(shared_act, out_grad)
        sgate_grad = dot_tn(normed_mid, shared_dgate)
        sup_grad = dot_tn(normed_mid, shared_dup)
        shared_kinds = ("row", "row", "col")
        shared_parts = [
            fo_sum(part.astype(BF16), kind)
            for part, kind in zip((sgate_grad, sup_grad, sdown_grad), shared_kinds)
        ]
        slot_dout = (slot_grads.astype(F32) * slot_gate).astype(BF16)
        shared_own, (mid_routed, prob_grad), expert_grads = exchange(
            sizes,
            [
                finish_job(sizes, shared_kinds, shared_parts, []),
                give_back(slot_drows.astype(BF16), gate_rows),
                products_job(
                    sizes,
                    [expert_dgate, expert_dup, expert_act],
                    [slot_rows, slot_dout],
                    [0, 0, 1],
                ),
            ],
            2,
            "give_back_rows",
            vmem=60,
        )
        sgate_grad, sup_grad, sdown_grad = (part.astype(F32) for part in shared_own)
        prob_grad = prob_grad.T
        logit_grad = (
            router_prob * (prob_grad - jnp.sum(router_prob * prob_grad, axis=-1, keepdims=True))
        ).astype(BF16)

        mid_routed, mid_shared, out_shared = lax.optimization_barrier(
            (mid_routed, mid_shared, out_shared)
        )
        mid_total = mid_shared + mid_routed + dot_nt(logit_grad, columns(router_full.T).T)
        gain_two_grad = jnp.sum(mid_total * normed_two, axis=0)
        dn_two = mid_total * gain_two_part
        dot_two = lax.psum(jnp.sum(dn_two * normed_two, axis=-1, keepdims=True), TP) / width
        residual_grad = columns(out_grad).astype(F32) + scale_two * (dn_two - normed_two * dot_two)
        (routed_grads,), (attn_dout,) = exchange(
            sizes,
            [pair_job(sizes, expert_grads), spread_job(sizes, residual_grad.astype(BF16))],
            7,
            "pair_sum",
        )

        out_weight_grad = dot_tn(attended, attn_dout)
        attended_grad = dot_nt(attn_dout, out_full).astype(BF16)
        attended_grad, routed_grads = lax.optimization_barrier((attended_grad, routed_grads))
        egate_grad, eup_grad, edown_grad = own_expert_grads(routed_grads)
        query_grad, kv_grad, rope_grad = attend_back(
            place, query_in, key_value, rope_all, attended_grad, log_totals, table,
            min(512, row_count),
        )
        late_act, query_grad = lax.optimization_barrier((expert_act, query_grad))
        expert_out = (dot(late_act, down_weight) * slot_gate).astype(BF16)
        up_grad = dot_tn(latent_all, kv_grad)
        latent_grad = dot_nt(kv_grad, up_full)
        query_wide_grad = dot_tn(normed_in, query_grad).reshape(width, head_count, HEAD)
        query_weight_grad = jnp.concatenate(
            [
                query_wide_grad[..., :NOPE],
                query_wide_grad[..., NOPE : NOPE + ROPE] - turned(query_wide_grad[..., NOPE + ROPE :]),
            ],
            axis=-1,
        ).reshape(width, head_count * (NOPE + ROPE))
        input_parts = jnp.stack(
            [dot_nt(query_grad, part).astype(BF16) for part in quarters(query_wide, 0)]
        )
        ((both_grad, input_part),) = exchange(
            sizes,
            [
                reduce_job(
                    sizes,
                    jnp.concatenate([latent_grad, rope_grad], axis=1).astype(BF16),
                    input_parts,
                )
            ],
            6,
            "sum_inputs",
        )
        both_grad = both_grad.astype(F32)
        latent_own = both_grad[:, :KVR]
        rope_own = both_grad[:, KVR : KVR + ROPE] + both_grad[:, KVR + ROPE :]
        gain_latent_grad = jnp.sum(latent_own * normed_latent, axis=0)
        latent_raw_grad = norm_back(latent_own * gain_latent, normed_latent, scale_latent)
        down_out_grad = jnp.concatenate(
            [latent_raw_grad, rotate(rope_own, cos_table, -sin_table)], axis=-1
        ).astype(BF16)
        down_grad = dot_tn(normed_in, down_out_grad)
        input_total = input_part + dot_nt(
            down_out_grad, lax.dynamic_slice_in_dim(down_full, tp_index * quarter, quarter, 0)
        )
        normed_one_part = columns(normed_one)
        gain_one_grad = jnp.sum(input_total * normed_one_part, axis=0)
        dn_one = input_total * columns(gain_one[None])
        dot_one = lax.psum(jnp.sum(dn_one * normed_one_part, axis=-1, keepdims=True), TP) / width
        token_grad = residual_grad + scale_one * (dn_one - normed_one_part * dot_one)
        token_grad, egate_grad, eup_grad, edown_grad = lax.optimization_barrier(
            (token_grad, egate_grad, eup_grad, edown_grad)
        )
        router_grad = dot_tn(normed_mid, logit_grad)
        pack_grad = jnp.concatenate([down_grad, router_grad], axis=1)
        pack_used = pack_grad.shape[1]
        pack_grad = jnp.pad(pack_grad, ((0, 0), (0, -pack_used % 128)))
        gains = jnp.stack([gain_one_grad, gain_two_grad])
        gains = lax.dynamic_update_slice_in_dim(
            jnp.zeros((2, width), F32), gains, tp_index * quarter, 1
        )
        latent_rows = jnp.pad(
            gain_latent_grad.reshape(row_shards, -1),
            ((0, 0), (0, depth - latent_gain.shape[0])),
        ).reshape(1, width)
        gains = jnp.concatenate([gains, latent_rows * (tp_index == 0).astype(F32)], axis=0)
        gains = jnp.pad(
            gains.reshape(3, row_shards, depth).transpose(1, 0, 2), ((0, 0), (0, 13), (0, 0))
        ).reshape(row_shards * 16, depth)
        kinds = ("share", "sum", "row", "row", "col")
        partials = (pack_grad, gains, query_weight_grad, up_grad, out_weight_grad)
        done, (output,) = exchange(
            sizes,
            [
                finish_job(
                    sizes,
                    kinds,
                    [fo_sum(part.astype(BF16), kind) for part, kind in zip(partials, kinds)],
                    [token_grad.astype(BF16)],
                ),
                give_back(expert_out, None, (residual, out_shared)),
            ],
            3,
            "finish_attention",
        )
        pack_own = done[0].reshape(depth, -1).astype(F32)
        gains_own = done[1].astype(F32)
        query_weight_grad, up_grad, out_weight_grad = (part.astype(F32) for part in done[2:5])
        token_grad = done[5].astype(F32)
        return (
            output,
            token_grad,
            gains_own[0],
            query_weight_grad,
            pack_own[:, :down_width],
            gains_own[2, : latent_gain.shape[0]],
            up_grad,
            out_weight_grad,
            gains_own[1],
            pack_own[:, down_width:pack_used],
            sgate_grad,
            sup_grad,
            sdown_grad,
            egate_grad,
            eup_grad,
            edown_grad,
        )

    return shards


EXPERTS = 16


def solution(mesh):
    ctx_n, tp_n = mesh.shape["ctx"], mesh.shape["tp"]
    tpc_n = 2
    tpx_n = tp_n // tpc_n
    fi_n = EXPERTS // (ctx_n * tpx_n)
    sizes = {
        "fo": mesh.shape["fsdp"] // fi_n,
        "fi": fi_n,
        "ctx": ctx_n,
        "tpx": tpx_n,
        "tpc": tpc_n,
    }
    fine = Mesh(mesh.devices.reshape(tuple(sizes.values())), tuple(sizes))
    rows = P(ROWS)
    rows_two = P(ROWS, None)
    rows_tp = P(ROWS, TP)
    tp_rows = P(TP, ROWS)
    wide_in = P(None, ROWS, TP)
    wide_out = P(None, TP, ROWS)
    weights = (
        rows,
        rows_tp,
        rows_two,
        rows,
        rows_tp,
        tp_rows,
        rows,
        rows_two,
        rows_tp,
        rows_tp,
        tp_rows,
        wide_in,
        wide_in,
        wide_out,
    )
    return jax.shard_map(
        build(sizes),
        mesh=fine,
        in_specs=(rows_two, rows_two, rows_two, rows_two, P()) + weights,
        out_specs=(rows_two, rows_two) + weights,
        check_vma=False,
    )
```

```python
import functools
import math

import jax
import jax.numpy as jnp
from jax import lax
from jax.experimental import pallas as pl
from jax.experimental.pallas import tpu as pltpu
from jax.sharding import Mesh
from jax.sharding import PartitionSpec as P

NOPE = 128
ROPE = 64
KVR = 512
VDIM = 128
HEAD = 256

EPSILON = 1e-06
THETA_BASE = 10000.0
F32 = jnp.float32
BF16 = jnp.bfloat16
MESH_ID = pl.DeviceIdType.MESH

ROWS = ("fo", "fi", "ctx")
TP = ("tpx", "tpc")
PLANE = ("ctx", "tpx", "tpc")
CHIPS = ("fi", "ctx", "tpx")


def rotation_tables(positions, half_width):
    freq_table = jnp.exp(jnp.arange(half_width, dtype=F32) * (-math.log(THETA_BASE) / half_width))
    angle_table = positions.astype(F32)[:, None] * freq_table[None, :]
    return (jnp.cos(angle_table), jnp.sin(angle_table))


def rotate(values, cos_table, sin_table):
    half_width = values.shape[-1] // 2
    first_half = values[..., :half_width]
    second_half = values[..., half_width:]
    return jnp.concatenate(
        [
            first_half * cos_table - second_half * sin_table,
            second_half * cos_table + first_half * sin_table,
        ],
        axis=-1,
    )


def silu_parts(values):
    sigma = jax.nn.sigmoid(values)
    return (values * sigma, sigma * (1.0 + values * (1.0 - sigma)))


def rms_scale(values):
    return lax.rsqrt(jnp.mean(values * values, axis=-1, keepdims=True) + EPSILON)


def norm_back(grad_normed, normed, scale_rows):
    return scale_rows * (
        grad_normed - normed * jnp.mean(grad_normed * normed, axis=-1, keepdims=True)
    )


def dot(left, right):
    return jnp.dot(left, right, preferred_element_type=F32)


def dot_nt(left, right):
    return lax.dot_general(left, right, (((1,), (1,)), ((), ())), preferred_element_type=F32)


def dot_tn(left, right):
    return lax.dot_general(left, right, (((0,), (0,)), ((), ())), preferred_element_type=F32)


def ein(spec, left, right):
    return jnp.einsum(spec, left, right, preferred_element_type=F32)


def plane_place(sizes):
    tpx_n, tpc_n = sizes["tpx"], sizes["tpc"]
    fo, z, y, x, c = (lax.axis_index(name) for name in ("fo", "fi", "ctx", "tpx", "tpc"))
    own = (y * tpx_n + x) * tpc_n + c

    def device(index, z_at=None):
        return (
            fo,
            z if z_at is None else z_at,
            index // (tpx_n * tpc_n),
            lax.rem(index // tpc_n, tpx_n),
            lax.rem(index, tpc_n),
        )

    return z, y, x, c, own, device


def greet_plane(sizes):
    fi_n = sizes["fi"]
    plane_n = sizes["ctx"] * sizes["tpx"] * sizes["tpc"]
    z, y, x, c, own, device = plane_place(sizes)
    barrier = pltpu.get_barrier_semaphore()
    for step in range(1, plane_n):
        pl.semaphore_signal(
            barrier,
            inc=1,
            device_id=device(lax.rem(own + step, plane_n)),
            device_id_type=MESH_ID,
        )
    for near in (-1, 1):

        @pl.when((z + near >= 0) & (z + near < fi_n))
        def _():
            pl.semaphore_signal(
                barrier, inc=1, device_id=device(own, z + near), device_id_type=MESH_ID
            )

    sides = (z > 0).astype(jnp.int32) + (z < fi_n - 1).astype(jnp.int32)
    pl.semaphore_wait(barrier, plane_n - 1 + sides)


HBM_SPEC = pl.BlockSpec(memory_space=pl.ANY)
VMEM_SPEC = pl.BlockSpec(memory_space=pltpu.VMEM)


def exchange(sizes, jobs, collective_id, name, vmem=56):
    counts = [(len(job["args"]), len(job["outs"]), len(job["scratch"])) for job in jobs]

    def body(*refs):
        at = [0, sum(n[0] for n in counts), sum(n[0] + n[1] for n in counts)]
        running = []
        for job, count in zip(jobs, counts):
            given = [refs[at[k] : at[k] + count[k]] for k in range(3)]
            at = [at[k] + count[k] for k in range(3)]
            running.append(job["run"](sizes, *given))
        greet_plane(sizes)
        while running:
            running = [run for run in running if next(run, "ended") != "ended"]

    results = pl.pallas_call(
        body,
        out_shape=tuple(shape for job in jobs for shape, _ in job["outs"]),
        in_specs=[spec for job in jobs for _, spec in job["args"]],
        out_specs=tuple(spec for job in jobs for _, spec in job["outs"]),
        scratch_shapes=[shape for job in jobs for shape in job["scratch"]],
        compiler_params=pltpu.CompilerParams(
            collective_id=collective_id, has_side_effects=True, vmem_limit_bytes=vmem << 20
        ),
        cost_estimate=pl.CostEstimate(
            flops=0, bytes_accessed=20_000_000, transcendentals=0
        ),
        name=name,
    )(*[arg for job in jobs for arg, _ in job["args"]])
    grouped, at = [], 0
    for _, count, _ in counts:
        grouped.append(results[at : at + count])
        at += count
    return grouped


def columns_of(whole, wide):
    def slab(owner):
        return whole.at[:, pl.ds(pl.multiple_of(owner * wide, wide), wide)]

    return slab


def tp_spread(sizes, source, held, slab_of, sems):
    tpx_n, tpc_n = sizes["tpx"], sizes["tpc"]
    keep_sem, x_send, x_recv, c_send, c_recv = sems
    fo, z, y, x, c = (lax.axis_index(n) for n in ("fo", "fi", "ctx", "tpx", "tpc"))

    def slab(side, core):
        return slab_of(side * tpc_n + core)

    def origin(dx):
        return lax.rem(x + tpx_n - dx, tpx_n)

    keep = None if held is None else pltpu.make_async_copy(held, slab(x, c), keep_sem)

    def to_chip(dx, side):
        return pltpu.make_async_remote_copy(
            src_ref=source,
            dst_ref=slab(side, c),
            send_sem=x_send.at[dx],
            recv_sem=x_recv.at[dx],
            device_id=(fo, z, y, lax.rem(x + dx, tpx_n), c),
            device_id_type=MESH_ID,
        )

    def to_core(dx, dc, core):
        return pltpu.make_async_remote_copy(
            src_ref=source if dx == 0 else slab(origin(dx), c),
            dst_ref=slab(origin(dx), core),
            send_sem=c_send.at[dx, dc],
            recv_sem=c_recv.at[dx, dc],
            device_id=(fo, z, y, x, lax.rem(c + dc, tpc_n)),
            device_id_type=MESH_ID,
        )

    def start():
        for dx in range(1, tpx_n):
            to_chip(dx, x).start()
        for dc in range(1, tpc_n):
            to_core(0, dc, c).start()

    def relay():
        for dx in range(1, tpx_n):
            to_chip(dx, origin(dx)).wait_recv()
            for dc in range(1, tpc_n):
                to_core(dx, dc, c).start()

    def settle():
        if keep is not None:
            keep.wait()
        for dx in range(tpx_n):
            if dx > 0:
                to_chip(dx, x).wait_send()
            for dc in range(1, tpc_n):
                to_core(dx, dc, c).wait_send()
                to_core(dx, dc, lax.rem(c + tpc_n - dc, tpc_n)).wait_recv()

    return start, keep, relay, settle


def tp_spread_sems(sizes):
    tpx_n, tpc_n = sizes["tpx"], sizes["tpc"]
    return [
        pltpu.SemaphoreType.DMA,
        pltpu.SemaphoreType.DMA((tpx_n,)),
        pltpu.SemaphoreType.DMA((tpx_n,)),
        pltpu.SemaphoreType.DMA((tpx_n, tpc_n)),
        pltpu.SemaphoreType.DMA((tpx_n, tpc_n)),
    ]


def spread_job(sizes, part):
    tp_n = sizes["tpx"] * sizes["tpc"]
    shape = (part.shape[0], part.shape[1] * tp_n)
    return {
        "args": [(part, HBM_SPEC)],
        "outs": [(jax.ShapeDtypeStruct(shape, BF16), HBM_SPEC)],
        "scratch": [pltpu.VMEM(part.shape, BF16), pltpu.SemaphoreType.DMA]
        + tp_spread_sems(sizes),
        "run": spread_run,
    }


def spread_run(sizes, args, outs, scratch):
    held, load_sem = scratch[:2]
    start, keep, relay, settle = tp_spread(
        sizes, args[0], held, columns_of(outs[0], held.shape[1]), scratch[2:]
    )
    load = pltpu.make_async_copy(args[0], held, load_sem)
    load.start()
    start()
    yield
    load.wait()
    keep.start()
    relay()
    yield
    settle()


def dispatch_job(sizes, part_rows, plane_slots, capacity):
    tokens, quarter = part_rows.shape
    fi_n, ctx_n, tpx_n, tpc_n = (sizes[n] for n in ("fi", "ctx", "tpx", "tpc"))
    z_part, plane_n, chips = fi_n // tpc_n, ctx_n * tpx_n * tpc_n, ctx_n * tpx_n
    shape = (z_part, ctx_n, capacity, quarter * tpx_n * tpc_n)
    return {
        "args": [(plane_slots, VMEM_SPEC), (part_rows, HBM_SPEC)],
        "outs": [(jax.ShapeDtypeStruct(shape, BF16), HBM_SPEC)],
        "scratch": [
            pltpu.VMEM((fi_n, tokens, quarter), BF16),
            pltpu.VMEM((fi_n, chips, capacity, quarter), BF16),
            pltpu.SemaphoreType.DMA,
            pltpu.SemaphoreType.DMA((2, fi_n)),
            pltpu.SemaphoreType.DMA((2, fi_n)),
            pltpu.SemaphoreType.DMA((fi_n, chips)),
            pltpu.SemaphoreType.DMA((plane_n, z_part)),
        ],
        "run": dispatch_run,
    }


def dispatch_run(sizes, args, outs, scratch):
    slots_ref, rows_ref = args
    (out_ref,) = outs
    held, picked, own_sem, line_send, line_recv, plane_send, plane_recv = scratch
    fi_n, tpx_n, tpc_n = sizes["fi"], sizes["tpx"], sizes["tpc"]
    plane_n = sizes["ctx"] * tpx_n * tpc_n
    chips = sizes["ctx"] * tpx_n
    z_part = fi_n // tpc_n
    capacity, quarter = picked.shape[2:]
    tokens = held.shape[1]
    z, y, x, c, own, device = plane_place(sizes)
    columns = pl.ds(pl.multiple_of((x * tpc_n + c) * quarter, quarter), quarter)
    load = pltpu.make_async_copy(rows_ref, held.at[z], own_sem)

    def line(side, step):
        block = z - step if side == 0 else z + step
        to = z + 1 if side == 0 else z - 1
        return pltpu.make_async_remote_copy(
            src_ref=held.at[block],
            dst_ref=held.at[block],
            send_sem=line_send.at[side, step],
            recv_sem=line_recv.at[side, step],
            device_id=device(own, to),
            device_id_type=MESH_ID,
        )

    def sends(side, step):
        block = z - step if side == 0 else z + step
        to = z + 1 if side == 0 else z - 1
        return (block >= 0) & (block < fi_n) & (to >= 0) & (to < fi_n)

    def plane_copy(block, chip):
        at = lax.rem(block, z_part)
        return pltpu.make_async_remote_copy(
            src_ref=picked.at[block, chip],
            dst_ref=out_ref.at[at, y, :, columns],
            send_sem=plane_send.at[block, chip],
            recv_sem=plane_recv.at[own, at],
            device_id=device(chip * tpc_n + block // z_part),
            device_id_type=MESH_ID,
        )

    def keep_copy(block, chip):
        return pltpu.make_async_copy(
            picked.at[block, chip],
            out_ref.at[lax.rem(block, z_part), y, :, columns],
            plane_send.at[block, chip],
        )

    def at_home(block, chip):
        return chip * tpc_n + block // z_part == own

    def pick(block):
        def one(chip, carry):
            wanted = slots_ref[block, pl.ds(chip, 1), :]
            rank = lax.broadcasted_iota(jnp.int32, (capacity, tokens), 0)
            hits = jnp.where(rank == wanted, 1.0, 0.0).astype(BF16)
            picked[block, chip] = jnp.dot(
                hits, held[block], preferred_element_type=F32
            ).astype(BF16)

            @pl.when(at_home(block, chip))
            def _():
                keep_copy(block, chip).start()

            @pl.when(jnp.logical_not(at_home(block, chip)))
            def _():
                plane_copy(block, chip).start()

            return carry

        lax.fori_loop(0, chips, one, 0)

    load.start()
    load.wait()
    for side in (0, 1):

        @pl.when(sends(side, 0))
        def _():
            line(side, 0).start()

    yield
    pick(z)
    for step in range(fi_n - 1):
        for side in (0, 1):
            block = z - 1 - step if side == 0 else z + 1 + step

            @pl.when((block >= 0) & (block < fi_n))
            def _():
                pltpu.make_async_remote_copy(
                    src_ref=held.at[block],
                    dst_ref=held.at[block],
                    send_sem=line_send.at[side, step],
                    recv_sem=line_recv.at[side, step],
                    device_id=device(own, z),
                    device_id_type=MESH_ID,
                ).wait_recv()

            if step < fi_n - 2:

                @pl.when(sends(side, step + 1))
                def _():
                    line(side, step + 1).start()

        for side in (0, 1):
            block = z - 1 - step if side == 0 else z + 1 + step

            @pl.when((block >= 0) & (block < fi_n))
            def _():
                pick(block)

        yield

    for step in range(fi_n - 1):
        for side in (0, 1):

            @pl.when(sends(side, step))
            def _():
                line(side, step).wait_send()

    def settle(index, carry):
        block, chip = index // chips, lax.rem(index, chips)

        @pl.when(at_home(block, chip))
        def _():
            keep_copy(block, chip).wait()

        @pl.when(jnp.logical_not(at_home(block, chip)))
        def _():
            plane_copy(block, chip).wait_send()

        return carry

    lax.fori_loop(0, fi_n * chips, settle, 0)

    def arrive(index, carry):
        source, at = index // z_part, lax.rem(index, z_part)

        @pl.when(source != own)
        def _():
            pltpu.make_async_remote_copy(
                src_ref=picked.at[0, 0],
                dst_ref=out_ref.at[at, y, :, columns],
                send_sem=plane_send.at[0, 0],
                recv_sem=plane_recv.at[source, at],
                device_id=device(own),
                device_id_type=MESH_ID,
            ).wait_recv()

        return carry

    lax.fori_loop(0, plane_n * z_part, arrive, 0)


def give_back_run(sizes, args, outs, scratch):
    fi_n, tpx_n, tpc_n = sizes["fi"], sizes["tpx"], sizes["tpc"]
    plane_n = sizes["ctx"] * tpx_n * tpc_n
    chips = sizes["ctx"] * tpx_n
    z_part = fi_n // tpc_n
    ends, gated = len(args) > 3, len(args) == 3
    slots_ref, rows_ref = args[:2]
    out_ref = outs[0]
    got, total, going, coming, plane_send, plane_recv, line_send, line_recv = scratch[:8]
    if gated:
        gates_ref, gate_out = args[2], outs[1]
        gates_got, gate_total, gate_going, gate_coming = scratch[8:12]
        gate_send, gate_recv, gate_line_send, gate_line_recv = scratch[12:]
    if ends:
        held = scratch[8]
        start, keep, relay, spread_settle = tp_spread(
            sizes, held, held, columns_of(out_ref, held.shape[1]), scratch[9:]
        )
    capacity, quarter = got.shape[2:]
    tokens = total.shape[0]
    z, y, x, c, own, device = plane_place(sizes)
    tile = min(256, tokens)

    def piece(target, at):
        side = lax.rem(target, tpx_n * tpc_n)
        return rows_ref.at[
            at,
            target // (tpx_n * tpc_n),
            :,
            pl.ds(pl.multiple_of(side * quarter, quarter), quarter),
        ]

    def plane_copies(target, at):
        made = [
            pltpu.make_async_remote_copy(
                src_ref=piece(target, at),
                dst_ref=got.at[c * z_part + at, own // tpc_n],
                send_sem=plane_send.at[target, at],
                recv_sem=plane_recv.at[own, at],
                device_id=device(target),
                device_id_type=MESH_ID,
            )
        ]
        if gated:
            made.append(
                pltpu.make_async_remote_copy(
                    src_ref=gates_ref.at[at, target // (tpx_n * tpc_n)],
                    dst_ref=gates_got.at[c * z_part + at, own // tpc_n],
                    send_sem=gate_send.at[target, at],
                    recv_sem=gate_recv.at[own, at],
                    device_id=device(target),
                    device_id_type=MESH_ID,
                )
            )
        return made

    def keep_copies(at):
        made = [
            pltpu.make_async_copy(
                piece(own, at), got.at[c * z_part + at, own // tpc_n], plane_recv.at[own, at]
            )
        ]
        if gated:
            made.append(
                pltpu.make_async_copy(
                    gates_ref.at[at, y],
                    gates_got.at[c * z_part + at, own // tpc_n],
                    gate_recv.at[own, at],
                )
            )
        return made

    high_first = z < fi_n // 2
    early = c == jnp.where(high_first, tpc_n - 1, 0)

    def at_turn(turn):
        far = jnp.where(high_first, z_part - 1 - turn, turn)
        return jnp.where(early, far, lax.rem(z + 1 + turn, z_part))

    def send_turn(turn):
        at = at_turn(turn)

        def one(step, carry):
            for copy in plane_copies(lax.rem(own + step, plane_n), at):
                copy.start()
            return carry

        for copy in keep_copies(at):
            copy.start()
        lax.fori_loop(1, plane_n, one, 0)

    def sent_turn(turn):
        def one(step, carry):
            for copy in plane_copies(lax.rem(own + step, plane_n), at_turn(turn)):
                copy.wait_send()
            return carry

        lax.fori_loop(1, plane_n, one, 0)

    @pl.when(early)
    def _():
        for turn in range(z_part):
            send_turn(turn)
            if turn < z_part - 1:
                sent_turn(turn)

    yield

    def gathered(block):
        def one(chip, carry):
            source, at = chip * tpc_n + block // z_part, lax.rem(block, z_part)

            @pl.when(source == own)
            def _():
                for copy in keep_copies(at):
                    copy.wait()

            @pl.when(source != own)
            def _():
                pltpu.make_async_remote_copy(
                    src_ref=got.at[block, chip],
                    dst_ref=got.at[block, chip],
                    send_sem=plane_send.at[own, at],
                    recv_sem=plane_recv.at[source, at],
                    device_id=device(own),
                    device_id_type=MESH_ID,
                ).wait_recv()
                if gated:
                    pltpu.make_async_remote_copy(
                        src_ref=gates_got.at[block, chip],
                        dst_ref=gates_got.at[block, chip],
                        send_sem=gate_send.at[own, at],
                        recv_sem=gate_recv.at[source, at],
                        device_id=device(own),
                        device_id_type=MESH_ID,
                    ).wait_recv()

            return carry

        lax.fori_loop(0, chips, one, 0)

        def rows(step, carry):
            first = pl.multiple_of(step * tile, tile)
            spots = slots_ref[block, pl.ds(first, tile), :]
            rank = lax.broadcasted_iota(jnp.int32, (tile, capacity), 1)
            summed = jnp.zeros((tile, quarter), F32)
            if gated:
                experts = gate_total.shape[0]
                gates = jnp.zeros((experts, tile), F32)
                expert = lax.broadcasted_iota(jnp.int32, (experts, capacity), 0)
            for chip in range(chips):
                hits = jnp.where(rank == spots[:, chip : chip + 1], 1.0, 0.0).astype(BF16)
                summed = summed + jnp.dot(hits, got[block, chip], preferred_element_type=F32)
                if gated:
                    left = jnp.where(
                        expert == z * chips + chip, gates_got[block, chip, 0:1, :], 0.0
                    ).astype(BF16)
                    gates = gates + dot_nt(left, hits)
            total[pl.ds(first, tile), :] = summed
            if gated:
                gate_total[:, pl.ds(first, tile)] = gates
            return carry

        lax.fori_loop(0, tokens // tile, rows, 0)

    def onward(side, target):
        if side == 0:
            return z + 1, target
        return z - 1, jnp.where(target == z - 1, fi_n, target)

    def lines(side, target, to, slot):
        made = [
            pltpu.make_async_remote_copy(
                src_ref=going.at[target],
                dst_ref=coming.at[slot],
                send_sem=line_send.at[side, target],
                recv_sem=line_recv.at[side, target],
                device_id=device(own, to),
                device_id_type=MESH_ID,
            )
        ]
        if gated:
            made.append(
                pltpu.make_async_remote_copy(
                    src_ref=gate_going.at[target],
                    dst_ref=gate_coming.at[side, target],
                    send_sem=gate_line_send.at[side, target],
                    recv_sem=gate_line_recv.at[side, target],
                    device_id=device(own, to),
                    device_id_type=MESH_ID,
                )
            )
        return made

    for step in range(fi_n - 1):
        for side in (0, 1):
            depth = z if side == 0 else fi_n - 1 - z
            target = fi_n - 1 - step + z if side == 0 else step - (fi_n - 1) + z
            passes, inner = depth <= step, depth > 0

            @pl.when(passes)
            def _():
                gathered(target)

                @pl.when(inner)
                def _():
                    for copy in lines(side, target, z, target):
                        copy.wait_recv()
                    going[target] = (total[...] + coming[target].astype(F32)).astype(BF16)
                    if gated:
                        gate_going[target] = gate_total[...] + gate_coming[side, target]

                @pl.when(jnp.logical_not(inner))
                def _():
                    going[target] = total[...].astype(BF16)
                    if gated:
                        gate_going[target] = gate_total[...]

                for copy in lines(side, target, *onward(side, target)):
                    copy.start()

        for turn in range(z_part):
            if min(turn, fi_n - 2) == step:

                @pl.when(jnp.logical_not(early))
                def _():
                    send_turn(turn)

        yield

    gathered(z)
    for side in (0, 1):

        @pl.when((z > 0) if side == 0 else (z < fi_n - 1))
        def _():
            for copy in lines(side, z, z, fi_n if side == 1 else z):
                copy.wait_recv()
            total[...] += coming[fi_n if side == 1 else z].astype(F32)
            if gated:
                gate_total[...] += gate_coming[side, z]

    if ends:
        held[...] = (total[...] + args[2][...] + args[3][...]).astype(BF16)
        start()
        keep.start()
    else:
        out_ref[...] = total[...]
    if gated:
        gate_out[...] = gate_total[...]
    yield
    if ends:
        relay()


    for target in range(fi_n):
        for side in (0, 1):

            @pl.when((z < target) if side == 0 else (z > target))
            def _():
                for copy in lines(side, target, *onward(side, target)):
                    copy.wait_send()

    for turn in range(z_part):

        @pl.when(jnp.logical_not(early) | (turn == z_part - 1))
        def _():
            sent_turn(turn)

    yield
    if ends:
        spread_settle()


def give_back_job(sizes, rows, token_slots, gates, bases=None):
    fi_n, ctx_n, tpx_n, tpc_n = (sizes[n] for n in ("fi", "ctx", "tpx", "tpc"))
    z_part, plane_n, chips = fi_n // tpc_n, ctx_n * tpx_n * tpc_n, ctx_n * tpx_n
    capacity, width = rows.shape[2:]
    quarter = width // (tpx_n * tpc_n)
    tokens = token_slots.shape[1]
    experts = fi_n * chips
    gated = gates is not None
    shapes = [jax.ShapeDtypeStruct((tokens, quarter), F32)]
    scratch = [
        pltpu.VMEM((fi_n, chips, capacity, quarter), BF16),
        pltpu.VMEM((tokens, quarter), F32),
        pltpu.VMEM((fi_n, tokens, quarter), BF16),
        pltpu.VMEM((fi_n + 1, tokens, quarter), BF16),
        pltpu.SemaphoreType.DMA((plane_n, z_part)),
        pltpu.SemaphoreType.DMA((plane_n, z_part)),
        pltpu.SemaphoreType.DMA((2, fi_n)),
        pltpu.SemaphoreType.DMA((2, fi_n)),
    ]
    args = [token_slots, rows]
    if gated:
        args.append(gates)
        shapes.append(jax.ShapeDtypeStruct((experts, tokens), F32))
        scratch += [
            pltpu.VMEM((fi_n, chips, 8, capacity), F32),
            pltpu.VMEM((experts, tokens), F32),
            pltpu.VMEM((fi_n, experts, tokens), F32),
            pltpu.VMEM((2, fi_n, experts, tokens), F32),
            pltpu.SemaphoreType.DMA((plane_n, z_part)),
            pltpu.SemaphoreType.DMA((plane_n, z_part)),
            pltpu.SemaphoreType.DMA((2, fi_n)),
            pltpu.SemaphoreType.DMA((2, fi_n)),
        ]
    specs = [VMEM_SPEC] + [HBM_SPEC] * (len(args) - 1)
    if bases is not None:
        args += list(bases)
        specs += [VMEM_SPEC] * 2
        shapes = [jax.ShapeDtypeStruct((tokens, width), BF16)]
        scratch += [pltpu.VMEM((tokens, quarter), BF16)] + tp_spread_sems(sizes)
    return {
        "args": list(zip(args, specs)),
        "outs": [(shape, HBM_SPEC if bases is not None else VMEM_SPEC) for shape in shapes],
        "scratch": scratch,
        "run": give_back_run,
    }


def collect_run(kinds, sizes, args, outs, scratch):
    fo_n, fi_n, ctx_n, tpx_n, tpc_n = (sizes[n] for n in ("fo", "fi", "ctx", "tpx", "tpc"))
    tp_n = tpx_n * tpc_n
    count = len(kinds)
    shards = args
    own_sem, line_send, line_recv, col_send, col_recv = scratch[:5]
    staged, spread_sems = scratch[5 : 5 + count * fo_n], scratch[5 + count * fo_n :]
    fo, z, y, x, c = (lax.axis_index(n) for n in ("fo", "fi", "ctx", "tpx", "tpc"))
    q = x * tpc_n + c

    items = [(i, f) for f in range(fo_n) for i in range(count)]

    def source(n):
        i, f = items[n]
        if kinds[i] == "share":
            a = shards[i].shape[1] // tp_n
            return shards[i].at[f, pl.ds(pl.multiple_of(q * a, a), a), :]
        return shards[i].at[f]

    def place(n, zb, yb):
        i, f = items[n]
        a, b = shards[i].shape[1:]
        block = (f * fi_n + zb) * ctx_n + yb
        if kinds[i] == "col":
            return outs[i].at[:, pl.ds(pl.multiple_of(block * b, b), b)]
        if kinds[i] == "share":
            return outs[i].at[block, q]
        return outs[i].at[pl.ds(pl.multiple_of(block * a, a), a), :]

    def parts_of(n):
        i, f = items[n]
        blocks = pl.ds(f * fi_n * ctx_n, fi_n * ctx_n)
        return lambda owner: outs[i].at[blocks, owner]

    spreads = {}
    for n, (i, f) in enumerate(items):
        if kinds[i] == "share":
            at = 5 * len(spreads)
            spreads[n] = tp_spread(
                sizes, parts_of(n)(q), None, parts_of(n), spread_sems[at : at + 5]
            )

    def line(n, side, step, first):
        block = z - step if side == 0 else z + step
        to = z + 1 if side == 0 else z - 1
        return pltpu.make_async_remote_copy(
            src_ref=source(n) if first else place(n, block, y),
            dst_ref=place(n, block, y),
            send_sem=line_send.at[n, side, step],
            recv_sem=line_recv.at[n, side, step],
            device_id=(fo, to, y, x, c),
            device_id_type=MESH_ID,
        )

    def sends(side, step):
        block = z - step if side == 0 else z + step
        to = z + 1 if side == 0 else z - 1
        return (block >= 0) & (block < fi_n) & (to >= 0) & (to < fi_n)

    def across(n, zb, dy, first=False):
        return pltpu.make_async_remote_copy(
            src_ref=source(n) if first else place(n, zb, y),
            dst_ref=place(n, zb, y),
            send_sem=col_send.at[n, zb, dy],
            recv_sem=col_recv.at[n, zb, dy],
            device_id=(fo, z, lax.rem(y + dy, ctx_n), x, c),
            device_id_type=MESH_ID,
        )

    def stage(n):
        return pltpu.make_async_copy(source(n), staged[n], own_sem.at[n, 0])

    def keep(n):
        return pltpu.make_async_copy(staged[n], place(n, z, y), own_sem.at[n, 1])

    for n in range(len(items)):
        for side in (0, 1):

            @pl.when(sends(side, 0))
            def _():
                line(n, side, 0, True).start()

        for dy in range(1, ctx_n):
            across(n, z, dy, True).start()
        stage(n).start()

    yield
    for n in range(len(items)):
        stage(n).wait()
        keep(n).start()

    for step in range(fi_n - 1):
        for n in range(len(items)):
            for side in (0, 1):
                block = z - 1 - step if side == 0 else z + 1 + step

                @pl.when((block >= 0) & (block < fi_n))
                def _():
                    pltpu.make_async_remote_copy(
                        src_ref=place(n, block, y),
                        dst_ref=place(n, block, y),
                        send_sem=line_send.at[n, side, step],
                        recv_sem=line_recv.at[n, side, step],
                        device_id=(fo, z, y, x, c),
                        device_id_type=MESH_ID,
                    ).wait_recv()
                    for dy in range(1, ctx_n):
                        across(n, block, dy).start()

                if step < fi_n - 2:

                    @pl.when(sends(side, step + 1))
                    def _():
                        line(n, side, step + 1, False).start()

        yield

    for n in range(len(items)):
        keep(n).wait()
        for dy in range(1, ctx_n):
            for zb in range(fi_n):
                pltpu.make_async_remote_copy(
                    src_ref=place(n, zb, y),
                    dst_ref=place(n, zb, lax.rem(y + ctx_n - dy, ctx_n)),
                    send_sem=col_send.at[n, zb, dy],
                    recv_sem=col_recv.at[n, zb, dy],
                    device_id=(fo, z, y, x, c),
                    device_id_type=MESH_ID,
                ).wait_recv()
        if n in spreads:
            spreads[n][0]()

    yield

    for n in spreads:
        spreads[n][2]()

    for n in range(len(items)):
        if n in spreads:
            spreads[n][3]()
        for side in (0, 1):
            for step in range(fi_n - 1):

                @pl.when(sends(side, step))
                def _():
                    line(n, side, step, step == 0).wait_send()

        for dy in range(1, ctx_n):
            for zb in range(fi_n):
                across(n, zb, dy).wait_send()


def collect_job(sizes, kinds, shards):
    fo_n, fi_n, ctx_n, tpx_n, tpc_n = (sizes[n] for n in ("fo", "fi", "ctx", "tpx", "tpc"))
    tp_n = tpx_n * tpc_n
    blocks = fo_n * fi_n * ctx_n
    outs, staged = [], []
    for kind, shard in zip(kinds, shards):
        _, a, b = shard.shape
        shape = (a, blocks * b) if kind == "col" else (blocks * a, b)
        if kind == "share":
            shape = (blocks, tp_n, a // tp_n, b)
        outs.append((jax.ShapeDtypeStruct(shape, shard.dtype), HBM_SPEC))
        staged.append(pltpu.VMEM((a // tp_n if kind == "share" else a, b), shard.dtype))
    n = len(kinds) * fo_n
    return {
        "args": [(shard, HBM_SPEC) for shard in shards],
        "outs": outs,
        "scratch": [
            pltpu.SemaphoreType.DMA((n, 2)),
            pltpu.SemaphoreType.DMA((n, 2, fi_n)),
            pltpu.SemaphoreType.DMA((n, 2, fi_n)),
            pltpu.SemaphoreType.DMA((n, fi_n, ctx_n)),
            pltpu.SemaphoreType.DMA((n, fi_n, ctx_n)),
        ]
        + staged * fo_n
        + tp_spread_sems(sizes) * (kinds.count("share") * fo_n),
        "run": functools.partial(collect_run, tuple(kinds)),
    }


def place_job(sizes, local):
    fo_n, fi_n, ctx_n, tpx_n, tpc_n = (sizes[n] for n in ("fo", "fi", "ctx", "tpx", "tpc"))
    chip_n = fi_n * ctx_n * tpx_n
    rows, depth = local.shape[3:]
    shape = (rows * tpx_n * tpc_n, depth * fo_n * fi_n * ctx_n)
    return {
        "args": [(local, HBM_SPEC)],
        "outs": [(jax.ShapeDtypeStruct(shape, BF16), HBM_SPEC)] * 3,
        "scratch": [pltpu.VMEM(local.shape, BF16)]
        + [pltpu.SemaphoreType.DMA((fo_n, 3, chip_n))] * 2
        + [pltpu.SemaphoreType.DMA((fo_n, 3, chip_n, tpc_n))] * 2,
        "run": place_run,
    }


def place_run(sizes, args, outs, scratch):
    fo_n, fi_n, ctx_n, tpx_n, tpc_n = (sizes[n] for n in ("fo", "fi", "ctx", "tpx", "tpc"))
    (local,) = args
    staged, load_sem, keep_sem, pair_send, pair_recv = scratch
    chip_n = fi_n * ctx_n * tpx_n
    rows, depth = local.shape[3:]
    fo, z, y, x, c = (lax.axis_index(n) for n in ("fo", "fi", "ctx", "tpx", "tpc"))

    def spot(k, f, chip, core):
        block = f * fi_n * ctx_n + chip // tpx_n
        return outs[k].at[
            pl.ds(pl.multiple_of((lax.rem(chip, tpx_n) * tpc_n + core) * rows, rows), rows),
            pl.ds(pl.multiple_of(block * depth, depth), depth),
        ]

    def load(f, k, chip):
        return pltpu.make_async_copy(
            local.at[f, chip, k], staged.at[f, chip, k], load_sem.at[f, k, chip]
        )

    def keep(f, k, chip):
        return pltpu.make_async_copy(
            staged.at[f, chip, k], spot(k, f, chip, c), keep_sem.at[f, k, chip]
        )

    def pair_copy(f, k, chip, dc, core):
        return pltpu.make_async_remote_copy(
            src_ref=local.at[f, chip, k],
            dst_ref=spot(k, f, chip, core),
            send_sem=pair_send.at[f, k, chip, dc],
            recv_sem=pair_recv.at[f, k, chip, dc],
            device_id=(fo, z, y, x, lax.rem(c + dc, tpc_n)),
            device_id_type=MESH_ID,
        )

    def launch(step, carry):
        f, chip = step // chip_n, lax.rem(step, chip_n)
        for k in range(3):
            load(f, k, chip).start()
            for dc in range(1, tpc_n):
                pair_copy(f, k, chip, dc, c).start()
        return carry

    def store(step, carry):
        f, chip = step // chip_n, lax.rem(step, chip_n)
        for k in range(3):
            load(f, k, chip).wait()
            keep(f, k, chip).start()
        return carry

    def settle(step, carry):
        f, chip = step // chip_n, lax.rem(step, chip_n)
        for k in range(3):
            keep(f, k, chip).wait()
            for dc in range(1, tpc_n):
                pair_copy(f, k, chip, dc, c).wait_send()
                pair_copy(f, k, chip, dc, lax.rem(c + tpc_n - dc, tpc_n)).wait_recv()
        return carry

    lax.fori_loop(0, fo_n * chip_n, launch, 0)
    yield
    lax.fori_loop(0, fo_n * chip_n, store, 0)
    yield
    lax.fori_loop(0, fo_n * chip_n, settle, 0)


def pair_job(sizes, grads):
    fo_n, fi_n, ctx_n, tpx_n, tpc_n = (sizes[n] for n in ("fo", "fi", "ctx", "tpx", "tpc"))
    rows = grads[0].shape[0] // (tpx_n * tpc_n)
    depth = grads[0].shape[1] // (fo_n * fi_n * ctx_n)
    total = fo_n * fi_n * ctx_n * tpx_n
    shape = (total, 3, rows, depth)
    return {
        "args": [(grad, HBM_SPEC) for grad in grads],
        "outs": [(jax.ShapeDtypeStruct(shape, BF16), HBM_SPEC)],
        "scratch": [pltpu.VMEM(shape, BF16)] * 2 + [pltpu.SemaphoreType.DMA((total, 3))] * 4,
        "run": pair_run,
    }


def pair_run(sizes, grads, outs, scratch):
    tpx_n, tpc_n = sizes["tpx"], sizes["tpc"]
    (out_ref,) = outs
    mine, theirs, load_sem, store_sem, send_sem, recv_sem = scratch
    total, _, rows, depth = mine.shape
    fo, z, y, x, c = (lax.axis_index(n) for n in ("fo", "fi", "ctx", "tpx", "tpc"))
    sibling = (fo, z, y, x, 1 - c)

    def spot(k, at, core):
        block, side = at // tpx_n, lax.rem(at, tpx_n)
        return grads[k].at[
            pl.ds(pl.multiple_of((side * tpc_n + core) * rows, rows), rows),
            pl.ds(pl.multiple_of(block * depth, depth), depth),
        ]

    def load(k, at):
        return pltpu.make_async_copy(spot(k, at, c), mine.at[at, k], load_sem.at[at, k])

    def store(k, at):
        return pltpu.make_async_copy(mine.at[at, k], out_ref.at[at, k], store_sem.at[at, k])

    def give(k, at):
        return pltpu.make_async_remote_copy(
            src_ref=spot(k, at, 1 - c),
            dst_ref=theirs.at[at, k],
            send_sem=send_sem.at[at, k],
            recv_sem=recv_sem.at[at, k],
            device_id=sibling,
            device_id_type=MESH_ID,
        )

    def launch(at, carry):
        for k in range(3):
            give(k, at).start()
            load(k, at).start()
        return carry

    def add(at, carry):
        for k in range(3):
            load(k, at).wait()
            give(k, at).wait_recv()
            mine[at, k] = (mine[at, k].astype(F32) + theirs[at, k].astype(F32)).astype(BF16)
            store(k, at).start()
        return carry

    def settle(at, carry):
        for k in range(3):
            give(k, at).wait_send()
            store(k, at).wait()
        return carry

    lax.fori_loop(0, total, launch, 0)
    yield
    lax.fori_loop(0, total, add, 0)
    yield
    lax.fori_loop(0, total, settle, 0)


def finish_run(kinds, sizes, args, outs, scratch):
    fi_n, ctx_n, tpx_n, tpc_n = (sizes[n] for n in ("fi", "ctx", "tpx", "tpc"))
    tp_n = tpx_n * tpc_n
    count = len(kinds)
    extra = len(args) - count
    parts, quarters = args[:count], args[count:]
    outs, wholes = outs[:count], outs[count:]
    mine, other, coming = (scratch[k * count : (k + 1) * count] for k in range(3))
    staged, (tiny, *sems) = scratch[3 * count : 3 * count + extra], scratch[3 * count + extra :]
    load_sem, col_send, col_recv, line_send, line_recv, tp_send, tp_recv = sems[:7]
    fo, z, y, x, c = (lax.axis_index(n) for n in ("fo", "fi", "ctx", "tpx", "tpc"))
    q = x * tpc_n + c

    spreads = [
        tp_spread(
            sizes,
            quarters[j],
            staged[j],
            columns_of(wholes[j], quarters[j].shape[1]),
            sems[8 + 5 * j : 13 + 5 * j],
        )
        for j in range(extra)
    ]

    def stage(j):
        return pltpu.make_async_copy(quarters[j], staged[j], sems[7].at[j])

    for j in range(extra):
        spreads[j][0]()
        stage(j).start()

    def view(n, zb, yb):
        a, b = mine[n].shape[1:]
        block = zb * ctx_n + yb
        if kinds[n] == "col":
            return parts[n].at[:, pl.ds(pl.multiple_of(block * b, b), b)]
        if kinds[n] == "share":
            return parts[n].at[pl.ds(pl.multiple_of(block * a * tp_n + q * a, a), a), :]
        return parts[n].at[pl.ds(pl.multiple_of(block * a, a), a), :]

    def across(n, zb, dy):
        to = lax.rem(y + dy, ctx_n)
        return pltpu.make_async_remote_copy(
            src_ref=view(n, zb, to),
            dst_ref=other[n].at[dy - 1, zb],
            send_sem=col_send.at[n, zb, dy],
            recv_sem=col_recv.at[n, zb, dy],
            device_id=(fo, z, to, x, c),
            device_id_type=MESH_ID,
        )

    def load(n, zb):
        return pltpu.make_async_copy(view(n, zb, y), mine[n].at[zb], load_sem.at[n, zb])

    def block_turn(turn):
        high_first = z < fi_n // 2
        place = jnp.where(high_first, fi_n - 1 - z, z)
        at = turn + (place <= turn).astype(jnp.int32)
        far = jnp.where(high_first, fi_n - 1 - at, at)
        return z if turn == fi_n - 1 else far

    def send_turn(turn):
        zb = block_turn(turn)
        for n in range(count):
            for dy in range(1, ctx_n):
                across(n, zb, dy).start()
            load(n, zb).start()

    def sent_turn(turn):
        for n in range(count):
            for dy in range(1, ctx_n):
                across(n, block_turn(turn), dy).wait_send()

    send_turn(0)
    yield
    send_turn(1)
    for j in range(extra):
        stage(j).wait()
        spreads[j][1].start()

    def line(n, side, target):
        at = jnp.where(target == (z + 1 if side == 0 else z - 1), fi_n, target) if side == 1 else target
        return pltpu.make_async_remote_copy(
            src_ref=mine[n].at[target],
            dst_ref=coming[n].at[at],
            send_sem=line_send.at[n, side, target],
            recv_sem=line_recv.at[n, side, target],
            device_id=(fo, z + 1 if side == 0 else z - 1, y, x, c),
            device_id_type=MESH_ID,
        )

    def came(n, side, target, at):
        pltpu.make_async_remote_copy(
            src_ref=mine[n].at[target],
            dst_ref=coming[n].at[at],
            send_sem=line_send.at[n, side, target],
            recv_sem=line_recv.at[n, side, target],
            device_id=(fo, z, y, x, c),
            device_id_type=MESH_ID,
        ).wait_recv()

    def ready(n, target):
        load(n, target).wait()
        for dy in range(1, ctx_n):
            across(n, target, dy).wait_recv()

    def add(n, target, use, store):
        a = mine[n].shape[1]
        tile = math.gcd(a, 64)

        def rows(step, carry):
            at = pl.ds(pl.multiple_of(step * tile, tile), tile)
            summed = mine[n][target, at, :].astype(F32)
            for dy in range(1, ctx_n):
                summed = summed + other[n][dy - 1, target, at, :].astype(F32)
            for slot in use:
                summed = summed + coming[n][slot, at, :].astype(F32)
            store(at, summed.astype(BF16))
            return carry

        lax.fori_loop(0, a // tile, rows, 0)

    for step in range(fi_n - 1):
        for n in range(count):
            for side in (0, 1):
                depth = z if side == 0 else fi_n - 1 - z
                target = fi_n - 1 - step + z if side == 0 else step - (fi_n - 1) + z
                passes, inner = depth <= step, depth > 0

                def back(at, values, n=n, target=target):
                    mine[n][target, at, :] = values

                @pl.when(passes & inner)
                def _():
                    ready(n, target)
                    came(n, side, target, target)
                    add(n, target, (target,), back)
                    line(n, side, target).start()

                @pl.when(passes & jnp.logical_not(inner))
                def _():
                    ready(n, target)
                    add(n, target, (), back)
                    line(n, side, target).start()

        if step + 2 < fi_n:
            sent_turn(step)
            send_turn(step + 2)
        yield

    for n in range(count):
        ready(n, z)

        def out(at, values, n=n):
            if kinds[n] == "share":
                a = mine[n].shape[1]
                outs[n][q, at, :] = values
            elif kinds[n] == "sum":
                tiny[q, at, :] = values
            else:
                outs[n][at, :] = values

        @pl.when(z > 0)
        def _():
            came(n, 0, z, z)

        @pl.when(z < fi_n - 1)
        def _():
            came(n, 1, z, fi_n)

        @pl.when((z > 0) & (z < fi_n - 1))
        def _():
            add(n, z, (z, fi_n), out)

        @pl.when((z == 0) & (z < fi_n - 1))
        def _():
            add(n, z, (fi_n,), out)

        @pl.when((z > 0) & (z == fi_n - 1))
        def _():
            add(n, z, (z,), out)

        @pl.when((z == 0) & (z == fi_n - 1))
        def _():
            add(n, z, (), out)

        if kinds[n] in ("share", "sum"):
            held = outs[n] if kinds[n] == "share" else tiny
            for step in range(1, tp_n):
                peer = lax.rem(q + step, tp_n)
                pltpu.make_async_remote_copy(
                    src_ref=held.at[q],
                    dst_ref=held.at[q],
                    send_sem=tp_send.at[n, step],
                    recv_sem=tp_recv.at[n, step],
                    device_id=(fo, z, y, peer // tpc_n, lax.rem(peer, tpc_n)),
                    device_id_type=MESH_ID,
                ).start()

    yield
    for j in range(extra):
        spreads[j][2]()

    for n in range(count):
        if kinds[n] in ("share", "sum"):
            held = outs[n] if kinds[n] == "share" else tiny
            for step in range(1, tp_n):
                origin = lax.rem(q + tp_n - step, tp_n)
                copy = pltpu.make_async_remote_copy(
                    src_ref=held.at[q],
                    dst_ref=held.at[origin],
                    send_sem=tp_send.at[n, step],
                    recv_sem=tp_recv.at[n, step],
                    device_id=(fo, z, y, x, c),
                    device_id_type=MESH_ID,
                )
                copy.wait_send()
                copy.wait_recv()
            if kinds[n] == "sum":
                summed = tiny[0].astype(F32)
                for k in range(1, tp_n):
                    summed = summed + tiny[k].astype(F32)
                outs[n][...] = summed.astype(BF16)
        for target in range(fi_n):
            for side in (0, 1):

                @pl.when((z < target) if side == 0 else (z > target))
                def _():
                    line(n, side, target).wait_send()

    for turn in range(fi_n - 2, fi_n):
        sent_turn(turn)
    for j in range(extra):
        spreads[j][3]()


def finish_job(sizes, kinds, parts, quarters):
    fi_n, ctx_n, tpx_n, tpc_n = (sizes[n] for n in ("fi", "ctx", "tpx", "tpc"))
    tp_n = tpx_n * tpc_n
    blocks = fi_n * ctx_n
    count, extra = len(kinds), len(quarters)
    own, shapes = [], []
    sum_shape = (16, 256)
    for kind, part in zip(kinds, parts):
        a, b = part.shape
        if kind == "col":
            own.append((a, b // blocks))
            shapes.append(own[-1])
        elif kind == "share":
            own.append((a // (blocks * tp_n), b))
            shapes.append((tp_n,) + own[-1])
        else:
            own.append((a // blocks, b))
            shapes.append(own[-1])
        if kind == "sum":
            sum_shape = own[-1]
    wide = [(v.shape[0], v.shape[1] * tp_n) for v in quarters]
    some = max(extra, 1)
    shapes = [jax.ShapeDtypeStruct(shape, BF16) for shape in shapes + wide]
    return {
        "args": [(arg, HBM_SPEC) for arg in (*parts, *quarters)],
        "outs": list(zip(shapes, [VMEM_SPEC] * count + [HBM_SPEC] * extra)),
        "scratch": [pltpu.VMEM((fi_n,) + s, BF16) for s in own]
        + [pltpu.VMEM((max(ctx_n - 1, 1), fi_n) + s, BF16) for s in own]
        + [pltpu.VMEM((fi_n + 1,) + s, BF16) for s in own]
        + [pltpu.VMEM(v.shape, BF16) for v in quarters]
        + [
            pltpu.VMEM((tp_n,) + sum_shape, BF16),
            pltpu.SemaphoreType.DMA((count, fi_n)),
            pltpu.SemaphoreType.DMA((count, fi_n, ctx_n)),
            pltpu.SemaphoreType.DMA((count, fi_n, ctx_n)),
            pltpu.SemaphoreType.DMA((count, 2, fi_n)),
            pltpu.SemaphoreType.DMA((count, 2, fi_n)),
            pltpu.SemaphoreType.DMA((count, tp_n)),
            pltpu.SemaphoreType.DMA((count, tp_n)),
            pltpu.SemaphoreType.DMA((some,)),
            *(tp_spread_sems(sizes) * extra),
        ],
        "run": functools.partial(finish_run, tuple(kinds)),
    }


def products_job(sizes, lefts, rights, which):
    slots, hidden = lefts[0].shape
    width = rights[0].shape[1]
    tile = min(384, hidden)
    return {
        "args": [(arg, HBM_SPEC) for arg in (*lefts, *rights)],
        "outs": [(jax.ShapeDtypeStruct((hidden, width), BF16), HBM_SPEC)] * len(lefts),
        "scratch": [
            pltpu.VMEM((2, slots, tile), BF16),
            pltpu.VMEM((tile, slots), BF16),
            pltpu.VMEM((slots, width), BF16),
            pltpu.VMEM((2, tile, width), BF16),
            pltpu.SemaphoreType.DMA((2,)),
            pltpu.SemaphoreType.DMA,
            pltpu.SemaphoreType.DMA((2,)),
        ],
        "run": functools.partial(products_run, tuple(which), tile),
    }


def products_run(which, tile, sizes, args, outs, scratch):
    left_buf, turned, right_buf, out_buf, left_sem, right_sem, out_sem = scratch
    count = len(outs)
    lefts, rights = args[:count], args[count:]
    hidden = lefts[0].shape[1]
    width = right_buf.shape[1]
    cells = [(k, at, min(tile, hidden - at)) for k in range(count) for at in range(0, hidden, tile)]

    def load(n):
        k, at, size = cells[n]
        return pltpu.make_async_copy(
            lefts[k].at[:, pl.ds(at, size)],
            left_buf.at[n % 2, :, pl.ds(0, size)],
            left_sem.at[n % 2],
        )

    def fetch(k):
        return pltpu.make_async_copy(rights[which[k]], right_buf, right_sem)

    def store(n):
        k, at, size = cells[n]
        return pltpu.make_async_copy(
            out_buf.at[n % 2, pl.ds(0, size), :],
            outs[k].at[pl.ds(at, size), :],
            out_sem.at[n % 2],
        )

    columns = min(512, width)

    def products():
        for n, (k, at, size) in enumerate(cells):
            load(n).wait()
            if n + 1 < len(cells):
                load(n + 1).start()
            if at == 0 and (k == 0 or which[k] != which[k - 1]):
                if k > 0:
                    fetch(k).start()
                fetch(k).wait()
            if n >= 2:
                store(n - 2).wait()
            turned[pl.ds(0, size), :] = left_buf[n % 2, :, :size].T

            def one(step, carry, n=n, size=size):
                here = pl.ds(pl.multiple_of(step * columns, columns), columns)
                out_buf[n % 2, pl.ds(0, size), here] = jnp.dot(
                    turned[:size, :], right_buf[:, here], preferred_element_type=F32
                ).astype(BF16)
                return carry

            lax.fori_loop(0, width // columns, one, 0)
            store(n).start()
        for n in range(max(len(cells) - 2, 0), len(cells)):
            store(n).wait()

    fi_n = sizes["fi"]
    z = lax.axis_index("fi")
    inner = (z > 0) & (z < fi_n - 1)
    fetch(0).start()
    load(0).start()
    for phase in range(1, fi_n):
        yield
        if phase == 1:
            pl.when(inner)(products)
        if phase == fi_n - 1:
            pl.when(jnp.logical_not(inner))(products)


def reduce_job(sizes, both, parts):
    ctx_n, tpx_n, tpc_n = (sizes[n] for n in ("ctx", "tpx", "tpc"))
    tp_n = tpx_n * tpc_n
    tokens, quarter = parts.shape[1:]
    wide = both.shape[1]
    piece = (ctx_n, tokens // tp_n, wide)
    return {
        "args": [(both.reshape(ctx_n, tokens, wide), HBM_SPEC), (parts, HBM_SPEC)],
        "outs": [
            (jax.ShapeDtypeStruct((tokens, wide), BF16), VMEM_SPEC),
            (jax.ShapeDtypeStruct((tokens, quarter), F32), VMEM_SPEC),
        ],
        "scratch": [
            pltpu.VMEM((3, tpx_n) + piece, BF16),
            pltpu.VMEM((3, tpx_n, tokens, quarter), BF16),
            pltpu.VMEM((ctx_n,) + piece[1:], BF16),
            pltpu.SemaphoreType.DMA((2, tpx_n)),
            pltpu.SemaphoreType.DMA((2, tpx_n)),
            pltpu.SemaphoreType.DMA((2, tpx_n)),
            pltpu.SemaphoreType.DMA((2, tpx_n)),
            pltpu.SemaphoreType.DMA((2, tpx_n)),
            pltpu.SemaphoreType.DMA((2, ctx_n)),
            pltpu.SemaphoreType.DMA((2, tp_n)),
        ],
        "run": reduce_run,
    }


def reduce_run(sizes, args, outs, scratch):
    ctx_n, tpx_n, tpc_n = (sizes[n] for n in ("ctx", "tpx", "tpc"))
    tp_n = tpx_n * tpc_n
    both_ref, parts_ref = args
    both_out, parts_out = outs
    both_buf, parts_buf, halves = scratch[:3]
    load_sem, core_send, core_recv, x_send, x_recv, y_sem, tp_sem = scratch[3:]
    rows = halves.shape[1]
    fo, z, y, x, c = (lax.axis_index(n) for n in ("fo", "fi", "ctx", "tpx", "tpc"))
    q = x * tpc_n + c
    bufs = (both_buf, parts_buf)

    def view(kind, side, core):
        to = side * tpc_n + core
        if kind == 0:
            return both_ref.at[:, pl.ds(pl.multiple_of(to * rows, rows), rows), :]
        return parts_ref.at[to]

    def load(kind, side):
        return pltpu.make_async_copy(
            view(kind, side, c), bufs[kind].at[0, side], load_sem.at[kind, side]
        )

    def to_core(kind, side):
        return pltpu.make_async_remote_copy(
            src_ref=view(kind, side, 1 - c),
            dst_ref=bufs[kind].at[1, side],
            send_sem=core_send.at[kind, side],
            recv_sem=core_recv.at[kind, side],
            device_id=(fo, z, y, x, 1 - c),
            device_id_type=MESH_ID,
        )

    def to_chip(kind, side, slot):
        return pltpu.make_async_remote_copy(
            src_ref=bufs[kind].at[0, side],
            dst_ref=bufs[kind].at[2, slot],
            send_sem=x_send.at[kind, side],
            recv_sem=x_recv.at[kind, slot],
            device_id=(fo, z, y, side, c),
            device_id_type=MESH_ID,
        )

    def side_of(dx):
        return lax.rem(x + dx, tpx_n)

    def add(kind, side):
        count = bufs[kind].shape[2] if kind == 1 else bufs[kind].shape[3]
        tile = math.gcd(count, 64)

        def one(step, carry):
            at = pl.ds(pl.multiple_of(step * tile, tile), tile)
            if kind == 1:
                mine, other = parts_buf[0, side, at, :], parts_buf[1, side, at, :]
                parts_buf[0, side, at, :] = (mine.astype(F32) + other.astype(F32)).astype(BF16)
            else:
                for half in range(ctx_n):
                    mine = both_buf[0, side, half, at, :]
                    other = both_buf[1, side, half, at, :]
                    both_buf[0, side, half, at, :] = (
                        mine.astype(F32) + other.astype(F32)
                    ).astype(BF16)
            return carry

        lax.fori_loop(0, count // tile, one, 0)

    order = list(range(1, tpx_n)) + [0]
    for kind in (0, 1):
        for dx in order:
            to_core(kind, side_of(dx)).start()
            load(kind, side_of(dx)).start()
    yield
    for kind in (0, 1):
        for dx in order:
            side = side_of(dx)
            load(kind, side).wait()
            to_core(kind, side).wait_recv()
            add(kind, side)
            if dx > 0:
                to_chip(kind, side, x).start()
    yield

    for dx in range(1, tpx_n):
        to_chip(0, side_of(dx), side_of(dx)).wait_recv()
    tile = math.gcd(rows, 64)

    def over_x(step, carry):
        at = pl.ds(pl.multiple_of(step * tile, tile), tile)
        for half in range(ctx_n):
            summed = both_buf[0, x, half, at, :].astype(F32)
            for dx in range(1, tpx_n):
                summed = summed + both_buf[2, side_of(dx), half, at, :].astype(F32)
            both_buf[0, x, half, at, :] = summed.astype(BF16)
        return carry

    lax.fori_loop(0, rows // tile, over_x, 0)

    def to_y(dy, half, slot):
        return pltpu.make_async_remote_copy(
            src_ref=both_buf.at[0, x, half],
            dst_ref=halves.at[slot],
            send_sem=y_sem.at[0, dy],
            recv_sem=y_sem.at[1, dy],
            device_id=(fo, z, half, x, c),
            device_id_type=MESH_ID,
        )

    for dy in range(1, ctx_n):
        to_y(dy, lax.rem(y + dy, ctx_n), y).start()
    yield
    for dy in range(1, ctx_n):
        source = lax.rem(y + ctx_n - dy, ctx_n)
        to_y(dy, y, source).wait_recv()

    def over_y(step, carry):
        at = pl.ds(pl.multiple_of(step * tile, tile), tile)
        summed = both_buf[0, x, y, at, :].astype(F32)
        for dy in range(1, ctx_n):
            summed = summed + halves[lax.rem(y + ctx_n - dy, ctx_n), at, :].astype(F32)
        both_out[pl.ds(pl.multiple_of(q * rows + step * tile, tile), tile), :] = summed.astype(BF16)
        return carry

    lax.fori_loop(0, rows // tile, over_y, 0)

    def to_tp(step, owner):
        peer = lax.rem(q + step, tp_n)
        held = both_out.at[pl.ds(pl.multiple_of(owner * rows, rows), rows), :]
        return pltpu.make_async_remote_copy(
            src_ref=both_out.at[pl.ds(pl.multiple_of(q * rows, rows), rows), :],
            dst_ref=held,
            send_sem=tp_sem.at[0, step],
            recv_sem=tp_sem.at[1, step],
            device_id=(fo, z, y, peer // tpc_n, lax.rem(peer, tpc_n)),
            device_id_type=MESH_ID,
        )

    for step in range(1, tp_n):
        to_tp(step, q).start()
    yield
    for dx in range(1, tpx_n):
        to_chip(1, side_of(dx), side_of(dx)).wait_recv()
    tall = math.gcd(parts_out.shape[0], 64)

    def last(step, carry):
        at = pl.ds(pl.multiple_of(step * tall, tall), tall)
        summed = parts_buf[0, x, at, :].astype(F32)
        for dx in range(1, tpx_n):
            summed = summed + parts_buf[2, side_of(dx), at, :].astype(F32)
        parts_out[at, :] = summed
        return carry

    lax.fori_loop(0, parts_out.shape[0] // tall, last, 0)
    for step in range(1, tp_n):
        to_tp(step, q).wait_send()
        to_tp(step, lax.rem(q + tp_n - step, tp_n)).wait_recv()
    for dy in range(1, ctx_n):
        to_y(dy, lax.rem(y + dy, ctx_n), y).wait_send()
    for kind in (0, 1):
        for dx in range(tpx_n):
            to_core(kind, side_of(dx)).wait_send()
            if dx > 0:
                to_chip(kind, side_of(dx), x).wait_send()


def attend_body(place_ref, q_ref, kv_ref, rope_ref, out_ref, log_ref):
    block_rows, key_count = q_ref.shape[0], kv_ref.shape[0]
    first = place_ref[0] + pl.program_id(1) * block_rows
    keys = jnp.concatenate([kv_ref[:, :NOPE], rope_ref[...]], axis=1)
    scores = dot_nt(q_ref[...], keys)
    row = first + lax.broadcasted_iota(jnp.int32, (block_rows, 1), 0)
    limit = jnp.maximum(row, place_ref[1] - 1)
    key = lax.broadcasted_iota(jnp.int32, (block_rows, key_count), 1)
    scores = jnp.where(key <= limit, scores, -1e30)
    top = jnp.max(scores, axis=1, keepdims=True)
    exponent = jnp.exp(scores - top)
    row_total = jnp.sum(exponent, axis=1, keepdims=True)
    summed = jnp.dot(exponent.astype(BF16), kv_ref[:, NOPE:], preferred_element_type=F32)
    out_ref[...] = (summed / row_total).astype(BF16)
    log_total = jnp.broadcast_to(top + jnp.log(row_total), (block_rows, 128))
    log_ref[0] = log_total.T[:1]

def attend(place, query, key_value, rope, block_rows):
    rows, key_count = query.shape[0], key_value.shape[0]
    heads = query.shape[1] // HEAD
    return pl.pallas_call(
        attend_body,
        out_shape=(jax.ShapeDtypeStruct((rows, heads * VDIM), BF16), jax.ShapeDtypeStruct((heads, 1, rows), F32)),
        grid_spec=pltpu.PrefetchScalarGridSpec(
            num_scalar_prefetch=1,
            grid=(heads, rows // block_rows),
            in_specs=[
                pl.BlockSpec((block_rows, HEAD), lambda h, i, s: (i, h)),
                pl.BlockSpec((key_count, HEAD), lambda h, i, s: (0, h)),
                pl.BlockSpec((key_count, NOPE), lambda h, i, s: (0, 0)),
            ],
            out_specs=[
                pl.BlockSpec((block_rows, VDIM), lambda h, i, s: (i, h)),
                pl.BlockSpec((1, 1, block_rows), lambda h, i, s: (h, 0, i)),
            ],
        ),
        compiler_params=pltpu.CompilerParams(vmem_limit_bytes=48 << 20),
        cost_estimate=pl.CostEstimate(flops=4 * rows * key_count * heads * HEAD, bytes_accessed=20_000_000, transcendentals=rows * key_count * heads),
        name="attend",
    )(place, query, key_value, rope)

def attend_back_body(place_ref, q_ref, kv_ref, rope_ref, dout_ref, log_ref, table_ref, dq_ref, dkv_ref, drope_ref, keys_acc, values_acc):
    block_rows, key_count = q_ref.shape[0], kv_ref.shape[0]
    head, step = pl.program_id(0), pl.program_id(1)
    first = place_ref[0] + step * block_rows
    keys = jnp.concatenate([kv_ref[:, :NOPE], rope_ref[...]], axis=1)
    scores = dot_nt(keys, q_ref[...])
    row = first + lax.broadcasted_iota(jnp.int32, (1, block_rows), 1)
    limit = jnp.maximum(row, place_ref[1] - 1)
    key = lax.broadcasted_iota(jnp.int32, (key_count, block_rows), 0)
    soft = jnp.exp(jnp.where(key <= limit, scores, -1e30) - log_ref[0])
    soft_grad = dot_nt(kv_ref[:, NOPE:], dout_ref[...])
    mean = jnp.sum(soft * soft_grad, axis=0, keepdims=True)
    score_grad = (soft * (soft_grad - mean)).astype(BF16)
    values = jnp.dot(soft.astype(BF16), dout_ref[...], preferred_element_type=F32)
    keys_grad = jnp.dot(score_grad, q_ref[...], preferred_element_type=F32)
    dq_ref[...] = (dot_tn(score_grad, keys) * table_ref[...]).astype(BF16)

    @pl.when(step == 0)
    def _():
        keys_acc[...] = keys_grad
        values_acc[...] = values

    @pl.when(step > 0)
    def _():
        keys_acc[...] += keys_grad
        values_acc[...] += values

    @pl.when(step == pl.num_programs(1) - 1)
    def _():
        dkv_ref[...] = jnp.concatenate([keys_acc[:, :NOPE], values_acc[...]], axis=1).astype(BF16)

        @pl.when(head == 0)
        def _():
            drope_ref[...] = keys_acc[:, NOPE:]

        @pl.when(head > 0)
        def _():
            drope_ref[...] += keys_acc[:, NOPE:]

def attend_back(place, query, key_value, rope, dout, log_total, table, block_rows):
    rows, key_count = query.shape[0], key_value.shape[0]
    heads = query.shape[1] // HEAD
    return pl.pallas_call(
        attend_back_body,
        out_shape=(jax.ShapeDtypeStruct((rows, heads * HEAD), BF16), jax.ShapeDtypeStruct((key_count, heads * HEAD), BF16), jax.ShapeDtypeStruct((key_count, NOPE), F32)),
        grid_spec=pltpu.PrefetchScalarGridSpec(
            num_scalar_prefetch=1,
            grid=(heads, rows // block_rows),
            in_specs=[
                pl.BlockSpec((block_rows, HEAD), lambda h, i, s: (i, h)),
                pl.BlockSpec((key_count, HEAD), lambda h, i, s: (0, h)),
                pl.BlockSpec((key_count, NOPE), lambda h, i, s: (0, 0)),
                pl.BlockSpec((block_rows, VDIM), lambda h, i, s: (i, h)),
                pl.BlockSpec((1, 1, block_rows), lambda h, i, s: (h, 0, i)),
                pl.BlockSpec((block_rows, HEAD), lambda h, i, s: (i, 0)),
            ],
            out_specs=[
                pl.BlockSpec((block_rows, HEAD), lambda h, i, s: (i, h)),
                pl.BlockSpec((key_count, HEAD), lambda h, i, s: (0, h)),
                pl.BlockSpec((key_count, NOPE), lambda h, i, s: (0, 0)),
            ],
            scratch_shapes=[pltpu.VMEM((key_count, HEAD), F32), pltpu.VMEM((key_count, VDIM), F32)],
        ),
        compiler_params=pltpu.CompilerParams(vmem_limit_bytes=56 << 20),
        cost_estimate=pl.CostEstimate(
            flops=10 * rows * key_count * heads * HEAD,
            bytes_accessed=40_000_000,
            transcendentals=rows * key_count * heads,
        ),
        name="attend_back",
    )(place, query, key_value, rope, dout, log_total, table)


def build(sizes):
    fo_n, fi_n, ctx_n, tpx_n, tpc_n = (sizes[name] for name in ("fo", "fi", "ctx", "tpx", "tpc"))
    tp_n = tpx_n * tpc_n
    row_shards = fo_n * fi_n * ctx_n
    plane_experts = ctx_n * tpx_n
    z_part = fi_n // tpc_n

    def expert_weights(gate, up, down):
        local = jnp.stack([gate.transpose(0, 2, 1), up.transpose(0, 2, 1), down], axis=1)
        return lax.all_gather(local, "fo", axis=0) if fo_n > 1 else local[None]

    def shard_of(weight):
        return lax.all_gather(weight, "fo", axis=0) if fo_n > 1 else weight[None]

    def fo_sum(part, kind):
        if fo_n == 1:
            return part
        if kind == "col":
            a = part.shape[0]
            part = part.reshape(a, fo_n, -1)
            return lax.psum_scatter(part, "fo", scatter_dimension=1, tiled=True).reshape(a, -1)
        return lax.psum_scatter(part, "fo", scatter_dimension=0, tiled=True)

    def own_expert_grads(mine):
        mine = mine.reshape((fo_n, -1) + mine.shape[1:])
        got = lax.all_to_all(mine, CHIPS, split_axis=1, concat_axis=1, tiled=True)
        if fo_n > 1:
            got = lax.psum_scatter(got, "fo", scatter_dimension=0, tiled=True)
        got = got[0].astype(F32)
        return (got[:, 0].transpose(0, 2, 1), got[:, 1].transpose(0, 2, 1), got[:, 2])

    def shards(
        tokens,
        out_grad,
        routes,
        slot_index,
        prefix,
        attn_gain,
        query_weight,
        latent_down,
        latent_gain,
        latent_up,
        out_weight,
        moe_gain,
        router_weight,
        shared_gate,
        shared_up,
        shared_down,
        expert_gate,
        expert_up,
        expert_down,
    ):
        row_count, width = tokens.shape
        expert_count = expert_gate.shape[0]
        capacity = row_count * routes.shape[1] // expert_count
        quarter = width // tp_n
        tp_index = lax.axis_index(TP)
        own_expert = lax.axis_index(CHIPS)
        plane_base = lax.axis_index("fi") * plane_experts

        def columns(values):
            return lax.dynamic_slice_in_dim(values, tp_index * quarter, quarter, values.ndim - 1)

        depth = latent_down.shape[0]
        down_width = latent_down.shape[1]

        def turned(weight):
            half = weight.shape[-1] // 2
            return jnp.concatenate([-weight[..., half:], weight[..., :half]], axis=-1)

        small = jnp.concatenate(
            [
                latent_down,
                turned(latent_down[:, KVR:]),
                attn_gain[:, None],
                moe_gain[:, None],
                jnp.pad(latent_gain, (0, depth - latent_gain.shape[0]))[:, None],
                router_weight,
            ],
            axis=1,
        )
        used = small.shape[1]
        small = jnp.pad(small, ((0, 0), (0, -used % 128)))
        keys = jnp.where(slot_index < capacity, routes * capacity + slot_index, -1).T
        keys = jnp.pad(keys, ((0, 8 - keys.shape[0]), (0, 0)), constant_values=-1)
        (small, query_full, up_full, out_full, keys_all), *_ = exchange(
            sizes,
            [
                collect_job(
                    sizes,
                    ("share", "row", "row", "col", "row"),
                    [shard_of(w) for w in (small, query_weight, latent_up, out_weight, keys)],
                )
            ],
            4,
            "collect_attention",
        )
        local_weights, small = lax.optimization_barrier(
            (expert_weights(expert_gate, expert_up, expert_down), small)
        )
        routed_weights = lax.all_to_all(
            local_weights, CHIPS, split_axis=1, concat_axis=1, tiled=True
        )
        small = small.reshape(row_shards * depth, -1)
        wide_down = small[:, : down_width + ROPE]
        down_full = small[:, :down_width]
        gain_at = down_width + ROPE
        gain_one = small[:, gain_at].astype(F32)
        gain_two = small[:, gain_at + 1].astype(F32)
        gain_latent = (
            small[:, gain_at + 2]
            .reshape(row_shards, depth)[:, : latent_gain.shape[0]]
            .reshape(-1)
            .astype(F32)
        )
        router_full = small[:, gain_at + 3 : used]

        keys_all = lax.dynamic_slice_in_dim(
            keys_all, lax.axis_index("fo") * (fi_n * ctx_n * 8), fi_n * ctx_n * 8, 0
        ).reshape(fi_n, ctx_n, 8, row_count)
        keys_column = lax.dynamic_index_in_dim(keys_all, lax.axis_index("ctx"), 1, keepdims=False)
        first_keys = (plane_base + jnp.arange(plane_experts, dtype=jnp.int32)) * capacity
        rel = keys_column[:, None] - first_keys[:, None, None]
        plane_slots = jnp.max(jnp.where((rel >= 0) & (rel < capacity), rel, -1), axis=2)
        token_slots = plane_slots.transpose(0, 2, 1)

        def give_back(rows, gates, bases=None):
            rows = rows.reshape(z_part, ctx_n, capacity, width)
            return give_back_job(sizes, rows, token_slots, gates, bases)

        (slot_grads,), (shared_gate_full, shared_up_full, shared_down_full) = exchange(
            sizes,
            [
                dispatch_job(sizes, columns(out_grad), plane_slots, capacity),
                collect_job(
                    sizes,
                    ("row", "row", "col"),
                    [shard_of(w) for w in (shared_gate, shared_up, shared_down)],
                ),
            ],
            0,
            "dispatch_grads",
        )
        slot_grads = slot_grads.reshape(-1, width)

        head_count = query_full.shape[1] // (NOPE + ROPE)
        hidden = tokens.astype(F32)
        scale_one = rms_scale(hidden)
        normed_one = hidden * scale_one
        normed_in = (normed_one * gain_one).astype(BF16)
        seq_index = lax.axis_index(("fo", "fi"))
        prefix_len = lax.dynamic_index_in_dim(prefix, seq_index, keepdims=False)
        row_offset = lax.axis_index("ctx") * row_count
        query_pos = row_offset + jnp.arange(row_count, dtype=jnp.int32)
        cos_table, sin_table = rotation_tables(query_pos, ROPE // 2)
        score_scale = (NOPE + ROPE) ** (-0.5)
        cos_wide = jnp.concatenate([cos_table, cos_table], axis=1)
        sin_wide = jnp.concatenate([sin_table, sin_table], axis=1)
        table = score_scale * jnp.concatenate(
            [jnp.ones((row_count, NOPE), F32), cos_wide, sin_wide], axis=1
        )

        latent_raw = dot(normed_in, wide_down)
        latent_part = latent_raw[:, :KVR]
        scale_latent = rms_scale(latent_part)
        normed_latent = latent_part * scale_latent
        latent = (normed_latent * gain_latent).astype(BF16)
        key_rope = (
            latent_raw[:, KVR : KVR + ROPE] * cos_wide + latent_raw[:, KVR + ROPE :] * sin_wide
        ).astype(BF16)
        both = lax.all_gather(
            jnp.concatenate([latent, key_rope, key_rope], axis=1), "ctx", axis=0, tiled=True
        )
        latent_all, rope_all = both[:, :KVR], both[:, KVR:]
        query_heads = query_full.reshape(width, head_count, NOPE + ROPE)
        query_wide = jnp.concatenate(
            [query_heads, turned(query_heads[..., NOPE:])], axis=-1
        ).reshape(width, head_count * HEAD)
        query_in = (
            dot(normed_in, query_wide).reshape(row_count, head_count, HEAD) * table[:, None]
        ).astype(BF16).reshape(row_count, head_count * HEAD)
        key_value = dot(latent_all, up_full).astype(BF16)
        place = jnp.stack([row_offset, prefix_len]).astype(jnp.int32)
        block_rows = min(256, row_count)
        attended, log_totals = attend(place, query_in, key_value, rope_all, block_rows)

        def tp_scatter(parts):
            parts = jnp.stack([part.astype(BF16) for part in parts])
            return lax.psum_scatter(parts, TP, scatter_dimension=0, tiled=True)[0].astype(F32)

        def quarters(weight, axis):
            return jnp.split(weight, tp_n, axis=axis)

        attn_out = tp_scatter([dot(attended, part) for part in quarters(out_full, 1)])
        attn_out, slot_grads = lax.optimization_barrier((attn_out, slot_grads))
        residual = columns(tokens).astype(F32) + attn_out
        scale_two = lax.rsqrt(
            lax.psum(jnp.sum(residual * residual, axis=-1, keepdims=True), TP) / width + EPSILON
        )
        normed_two = residual * scale_two
        gain_two_part = columns(gain_two[None])
        mid_part = (normed_two * gain_two_part).astype(BF16)

        (slot_rows,), (gate_full, expert_up_full, down_weight), (normed_mid,) = exchange(
            sizes,
            [
                dispatch_job(sizes, mid_part, plane_slots, capacity),
                place_job(sizes, routed_weights),
                spread_job(sizes, mid_part),
            ],
            1,
            "dispatch_rows",
        )
        slot_rows = slot_rows.reshape(-1, width)

        logits = dot(normed_mid, router_full)
        router_prob = jax.nn.softmax(logits, axis=-1)
        slot_prob = jax.nn.softmax(dot(slot_rows, router_full), axis=-1)
        slot_gate = lax.dynamic_slice_in_dim(slot_prob, own_expert, 1, 1)

        gate_pre = dot(normed_mid, shared_gate_full)
        up_pre = dot(normed_mid, shared_up_full)
        shared_dact = dot_nt(out_grad, shared_down_full)
        shared_silu, shared_slope = silu_parts(gate_pre)
        shared_act = (shared_silu * up_pre).astype(BF16)
        shared_dgate = (shared_dact * up_pre * shared_slope).astype(BF16)
        shared_dup = (shared_dact * shared_silu).astype(BF16)
        mid_shared = tp_scatter(
            [
                dot_nt(shared_dgate, gate_part) + dot_nt(shared_dup, up_part)
                for gate_part, up_part in zip(
                    quarters(shared_gate_full, 0), quarters(shared_up_full, 0)
                )
            ]
        )
        out_shared = tp_scatter([dot(shared_act, part) for part in quarters(shared_down_full, 1)])

        expert_dact_raw = dot_nt(slot_grads, down_weight)
        expert_gpre = dot_nt(slot_rows, gate_full)
        expert_upre = dot_nt(slot_rows, expert_up_full)
        expert_silu, expert_slope = silu_parts(expert_gpre)
        expert_act_wide = expert_silu * expert_upre
        expert_act = expert_act_wide.astype(BF16)
        slot_gate_grad = jnp.sum(expert_act.astype(F32) * expert_dact_raw, axis=-1)
        expert_dact = expert_dact_raw * slot_gate
        expert_dgate = (expert_dact * expert_upre * expert_slope).astype(BF16)
        expert_dup = (expert_dact * expert_silu).astype(BF16)
        slot_drows = dot(expert_dgate, gate_full) + dot(expert_dup, expert_up_full)
        gate_rows = jnp.broadcast_to(
            slot_gate_grad.reshape(z_part, ctx_n, 1, capacity), (z_part, ctx_n, 8, capacity)
        )
        sdown_grad = dot_tn(shared_act, out_grad)
        sgate_grad = dot_tn(normed_mid, shared_dgate)
        sup_grad = dot_tn(normed_mid, shared_dup)
        shared_kinds = ("row", "row", "col")
        shared_parts = [
            fo_sum(part.astype(BF16), kind)
            for part, kind in zip((sgate_grad, sup_grad, sdown_grad), shared_kinds)
        ]
        slot_dout = (slot_grads.astype(F32) * slot_gate).astype(BF16)
        shared_own, (mid_routed, prob_grad), expert_grads = exchange(
            sizes,
            [
                finish_job(sizes, shared_kinds, shared_parts, []),
                give_back(slot_drows.astype(BF16), gate_rows),
                products_job(
                    sizes,
                    [expert_dgate, expert_dup, expert_act],
                    [slot_rows, slot_dout],
                    [0, 0, 1],
                ),
            ],
            2,
            "give_back_rows",
            vmem=60,
        )
        sgate_grad, sup_grad, sdown_grad = (part.astype(F32) for part in shared_own)
        prob_grad = prob_grad.T
        logit_grad = (
            router_prob * (prob_grad - jnp.sum(router_prob * prob_grad, axis=-1, keepdims=True))
        ).astype(BF16)

        mid_routed, mid_shared, out_shared = lax.optimization_barrier(
            (mid_routed, mid_shared, out_shared)
        )
        mid_total = mid_shared + mid_routed + dot_nt(logit_grad, columns(router_full.T).T)
        gain_two_grad = jnp.sum(mid_total * normed_two, axis=0)
        dn_two = mid_total * gain_two_part
        dot_two = lax.psum(jnp.sum(dn_two * normed_two, axis=-1, keepdims=True), TP) / width
        residual_grad = columns(out_grad).astype(F32) + scale_two * (dn_two - normed_two * dot_two)
        (routed_grads,), (attn_dout,) = exchange(
            sizes,
            [pair_job(sizes, expert_grads), spread_job(sizes, residual_grad.astype(BF16))],
            7,
            "pair_sum",
        )

        out_weight_grad = dot_tn(attended, attn_dout)
        attended_grad = dot_nt(attn_dout, out_full).astype(BF16)
        attended_grad, routed_grads = lax.optimization_barrier((attended_grad, routed_grads))
        egate_grad, eup_grad, edown_grad = own_expert_grads(routed_grads)
        query_grad, kv_grad, rope_grad = attend_back(
            place, query_in, key_value, rope_all, attended_grad, log_totals, table,
            min(512, row_count),
        )
        late_act, query_grad = lax.optimization_barrier((expert_act, query_grad))
        expert_out = (dot(late_act, down_weight) * slot_gate).astype(BF16)
        up_grad = dot_tn(latent_all, kv_grad)
        latent_grad = dot_nt(kv_grad, up_full)
        query_wide_grad = dot_tn(normed_in, query_grad).reshape(width, head_count, HEAD)
        query_weight_grad = jnp.concatenate(
            [
                query_wide_grad[..., :NOPE],
                query_wide_grad[..., NOPE : NOPE + ROPE] - turned(query_wide_grad[..., NOPE + ROPE :]),
            ],
            axis=-1,
        ).reshape(width, head_count * (NOPE + ROPE))
        input_parts = jnp.stack(
            [dot_nt(query_grad, part).astype(BF16) for part in quarters(query_wide, 0)]
        )
        ((both_grad, input_part),) = exchange(
            sizes,
            [
                reduce_job(
                    sizes,
                    jnp.concatenate([latent_grad, rope_grad], axis=1).astype(BF16),
                    input_parts,
                )
            ],
            6,
            "sum_inputs",
        )
        both_grad = both_grad.astype(F32)
        latent_own = both_grad[:, :KVR]
        rope_own = both_grad[:, KVR : KVR + ROPE] + both_grad[:, KVR + ROPE :]
        gain_latent_grad = jnp.sum(latent_own * normed_latent, axis=0)
        latent_raw_grad = norm_back(latent_own * gain_latent, normed_latent, scale_latent)
        down_out_grad = jnp.concatenate(
            [latent_raw_grad, rotate(rope_own, cos_table, -sin_table)], axis=-1
        ).astype(BF16)
        down_grad = dot_tn(normed_in, down_out_grad)
        input_total = input_part + dot_nt(
            down_out_grad, lax.dynamic_slice_in_dim(down_full, tp_index * quarter, quarter, 0)
        )
        normed_one_part = columns(normed_one)
        gain_one_grad = jnp.sum(input_total * normed_one_part, axis=0)
        dn_one = input_total * columns(gain_one[None])
        dot_one = lax.psum(jnp.sum(dn_one * normed_one_part, axis=-1, keepdims=True), TP) / width
        token_grad = residual_grad + scale_one * (dn_one - normed_one_part * dot_one)
        token_grad, egate_grad, eup_grad, edown_grad = lax.optimization_barrier(
            (token_grad, egate_grad, eup_grad, edown_grad)
        )
        router_grad = dot_tn(normed_mid, logit_grad)
        pack_grad = jnp.concatenate([down_grad, router_grad], axis=1)
        pack_used = pack_grad.shape[1]
        pack_grad = jnp.pad(pack_grad, ((0, 0), (0, -pack_used % 128)))
        gains = jnp.stack([gain_one_grad, gain_two_grad])
        gains = lax.dynamic_update_slice_in_dim(
            jnp.zeros((2, width), F32), gains, tp_index * quarter, 1
        )
        latent_rows = jnp.pad(
            gain_latent_grad.reshape(row_shards, -1),
            ((0, 0), (0, depth - latent_gain.shape[0])),
        ).reshape(1, width)
        gains = jnp.concatenate([gains, latent_rows * (tp_index == 0).astype(F32)], axis=0)
        gains = jnp.pad(
            gains.reshape(3, row_shards, depth).transpose(1, 0, 2), ((0, 0), (0, 13), (0, 0))
        ).reshape(row_shards * 16, depth)
        kinds = ("share", "sum", "row", "row", "col")
        partials = (pack_grad, gains, query_weight_grad, up_grad, out_weight_grad)
        (output,), done = exchange(
            sizes,
            [
                give_back(expert_out, None, (residual, out_shared)),
                finish_job(
                    sizes,
                    kinds,
                    [fo_sum(part.astype(BF16), kind) for part, kind in zip(partials, kinds)],
                    [token_grad.astype(BF16)],
                ),
            ],
            3,
            "finish_attention",
        )
        pack_own = done[0].reshape(depth, -1).astype(F32)
        gains_own = done[1].astype(F32)
        query_weight_grad, up_grad, out_weight_grad = (part.astype(F32) for part in done[2:5])
        token_grad = done[5].astype(F32)
        return (
            output,
            token_grad,
            gains_own[0],
            query_weight_grad,
            pack_own[:, :down_width],
            gains_own[2, : latent_gain.shape[0]],
            up_grad,
            out_weight_grad,
            gains_own[1],
            pack_own[:, down_width:pack_used],
            sgate_grad,
            sup_grad,
            sdown_grad,
            egate_grad,
            eup_grad,
            edown_grad,
        )

    return shards


EXPERTS = 16


def solution(mesh):
    ctx_n, tp_n = mesh.shape["ctx"], mesh.shape["tp"]
    tpc_n = 2
    tpx_n = tp_n // tpc_n
    fi_n = EXPERTS // (ctx_n * tpx_n)
    sizes = {
        "fo": mesh.shape["fsdp"] // fi_n,
        "fi": fi_n,
        "ctx": ctx_n,
        "tpx": tpx_n,
        "tpc": tpc_n,
    }
    fine = Mesh(mesh.devices.reshape(tuple(sizes.values())), tuple(sizes))
    rows = P(ROWS)
    rows_two = P(ROWS, None)
    rows_tp = P(ROWS, TP)
    tp_rows = P(TP, ROWS)
    wide_in = P(None, ROWS, TP)
    wide_out = P(None, TP, ROWS)
    weights = (
        rows,
        rows_tp,
        rows_two,
        rows,
        rows_tp,
        tp_rows,
        rows,
        rows_two,
        rows_tp,
        rows_tp,
        tp_rows,
        wide_in,
        wide_in,
        wide_out,
    )
    return jax.shard_map(
        build(sizes),
        mesh=fine,
        in_specs=(rows_two, rows_two, rows_two, rows_two, P()) + weights,
        out_specs=(rows_two, rows_two) + weights,
        check_vma=False,
    )
```

```python
import functools
import math

import jax
import jax.numpy as jnp
from jax import lax
from jax.experimental import pallas as pl
from jax.experimental.pallas import tpu as pltpu
from jax.sharding import Mesh
from jax.sharding import PartitionSpec as P

NOPE = 128
ROPE = 64
KVR = 512
VDIM = 128
HEAD = 256

EPSILON = 1e-06
THETA_BASE = 10000.0
F32 = jnp.float32
BF16 = jnp.bfloat16
MESH_ID = pl.DeviceIdType.MESH

ROWS = ("fo", "fi", "ctx")
TP = ("tpx", "tpc")
PLANE = ("ctx", "tpx", "tpc")
CHIPS = ("fi", "ctx", "tpx")


def rotation_tables(positions, half_width):
    freq_table = jnp.exp(jnp.arange(half_width, dtype=F32) * (-math.log(THETA_BASE) / half_width))
    angle_table = positions.astype(F32)[:, None] * freq_table[None, :]
    return (jnp.cos(angle_table), jnp.sin(angle_table))


def rotate(values, cos_table, sin_table):
    half_width = values.shape[-1] // 2
    first_half = values[..., :half_width]
    second_half = values[..., half_width:]
    return jnp.concatenate(
        [
            first_half * cos_table - second_half * sin_table,
            second_half * cos_table + first_half * sin_table,
        ],
        axis=-1,
    )


def silu_parts(values):
    sigma = jax.nn.sigmoid(values)
    return (values * sigma, sigma * (1.0 + values * (1.0 - sigma)))


def rms_scale(values):
    return lax.rsqrt(jnp.mean(values * values, axis=-1, keepdims=True) + EPSILON)


def norm_back(grad_normed, normed, scale_rows):
    return scale_rows * (
        grad_normed - normed * jnp.mean(grad_normed * normed, axis=-1, keepdims=True)
    )


def dot(left, right):
    return jnp.dot(left, right, preferred_element_type=F32)


def dot_nt(left, right):
    return lax.dot_general(left, right, (((1,), (1,)), ((), ())), preferred_element_type=F32)


def dot_tn(left, right):
    return lax.dot_general(left, right, (((0,), (0,)), ((), ())), preferred_element_type=F32)


def ein(spec, left, right):
    return jnp.einsum(spec, left, right, preferred_element_type=F32)


def plane_place(sizes):
    tpx_n, tpc_n = sizes["tpx"], sizes["tpc"]
    fo, z, y, x, c = (lax.axis_index(name) for name in ("fo", "fi", "ctx", "tpx", "tpc"))
    own = (y * tpx_n + x) * tpc_n + c

    def device(index, z_at=None):
        return (
            fo,
            z if z_at is None else z_at,
            index // (tpx_n * tpc_n),
            lax.rem(index // tpc_n, tpx_n),
            lax.rem(index, tpc_n),
        )

    return z, y, x, c, own, device


def greet_plane(sizes):
    fi_n = sizes["fi"]
    plane_n = sizes["ctx"] * sizes["tpx"] * sizes["tpc"]
    z, y, x, c, own, device = plane_place(sizes)
    barrier = pltpu.get_barrier_semaphore()
    for step in range(1, plane_n):
        pl.semaphore_signal(
            barrier,
            inc=1,
            device_id=device(lax.rem(own + step, plane_n)),
            device_id_type=MESH_ID,
        )
    for near in (-1, 1):

        @pl.when((z + near >= 0) & (z + near < fi_n))
        def _():
            pl.semaphore_signal(
                barrier, inc=1, device_id=device(own, z + near), device_id_type=MESH_ID
            )

    sides = (z > 0).astype(jnp.int32) + (z < fi_n - 1).astype(jnp.int32)
    pl.semaphore_wait(barrier, plane_n - 1 + sides)


HBM_SPEC = pl.BlockSpec(memory_space=pl.ANY)
VMEM_SPEC = pl.BlockSpec(memory_space=pltpu.VMEM)


def exchange(sizes, jobs, collective_id, name, vmem=56):
    counts = [(len(job["args"]), len(job["outs"]), len(job["scratch"])) for job in jobs]

    def body(*refs):
        at = [0, sum(n[0] for n in counts), sum(n[0] + n[1] for n in counts)]
        running = []
        for job, count in zip(jobs, counts):
            given = [refs[at[k] : at[k] + count[k]] for k in range(3)]
            at = [at[k] + count[k] for k in range(3)]
            running.append(job["run"](sizes, *given))
        greet_plane(sizes)
        while running:
            running = [run for run in running if next(run, "ended") != "ended"]

    results = pl.pallas_call(
        body,
        out_shape=tuple(shape for job in jobs for shape, _ in job["outs"]),
        in_specs=[spec for job in jobs for _, spec in job["args"]],
        out_specs=tuple(spec for job in jobs for _, spec in job["outs"]),
        scratch_shapes=[shape for job in jobs for shape in job["scratch"]],
        compiler_params=pltpu.CompilerParams(
            collective_id=collective_id, has_side_effects=True, vmem_limit_bytes=vmem << 20
        ),
        cost_estimate=pl.CostEstimate(
            flops=0, bytes_accessed=20_000_000, transcendentals=0
        ),
        name=name,
    )(*[arg for job in jobs for arg, _ in job["args"]])
    grouped, at = [], 0
    for _, count, _ in counts:
        grouped.append(results[at : at + count])
        at += count
    return grouped


def columns_of(whole, wide):
    def slab(owner):
        return whole.at[:, pl.ds(pl.multiple_of(owner * wide, wide), wide)]

    return slab


def tp_spread(sizes, source, held, slab_of, sems):
    tpx_n, tpc_n = sizes["tpx"], sizes["tpc"]
    keep_sem, x_send, x_recv, c_send, c_recv = sems
    fo, z, y, x, c = (lax.axis_index(n) for n in ("fo", "fi", "ctx", "tpx", "tpc"))

    def slab(side, core):
        return slab_of(side * tpc_n + core)

    def origin(dx):
        return lax.rem(x + tpx_n - dx, tpx_n)

    keep = None if held is None else pltpu.make_async_copy(held, slab(x, c), keep_sem)

    def to_chip(dx, side):
        return pltpu.make_async_remote_copy(
            src_ref=source,
            dst_ref=slab(side, c),
            send_sem=x_send.at[dx],
            recv_sem=x_recv.at[dx],
            device_id=(fo, z, y, lax.rem(x + dx, tpx_n), c),
            device_id_type=MESH_ID,
        )

    def to_core(dx, dc, core):
        return pltpu.make_async_remote_copy(
            src_ref=source if dx == 0 else slab(origin(dx), c),
            dst_ref=slab(origin(dx), core),
            send_sem=c_send.at[dx, dc],
            recv_sem=c_recv.at[dx, dc],
            device_id=(fo, z, y, x, lax.rem(c + dc, tpc_n)),
            device_id_type=MESH_ID,
        )

    def start():
        for dx in range(1, tpx_n):
            to_chip(dx, x).start()
        for dc in range(1, tpc_n):
            to_core(0, dc, c).start()

    def relay():
        for dx in range(1, tpx_n):
            to_chip(dx, origin(dx)).wait_recv()
            for dc in range(1, tpc_n):
                to_core(dx, dc, c).start()

    def settle():
        if keep is not None:
            keep.wait()
        for dx in range(tpx_n):
            if dx > 0:
                to_chip(dx, x).wait_send()
            for dc in range(1, tpc_n):
                to_core(dx, dc, c).wait_send()
                to_core(dx, dc, lax.rem(c + tpc_n - dc, tpc_n)).wait_recv()

    return start, keep, relay, settle


def tp_spread_sems(sizes):
    tpx_n, tpc_n = sizes["tpx"], sizes["tpc"]
    return [
        pltpu.SemaphoreType.DMA,
        pltpu.SemaphoreType.DMA((tpx_n,)),
        pltpu.SemaphoreType.DMA((tpx_n,)),
        pltpu.SemaphoreType.DMA((tpx_n, tpc_n)),
        pltpu.SemaphoreType.DMA((tpx_n, tpc_n)),
    ]


def spread_job(sizes, part):
    tp_n = sizes["tpx"] * sizes["tpc"]
    shape = (part.shape[0], part.shape[1] * tp_n)
    return {
        "args": [(part, HBM_SPEC)],
        "outs": [(jax.ShapeDtypeStruct(shape, BF16), HBM_SPEC)],
        "scratch": [pltpu.VMEM(part.shape, BF16), pltpu.SemaphoreType.DMA]
        + tp_spread_sems(sizes),
        "run": spread_run,
    }


def spread_run(sizes, args, outs, scratch):
    held, load_sem = scratch[:2]
    start, keep, relay, settle = tp_spread(
        sizes, args[0], held, columns_of(outs[0], held.shape[1]), scratch[2:]
    )
    load = pltpu.make_async_copy(args[0], held, load_sem)
    load.start()
    start()
    yield
    load.wait()
    keep.start()
    relay()
    yield
    settle()


def dispatch_job(sizes, part_rows, plane_slots, capacity):
    tokens, quarter = part_rows.shape
    fi_n, ctx_n, tpx_n, tpc_n = (sizes[n] for n in ("fi", "ctx", "tpx", "tpc"))
    z_part, plane_n, chips = fi_n // tpc_n, ctx_n * tpx_n * tpc_n, ctx_n * tpx_n
    shape = (z_part, ctx_n, capacity, quarter * tpx_n * tpc_n)
    return {
        "args": [(plane_slots, VMEM_SPEC), (part_rows, HBM_SPEC)],
        "outs": [(jax.ShapeDtypeStruct(shape, BF16), HBM_SPEC)],
        "scratch": [
            pltpu.VMEM((fi_n, tokens, quarter), BF16),
            pltpu.VMEM((fi_n, chips, capacity, quarter), BF16),
            pltpu.SemaphoreType.DMA,
            pltpu.SemaphoreType.DMA((2, fi_n)),
            pltpu.SemaphoreType.DMA((2, fi_n)),
            pltpu.SemaphoreType.DMA((fi_n, chips)),
            pltpu.SemaphoreType.DMA((plane_n, z_part)),
        ],
        "run": dispatch_run,
    }


def dispatch_run(sizes, args, outs, scratch):
    slots_ref, rows_ref = args
    (out_ref,) = outs
    held, picked, own_sem, line_send, line_recv, plane_send, plane_recv = scratch
    fi_n, tpx_n, tpc_n = sizes["fi"], sizes["tpx"], sizes["tpc"]
    plane_n = sizes["ctx"] * tpx_n * tpc_n
    chips = sizes["ctx"] * tpx_n
    z_part = fi_n // tpc_n
    capacity, quarter = picked.shape[2:]
    tokens = held.shape[1]
    z, y, x, c, own, device = plane_place(sizes)
    columns = pl.ds(pl.multiple_of((x * tpc_n + c) * quarter, quarter), quarter)
    load = pltpu.make_async_copy(rows_ref, held.at[z], own_sem)

    def line(side, step):
        block = z - step if side == 0 else z + step
        to = z + 1 if side == 0 else z - 1
        return pltpu.make_async_remote_copy(
            src_ref=held.at[block],
            dst_ref=held.at[block],
            send_sem=line_send.at[side, step],
            recv_sem=line_recv.at[side, step],
            device_id=device(own, to),
            device_id_type=MESH_ID,
        )

    def sends(side, step):
        block = z - step if side == 0 else z + step
        to = z + 1 if side == 0 else z - 1
        return (block >= 0) & (block < fi_n) & (to >= 0) & (to < fi_n)

    def plane_copy(block, chip):
        at = lax.rem(block, z_part)
        return pltpu.make_async_remote_copy(
            src_ref=picked.at[block, chip],
            dst_ref=out_ref.at[at, y, :, columns],
            send_sem=plane_send.at[block, chip],
            recv_sem=plane_recv.at[own, at],
            device_id=device(chip * tpc_n + block // z_part),
            device_id_type=MESH_ID,
        )

    def keep_copy(block, chip):
        return pltpu.make_async_copy(
            picked.at[block, chip],
            out_ref.at[lax.rem(block, z_part), y, :, columns],
            plane_send.at[block, chip],
        )

    def at_home(block, chip):
        return chip * tpc_n + block // z_part == own

    def pick(block):
        def one(chip, carry):
            wanted = slots_ref[block, pl.ds(chip, 1), :]
            rank = lax.broadcasted_iota(jnp.int32, (capacity, tokens), 0)
            hits = jnp.where(rank == wanted, 1.0, 0.0).astype(BF16)
            picked[block, chip] = jnp.dot(
                hits, held[block], preferred_element_type=F32
            ).astype(BF16)

            @pl.when(at_home(block, chip))
            def _():
                keep_copy(block, chip).start()

            @pl.when(jnp.logical_not(at_home(block, chip)))
            def _():
                plane_copy(block, chip).start()

            return carry

        lax.fori_loop(0, chips, one, 0)

    load.start()
    load.wait()
    for side in (0, 1):

        @pl.when(sends(side, 0))
        def _():
            line(side, 0).start()

    yield
    pick(z)
    for step in range(fi_n - 1):
        for side in (0, 1):
            block = z - 1 - step if side == 0 else z + 1 + step

            @pl.when((block >= 0) & (block < fi_n))
            def _():
                pltpu.make_async_remote_copy(
                    src_ref=held.at[block],
                    dst_ref=held.at[block],
                    send_sem=line_send.at[side, step],
                    recv_sem=line_recv.at[side, step],
                    device_id=device(own, z),
                    device_id_type=MESH_ID,
                ).wait_recv()

            if step < fi_n - 2:

                @pl.when(sends(side, step + 1))
                def _():
                    line(side, step + 1).start()

        for side in (0, 1):
            block = z - 1 - step if side == 0 else z + 1 + step

            @pl.when((block >= 0) & (block < fi_n))
            def _():
                pick(block)

        yield

    for step in range(fi_n - 1):
        for side in (0, 1):

            @pl.when(sends(side, step))
            def _():
                line(side, step).wait_send()

    def settle(index, carry):
        block, chip = index // chips, lax.rem(index, chips)

        @pl.when(at_home(block, chip))
        def _():
            keep_copy(block, chip).wait()

        @pl.when(jnp.logical_not(at_home(block, chip)))
        def _():
            plane_copy(block, chip).wait_send()

        return carry

    lax.fori_loop(0, fi_n * chips, settle, 0)

    def arrive(index, carry):
        source, at = index // z_part, lax.rem(index, z_part)

        @pl.when(source != own)
        def _():
            pltpu.make_async_remote_copy(
                src_ref=picked.at[0, 0],
                dst_ref=out_ref.at[at, y, :, columns],
                send_sem=plane_send.at[0, 0],
                recv_sem=plane_recv.at[source, at],
                device_id=device(own),
                device_id_type=MESH_ID,
            ).wait_recv()

        return carry

    lax.fori_loop(0, plane_n * z_part, arrive, 0)


def give_back_run(sizes, args, outs, scratch):
    fi_n, tpx_n, tpc_n = sizes["fi"], sizes["tpx"], sizes["tpc"]
    plane_n = sizes["ctx"] * tpx_n * tpc_n
    chips = sizes["ctx"] * tpx_n
    z_part = fi_n // tpc_n
    ends, gated = len(args) > 3, len(args) == 3
    slots_ref, rows_ref = args[:2]
    out_ref = outs[0]
    got, total, going, coming, plane_send, plane_recv, line_send, line_recv = scratch[:8]
    if gated:
        gates_ref, gate_out = args[2], outs[1]
        gates_got, gate_total, gate_going, gate_coming = scratch[8:12]
        gate_send, gate_recv, gate_line_send, gate_line_recv = scratch[12:]
    if ends:
        held = scratch[8]
        start, keep, relay, spread_settle = tp_spread(
            sizes, held, held, columns_of(out_ref, held.shape[1]), scratch[9:]
        )
    capacity, quarter = got.shape[2:]
    tokens = total.shape[0]
    z, y, x, c, own, device = plane_place(sizes)
    tile = min(256, tokens)

    def piece(target, at):
        side = lax.rem(target, tpx_n * tpc_n)
        return rows_ref.at[
            at,
            target // (tpx_n * tpc_n),
            :,
            pl.ds(pl.multiple_of(side * quarter, quarter), quarter),
        ]

    def plane_copies(target, at):
        made = [
            pltpu.make_async_remote_copy(
                src_ref=piece(target, at),
                dst_ref=got.at[c * z_part + at, own // tpc_n],
                send_sem=plane_send.at[target, at],
                recv_sem=plane_recv.at[own, at],
                device_id=device(target),
                device_id_type=MESH_ID,
            )
        ]
        if gated:
            made.append(
                pltpu.make_async_remote_copy(
                    src_ref=gates_ref.at[at, target // (tpx_n * tpc_n)],
                    dst_ref=gates_got.at[c * z_part + at, own // tpc_n],
                    send_sem=gate_send.at[target, at],
                    recv_sem=gate_recv.at[own, at],
                    device_id=device(target),
                    device_id_type=MESH_ID,
                )
            )
        return made

    def keep_copies(at):
        made = [
            pltpu.make_async_copy(
                piece(own, at), got.at[c * z_part + at, own // tpc_n], plane_recv.at[own, at]
            )
        ]
        if gated:
            made.append(
                pltpu.make_async_copy(
                    gates_ref.at[at, y],
                    gates_got.at[c * z_part + at, own // tpc_n],
                    gate_recv.at[own, at],
                )
            )
        return made

    high_first = z < fi_n // 2
    early = c == jnp.where(high_first, tpc_n - 1, 0)

    def at_turn(turn):
        far = jnp.where(high_first, z_part - 1 - turn, turn)
        return jnp.where(early, far, lax.rem(z + 1 + turn, z_part))

    def send_turn(turn):
        at = at_turn(turn)

        def one(step, carry):
            for copy in plane_copies(lax.rem(own + step, plane_n), at):
                copy.start()
            return carry

        for copy in keep_copies(at):
            copy.start()
        lax.fori_loop(1, plane_n, one, 0)

    def sent_turn(turn):
        def one(step, carry):
            for copy in plane_copies(lax.rem(own + step, plane_n), at_turn(turn)):
                copy.wait_send()
            return carry

        lax.fori_loop(1, plane_n, one, 0)

    @pl.when(early)
    def _():
        for turn in range(z_part):
            send_turn(turn)
            if turn < z_part - 1:
                sent_turn(turn)

    yield

    def gathered(block):
        def one(chip, carry):
            source, at = chip * tpc_n + block // z_part, lax.rem(block, z_part)

            @pl.when(source == own)
            def _():
                for copy in keep_copies(at):
                    copy.wait()

            @pl.when(source != own)
            def _():
                pltpu.make_async_remote_copy(
                    src_ref=got.at[block, chip],
                    dst_ref=got.at[block, chip],
                    send_sem=plane_send.at[own, at],
                    recv_sem=plane_recv.at[source, at],
                    device_id=device(own),
                    device_id_type=MESH_ID,
                ).wait_recv()
                if gated:
                    pltpu.make_async_remote_copy(
                        src_ref=gates_got.at[block, chip],
                        dst_ref=gates_got.at[block, chip],
                        send_sem=gate_send.at[own, at],
                        recv_sem=gate_recv.at[source, at],
                        device_id=device(own),
                        device_id_type=MESH_ID,
                    ).wait_recv()

            return carry

        lax.fori_loop(0, chips, one, 0)

        def rows(step, carry):
            first = pl.multiple_of(step * tile, tile)
            spots = slots_ref[block, pl.ds(first, tile), :]
            rank = lax.broadcasted_iota(jnp.int32, (tile, capacity), 1)
            summed = jnp.zeros((tile, quarter), F32)
            if gated:
                experts = gate_total.shape[0]
                gates = jnp.zeros((experts, tile), F32)
                expert = lax.broadcasted_iota(jnp.int32, (experts, capacity), 0)
            for chip in range(chips):
                hits = jnp.where(rank == spots[:, chip : chip + 1], 1.0, 0.0).astype(BF16)
                summed = summed + jnp.dot(hits, got[block, chip], preferred_element_type=F32)
                if gated:
                    left = jnp.where(
                        expert == z * chips + chip, gates_got[block, chip, 0:1, :], 0.0
                    ).astype(BF16)
                    gates = gates + dot_nt(left, hits)
            total[pl.ds(first, tile), :] = summed
            if gated:
                gate_total[:, pl.ds(first, tile)] = gates
            return carry

        lax.fori_loop(0, tokens // tile, rows, 0)

    def onward(side, target):
        if side == 0:
            return z + 1, target
        return z - 1, jnp.where(target == z - 1, fi_n, target)

    def lines(side, target, to, slot):
        made = [
            pltpu.make_async_remote_copy(
                src_ref=going.at[target],
                dst_ref=coming.at[slot],
                send_sem=line_send.at[side, target],
                recv_sem=line_recv.at[side, target],
                device_id=device(own, to),
                device_id_type=MESH_ID,
            )
        ]
        if gated:
            made.append(
                pltpu.make_async_remote_copy(
                    src_ref=gate_going.at[target],
                    dst_ref=gate_coming.at[side, target],
                    send_sem=gate_line_send.at[side, target],
                    recv_sem=gate_line_recv.at[side, target],
                    device_id=device(own, to),
                    device_id_type=MESH_ID,
                )
            )
        return made

    for step in range(fi_n - 1):
        for side in (0, 1):
            depth = z if side == 0 else fi_n - 1 - z
            target = fi_n - 1 - step + z if side == 0 else step - (fi_n - 1) + z
            passes, inner = depth <= step, depth > 0

            @pl.when(passes)
            def _():
                gathered(target)

                @pl.when(inner)
                def _():
                    for copy in lines(side, target, z, target):
                        copy.wait_recv()
                    going[target] = (total[...] + coming[target].astype(F32)).astype(BF16)
                    if gated:
                        gate_going[target] = gate_total[...] + gate_coming[side, target]

                @pl.when(jnp.logical_not(inner))
                def _():
                    going[target] = total[...].astype(BF16)
                    if gated:
                        gate_going[target] = gate_total[...]

                for copy in lines(side, target, *onward(side, target)):
                    copy.start()

        for turn in range(z_part):
            if min(turn, fi_n - 2) == step:

                @pl.when(jnp.logical_not(early))
                def _():
                    send_turn(turn)

        yield

    gathered(z)
    for side in (0, 1):

        @pl.when((z > 0) if side == 0 else (z < fi_n - 1))
        def _():
            for copy in lines(side, z, z, fi_n if side == 1 else z):
                copy.wait_recv()
            total[...] += coming[fi_n if side == 1 else z].astype(F32)
            if gated:
                gate_total[...] += gate_coming[side, z]

    if ends:
        held[...] = (total[...] + args[2][...] + args[3][...]).astype(BF16)
        start()
        keep.start()
    else:
        out_ref[...] = total[...]
    if gated:
        gate_out[...] = gate_total[...]
    yield
    if ends:
        relay()


    for target in range(fi_n):
        for side in (0, 1):

            @pl.when((z < target) if side == 0 else (z > target))
            def _():
                for copy in lines(side, target, *onward(side, target)):
                    copy.wait_send()

    for turn in range(z_part):

        @pl.when(jnp.logical_not(early) | (turn == z_part - 1))
        def _():
            sent_turn(turn)

    yield
    if ends:
        spread_settle()


def give_back_job(sizes, rows, token_slots, gates, bases=None):
    fi_n, ctx_n, tpx_n, tpc_n = (sizes[n] for n in ("fi", "ctx", "tpx", "tpc"))
    z_part, plane_n, chips = fi_n // tpc_n, ctx_n * tpx_n * tpc_n, ctx_n * tpx_n
    capacity, width = rows.shape[2:]
    quarter = width // (tpx_n * tpc_n)
    tokens = token_slots.shape[1]
    experts = fi_n * chips
    gated = gates is not None
    shapes = [jax.ShapeDtypeStruct((tokens, quarter), F32)]
    scratch = [
        pltpu.VMEM((fi_n, chips, capacity, quarter), BF16),
        pltpu.VMEM((tokens, quarter), F32),
        pltpu.VMEM((fi_n, tokens, quarter), BF16),
        pltpu.VMEM((fi_n + 1, tokens, quarter), BF16),
        pltpu.SemaphoreType.DMA((plane_n, z_part)),
        pltpu.SemaphoreType.DMA((plane_n, z_part)),
        pltpu.SemaphoreType.DMA((2, fi_n)),
        pltpu.SemaphoreType.DMA((2, fi_n)),
    ]
    args = [token_slots, rows]
    if gated:
        args.append(gates)
        shapes.append(jax.ShapeDtypeStruct((experts, tokens), F32))
        scratch += [
            pltpu.VMEM((fi_n, chips, 8, capacity), F32),
            pltpu.VMEM((experts, tokens), F32),
            pltpu.VMEM((fi_n, experts, tokens), F32),
            pltpu.VMEM((2, fi_n, experts, tokens), F32),
            pltpu.SemaphoreType.DMA((plane_n, z_part)),
            pltpu.SemaphoreType.DMA((plane_n, z_part)),
            pltpu.SemaphoreType.DMA((2, fi_n)),
            pltpu.SemaphoreType.DMA((2, fi_n)),
        ]
    specs = [VMEM_SPEC] + [HBM_SPEC] * (len(args) - 1)
    if bases is not None:
        args += list(bases)
        specs += [VMEM_SPEC] * 2
        shapes = [jax.ShapeDtypeStruct((tokens, width), BF16)]
        scratch += [pltpu.VMEM((tokens, quarter), BF16)] + tp_spread_sems(sizes)
    return {
        "args": list(zip(args, specs)),
        "outs": [(shape, HBM_SPEC if bases is not None else VMEM_SPEC) for shape in shapes],
        "scratch": scratch,
        "run": give_back_run,
    }


def collect_run(kinds, sizes, args, outs, scratch):
    fo_n, fi_n, ctx_n, tpx_n, tpc_n = (sizes[n] for n in ("fo", "fi", "ctx", "tpx", "tpc"))
    tp_n = tpx_n * tpc_n
    count = len(kinds)
    shards = args
    own_sem, line_send, line_recv, col_send, col_recv = scratch[:5]
    staged, spread_sems = scratch[5 : 5 + count * fo_n], scratch[5 + count * fo_n :]
    fo, z, y, x, c = (lax.axis_index(n) for n in ("fo", "fi", "ctx", "tpx", "tpc"))
    q = x * tpc_n + c

    items = [(i, f) for f in range(fo_n) for i in range(count)]

    def source(n):
        i, f = items[n]
        if kinds[i] == "share":
            a = shards[i].shape[1] // tp_n
            return shards[i].at[f, pl.ds(pl.multiple_of(q * a, a), a), :]
        return shards[i].at[f]

    def place(n, zb, yb):
        i, f = items[n]
        a, b = shards[i].shape[1:]
        block = (f * fi_n + zb) * ctx_n + yb
        if kinds[i] == "col":
            return outs[i].at[:, pl.ds(pl.multiple_of(block * b, b), b)]
        if kinds[i] == "share":
            return outs[i].at[block, q]
        return outs[i].at[pl.ds(pl.multiple_of(block * a, a), a), :]

    def parts_of(n):
        i, f = items[n]
        blocks = pl.ds(f * fi_n * ctx_n, fi_n * ctx_n)
        return lambda owner: outs[i].at[blocks, owner]

    spreads = {}
    for n, (i, f) in enumerate(items):
        if kinds[i] == "share":
            at = 5 * len(spreads)
            spreads[n] = tp_spread(
                sizes, parts_of(n)(q), None, parts_of(n), spread_sems[at : at + 5]
            )

    def line(n, side, step, first):
        block = z - step if side == 0 else z + step
        to = z + 1 if side == 0 else z - 1
        return pltpu.make_async_remote_copy(
            src_ref=source(n) if first else place(n, block, y),
            dst_ref=place(n, block, y),
            send_sem=line_send.at[n, side, step],
            recv_sem=line_recv.at[n, side, step],
            device_id=(fo, to, y, x, c),
            device_id_type=MESH_ID,
        )

    def sends(side, step):
        block = z - step if side == 0 else z + step
        to = z + 1 if side == 0 else z - 1
        return (block >= 0) & (block < fi_n) & (to >= 0) & (to < fi_n)

    def across(n, zb, dy, first=False):
        return pltpu.make_async_remote_copy(
            src_ref=source(n) if first else place(n, zb, y),
            dst_ref=place(n, zb, y),
            send_sem=col_send.at[n, zb, dy],
            recv_sem=col_recv.at[n, zb, dy],
            device_id=(fo, z, lax.rem(y + dy, ctx_n), x, c),
            device_id_type=MESH_ID,
        )

    def stage(n):
        return pltpu.make_async_copy(source(n), staged[n], own_sem.at[n, 0])

    def keep(n):
        return pltpu.make_async_copy(staged[n], place(n, z, y), own_sem.at[n, 1])

    for n in range(len(items)):
        for side in (0, 1):

            @pl.when(sends(side, 0))
            def _():
                line(n, side, 0, True).start()

        for dy in range(1, ctx_n):
            across(n, z, dy, True).start()
        stage(n).start()

    yield
    for n in range(len(items)):
        stage(n).wait()
        keep(n).start()

    for step in range(fi_n - 1):
        for n in range(len(items)):
            for side in (0, 1):
                block = z - 1 - step if side == 0 else z + 1 + step

                @pl.when((block >= 0) & (block < fi_n))
                def _():
                    pltpu.make_async_remote_copy(
                        src_ref=place(n, block, y),
                        dst_ref=place(n, block, y),
                        send_sem=line_send.at[n, side, step],
                        recv_sem=line_recv.at[n, side, step],
                        device_id=(fo, z, y, x, c),
                        device_id_type=MESH_ID,
                    ).wait_recv()
                    for dy in range(1, ctx_n):
                        across(n, block, dy).start()

                if step < fi_n - 2:

                    @pl.when(sends(side, step + 1))
                    def _():
                        line(n, side, step + 1, False).start()

        yield

    for n in range(len(items)):
        keep(n).wait()
        for dy in range(1, ctx_n):
            for zb in range(fi_n):
                pltpu.make_async_remote_copy(
                    src_ref=place(n, zb, y),
                    dst_ref=place(n, zb, lax.rem(y + ctx_n - dy, ctx_n)),
                    send_sem=col_send.at[n, zb, dy],
                    recv_sem=col_recv.at[n, zb, dy],
                    device_id=(fo, z, y, x, c),
                    device_id_type=MESH_ID,
                ).wait_recv()
        if n in spreads:
            spreads[n][0]()

    yield

    for n in spreads:
        spreads[n][2]()

    for n in range(len(items)):
        if n in spreads:
            spreads[n][3]()
        for side in (0, 1):
            for step in range(fi_n - 1):

                @pl.when(sends(side, step))
                def _():
                    line(n, side, step, step == 0).wait_send()

        for dy in range(1, ctx_n):
            for zb in range(fi_n):
                across(n, zb, dy).wait_send()


def collect_job(sizes, kinds, shards):
    fo_n, fi_n, ctx_n, tpx_n, tpc_n = (sizes[n] for n in ("fo", "fi", "ctx", "tpx", "tpc"))
    tp_n = tpx_n * tpc_n
    blocks = fo_n * fi_n * ctx_n
    outs, staged = [], []
    for kind, shard in zip(kinds, shards):
        _, a, b = shard.shape
        shape = (a, blocks * b) if kind == "col" else (blocks * a, b)
        if kind == "share":
            shape = (blocks, tp_n, a // tp_n, b)
        outs.append((jax.ShapeDtypeStruct(shape, shard.dtype), HBM_SPEC))
        staged.append(pltpu.VMEM((a // tp_n if kind == "share" else a, b), shard.dtype))
    n = len(kinds) * fo_n
    return {
        "args": [(shard, HBM_SPEC) for shard in shards],
        "outs": outs,
        "scratch": [
            pltpu.SemaphoreType.DMA((n, 2)),
            pltpu.SemaphoreType.DMA((n, 2, fi_n)),
            pltpu.SemaphoreType.DMA((n, 2, fi_n)),
            pltpu.SemaphoreType.DMA((n, fi_n, ctx_n)),
            pltpu.SemaphoreType.DMA((n, fi_n, ctx_n)),
        ]
        + staged * fo_n
        + tp_spread_sems(sizes) * (kinds.count("share") * fo_n),
        "run": functools.partial(collect_run, tuple(kinds)),
    }


def place_job(sizes, local):
    fo_n, fi_n, ctx_n, tpx_n, tpc_n = (sizes[n] for n in ("fo", "fi", "ctx", "tpx", "tpc"))
    chip_n = fi_n * ctx_n * tpx_n
    rows, depth = local.shape[3:]
    shape = (rows * tpx_n * tpc_n, depth * fo_n * fi_n * ctx_n)
    return {
        "args": [(local, HBM_SPEC)],
        "outs": [(jax.ShapeDtypeStruct(shape, BF16), HBM_SPEC)] * 3,
        "scratch": [pltpu.VMEM(local.shape, BF16)]
        + [pltpu.SemaphoreType.DMA((fo_n, 3, chip_n))] * 2
        + [pltpu.SemaphoreType.DMA((fo_n, 3, chip_n, tpc_n))] * 2,
        "run": place_run,
    }


def place_run(sizes, args, outs, scratch):
    fo_n, fi_n, ctx_n, tpx_n, tpc_n = (sizes[n] for n in ("fo", "fi", "ctx", "tpx", "tpc"))
    (local,) = args
    staged, load_sem, keep_sem, pair_send, pair_recv = scratch
    chip_n = fi_n * ctx_n * tpx_n
    rows, depth = local.shape[3:]
    fo, z, y, x, c = (lax.axis_index(n) for n in ("fo", "fi", "ctx", "tpx", "tpc"))

    def spot(k, f, chip, core):
        block = f * fi_n * ctx_n + chip // tpx_n
        return outs[k].at[
            pl.ds(pl.multiple_of((lax.rem(chip, tpx_n) * tpc_n + core) * rows, rows), rows),
            pl.ds(pl.multiple_of(block * depth, depth), depth),
        ]

    def load(f, k, chip):
        return pltpu.make_async_copy(
            local.at[f, chip, k], staged.at[f, chip, k], load_sem.at[f, k, chip]
        )

    def keep(f, k, chip):
        return pltpu.make_async_copy(
            staged.at[f, chip, k], spot(k, f, chip, c), keep_sem.at[f, k, chip]
        )

    def pair_copy(f, k, chip, dc, core):
        return pltpu.make_async_remote_copy(
            src_ref=local.at[f, chip, k],
            dst_ref=spot(k, f, chip, core),
            send_sem=pair_send.at[f, k, chip, dc],
            recv_sem=pair_recv.at[f, k, chip, dc],
            device_id=(fo, z, y, x, lax.rem(c + dc, tpc_n)),
            device_id_type=MESH_ID,
        )

    def launch(step, carry):
        f, chip = step // chip_n, lax.rem(step, chip_n)
        for k in range(3):
            load(f, k, chip).start()
            for dc in range(1, tpc_n):
                pair_copy(f, k, chip, dc, c).start()
        return carry

    def store(step, carry):
        f, chip = step // chip_n, lax.rem(step, chip_n)
        for k in range(3):
            load(f, k, chip).wait()
            keep(f, k, chip).start()
        return carry

    def settle(step, carry):
        f, chip = step // chip_n, lax.rem(step, chip_n)
        for k in range(3):
            keep(f, k, chip).wait()
            for dc in range(1, tpc_n):
                pair_copy(f, k, chip, dc, c).wait_send()
                pair_copy(f, k, chip, dc, lax.rem(c + tpc_n - dc, tpc_n)).wait_recv()
        return carry

    lax.fori_loop(0, fo_n * chip_n, launch, 0)
    yield
    lax.fori_loop(0, fo_n * chip_n, store, 0)
    yield
    lax.fori_loop(0, fo_n * chip_n, settle, 0)


def pair_job(sizes, grads):
    fo_n, fi_n, ctx_n, tpx_n, tpc_n = (sizes[n] for n in ("fo", "fi", "ctx", "tpx", "tpc"))
    rows = grads[0].shape[0] // (tpx_n * tpc_n)
    depth = grads[0].shape[1] // (fo_n * fi_n * ctx_n)
    total = fo_n * fi_n * ctx_n * tpx_n
    shape = (total, 3, rows, depth)
    return {
        "args": [(grad, HBM_SPEC) for grad in grads],
        "outs": [(jax.ShapeDtypeStruct(shape, BF16), HBM_SPEC)],
        "scratch": [pltpu.VMEM(shape, BF16)] * 2 + [pltpu.SemaphoreType.DMA((total, 3))] * 4,
        "run": pair_run,
    }


def pair_run(sizes, grads, outs, scratch):
    tpx_n, tpc_n = sizes["tpx"], sizes["tpc"]
    (out_ref,) = outs
    mine, theirs, load_sem, store_sem, send_sem, recv_sem = scratch
    total, _, rows, depth = mine.shape
    fo, z, y, x, c = (lax.axis_index(n) for n in ("fo", "fi", "ctx", "tpx", "tpc"))
    sibling = (fo, z, y, x, 1 - c)

    def spot(k, at, core):
        block, side = at // tpx_n, lax.rem(at, tpx_n)
        return grads[k].at[
            pl.ds(pl.multiple_of((side * tpc_n + core) * rows, rows), rows),
            pl.ds(pl.multiple_of(block * depth, depth), depth),
        ]

    def load(k, at):
        return pltpu.make_async_copy(spot(k, at, c), mine.at[at, k], load_sem.at[at, k])

    def store(k, at):
        return pltpu.make_async_copy(mine.at[at, k], out_ref.at[at, k], store_sem.at[at, k])

    def give(k, at):
        return pltpu.make_async_remote_copy(
            src_ref=spot(k, at, 1 - c),
            dst_ref=theirs.at[at, k],
            send_sem=send_sem.at[at, k],
            recv_sem=recv_sem.at[at, k],
            device_id=sibling,
            device_id_type=MESH_ID,
        )

    def launch(at, carry):
        for k in range(3):
            give(k, at).start()
            load(k, at).start()
        return carry

    def add(at, carry):
        for k in range(3):
            load(k, at).wait()
            give(k, at).wait_recv()
            mine[at, k] = (mine[at, k].astype(F32) + theirs[at, k].astype(F32)).astype(BF16)
            store(k, at).start()
        return carry

    def settle(at, carry):
        for k in range(3):
            give(k, at).wait_send()
            store(k, at).wait()
        return carry

    lax.fori_loop(0, total, launch, 0)
    yield
    lax.fori_loop(0, total, add, 0)
    yield
    lax.fori_loop(0, total, settle, 0)


def finish_run(kinds, sizes, args, outs, scratch):
    fi_n, ctx_n, tpx_n, tpc_n = (sizes[n] for n in ("fi", "ctx", "tpx", "tpc"))
    tp_n = tpx_n * tpc_n
    count = len(kinds)
    extra = len(args) - count
    parts, quarters = args[:count], args[count:]
    outs, wholes = outs[:count], outs[count:]
    mine, other, coming = (scratch[k * count : (k + 1) * count] for k in range(3))
    staged, (tiny, *sems) = scratch[3 * count : 3 * count + extra], scratch[3 * count + extra :]
    load_sem, col_send, col_recv, line_send, line_recv, tp_send, tp_recv = sems[:7]
    fo, z, y, x, c = (lax.axis_index(n) for n in ("fo", "fi", "ctx", "tpx", "tpc"))
    q = x * tpc_n + c

    spreads = [
        tp_spread(
            sizes,
            quarters[j],
            staged[j],
            columns_of(wholes[j], quarters[j].shape[1]),
            sems[8 + 5 * j : 13 + 5 * j],
        )
        for j in range(extra)
    ]

    def stage(j):
        return pltpu.make_async_copy(quarters[j], staged[j], sems[7].at[j])

    for j in range(extra):
        spreads[j][0]()
        stage(j).start()

    def view(n, zb, yb):
        a, b = mine[n].shape[1:]
        block = zb * ctx_n + yb
        if kinds[n] == "col":
            return parts[n].at[:, pl.ds(pl.multiple_of(block * b, b), b)]
        if kinds[n] == "share":
            return parts[n].at[pl.ds(pl.multiple_of(block * a * tp_n + q * a, a), a), :]
        return parts[n].at[pl.ds(pl.multiple_of(block * a, a), a), :]

    def across(n, zb, dy):
        to = lax.rem(y + dy, ctx_n)
        return pltpu.make_async_remote_copy(
            src_ref=view(n, zb, to),
            dst_ref=other[n].at[dy - 1, zb],
            send_sem=col_send.at[n, zb, dy],
            recv_sem=col_recv.at[n, zb, dy],
            device_id=(fo, z, to, x, c),
            device_id_type=MESH_ID,
        )

    def load(n, zb):
        return pltpu.make_async_copy(view(n, zb, y), mine[n].at[zb], load_sem.at[n, zb])

    def block_turn(turn):
        high_first = z < fi_n // 2
        place = jnp.where(high_first, fi_n - 1 - z, z)
        at = turn + (place <= turn).astype(jnp.int32)
        far = jnp.where(high_first, fi_n - 1 - at, at)
        return z if turn == fi_n - 1 else far

    def send_turn(turn):
        zb = block_turn(turn)
        for n in range(count):
            for dy in range(1, ctx_n):
                across(n, zb, dy).start()
            load(n, zb).start()

    def sent_turn(turn):
        for n in range(count):
            for dy in range(1, ctx_n):
                across(n, block_turn(turn), dy).wait_send()

    send_turn(0)
    yield
    send_turn(1)
    for j in range(extra):
        stage(j).wait()
        spreads[j][1].start()

    def line(n, side, target):
        at = jnp.where(target == (z + 1 if side == 0 else z - 1), fi_n, target) if side == 1 else target
        return pltpu.make_async_remote_copy(
            src_ref=mine[n].at[target],
            dst_ref=coming[n].at[at],
            send_sem=line_send.at[n, side, target],
            recv_sem=line_recv.at[n, side, target],
            device_id=(fo, z + 1 if side == 0 else z - 1, y, x, c),
            device_id_type=MESH_ID,
        )

    def came(n, side, target, at):
        pltpu.make_async_remote_copy(
            src_ref=mine[n].at[target],
            dst_ref=coming[n].at[at],
            send_sem=line_send.at[n, side, target],
            recv_sem=line_recv.at[n, side, target],
            device_id=(fo, z, y, x, c),
            device_id_type=MESH_ID,
        ).wait_recv()

    def ready(n, target):
        load(n, target).wait()
        for dy in range(1, ctx_n):
            across(n, target, dy).wait_recv()

    def add(n, target, use, store):
        a = mine[n].shape[1]
        tile = math.gcd(a, 64)

        def rows(step, carry):
            at = pl.ds(pl.multiple_of(step * tile, tile), tile)
            summed = mine[n][target, at, :].astype(F32)
            for dy in range(1, ctx_n):
                summed = summed + other[n][dy - 1, target, at, :].astype(F32)
            for slot in use:
                summed = summed + coming[n][slot, at, :].astype(F32)
            store(at, summed.astype(BF16))
            return carry

        lax.fori_loop(0, a // tile, rows, 0)

    for step in range(fi_n - 1):
        for n in range(count):
            for side in (0, 1):
                depth = z if side == 0 else fi_n - 1 - z
                target = fi_n - 1 - step + z if side == 0 else step - (fi_n - 1) + z
                passes, inner = depth <= step, depth > 0

                def back(at, values, n=n, target=target):
                    mine[n][target, at, :] = values

                @pl.when(passes & inner)
                def _():
                    ready(n, target)
                    came(n, side, target, target)
                    add(n, target, (target,), back)
                    line(n, side, target).start()

                @pl.when(passes & jnp.logical_not(inner))
                def _():
                    ready(n, target)
                    add(n, target, (), back)
                    line(n, side, target).start()

        if step + 2 < fi_n:
            sent_turn(step)
            send_turn(step + 2)
        yield

    for n in range(count):
        ready(n, z)

        def out(at, values, n=n):
            if kinds[n] == "share":
                a = mine[n].shape[1]
                outs[n][q, at, :] = values
            elif kinds[n] == "sum":
                tiny[q, at, :] = values
            else:
                outs[n][at, :] = values

        @pl.when(z > 0)
        def _():
            came(n, 0, z, z)

        @pl.when(z < fi_n - 1)
        def _():
            came(n, 1, z, fi_n)

        @pl.when((z > 0) & (z < fi_n - 1))
        def _():
            add(n, z, (z, fi_n), out)

        @pl.when((z == 0) & (z < fi_n - 1))
        def _():
            add(n, z, (fi_n,), out)

        @pl.when((z > 0) & (z == fi_n - 1))
        def _():
            add(n, z, (z,), out)

        @pl.when((z == 0) & (z == fi_n - 1))
        def _():
            add(n, z, (), out)

        if kinds[n] in ("share", "sum"):
            held = outs[n] if kinds[n] == "share" else tiny
            for step in range(1, tp_n):
                peer = lax.rem(q + step, tp_n)
                pltpu.make_async_remote_copy(
                    src_ref=held.at[q],
                    dst_ref=held.at[q],
                    send_sem=tp_send.at[n, step],
                    recv_sem=tp_recv.at[n, step],
                    device_id=(fo, z, y, peer // tpc_n, lax.rem(peer, tpc_n)),
                    device_id_type=MESH_ID,
                ).start()

    yield
    for j in range(extra):
        spreads[j][2]()

    for n in range(count):
        if kinds[n] in ("share", "sum"):
            held = outs[n] if kinds[n] == "share" else tiny
            for step in range(1, tp_n):
                origin = lax.rem(q + tp_n - step, tp_n)
                copy = pltpu.make_async_remote_copy(
                    src_ref=held.at[q],
                    dst_ref=held.at[origin],
                    send_sem=tp_send.at[n, step],
                    recv_sem=tp_recv.at[n, step],
                    device_id=(fo, z, y, x, c),
                    device_id_type=MESH_ID,
                )
                copy.wait_send()
                copy.wait_recv()
            if kinds[n] == "sum":
                summed = tiny[0].astype(F32)
                for k in range(1, tp_n):
                    summed = summed + tiny[k].astype(F32)
                outs[n][...] = summed.astype(BF16)
        for target in range(fi_n):
            for side in (0, 1):

                @pl.when((z < target) if side == 0 else (z > target))
                def _():
                    line(n, side, target).wait_send()

    for turn in range(fi_n - 2, fi_n):
        sent_turn(turn)
    for j in range(extra):
        spreads[j][3]()


def finish_job(sizes, kinds, parts, quarters):
    fi_n, ctx_n, tpx_n, tpc_n = (sizes[n] for n in ("fi", "ctx", "tpx", "tpc"))
    tp_n = tpx_n * tpc_n
    blocks = fi_n * ctx_n
    count, extra = len(kinds), len(quarters)
    own, shapes = [], []
    sum_shape = (16, 256)
    for kind, part in zip(kinds, parts):
        a, b = part.shape
        if kind == "col":
            own.append((a, b // blocks))
            shapes.append(own[-1])
        elif kind == "share":
            own.append((a // (blocks * tp_n), b))
            shapes.append((tp_n,) + own[-1])
        else:
            own.append((a // blocks, b))
            shapes.append(own[-1])
        if kind == "sum":
            sum_shape = own[-1]
    wide = [(v.shape[0], v.shape[1] * tp_n) for v in quarters]
    some = max(extra, 1)
    shapes = [jax.ShapeDtypeStruct(shape, BF16) for shape in shapes + wide]
    return {
        "args": [(arg, HBM_SPEC) for arg in (*parts, *quarters)],
        "outs": list(zip(shapes, [VMEM_SPEC] * count + [HBM_SPEC] * extra)),
        "scratch": [pltpu.VMEM((fi_n,) + s, BF16) for s in own]
        + [pltpu.VMEM((max(ctx_n - 1, 1), fi_n) + s, BF16) for s in own]
        + [pltpu.VMEM((fi_n + 1,) + s, BF16) for s in own]
        + [pltpu.VMEM(v.shape, BF16) for v in quarters]
        + [
            pltpu.VMEM((tp_n,) + sum_shape, BF16),
            pltpu.SemaphoreType.DMA((count, fi_n)),
            pltpu.SemaphoreType.DMA((count, fi_n, ctx_n)),
            pltpu.SemaphoreType.DMA((count, fi_n, ctx_n)),
            pltpu.SemaphoreType.DMA((count, 2, fi_n)),
            pltpu.SemaphoreType.DMA((count, 2, fi_n)),
            pltpu.SemaphoreType.DMA((count, tp_n)),
            pltpu.SemaphoreType.DMA((count, tp_n)),
            pltpu.SemaphoreType.DMA((some,)),
            *(tp_spread_sems(sizes) * extra),
        ],
        "run": functools.partial(finish_run, tuple(kinds)),
    }


def products_job(sizes, lefts, rights, which):
    slots, hidden = lefts[0].shape
    width = rights[0].shape[1]
    tile = min(384, hidden)
    return {
        "args": [(arg, HBM_SPEC) for arg in (*lefts, *rights)],
        "outs": [(jax.ShapeDtypeStruct((hidden, width), BF16), HBM_SPEC)] * len(lefts),
        "scratch": [
            pltpu.VMEM((2, slots, tile), BF16),
            pltpu.VMEM((tile, slots), BF16),
            pltpu.VMEM((slots, width), BF16),
            pltpu.VMEM((2, tile, width), BF16),
            pltpu.SemaphoreType.DMA((2,)),
            pltpu.SemaphoreType.DMA,
            pltpu.SemaphoreType.DMA((2,)),
        ],
        "run": functools.partial(products_run, tuple(which), tile),
    }


def products_run(which, tile, sizes, args, outs, scratch):
    left_buf, turned, right_buf, out_buf, left_sem, right_sem, out_sem = scratch
    count = len(outs)
    lefts, rights = args[:count], args[count:]
    hidden = lefts[0].shape[1]
    width = right_buf.shape[1]
    cells = [(k, at, min(tile, hidden - at)) for k in range(count) for at in range(0, hidden, tile)]

    def load(n):
        k, at, size = cells[n]
        return pltpu.make_async_copy(
            lefts[k].at[:, pl.ds(at, size)],
            left_buf.at[n % 2, :, pl.ds(0, size)],
            left_sem.at[n % 2],
        )

    def fetch(k):
        return pltpu.make_async_copy(rights[which[k]], right_buf, right_sem)

    def store(n):
        k, at, size = cells[n]
        return pltpu.make_async_copy(
            out_buf.at[n % 2, pl.ds(0, size), :],
            outs[k].at[pl.ds(at, size), :],
            out_sem.at[n % 2],
        )

    columns = min(512, width)

    def products():
        for n, (k, at, size) in enumerate(cells):
            load(n).wait()
            if n + 1 < len(cells):
                load(n + 1).start()
            if at == 0 and (k == 0 or which[k] != which[k - 1]):
                if k > 0:
                    fetch(k).start()
                fetch(k).wait()
            if n >= 2:
                store(n - 2).wait()
            turned[pl.ds(0, size), :] = left_buf[n % 2, :, :size].T

            def one(step, carry, n=n, size=size):
                here = pl.ds(pl.multiple_of(step * columns, columns), columns)
                out_buf[n % 2, pl.ds(0, size), here] = jnp.dot(
                    turned[:size, :], right_buf[:, here], preferred_element_type=F32
                ).astype(BF16)
                return carry

            lax.fori_loop(0, width // columns, one, 0)
            store(n).start()
        for n in range(max(len(cells) - 2, 0), len(cells)):
            store(n).wait()

    fi_n = sizes["fi"]
    z = lax.axis_index("fi")
    inner = (z > 0) & (z < fi_n - 1)
    fetch(0).start()
    load(0).start()
    for phase in range(1, fi_n):
        yield
        if phase == 1:
            pl.when(inner)(products)
        if phase == fi_n - 1:
            pl.when(jnp.logical_not(inner))(products)


def reduce_job(sizes, both, parts):
    ctx_n, tpx_n, tpc_n = (sizes[n] for n in ("ctx", "tpx", "tpc"))
    tp_n = tpx_n * tpc_n
    tokens, quarter = parts.shape[1:]
    wide = both.shape[1]
    piece = (ctx_n, tokens // tp_n, wide)
    return {
        "args": [(both.reshape(ctx_n, tokens, wide), HBM_SPEC), (parts, HBM_SPEC)],
        "outs": [
            (jax.ShapeDtypeStruct((tokens, wide), BF16), VMEM_SPEC),
            (jax.ShapeDtypeStruct((tokens, quarter), F32), VMEM_SPEC),
        ],
        "scratch": [
            pltpu.VMEM((3, tpx_n) + piece, BF16),
            pltpu.VMEM((3, tpx_n, tokens, quarter), BF16),
            pltpu.VMEM((ctx_n,) + piece[1:], BF16),
            pltpu.SemaphoreType.DMA((2, tpx_n)),
            pltpu.SemaphoreType.DMA((2, tpx_n)),
            pltpu.SemaphoreType.DMA((2, tpx_n)),
            pltpu.SemaphoreType.DMA((2, tpx_n)),
            pltpu.SemaphoreType.DMA((2, tpx_n)),
            pltpu.SemaphoreType.DMA((2, ctx_n)),
            pltpu.SemaphoreType.DMA((2, tp_n)),
        ],
        "run": reduce_run,
    }


def reduce_run(sizes, args, outs, scratch):
    ctx_n, tpx_n, tpc_n = (sizes[n] for n in ("ctx", "tpx", "tpc"))
    tp_n = tpx_n * tpc_n
    both_ref, parts_ref = args
    both_out, parts_out = outs
    both_buf, parts_buf, halves = scratch[:3]
    load_sem, core_send, core_recv, x_send, x_recv, y_sem, tp_sem = scratch[3:]
    rows = halves.shape[1]
    fo, z, y, x, c = (lax.axis_index(n) for n in ("fo", "fi", "ctx", "tpx", "tpc"))
    q = x * tpc_n + c
    bufs = (both_buf, parts_buf)

    def view(kind, side, core):
        to = side * tpc_n + core
        if kind == 0:
            return both_ref.at[:, pl.ds(pl.multiple_of(to * rows, rows), rows), :]
        return parts_ref.at[to]

    def load(kind, side):
        return pltpu.make_async_copy(
            view(kind, side, c), bufs[kind].at[0, side], load_sem.at[kind, side]
        )

    def to_core(kind, side):
        return pltpu.make_async_remote_copy(
            src_ref=view(kind, side, 1 - c),
            dst_ref=bufs[kind].at[1, side],
            send_sem=core_send.at[kind, side],
            recv_sem=core_recv.at[kind, side],
            device_id=(fo, z, y, x, 1 - c),
            device_id_type=MESH_ID,
        )

    def to_chip(kind, side, slot):
        return pltpu.make_async_remote_copy(
            src_ref=bufs[kind].at[0, side],
            dst_ref=bufs[kind].at[2, slot],
            send_sem=x_send.at[kind, side],
            recv_sem=x_recv.at[kind, slot],
            device_id=(fo, z, y, side, c),
            device_id_type=MESH_ID,
        )

    def side_of(dx):
        return lax.rem(x + dx, tpx_n)

    def add(kind, side):
        count = bufs[kind].shape[2] if kind == 1 else bufs[kind].shape[3]
        tile = math.gcd(count, 64)

        def one(step, carry):
            at = pl.ds(pl.multiple_of(step * tile, tile), tile)
            if kind == 1:
                mine, other = parts_buf[0, side, at, :], parts_buf[1, side, at, :]
                parts_buf[0, side, at, :] = (mine.astype(F32) + other.astype(F32)).astype(BF16)
            else:
                for half in range(ctx_n):
                    mine = both_buf[0, side, half, at, :]
                    other = both_buf[1, side, half, at, :]
                    both_buf[0, side, half, at, :] = (
                        mine.astype(F32) + other.astype(F32)
                    ).astype(BF16)
            return carry

        lax.fori_loop(0, count // tile, one, 0)

    order = list(range(1, tpx_n)) + [0]
    for kind in (0, 1):
        for dx in order:
            to_core(kind, side_of(dx)).start()
            load(kind, side_of(dx)).start()
    yield
    for kind in (0, 1):
        for dx in order:
            side = side_of(dx)
            load(kind, side).wait()
            to_core(kind, side).wait_recv()
            add(kind, side)
            if dx > 0:
                to_chip(kind, side, x).start()
    yield

    for dx in range(1, tpx_n):
        to_chip(0, side_of(dx), side_of(dx)).wait_recv()
    tile = math.gcd(rows, 64)

    def over_x(step, carry):
        at = pl.ds(pl.multiple_of(step * tile, tile), tile)
        for half in range(ctx_n):
            summed = both_buf[0, x, half, at, :].astype(F32)
            for dx in range(1, tpx_n):
                summed = summed + both_buf[2, side_of(dx), half, at, :].astype(F32)
            both_buf[0, x, half, at, :] = summed.astype(BF16)
        return carry

    lax.fori_loop(0, rows // tile, over_x, 0)

    def to_y(dy, half, slot):
        return pltpu.make_async_remote_copy(
            src_ref=both_buf.at[0, x, half],
            dst_ref=halves.at[slot],
            send_sem=y_sem.at[0, dy],
            recv_sem=y_sem.at[1, dy],
            device_id=(fo, z, half, x, c),
            device_id_type=MESH_ID,
        )

    for dy in range(1, ctx_n):
        to_y(dy, lax.rem(y + dy, ctx_n), y).start()
    yield
    for dy in range(1, ctx_n):
        source = lax.rem(y + ctx_n - dy, ctx_n)
        to_y(dy, y, source).wait_recv()

    def over_y(step, carry):
        at = pl.ds(pl.multiple_of(step * tile, tile), tile)
        summed = both_buf[0, x, y, at, :].astype(F32)
        for dy in range(1, ctx_n):
            summed = summed + halves[lax.rem(y + ctx_n - dy, ctx_n), at, :].astype(F32)
        both_out[pl.ds(pl.multiple_of(q * rows + step * tile, tile), tile), :] = summed.astype(BF16)
        return carry

    lax.fori_loop(0, rows // tile, over_y, 0)

    def to_tp(step, owner):
        peer = lax.rem(q + step, tp_n)
        held = both_out.at[pl.ds(pl.multiple_of(owner * rows, rows), rows), :]
        return pltpu.make_async_remote_copy(
            src_ref=both_out.at[pl.ds(pl.multiple_of(q * rows, rows), rows), :],
            dst_ref=held,
            send_sem=tp_sem.at[0, step],
            recv_sem=tp_sem.at[1, step],
            device_id=(fo, z, y, peer // tpc_n, lax.rem(peer, tpc_n)),
            device_id_type=MESH_ID,
        )

    for step in range(1, tp_n):
        to_tp(step, q).start()
    yield
    for dx in range(1, tpx_n):
        to_chip(1, side_of(dx), side_of(dx)).wait_recv()
    tall = math.gcd(parts_out.shape[0], 64)

    def last(step, carry):
        at = pl.ds(pl.multiple_of(step * tall, tall), tall)
        summed = parts_buf[0, x, at, :].astype(F32)
        for dx in range(1, tpx_n):
            summed = summed + parts_buf[2, side_of(dx), at, :].astype(F32)
        parts_out[at, :] = summed
        return carry

    lax.fori_loop(0, parts_out.shape[0] // tall, last, 0)
    for step in range(1, tp_n):
        to_tp(step, q).wait_send()
        to_tp(step, lax.rem(q + tp_n - step, tp_n)).wait_recv()
    for dy in range(1, ctx_n):
        to_y(dy, lax.rem(y + dy, ctx_n), y).wait_send()
    for kind in (0, 1):
        for dx in range(tpx_n):
            to_core(kind, side_of(dx)).wait_send()
            if dx > 0:
                to_chip(kind, side_of(dx), x).wait_send()


def routed_body(
    rows_ref, grads_ref, gate_ref, gate_w, up_w, down_w, dgate_ref, dup_ref, act_ref, sum_ref, drows_ref
):
    gate_pre = dot_nt(rows_ref[...], gate_w[...])
    up_pre = dot_nt(rows_ref[...], up_w[...])
    silu, slope = silu_parts(gate_pre)
    act = (silu * up_pre).astype(BF16)
    act_ref[...] = act
    dact = dot_nt(grads_ref[...], down_w[...])
    sum_ref[...] = jnp.sum(act.astype(F32) * dact, axis=1, keepdims=True)
    dact = dact * gate_ref[...]
    dgate = (dact * up_pre * slope).astype(BF16)
    dup = (dact * silu).astype(BF16)
    dgate_ref[...] = dgate
    dup_ref[...] = dup
    drows_ref[...] = (dot(dgate, gate_w[...]) + dot(dup, up_w[...])).astype(BF16)


def routed(rows, grads, gate, gate_w, up_w, down_w):
    slots, width = rows.shape
    hidden = gate_w.shape[0]
    tile = math.gcd(slots, 256)

    def tiles(columns):
        return pl.BlockSpec((tile, columns), lambda i: (i, 0))

    held = pl.BlockSpec((hidden, width), lambda i: (0, 0), pipeline_mode=pl.Buffered(1))
    wide = jax.ShapeDtypeStruct((slots, hidden), BF16)
    return pl.pallas_call(
        routed_body,
        out_shape=(
            wide,
            wide,
            wide,
            jax.ShapeDtypeStruct((slots, 1), F32),
            jax.ShapeDtypeStruct((slots, width), BF16),
        ),
        grid=(slots // tile,),
        in_specs=[tiles(width), tiles(width), tiles(1), held, held, held],
        out_specs=[tiles(hidden), tiles(hidden), tiles(hidden), tiles(1), tiles(width)],
        compiler_params=pltpu.CompilerParams(vmem_limit_bytes=58 << 20),
        cost_estimate=pl.CostEstimate(
            flops=10 * slots * width * hidden,
            bytes_accessed=50_000_000,
            transcendentals=slots * hidden,
        ),
        name="routed",
    )(rows, grads, gate, gate_w, up_w, down_w)


def attend_body(place_ref, q_ref, kv_ref, rope_ref, out_ref, log_ref):
    block_rows, key_count = q_ref.shape[0], kv_ref.shape[0]
    first = place_ref[0] + pl.program_id(1) * block_rows
    keys = jnp.concatenate([kv_ref[:, :NOPE], rope_ref[...]], axis=1)
    scores = dot_nt(q_ref[...], keys)
    row = first + lax.broadcasted_iota(jnp.int32, (block_rows, 1), 0)
    limit = jnp.maximum(row, place_ref[1] - 1)
    key = lax.broadcasted_iota(jnp.int32, (block_rows, key_count), 1)
    scores = jnp.where(key <= limit, scores, -1e30)
    top = jnp.max(scores, axis=1, keepdims=True)
    exponent = jnp.exp(scores - top)
    row_total = jnp.sum(exponent, axis=1, keepdims=True)
    summed = jnp.dot(exponent.astype(BF16), kv_ref[:, NOPE:], preferred_element_type=F32)
    out_ref[...] = (summed / row_total).astype(BF16)
    log_total = jnp.broadcast_to(top + jnp.log(row_total), (block_rows, 128))
    log_ref[0] = log_total.T[:1]

def attend(place, query, key_value, rope, block_rows):
    rows, key_count = query.shape[0], key_value.shape[0]
    heads = query.shape[1] // HEAD
    return pl.pallas_call(
        attend_body,
        out_shape=(jax.ShapeDtypeStruct((rows, heads * VDIM), BF16), jax.ShapeDtypeStruct((heads, 1, rows), F32)),
        grid_spec=pltpu.PrefetchScalarGridSpec(
            num_scalar_prefetch=1,
            grid=(heads, rows // block_rows),
            in_specs=[
                pl.BlockSpec((block_rows, HEAD), lambda h, i, s: (i, h)),
                pl.BlockSpec((key_count, HEAD), lambda h, i, s: (0, h)),
                pl.BlockSpec((key_count, NOPE), lambda h, i, s: (0, 0)),
            ],
            out_specs=[
                pl.BlockSpec((block_rows, VDIM), lambda h, i, s: (i, h)),
                pl.BlockSpec((1, 1, block_rows), lambda h, i, s: (h, 0, i)),
            ],
        ),
        compiler_params=pltpu.CompilerParams(vmem_limit_bytes=48 << 20),
        cost_estimate=pl.CostEstimate(flops=4 * rows * key_count * heads * HEAD, bytes_accessed=20_000_000, transcendentals=rows * key_count * heads),
        name="attend",
    )(place, query, key_value, rope)

def attend_back_body(place_ref, q_ref, kv_ref, rope_ref, dout_ref, log_ref, table_ref, dq_ref, dkv_ref, drope_ref, keys_acc, values_acc):
    block_rows, key_count = q_ref.shape[0], kv_ref.shape[0]
    head, step = pl.program_id(0), pl.program_id(1)
    first = place_ref[0] + step * block_rows
    keys = jnp.concatenate([kv_ref[:, :NOPE], rope_ref[...]], axis=1)
    scores = dot_nt(keys, q_ref[...])
    row = first + lax.broadcasted_iota(jnp.int32, (1, block_rows), 1)
    limit = jnp.maximum(row, place_ref[1] - 1)
    key = lax.broadcasted_iota(jnp.int32, (key_count, block_rows), 0)
    soft = jnp.exp(jnp.where(key <= limit, scores, -1e30) - log_ref[0])
    soft_grad = dot_nt(kv_ref[:, NOPE:], dout_ref[...])
    mean = jnp.sum(soft * soft_grad, axis=0, keepdims=True)
    score_grad = (soft * (soft_grad - mean)).astype(BF16)
    values = jnp.dot(soft.astype(BF16), dout_ref[...], preferred_element_type=F32)
    keys_grad = jnp.dot(score_grad, q_ref[...], preferred_element_type=F32)
    dq_ref[...] = (dot_tn(score_grad, keys) * table_ref[...]).astype(BF16)

    @pl.when(step == 0)
    def _():
        keys_acc[...] = keys_grad
        values_acc[...] = values

    @pl.when(step > 0)
    def _():
        keys_acc[...] += keys_grad
        values_acc[...] += values

    @pl.when(step == pl.num_programs(1) - 1)
    def _():
        dkv_ref[...] = jnp.concatenate([keys_acc[:, :NOPE], values_acc[...]], axis=1).astype(BF16)

        @pl.when(head == 0)
        def _():
            drope_ref[...] = keys_acc[:, NOPE:]

        @pl.when(head > 0)
        def _():
            drope_ref[...] += keys_acc[:, NOPE:]

def attend_back(place, query, key_value, rope, dout, log_total, table, block_rows):
    rows, key_count = query.shape[0], key_value.shape[0]
    heads = query.shape[1] // HEAD
    return pl.pallas_call(
        attend_back_body,
        out_shape=(jax.ShapeDtypeStruct((rows, heads * HEAD), BF16), jax.ShapeDtypeStruct((key_count, heads * HEAD), BF16), jax.ShapeDtypeStruct((key_count, NOPE), F32)),
        grid_spec=pltpu.PrefetchScalarGridSpec(
            num_scalar_prefetch=1,
            grid=(heads, rows // block_rows),
            in_specs=[
                pl.BlockSpec((block_rows, HEAD), lambda h, i, s: (i, h)),
                pl.BlockSpec((key_count, HEAD), lambda h, i, s: (0, h)),
                pl.BlockSpec((key_count, NOPE), lambda h, i, s: (0, 0)),
                pl.BlockSpec((block_rows, VDIM), lambda h, i, s: (i, h)),
                pl.BlockSpec((1, 1, block_rows), lambda h, i, s: (h, 0, i)),
                pl.BlockSpec((block_rows, HEAD), lambda h, i, s: (i, 0)),
            ],
            out_specs=[
                pl.BlockSpec((block_rows, HEAD), lambda h, i, s: (i, h)),
                pl.BlockSpec((key_count, HEAD), lambda h, i, s: (0, h)),
                pl.BlockSpec((key_count, NOPE), lambda h, i, s: (0, 0)),
            ],
            scratch_shapes=[pltpu.VMEM((key_count, HEAD), F32), pltpu.VMEM((key_count, VDIM), F32)],
        ),
        compiler_params=pltpu.CompilerParams(vmem_limit_bytes=56 << 20),
        cost_estimate=pl.CostEstimate(
            flops=10 * rows * key_count * heads * HEAD,
            bytes_accessed=40_000_000,
            transcendentals=rows * key_count * heads,
        ),
        name="attend_back",
    )(place, query, key_value, rope, dout, log_total, table)


def build(sizes):
    fo_n, fi_n, ctx_n, tpx_n, tpc_n = (sizes[name] for name in ("fo", "fi", "ctx", "tpx", "tpc"))
    tp_n = tpx_n * tpc_n
    row_shards = fo_n * fi_n * ctx_n
    plane_experts = ctx_n * tpx_n
    z_part = fi_n // tpc_n

    def expert_weights(gate, up, down):
        local = jnp.stack([gate.transpose(0, 2, 1), up.transpose(0, 2, 1), down], axis=1)
        return lax.all_gather(local, "fo", axis=0) if fo_n > 1 else local[None]

    def shard_of(weight):
        return lax.all_gather(weight, "fo", axis=0) if fo_n > 1 else weight[None]

    def fo_sum(part, kind):
        if fo_n == 1:
            return part
        if kind == "col":
            a = part.shape[0]
            part = part.reshape(a, fo_n, -1)
            return lax.psum_scatter(part, "fo", scatter_dimension=1, tiled=True).reshape(a, -1)
        return lax.psum_scatter(part, "fo", scatter_dimension=0, tiled=True)

    def own_expert_grads(mine):
        mine = mine.reshape((fo_n, -1) + mine.shape[1:])
        got = lax.all_to_all(mine, CHIPS, split_axis=1, concat_axis=1, tiled=True)
        if fo_n > 1:
            got = lax.psum_scatter(got, "fo", scatter_dimension=0, tiled=True)
        got = got[0].astype(F32)
        return (got[:, 0].transpose(0, 2, 1), got[:, 1].transpose(0, 2, 1), got[:, 2])

    def shards(
        tokens,
        out_grad,
        routes,
        slot_index,
        prefix,
        attn_gain,
        query_weight,
        latent_down,
        latent_gain,
        latent_up,
        out_weight,
        moe_gain,
        router_weight,
        shared_gate,
        shared_up,
        shared_down,
        expert_gate,
        expert_up,
        expert_down,
    ):
        row_count, width = tokens.shape
        expert_count = expert_gate.shape[0]
        capacity = row_count * routes.shape[1] // expert_count
        quarter = width // tp_n
        tp_index = lax.axis_index(TP)
        own_expert = lax.axis_index(CHIPS)
        plane_base = lax.axis_index("fi") * plane_experts

        def columns(values):
            return lax.dynamic_slice_in_dim(values, tp_index * quarter, quarter, values.ndim - 1)

        depth = latent_down.shape[0]
        down_width = latent_down.shape[1]

        def turned(weight):
            half = weight.shape[-1] // 2
            return jnp.concatenate([-weight[..., half:], weight[..., :half]], axis=-1)

        small = jnp.concatenate(
            [
                latent_down,
                turned(latent_down[:, KVR:]),
                attn_gain[:, None],
                moe_gain[:, None],
                jnp.pad(latent_gain, (0, depth - latent_gain.shape[0]))[:, None],
                router_weight,
            ],
            axis=1,
        )
        used = small.shape[1]
        small = jnp.pad(small, ((0, 0), (0, -used % 128)))
        keys = jnp.where(slot_index < capacity, routes * capacity + slot_index, -1).T
        keys = jnp.pad(keys, ((0, 8 - keys.shape[0]), (0, 0)), constant_values=-1)
        (small, query_full, up_full, out_full, keys_all), *_ = exchange(
            sizes,
            [
                collect_job(
                    sizes,
                    ("share", "row", "row", "col", "row"),
                    [shard_of(w) for w in (small, query_weight, latent_up, out_weight, keys)],
                )
            ],
            4,
            "collect_attention",
        )
        local_weights, small = lax.optimization_barrier(
            (expert_weights(expert_gate, expert_up, expert_down), small)
        )
        routed_weights = lax.all_to_all(
            local_weights, CHIPS, split_axis=1, concat_axis=1, tiled=True
        )
        small = small.reshape(row_shards * depth, -1)
        wide_down = small[:, : down_width + ROPE]
        down_full = small[:, :down_width]
        gain_at = down_width + ROPE
        gain_one = small[:, gain_at].astype(F32)
        gain_two = small[:, gain_at + 1].astype(F32)
        gain_latent = (
            small[:, gain_at + 2]
            .reshape(row_shards, depth)[:, : latent_gain.shape[0]]
            .reshape(-1)
            .astype(F32)
        )
        router_full = small[:, gain_at + 3 : used]

        keys_all = lax.dynamic_slice_in_dim(
            keys_all, lax.axis_index("fo") * (fi_n * ctx_n * 8), fi_n * ctx_n * 8, 0
        ).reshape(fi_n, ctx_n, 8, row_count)
        keys_column = lax.dynamic_index_in_dim(keys_all, lax.axis_index("ctx"), 1, keepdims=False)
        first_keys = (plane_base + jnp.arange(plane_experts, dtype=jnp.int32)) * capacity
        rel = keys_column[:, None] - first_keys[:, None, None]
        plane_slots = jnp.max(jnp.where((rel >= 0) & (rel < capacity), rel, -1), axis=2)
        token_slots = plane_slots.transpose(0, 2, 1)

        def give_back(rows, gates, bases=None):
            rows = rows.reshape(z_part, ctx_n, capacity, width)
            return give_back_job(sizes, rows, token_slots, gates, bases)

        (slot_grads,), (shared_gate_full, shared_up_full, shared_down_full) = exchange(
            sizes,
            [
                dispatch_job(sizes, columns(out_grad), plane_slots, capacity),
                collect_job(
                    sizes,
                    ("row", "row", "col"),
                    [shard_of(w) for w in (shared_gate, shared_up, shared_down)],
                ),
            ],
            0,
            "dispatch_grads",
        )
        slot_grads = slot_grads.reshape(-1, width)

        head_count = query_full.shape[1] // (NOPE + ROPE)
        hidden = tokens.astype(F32)
        scale_one = rms_scale(hidden)
        normed_one = hidden * scale_one
        normed_in = (normed_one * gain_one).astype(BF16)
        seq_index = lax.axis_index(("fo", "fi"))
        prefix_len = lax.dynamic_index_in_dim(prefix, seq_index, keepdims=False)
        row_offset = lax.axis_index("ctx") * row_count
        query_pos = row_offset + jnp.arange(row_count, dtype=jnp.int32)
        cos_table, sin_table = rotation_tables(query_pos, ROPE // 2)
        score_scale = (NOPE + ROPE) ** (-0.5)
        cos_wide = jnp.concatenate([cos_table, cos_table], axis=1)
        sin_wide = jnp.concatenate([sin_table, sin_table], axis=1)
        table = score_scale * jnp.concatenate(
            [jnp.ones((row_count, NOPE), F32), cos_wide, sin_wide], axis=1
        )

        latent_raw = dot(normed_in, wide_down)
        latent_part = latent_raw[:, :KVR]
        scale_latent = rms_scale(latent_part)
        normed_latent = latent_part * scale_latent
        latent = (normed_latent * gain_latent).astype(BF16)
        key_rope = (
            latent_raw[:, KVR : KVR + ROPE] * cos_wide + latent_raw[:, KVR + ROPE :] * sin_wide
        ).astype(BF16)
        both = lax.all_gather(
            jnp.concatenate([latent, key_rope, key_rope], axis=1), "ctx", axis=0, tiled=True
        )
        latent_all, rope_all = both[:, :KVR], both[:, KVR:]
        query_heads = query_full.reshape(width, head_count, NOPE + ROPE)
        query_wide = jnp.concatenate(
            [query_heads, turned(query_heads[..., NOPE:])], axis=-1
        ).reshape(width, head_count * HEAD)
        query_in = (
            dot(normed_in, query_wide).reshape(row_count, head_count, HEAD) * table[:, None]
        ).astype(BF16).reshape(row_count, head_count * HEAD)
        key_value = dot(latent_all, up_full).astype(BF16)
        place = jnp.stack([row_offset, prefix_len]).astype(jnp.int32)
        block_rows = min(256, row_count)
        attended, log_totals = attend(place, query_in, key_value, rope_all, block_rows)

        def tp_scatter(parts):
            parts = jnp.stack([part.astype(BF16) for part in parts])
            return lax.psum_scatter(parts, TP, scatter_dimension=0, tiled=True)[0].astype(F32)

        def quarters(weight, axis):
            return jnp.split(weight, tp_n, axis=axis)

        attn_out = tp_scatter([dot(attended, part) for part in quarters(out_full, 1)])
        attn_out, slot_grads = lax.optimization_barrier((attn_out, slot_grads))
        residual = columns(tokens).astype(F32) + attn_out
        scale_two = lax.rsqrt(
            lax.psum(jnp.sum(residual * residual, axis=-1, keepdims=True), TP) / width + EPSILON
        )
        normed_two = residual * scale_two
        gain_two_part = columns(gain_two[None])
        mid_part = (normed_two * gain_two_part).astype(BF16)

        (slot_rows,), (gate_full, expert_up_full, down_weight), (normed_mid,) = exchange(
            sizes,
            [
                dispatch_job(sizes, mid_part, plane_slots, capacity),
                place_job(sizes, routed_weights),
                spread_job(sizes, mid_part),
            ],
            1,
            "dispatch_rows",
        )
        slot_rows = slot_rows.reshape(-1, width)

        logits = dot(normed_mid, router_full)
        router_prob = jax.nn.softmax(logits, axis=-1)
        slot_prob = jax.nn.softmax(dot(slot_rows, router_full), axis=-1)
        slot_gate = lax.dynamic_slice_in_dim(slot_prob, own_expert, 1, 1)

        gate_pre = dot(normed_mid, shared_gate_full)
        up_pre = dot(normed_mid, shared_up_full)
        shared_dact = dot_nt(out_grad, shared_down_full)
        shared_silu, shared_slope = silu_parts(gate_pre)
        shared_act = (shared_silu * up_pre).astype(BF16)
        shared_dgate = (shared_dact * up_pre * shared_slope).astype(BF16)
        shared_dup = (shared_dact * shared_silu).astype(BF16)
        mid_shared = tp_scatter(
            [
                dot_nt(shared_dgate, gate_part) + dot_nt(shared_dup, up_part)
                for gate_part, up_part in zip(
                    quarters(shared_gate_full, 0), quarters(shared_up_full, 0)
                )
            ]
        )
        out_shared = tp_scatter([dot(shared_act, part) for part in quarters(shared_down_full, 1)])

        expert_dgate, expert_dup, expert_act, slot_gate_grad, slot_drows = routed(
            slot_rows, slot_grads, slot_gate, gate_full, expert_up_full, down_weight
        )
        gate_rows = jnp.broadcast_to(
            slot_gate_grad.reshape(z_part, ctx_n, 1, capacity), (z_part, ctx_n, 8, capacity)
        )
        sdown_grad = dot_tn(shared_act, out_grad)
        sgate_grad = dot_tn(normed_mid, shared_dgate)
        sup_grad = dot_tn(normed_mid, shared_dup)
        shared_kinds = ("row", "row", "col")
        shared_parts = [
            fo_sum(part.astype(BF16), kind)
            for part, kind in zip((sgate_grad, sup_grad, sdown_grad), shared_kinds)
        ]
        slot_dout = (slot_grads.astype(F32) * slot_gate).astype(BF16)
        shared_own, (mid_routed, prob_grad), expert_grads = exchange(
            sizes,
            [
                finish_job(sizes, shared_kinds, shared_parts, []),
                give_back(slot_drows.astype(BF16), gate_rows),
                products_job(
                    sizes,
                    [expert_dgate, expert_dup, expert_act],
                    [slot_rows, slot_dout],
                    [0, 0, 1],
                ),
            ],
            2,
            "give_back_rows",
            vmem=60,
        )
        sgate_grad, sup_grad, sdown_grad = (part.astype(F32) for part in shared_own)
        prob_grad = prob_grad.T
        logit_grad = (
            router_prob * (prob_grad - jnp.sum(router_prob * prob_grad, axis=-1, keepdims=True))
        ).astype(BF16)

        mid_routed, mid_shared, out_shared = lax.optimization_barrier(
            (mid_routed, mid_shared, out_shared)
        )
        mid_total = mid_shared + mid_routed + dot_nt(logit_grad, columns(router_full.T).T)
        gain_two_grad = jnp.sum(mid_total * normed_two, axis=0)
        dn_two = mid_total * gain_two_part
        dot_two = lax.psum(jnp.sum(dn_two * normed_two, axis=-1, keepdims=True), TP) / width
        residual_grad = columns(out_grad).astype(F32) + scale_two * (dn_two - normed_two * dot_two)
        (routed_grads,), (attn_dout,) = exchange(
            sizes,
            [pair_job(sizes, expert_grads), spread_job(sizes, residual_grad.astype(BF16))],
            7,
            "pair_sum",
        )

        out_weight_grad = dot_tn(attended, attn_dout)
        attended_grad = dot_nt(attn_dout, out_full).astype(BF16)
        attended_grad, routed_grads = lax.optimization_barrier((attended_grad, routed_grads))
        egate_grad, eup_grad, edown_grad = own_expert_grads(routed_grads)
        query_grad, kv_grad, rope_grad = attend_back(
            place, query_in, key_value, rope_all, attended_grad, log_totals, table,
            min(512, row_count),
        )
        late_act, query_grad = lax.optimization_barrier((expert_act, query_grad))
        expert_out = (dot(late_act, down_weight) * slot_gate).astype(BF16)
        up_grad = dot_tn(latent_all, kv_grad)
        latent_grad = dot_nt(kv_grad, up_full)
        query_wide_grad = dot_tn(normed_in, query_grad).reshape(width, head_count, HEAD)
        query_weight_grad = jnp.concatenate(
            [
                query_wide_grad[..., :NOPE],
                query_wide_grad[..., NOPE : NOPE + ROPE] - turned(query_wide_grad[..., NOPE + ROPE :]),
            ],
            axis=-1,
        ).reshape(width, head_count * (NOPE + ROPE))
        input_parts = jnp.stack(
            [dot_nt(query_grad, part).astype(BF16) for part in quarters(query_wide, 0)]
        )
        ((both_grad, input_part),) = exchange(
            sizes,
            [
                reduce_job(
                    sizes,
                    jnp.concatenate([latent_grad, rope_grad], axis=1).astype(BF16),
                    input_parts,
                )
            ],
            6,
            "sum_inputs",
        )
        both_grad = both_grad.astype(F32)
        latent_own = both_grad[:, :KVR]
        rope_own = both_grad[:, KVR : KVR + ROPE] + both_grad[:, KVR + ROPE :]
        gain_latent_grad = jnp.sum(latent_own * normed_latent, axis=0)
        latent_raw_grad = norm_back(latent_own * gain_latent, normed_latent, scale_latent)
        down_out_grad = jnp.concatenate(
            [latent_raw_grad, rotate(rope_own, cos_table, -sin_table)], axis=-1
        ).astype(BF16)
        down_grad = dot_tn(normed_in, down_out_grad)
        input_total = input_part + dot_nt(
            down_out_grad, lax.dynamic_slice_in_dim(down_full, tp_index * quarter, quarter, 0)
        )
        normed_one_part = columns(normed_one)
        gain_one_grad = jnp.sum(input_total * normed_one_part, axis=0)
        dn_one = input_total * columns(gain_one[None])
        dot_one = lax.psum(jnp.sum(dn_one * normed_one_part, axis=-1, keepdims=True), TP) / width
        token_grad = residual_grad + scale_one * (dn_one - normed_one_part * dot_one)
        token_grad, egate_grad, eup_grad, edown_grad = lax.optimization_barrier(
            (token_grad, egate_grad, eup_grad, edown_grad)
        )
        router_grad = dot_tn(normed_mid, logit_grad)
        pack_grad = jnp.concatenate([down_grad, router_grad], axis=1)
        pack_used = pack_grad.shape[1]
        pack_grad = jnp.pad(pack_grad, ((0, 0), (0, -pack_used % 128)))
        gains = jnp.stack([gain_one_grad, gain_two_grad])
        gains = lax.dynamic_update_slice_in_dim(
            jnp.zeros((2, width), F32), gains, tp_index * quarter, 1
        )
        latent_rows = jnp.pad(
            gain_latent_grad.reshape(row_shards, -1),
            ((0, 0), (0, depth - latent_gain.shape[0])),
        ).reshape(1, width)
        gains = jnp.concatenate([gains, latent_rows * (tp_index == 0).astype(F32)], axis=0)
        gains = jnp.pad(
            gains.reshape(3, row_shards, depth).transpose(1, 0, 2), ((0, 0), (0, 13), (0, 0))
        ).reshape(row_shards * 16, depth)
        kinds = ("share", "sum", "row", "row", "col")
        partials = (pack_grad, gains, query_weight_grad, up_grad, out_weight_grad)
        (output,), done = exchange(
            sizes,
            [
                give_back(expert_out, None, (residual, out_shared)),
                finish_job(
                    sizes,
                    kinds,
                    [fo_sum(part.astype(BF16), kind) for part, kind in zip(partials, kinds)],
                    [token_grad.astype(BF16)],
                ),
            ],
            3,
            "finish_attention",
        )
        pack_own = done[0].reshape(depth, -1).astype(F32)
        gains_own = done[1].astype(F32)
        query_weight_grad, up_grad, out_weight_grad = (part.astype(F32) for part in done[2:5])
        token_grad = done[5].astype(F32)
        return (
            output,
            token_grad,
            gains_own[0],
            query_weight_grad,
            pack_own[:, :down_width],
            gains_own[2, : latent_gain.shape[0]],
            up_grad,
            out_weight_grad,
            gains_own[1],
            pack_own[:, down_width:pack_used],
            sgate_grad,
            sup_grad,
            sdown_grad,
            egate_grad,
            eup_grad,
            edown_grad,
        )

    return shards


EXPERTS = 16


def solution(mesh):
    ctx_n, tp_n = mesh.shape["ctx"], mesh.shape["tp"]
    tpc_n = 2
    tpx_n = tp_n // tpc_n
    fi_n = EXPERTS // (ctx_n * tpx_n)
    sizes = {
        "fo": mesh.shape["fsdp"] // fi_n,
        "fi": fi_n,
        "ctx": ctx_n,
        "tpx": tpx_n,
        "tpc": tpc_n,
    }
    fine = Mesh(mesh.devices.reshape(tuple(sizes.values())), tuple(sizes))
    rows = P(ROWS)
    rows_two = P(ROWS, None)
    rows_tp = P(ROWS, TP)
    tp_rows = P(TP, ROWS)
    wide_in = P(None, ROWS, TP)
    wide_out = P(None, TP, ROWS)
    weights = (
        rows,
        rows_tp,
        rows_two,
        rows,
        rows_tp,
        tp_rows,
        rows,
        rows_two,
        rows_tp,
        rows_tp,
        tp_rows,
        wide_in,
        wide_in,
        wide_out,
    )
    return jax.shard_map(
        build(sizes),
        mesh=fine,
        in_specs=(rows_two, rows_two, rows_two, rows_two, P()) + weights,
        out_specs=(rows_two, rows_two) + weights,
        check_vma=False,
    )
```

```python
import functools
import math

import jax
import jax.numpy as jnp
from jax import lax
from jax.experimental import pallas as pl
from jax.experimental.pallas import tpu as pltpu
from jax.sharding import Mesh
from jax.sharding import PartitionSpec as P

NOPE = 128
ROPE = 64
KVR = 512
VDIM = 128
HEAD = 256

EPSILON = 1e-06
THETA_BASE = 10000.0
F32 = jnp.float32
BF16 = jnp.bfloat16
MESH_ID = pl.DeviceIdType.MESH

ROWS = ("fo", "fi", "ctx")
TP = ("tpx", "tpc")
PLANE = ("ctx", "tpx", "tpc")
CHIPS = ("fi", "ctx", "tpx")


def rotation_tables(positions, half_width):
    freq_table = jnp.exp(jnp.arange(half_width, dtype=F32) * (-math.log(THETA_BASE) / half_width))
    angle_table = positions.astype(F32)[:, None] * freq_table[None, :]
    return (jnp.cos(angle_table), jnp.sin(angle_table))


def rotate(values, cos_table, sin_table):
    half_width = values.shape[-1] // 2
    first_half = values[..., :half_width]
    second_half = values[..., half_width:]
    return jnp.concatenate(
        [
            first_half * cos_table - second_half * sin_table,
            second_half * cos_table + first_half * sin_table,
        ],
        axis=-1,
    )


def silu_parts(values):
    sigma = jax.nn.sigmoid(values)
    return (values * sigma, sigma * (1.0 + values * (1.0 - sigma)))


def rms_scale(values):
    return lax.rsqrt(jnp.mean(values * values, axis=-1, keepdims=True) + EPSILON)


def norm_back(grad_normed, normed, scale_rows):
    return scale_rows * (
        grad_normed - normed * jnp.mean(grad_normed * normed, axis=-1, keepdims=True)
    )


def dot(left, right):
    return jnp.dot(left, right, preferred_element_type=F32)


def dot_nt(left, right):
    return lax.dot_general(left, right, (((1,), (1,)), ((), ())), preferred_element_type=F32)


def dot_tn(left, right):
    return lax.dot_general(left, right, (((0,), (0,)), ((), ())), preferred_element_type=F32)


def ein(spec, left, right):
    return jnp.einsum(spec, left, right, preferred_element_type=F32)


def plane_place(sizes):
    tpx_n, tpc_n = sizes["tpx"], sizes["tpc"]
    fo, z, y, x, c = (lax.axis_index(name) for name in ("fo", "fi", "ctx", "tpx", "tpc"))
    own = (y * tpx_n + x) * tpc_n + c

    def device(index, z_at=None):
        return (
            fo,
            z if z_at is None else z_at,
            index // (tpx_n * tpc_n),
            lax.rem(index // tpc_n, tpx_n),
            lax.rem(index, tpc_n),
        )

    return z, y, x, c, own, device


def greet_plane(sizes):
    fi_n = sizes["fi"]
    plane_n = sizes["ctx"] * sizes["tpx"] * sizes["tpc"]
    z, y, x, c, own, device = plane_place(sizes)
    barrier = pltpu.get_barrier_semaphore()
    for step in range(1, plane_n):
        pl.semaphore_signal(
            barrier,
            inc=1,
            device_id=device(lax.rem(own + step, plane_n)),
            device_id_type=MESH_ID,
        )
    for near in (-1, 1):

        @pl.when((z + near >= 0) & (z + near < fi_n))
        def _():
            pl.semaphore_signal(
                barrier, inc=1, device_id=device(own, z + near), device_id_type=MESH_ID
            )

    sides = (z > 0).astype(jnp.int32) + (z < fi_n - 1).astype(jnp.int32)
    pl.semaphore_wait(barrier, plane_n - 1 + sides)


HBM_SPEC = pl.BlockSpec(memory_space=pl.ANY)
VMEM_SPEC = pl.BlockSpec(memory_space=pltpu.VMEM)


def exchange(sizes, jobs, collective_id, name, vmem=56):
    counts = [(len(job["args"]), len(job["outs"]), len(job["scratch"])) for job in jobs]

    def body(*refs):
        at = [0, sum(n[0] for n in counts), sum(n[0] + n[1] for n in counts)]
        running = []
        for job, count in zip(jobs, counts):
            given = [refs[at[k] : at[k] + count[k]] for k in range(3)]
            at = [at[k] + count[k] for k in range(3)]
            running.append(job["run"](sizes, *given))
        greet_plane(sizes)
        while running:
            running = [run for run in running if next(run, "ended") != "ended"]

    results = pl.pallas_call(
        body,
        out_shape=tuple(shape for job in jobs for shape, _ in job["outs"]),
        in_specs=[spec for job in jobs for _, spec in job["args"]],
        out_specs=tuple(spec for job in jobs for _, spec in job["outs"]),
        scratch_shapes=[shape for job in jobs for shape in job["scratch"]],
        compiler_params=pltpu.CompilerParams(
            collective_id=collective_id, has_side_effects=True, vmem_limit_bytes=vmem << 20
        ),
        cost_estimate=pl.CostEstimate(
            flops=0, bytes_accessed=20_000_000, transcendentals=0
        ),
        name=name,
    )(*[arg for job in jobs for arg, _ in job["args"]])
    grouped, at = [], 0
    for _, count, _ in counts:
        grouped.append(results[at : at + count])
        at += count
    return grouped


def columns_of(whole, wide):
    def slab(owner):
        return whole.at[:, pl.ds(pl.multiple_of(owner * wide, wide), wide)]

    return slab


def tp_spread(sizes, source, held, slab_of, sems):
    tpx_n, tpc_n = sizes["tpx"], sizes["tpc"]
    keep_sem, x_send, x_recv, c_send, c_recv = sems
    fo, z, y, x, c = (lax.axis_index(n) for n in ("fo", "fi", "ctx", "tpx", "tpc"))

    def slab(side, core):
        return slab_of(side * tpc_n + core)

    def origin(dx):
        return lax.rem(x + tpx_n - dx, tpx_n)

    keep = None if held is None else pltpu.make_async_copy(held, slab(x, c), keep_sem)

    def to_chip(dx, side):
        return pltpu.make_async_remote_copy(
            src_ref=source,
            dst_ref=slab(side, c),
            send_sem=x_send.at[dx],
            recv_sem=x_recv.at[dx],
            device_id=(fo, z, y, lax.rem(x + dx, tpx_n), c),
            device_id_type=MESH_ID,
        )

    def to_core(dx, dc, core):
        return pltpu.make_async_remote_copy(
            src_ref=source if dx == 0 else slab(origin(dx), c),
            dst_ref=slab(origin(dx), core),
            send_sem=c_send.at[dx, dc],
            recv_sem=c_recv.at[dx, dc],
            device_id=(fo, z, y, x, lax.rem(c + dc, tpc_n)),
            device_id_type=MESH_ID,
        )

    def start():
        for dx in range(1, tpx_n):
            to_chip(dx, x).start()
        for dc in range(1, tpc_n):
            to_core(0, dc, c).start()

    def relay():
        for dx in range(1, tpx_n):
            to_chip(dx, origin(dx)).wait_recv()
            for dc in range(1, tpc_n):
                to_core(dx, dc, c).start()

    def settle():
        if keep is not None:
            keep.wait()
        for dx in range(tpx_n):
            if dx > 0:
                to_chip(dx, x).wait_send()
            for dc in range(1, tpc_n):
                to_core(dx, dc, c).wait_send()
                to_core(dx, dc, lax.rem(c + tpc_n - dc, tpc_n)).wait_recv()

    return start, keep, relay, settle


def tp_spread_sems(sizes):
    tpx_n, tpc_n = sizes["tpx"], sizes["tpc"]
    return [
        pltpu.SemaphoreType.DMA,
        pltpu.SemaphoreType.DMA((tpx_n,)),
        pltpu.SemaphoreType.DMA((tpx_n,)),
        pltpu.SemaphoreType.DMA((tpx_n, tpc_n)),
        pltpu.SemaphoreType.DMA((tpx_n, tpc_n)),
    ]


def spread_job(sizes, part):
    tp_n = sizes["tpx"] * sizes["tpc"]
    shape = (part.shape[0], part.shape[1] * tp_n)
    return {
        "args": [(part, HBM_SPEC)],
        "outs": [(jax.ShapeDtypeStruct(shape, BF16), HBM_SPEC)],
        "scratch": [pltpu.VMEM(part.shape, BF16), pltpu.SemaphoreType.DMA]
        + tp_spread_sems(sizes),
        "run": spread_run,
    }


def spread_run(sizes, args, outs, scratch):
    held, load_sem = scratch[:2]
    start, keep, relay, settle = tp_spread(
        sizes, args[0], held, columns_of(outs[0], held.shape[1]), scratch[2:]
    )
    load = pltpu.make_async_copy(args[0], held, load_sem)
    load.start()
    start()
    yield
    load.wait()
    keep.start()
    relay()
    yield
    settle()


def dispatch_job(sizes, part_rows, plane_slots, capacity):
    tokens, quarter = part_rows.shape
    fi_n, ctx_n, tpx_n, tpc_n = (sizes[n] for n in ("fi", "ctx", "tpx", "tpc"))
    z_part, plane_n, chips = fi_n // tpc_n, ctx_n * tpx_n * tpc_n, ctx_n * tpx_n
    shape = (z_part, ctx_n, capacity, quarter * tpx_n * tpc_n)
    return {
        "args": [(plane_slots, VMEM_SPEC), (part_rows, HBM_SPEC)],
        "outs": [(jax.ShapeDtypeStruct(shape, BF16), HBM_SPEC)],
        "scratch": [
            pltpu.VMEM((fi_n, tokens, quarter), BF16),
            pltpu.VMEM((fi_n, chips, capacity, quarter), BF16),
            pltpu.SemaphoreType.DMA,
            pltpu.SemaphoreType.DMA((2, fi_n)),
            pltpu.SemaphoreType.DMA((2, fi_n)),
            pltpu.SemaphoreType.DMA((fi_n, chips)),
            pltpu.SemaphoreType.DMA((plane_n, z_part)),
        ],
        "run": dispatch_run,
    }


def dispatch_run(sizes, args, outs, scratch):
    slots_ref, rows_ref = args
    (out_ref,) = outs
    held, picked, own_sem, line_send, line_recv, plane_send, plane_recv = scratch
    fi_n, tpx_n, tpc_n = sizes["fi"], sizes["tpx"], sizes["tpc"]
    plane_n = sizes["ctx"] * tpx_n * tpc_n
    chips = sizes["ctx"] * tpx_n
    z_part = fi_n // tpc_n
    capacity, quarter = picked.shape[2:]
    tokens = held.shape[1]
    z, y, x, c, own, device = plane_place(sizes)
    columns = pl.ds(pl.multiple_of((x * tpc_n + c) * quarter, quarter), quarter)
    load = pltpu.make_async_copy(rows_ref, held.at[z], own_sem)

    def line(side, step):
        block = z - step if side == 0 else z + step
        to = z + 1 if side == 0 else z - 1
        return pltpu.make_async_remote_copy(
            src_ref=held.at[block],
            dst_ref=held.at[block],
            send_sem=line_send.at[side, step],
            recv_sem=line_recv.at[side, step],
            device_id=device(own, to),
            device_id_type=MESH_ID,
        )

    def sends(side, step):
        block = z - step if side == 0 else z + step
        to = z + 1 if side == 0 else z - 1
        return (block >= 0) & (block < fi_n) & (to >= 0) & (to < fi_n)

    def plane_copy(block, chip):
        at = lax.rem(block, z_part)
        return pltpu.make_async_remote_copy(
            src_ref=picked.at[block, chip],
            dst_ref=out_ref.at[at, y, :, columns],
            send_sem=plane_send.at[block, chip],
            recv_sem=plane_recv.at[own, at],
            device_id=device(chip * tpc_n + block // z_part),
            device_id_type=MESH_ID,
        )

    def keep_copy(block, chip):
        return pltpu.make_async_copy(
            picked.at[block, chip],
            out_ref.at[lax.rem(block, z_part), y, :, columns],
            plane_send.at[block, chip],
        )

    def at_home(block, chip):
        return chip * tpc_n + block // z_part == own

    def pick(block):
        def one(chip, carry):
            wanted = slots_ref[block, pl.ds(chip, 1), :]
            rank = lax.broadcasted_iota(jnp.int32, (capacity, tokens), 0)
            hits = jnp.where(rank == wanted, 1.0, 0.0).astype(BF16)
            picked[block, chip] = jnp.dot(
                hits, held[block], preferred_element_type=F32
            ).astype(BF16)

            @pl.when(at_home(block, chip))
            def _():
                keep_copy(block, chip).start()

            @pl.when(jnp.logical_not(at_home(block, chip)))
            def _():
                plane_copy(block, chip).start()

            return carry

        lax.fori_loop(0, chips, one, 0)

    load.start()
    load.wait()
    for side in (0, 1):

        @pl.when(sends(side, 0))
        def _():
            line(side, 0).start()

    yield
    pick(z)
    for step in range(fi_n - 1):
        for side in (0, 1):
            block = z - 1 - step if side == 0 else z + 1 + step

            @pl.when((block >= 0) & (block < fi_n))
            def _():
                pltpu.make_async_remote_copy(
                    src_ref=held.at[block],
                    dst_ref=held.at[block],
                    send_sem=line_send.at[side, step],
                    recv_sem=line_recv.at[side, step],
                    device_id=device(own, z),
                    device_id_type=MESH_ID,
                ).wait_recv()

            if step < fi_n - 2:

                @pl.when(sends(side, step + 1))
                def _():
                    line(side, step + 1).start()

        for side in (0, 1):
            block = z - 1 - step if side == 0 else z + 1 + step

            @pl.when((block >= 0) & (block < fi_n))
            def _():
                pick(block)

        yield

    for step in range(fi_n - 1):
        for side in (0, 1):

            @pl.when(sends(side, step))
            def _():
                line(side, step).wait_send()

    def settle(index, carry):
        block, chip = index // chips, lax.rem(index, chips)

        @pl.when(at_home(block, chip))
        def _():
            keep_copy(block, chip).wait()

        @pl.when(jnp.logical_not(at_home(block, chip)))
        def _():
            plane_copy(block, chip).wait_send()

        return carry

    lax.fori_loop(0, fi_n * chips, settle, 0)

    def arrive(index, carry):
        source, at = index // z_part, lax.rem(index, z_part)

        @pl.when(source != own)
        def _():
            pltpu.make_async_remote_copy(
                src_ref=picked.at[0, 0],
                dst_ref=out_ref.at[at, y, :, columns],
                send_sem=plane_send.at[0, 0],
                recv_sem=plane_recv.at[source, at],
                device_id=device(own),
                device_id_type=MESH_ID,
            ).wait_recv()

        return carry

    lax.fori_loop(0, plane_n * z_part, arrive, 0)


def give_back_run(sizes, args, outs, scratch):
    fi_n, tpx_n, tpc_n = sizes["fi"], sizes["tpx"], sizes["tpc"]
    plane_n = sizes["ctx"] * tpx_n * tpc_n
    chips = sizes["ctx"] * tpx_n
    z_part = fi_n // tpc_n
    ends, gated = len(args) > 3, len(args) == 3
    slots_ref, rows_ref = args[:2]
    out_ref = outs[0]
    got, total, going, coming, plane_send, plane_recv, line_send, line_recv = scratch[:8]
    if gated:
        gates_ref, gate_out = args[2], outs[1]
        gates_got, gate_total, gate_going, gate_coming = scratch[8:12]
        gate_send, gate_recv, gate_line_send, gate_line_recv = scratch[12:]
    if ends:
        held = scratch[8]
        start, keep, relay, spread_settle = tp_spread(
            sizes, held, held, columns_of(out_ref, held.shape[1]), scratch[9:]
        )
    capacity, quarter = got.shape[2:]
    tokens = total.shape[0]
    z, y, x, c, own, device = plane_place(sizes)
    tile = min(256, tokens)

    def piece(target, at):
        side = lax.rem(target, tpx_n * tpc_n)
        return rows_ref.at[
            at,
            target // (tpx_n * tpc_n),
            :,
            pl.ds(pl.multiple_of(side * quarter, quarter), quarter),
        ]

    def plane_copies(target, at):
        made = [
            pltpu.make_async_remote_copy(
                src_ref=piece(target, at),
                dst_ref=got.at[c * z_part + at, own // tpc_n],
                send_sem=plane_send.at[target, at],
                recv_sem=plane_recv.at[own, at],
                device_id=device(target),
                device_id_type=MESH_ID,
            )
        ]
        if gated:
            made.append(
                pltpu.make_async_remote_copy(
                    src_ref=gates_ref.at[at, target // (tpx_n * tpc_n)],
                    dst_ref=gates_got.at[c * z_part + at, own // tpc_n],
                    send_sem=gate_send.at[target, at],
                    recv_sem=gate_recv.at[own, at],
                    device_id=device(target),
                    device_id_type=MESH_ID,
                )
            )
        return made

    def keep_copies(at):
        made = [
            pltpu.make_async_copy(
                piece(own, at), got.at[c * z_part + at, own // tpc_n], plane_recv.at[own, at]
            )
        ]
        if gated:
            made.append(
                pltpu.make_async_copy(
                    gates_ref.at[at, y],
                    gates_got.at[c * z_part + at, own // tpc_n],
                    gate_recv.at[own, at],
                )
            )
        return made

    high_first = z < fi_n // 2
    early = c == jnp.where(high_first, tpc_n - 1, 0)

    def at_turn(turn):
        far = jnp.where(high_first, z_part - 1 - turn, turn)
        return jnp.where(early, far, lax.rem(z + 1 + turn, z_part))

    def send_turn(turn):
        at = at_turn(turn)

        def one(step, carry):
            for copy in plane_copies(lax.rem(own + step, plane_n), at):
                copy.start()
            return carry

        for copy in keep_copies(at):
            copy.start()
        lax.fori_loop(1, plane_n, one, 0)

    def sent_turn(turn):
        def one(step, carry):
            for copy in plane_copies(lax.rem(own + step, plane_n), at_turn(turn)):
                copy.wait_send()
            return carry

        lax.fori_loop(1, plane_n, one, 0)

    @pl.when(early)
    def _():
        for turn in range(z_part):
            send_turn(turn)
            if turn < z_part - 1:
                sent_turn(turn)

    yield

    def gathered(block):
        def one(chip, carry):
            source, at = chip * tpc_n + block // z_part, lax.rem(block, z_part)

            @pl.when(source == own)
            def _():
                for copy in keep_copies(at):
                    copy.wait()

            @pl.when(source != own)
            def _():
                pltpu.make_async_remote_copy(
                    src_ref=got.at[block, chip],
                    dst_ref=got.at[block, chip],
                    send_sem=plane_send.at[own, at],
                    recv_sem=plane_recv.at[source, at],
                    device_id=device(own),
                    device_id_type=MESH_ID,
                ).wait_recv()
                if gated:
                    pltpu.make_async_remote_copy(
                        src_ref=gates_got.at[block, chip],
                        dst_ref=gates_got.at[block, chip],
                        send_sem=gate_send.at[own, at],
                        recv_sem=gate_recv.at[source, at],
                        device_id=device(own),
                        device_id_type=MESH_ID,
                    ).wait_recv()

            return carry

        lax.fori_loop(0, chips, one, 0)

        def rows(step, carry):
            first = pl.multiple_of(step * tile, tile)
            spots = slots_ref[block, pl.ds(first, tile), :]
            rank = lax.broadcasted_iota(jnp.int32, (tile, capacity), 1)
            summed = jnp.zeros((tile, quarter), F32)
            if gated:
                experts = gate_total.shape[0]
                gates = jnp.zeros((experts, tile), F32)
                expert = lax.broadcasted_iota(jnp.int32, (experts, capacity), 0)
            for chip in range(chips):
                hits = jnp.where(rank == spots[:, chip : chip + 1], 1.0, 0.0).astype(BF16)
                summed = summed + jnp.dot(hits, got[block, chip], preferred_element_type=F32)
                if gated:
                    left = jnp.where(
                        expert == z * chips + chip, gates_got[block, chip, 0:1, :], 0.0
                    ).astype(BF16)
                    gates = gates + dot_nt(left, hits)
            total[pl.ds(first, tile), :] = summed
            if gated:
                gate_total[:, pl.ds(first, tile)] = gates
            return carry

        lax.fori_loop(0, tokens // tile, rows, 0)

    def onward(side, target):
        if side == 0:
            return z + 1, target
        return z - 1, jnp.where(target == z - 1, fi_n, target)

    def lines(side, target, to, slot):
        made = [
            pltpu.make_async_remote_copy(
                src_ref=going.at[target],
                dst_ref=coming.at[slot],
                send_sem=line_send.at[side, target],
                recv_sem=line_recv.at[side, target],
                device_id=device(own, to),
                device_id_type=MESH_ID,
            )
        ]
        if gated:
            made.append(
                pltpu.make_async_remote_copy(
                    src_ref=gate_going.at[target],
                    dst_ref=gate_coming.at[side, target],
                    send_sem=gate_line_send.at[side, target],
                    recv_sem=gate_line_recv.at[side, target],
                    device_id=device(own, to),
                    device_id_type=MESH_ID,
                )
            )
        return made

    for step in range(fi_n - 1):
        for side in (0, 1):
            depth = z if side == 0 else fi_n - 1 - z
            target = fi_n - 1 - step + z if side == 0 else step - (fi_n - 1) + z
            passes, inner = depth <= step, depth > 0

            @pl.when(passes)
            def _():
                gathered(target)

                @pl.when(inner)
                def _():
                    for copy in lines(side, target, z, target):
                        copy.wait_recv()
                    going[target] = (total[...] + coming[target].astype(F32)).astype(BF16)
                    if gated:
                        gate_going[target] = gate_total[...] + gate_coming[side, target]

                @pl.when(jnp.logical_not(inner))
                def _():
                    going[target] = total[...].astype(BF16)
                    if gated:
                        gate_going[target] = gate_total[...]

                for copy in lines(side, target, *onward(side, target)):
                    copy.start()

        for turn in range(z_part):
            if min(turn, fi_n - 2) == step:

                @pl.when(jnp.logical_not(early))
                def _():
                    send_turn(turn)

        yield

    gathered(z)
    for side in (0, 1):

        @pl.when((z > 0) if side == 0 else (z < fi_n - 1))
        def _():
            for copy in lines(side, z, z, fi_n if side == 1 else z):
                copy.wait_recv()
            total[...] += coming[fi_n if side == 1 else z].astype(F32)
            if gated:
                gate_total[...] += gate_coming[side, z]

    if ends:
        held[...] = (total[...] + args[2][...] + args[3][...]).astype(BF16)
        start()
        keep.start()
    else:
        out_ref[...] = total[...]
    if gated:
        gate_out[...] = gate_total[...]
    yield
    if ends:
        relay()


    for target in range(fi_n):
        for side in (0, 1):

            @pl.when((z < target) if side == 0 else (z > target))
            def _():
                for copy in lines(side, target, *onward(side, target)):
                    copy.wait_send()

    for turn in range(z_part):

        @pl.when(jnp.logical_not(early) | (turn == z_part - 1))
        def _():
            sent_turn(turn)

    yield
    if ends:
        spread_settle()


def give_back_job(sizes, rows, token_slots, gates, bases=None):
    fi_n, ctx_n, tpx_n, tpc_n = (sizes[n] for n in ("fi", "ctx", "tpx", "tpc"))
    z_part, plane_n, chips = fi_n // tpc_n, ctx_n * tpx_n * tpc_n, ctx_n * tpx_n
    capacity, width = rows.shape[2:]
    quarter = width // (tpx_n * tpc_n)
    tokens = token_slots.shape[1]
    experts = fi_n * chips
    gated = gates is not None
    shapes = [jax.ShapeDtypeStruct((tokens, quarter), F32)]
    scratch = [
        pltpu.VMEM((fi_n, chips, capacity, quarter), BF16),
        pltpu.VMEM((tokens, quarter), F32),
        pltpu.VMEM((fi_n, tokens, quarter), BF16),
        pltpu.VMEM((fi_n + 1, tokens, quarter), BF16),
        pltpu.SemaphoreType.DMA((plane_n, z_part)),
        pltpu.SemaphoreType.DMA((plane_n, z_part)),
        pltpu.SemaphoreType.DMA((2, fi_n)),
        pltpu.SemaphoreType.DMA((2, fi_n)),
    ]
    args = [token_slots, rows]
    if gated:
        args.append(gates)
        shapes.append(jax.ShapeDtypeStruct((experts, tokens), F32))
        scratch += [
            pltpu.VMEM((fi_n, chips, 8, capacity), F32),
            pltpu.VMEM((experts, tokens), F32),
            pltpu.VMEM((fi_n, experts, tokens), F32),
            pltpu.VMEM((2, fi_n, experts, tokens), F32),
            pltpu.SemaphoreType.DMA((plane_n, z_part)),
            pltpu.SemaphoreType.DMA((plane_n, z_part)),
            pltpu.SemaphoreType.DMA((2, fi_n)),
            pltpu.SemaphoreType.DMA((2, fi_n)),
        ]
    specs = [VMEM_SPEC] + [HBM_SPEC] * (len(args) - 1)
    if bases is not None:
        args += list(bases)
        specs += [VMEM_SPEC] * 2
        shapes = [jax.ShapeDtypeStruct((tokens, width), BF16)]
        scratch += [pltpu.VMEM((tokens, quarter), BF16)] + tp_spread_sems(sizes)
    return {
        "args": list(zip(args, specs)),
        "outs": [(shape, HBM_SPEC if bases is not None else VMEM_SPEC) for shape in shapes],
        "scratch": scratch,
        "run": give_back_run,
    }


def collect_run(kinds, sizes, args, outs, scratch):
    fo_n, fi_n, ctx_n, tpx_n, tpc_n = (sizes[n] for n in ("fo", "fi", "ctx", "tpx", "tpc"))
    tp_n = tpx_n * tpc_n
    count = len(kinds)
    shards = args
    own_sem, line_send, line_recv, col_send, col_recv = scratch[:5]
    staged, spread_sems = scratch[5 : 5 + count * fo_n], scratch[5 + count * fo_n :]
    fo, z, y, x, c = (lax.axis_index(n) for n in ("fo", "fi", "ctx", "tpx", "tpc"))
    q = x * tpc_n + c

    items = [(i, f) for f in range(fo_n) for i in range(count)]

    def source(n):
        i, f = items[n]
        if kinds[i] == "share":
            a = shards[i].shape[1] // tp_n
            return shards[i].at[f, pl.ds(pl.multiple_of(q * a, a), a), :]
        return shards[i].at[f]

    def place(n, zb, yb):
        i, f = items[n]
        a, b = shards[i].shape[1:]
        block = (f * fi_n + zb) * ctx_n + yb
        if kinds[i] == "col":
            return outs[i].at[:, pl.ds(pl.multiple_of(block * b, b), b)]
        if kinds[i] == "share":
            return outs[i].at[block, q]
        return outs[i].at[pl.ds(pl.multiple_of(block * a, a), a), :]

    def parts_of(n):
        i, f = items[n]
        blocks = pl.ds(f * fi_n * ctx_n, fi_n * ctx_n)
        return lambda owner: outs[i].at[blocks, owner]

    spreads = {}
    for n, (i, f) in enumerate(items):
        if kinds[i] == "share":
            at = 5 * len(spreads)
            spreads[n] = tp_spread(
                sizes, parts_of(n)(q), None, parts_of(n), spread_sems[at : at + 5]
            )

    def line(n, side, step, first):
        block = z - step if side == 0 else z + step
        to = z + 1 if side == 0 else z - 1
        return pltpu.make_async_remote_copy(
            src_ref=source(n) if first else place(n, block, y),
            dst_ref=place(n, block, y),
            send_sem=line_send.at[n, side, step],
            recv_sem=line_recv.at[n, side, step],
            device_id=(fo, to, y, x, c),
            device_id_type=MESH_ID,
        )

    def sends(side, step):
        block = z - step if side == 0 else z + step
        to = z + 1 if side == 0 else z - 1
        return (block >= 0) & (block < fi_n) & (to >= 0) & (to < fi_n)

    def across(n, zb, dy, first=False):
        return pltpu.make_async_remote_copy(
            src_ref=source(n) if first else place(n, zb, y),
            dst_ref=place(n, zb, y),
            send_sem=col_send.at[n, zb, dy],
            recv_sem=col_recv.at[n, zb, dy],
            device_id=(fo, z, lax.rem(y + dy, ctx_n), x, c),
            device_id_type=MESH_ID,
        )

    def stage(n):
        return pltpu.make_async_copy(source(n), staged[n], own_sem.at[n, 0])

    def keep(n):
        return pltpu.make_async_copy(staged[n], place(n, z, y), own_sem.at[n, 1])

    for n in range(len(items)):
        for side in (0, 1):

            @pl.when(sends(side, 0))
            def _():
                line(n, side, 0, True).start()

        for dy in range(1, ctx_n):
            across(n, z, dy, True).start()
        stage(n).start()

    yield
    for n in range(len(items)):
        stage(n).wait()
        keep(n).start()

    for step in range(fi_n - 1):
        for n in range(len(items)):
            for side in (0, 1):
                block = z - 1 - step if side == 0 else z + 1 + step

                @pl.when((block >= 0) & (block < fi_n))
                def _():
                    pltpu.make_async_remote_copy(
                        src_ref=place(n, block, y),
                        dst_ref=place(n, block, y),
                        send_sem=line_send.at[n, side, step],
                        recv_sem=line_recv.at[n, side, step],
                        device_id=(fo, z, y, x, c),
                        device_id_type=MESH_ID,
                    ).wait_recv()
                    for dy in range(1, ctx_n):
                        across(n, block, dy).start()

                if step < fi_n - 2:

                    @pl.when(sends(side, step + 1))
                    def _():
                        line(n, side, step + 1, False).start()

        yield

    for n in range(len(items)):
        keep(n).wait()
        for dy in range(1, ctx_n):
            for zb in range(fi_n):
                pltpu.make_async_remote_copy(
                    src_ref=place(n, zb, y),
                    dst_ref=place(n, zb, lax.rem(y + ctx_n - dy, ctx_n)),
                    send_sem=col_send.at[n, zb, dy],
                    recv_sem=col_recv.at[n, zb, dy],
                    device_id=(fo, z, y, x, c),
                    device_id_type=MESH_ID,
                ).wait_recv()
        if n in spreads:
            spreads[n][0]()

    yield

    for n in spreads:
        spreads[n][2]()

    for n in range(len(items)):
        if n in spreads:
            spreads[n][3]()
        for side in (0, 1):
            for step in range(fi_n - 1):

                @pl.when(sends(side, step))
                def _():
                    line(n, side, step, step == 0).wait_send()

        for dy in range(1, ctx_n):
            for zb in range(fi_n):
                across(n, zb, dy).wait_send()


def collect_job(sizes, kinds, shards):
    fo_n, fi_n, ctx_n, tpx_n, tpc_n = (sizes[n] for n in ("fo", "fi", "ctx", "tpx", "tpc"))
    tp_n = tpx_n * tpc_n
    blocks = fo_n * fi_n * ctx_n
    outs, staged = [], []
    for kind, shard in zip(kinds, shards):
        _, a, b = shard.shape
        shape = (a, blocks * b) if kind == "col" else (blocks * a, b)
        if kind == "share":
            shape = (blocks, tp_n, a // tp_n, b)
        outs.append((jax.ShapeDtypeStruct(shape, shard.dtype), HBM_SPEC))
        staged.append(pltpu.VMEM((a // tp_n if kind == "share" else a, b), shard.dtype))
    n = len(kinds) * fo_n
    return {
        "args": [(shard, HBM_SPEC) for shard in shards],
        "outs": outs,
        "scratch": [
            pltpu.SemaphoreType.DMA((n, 2)),
            pltpu.SemaphoreType.DMA((n, 2, fi_n)),
            pltpu.SemaphoreType.DMA((n, 2, fi_n)),
            pltpu.SemaphoreType.DMA((n, fi_n, ctx_n)),
            pltpu.SemaphoreType.DMA((n, fi_n, ctx_n)),
        ]
        + staged * fo_n
        + tp_spread_sems(sizes) * (kinds.count("share") * fo_n),
        "run": functools.partial(collect_run, tuple(kinds)),
    }


def place_job(sizes, local):
    fo_n, fi_n, ctx_n, tpx_n, tpc_n = (sizes[n] for n in ("fo", "fi", "ctx", "tpx", "tpc"))
    chip_n = fi_n * ctx_n * tpx_n
    rows, depth = local.shape[3:]
    shape = (rows * tpx_n * tpc_n, depth * fo_n * fi_n * ctx_n)
    return {
        "args": [(local, HBM_SPEC)],
        "outs": [(jax.ShapeDtypeStruct(shape, BF16), HBM_SPEC)] * 3,
        "scratch": [pltpu.VMEM(local.shape, BF16)]
        + [pltpu.SemaphoreType.DMA((fo_n, 3, chip_n))] * 2
        + [pltpu.SemaphoreType.DMA((fo_n, 3, chip_n, tpc_n))] * 2,
        "run": place_run,
    }


def place_run(sizes, args, outs, scratch):
    fo_n, fi_n, ctx_n, tpx_n, tpc_n = (sizes[n] for n in ("fo", "fi", "ctx", "tpx", "tpc"))
    (local,) = args
    staged, load_sem, keep_sem, pair_send, pair_recv = scratch
    chip_n = fi_n * ctx_n * tpx_n
    rows, depth = local.shape[3:]
    fo, z, y, x, c = (lax.axis_index(n) for n in ("fo", "fi", "ctx", "tpx", "tpc"))

    def spot(k, f, chip, core):
        block = f * fi_n * ctx_n + chip // tpx_n
        return outs[k].at[
            pl.ds(pl.multiple_of((lax.rem(chip, tpx_n) * tpc_n + core) * rows, rows), rows),
            pl.ds(pl.multiple_of(block * depth, depth), depth),
        ]

    def load(f, k, chip):
        return pltpu.make_async_copy(
            local.at[f, chip, k], staged.at[f, chip, k], load_sem.at[f, k, chip]
        )

    def keep(f, k, chip):
        return pltpu.make_async_copy(
            staged.at[f, chip, k], spot(k, f, chip, c), keep_sem.at[f, k, chip]
        )

    def pair_copy(f, k, chip, dc, core):
        return pltpu.make_async_remote_copy(
            src_ref=local.at[f, chip, k],
            dst_ref=spot(k, f, chip, core),
            send_sem=pair_send.at[f, k, chip, dc],
            recv_sem=pair_recv.at[f, k, chip, dc],
            device_id=(fo, z, y, x, lax.rem(c + dc, tpc_n)),
            device_id_type=MESH_ID,
        )

    def launch(step, carry):
        f, chip = step // chip_n, lax.rem(step, chip_n)
        for k in range(3):
            load(f, k, chip).start()
            for dc in range(1, tpc_n):
                pair_copy(f, k, chip, dc, c).start()
        return carry

    def store(step, carry):
        f, chip = step // chip_n, lax.rem(step, chip_n)
        for k in range(3):
            load(f, k, chip).wait()
            keep(f, k, chip).start()
        return carry

    def settle(step, carry):
        f, chip = step // chip_n, lax.rem(step, chip_n)
        for k in range(3):
            keep(f, k, chip).wait()
            for dc in range(1, tpc_n):
                pair_copy(f, k, chip, dc, c).wait_send()
                pair_copy(f, k, chip, dc, lax.rem(c + tpc_n - dc, tpc_n)).wait_recv()
        return carry

    lax.fori_loop(0, fo_n * chip_n, launch, 0)
    yield
    lax.fori_loop(0, fo_n * chip_n, store, 0)
    yield
    lax.fori_loop(0, fo_n * chip_n, settle, 0)


def pair_job(sizes, grads):
    fo_n, fi_n, ctx_n, tpx_n, tpc_n = (sizes[n] for n in ("fo", "fi", "ctx", "tpx", "tpc"))
    rows = grads[0].shape[0] // (tpx_n * tpc_n)
    depth = grads[0].shape[1] // (fo_n * fi_n * ctx_n)
    total = fo_n * fi_n * ctx_n * tpx_n
    shape = (total, 3, rows, depth)
    return {
        "args": [(grad, HBM_SPEC) for grad in grads],
        "outs": [(jax.ShapeDtypeStruct(shape, BF16), HBM_SPEC)],
        "scratch": [pltpu.VMEM(shape, BF16)] * 2 + [pltpu.SemaphoreType.DMA((total, 3))] * 4,
        "run": pair_run,
    }


def pair_run(sizes, grads, outs, scratch):
    tpx_n, tpc_n = sizes["tpx"], sizes["tpc"]
    (out_ref,) = outs
    mine, theirs, load_sem, store_sem, send_sem, recv_sem = scratch
    total, _, rows, depth = mine.shape
    fo, z, y, x, c = (lax.axis_index(n) for n in ("fo", "fi", "ctx", "tpx", "tpc"))
    sibling = (fo, z, y, x, 1 - c)

    def spot(k, at, core):
        block, side = at // tpx_n, lax.rem(at, tpx_n)
        return grads[k].at[
            pl.ds(pl.multiple_of((side * tpc_n + core) * rows, rows), rows),
            pl.ds(pl.multiple_of(block * depth, depth), depth),
        ]

    def load(k, at):
        return pltpu.make_async_copy(spot(k, at, c), mine.at[at, k], load_sem.at[at, k])

    def store(k, at):
        return pltpu.make_async_copy(mine.at[at, k], out_ref.at[at, k], store_sem.at[at, k])

    def give(k, at):
        return pltpu.make_async_remote_copy(
            src_ref=spot(k, at, 1 - c),
            dst_ref=theirs.at[at, k],
            send_sem=send_sem.at[at, k],
            recv_sem=recv_sem.at[at, k],
            device_id=sibling,
            device_id_type=MESH_ID,
        )

    def launch(at, carry):
        for k in range(3):
            give(k, at).start()
            load(k, at).start()
        return carry

    def add(at, carry):
        for k in range(3):
            load(k, at).wait()
            give(k, at).wait_recv()
            mine[at, k] = (mine[at, k].astype(F32) + theirs[at, k].astype(F32)).astype(BF16)
            store(k, at).start()
        return carry

    def settle(at, carry):
        for k in range(3):
            give(k, at).wait_send()
            store(k, at).wait()
        return carry

    lax.fori_loop(0, total, launch, 0)
    yield
    lax.fori_loop(0, total, add, 0)
    yield
    lax.fori_loop(0, total, settle, 0)


def finish_run(kinds, sizes, args, outs, scratch):
    fi_n, ctx_n, tpx_n, tpc_n = (sizes[n] for n in ("fi", "ctx", "tpx", "tpc"))
    tp_n = tpx_n * tpc_n
    count = len(kinds)
    extra = len(args) - count
    parts, quarters = args[:count], args[count:]
    outs, wholes = outs[:count], outs[count:]
    mine, other, coming = (scratch[k * count : (k + 1) * count] for k in range(3))
    staged, (tiny, *sems) = scratch[3 * count : 3 * count + extra], scratch[3 * count + extra :]
    load_sem, col_send, col_recv, line_send, line_recv, tp_send, tp_recv = sems[:7]
    fo, z, y, x, c = (lax.axis_index(n) for n in ("fo", "fi", "ctx", "tpx", "tpc"))
    q = x * tpc_n + c

    spreads = [
        tp_spread(
            sizes,
            quarters[j],
            staged[j],
            columns_of(wholes[j], quarters[j].shape[1]),
            sems[8 + 5 * j : 13 + 5 * j],
        )
        for j in range(extra)
    ]

    def stage(j):
        return pltpu.make_async_copy(quarters[j], staged[j], sems[7].at[j])

    for j in range(extra):
        spreads[j][0]()
        stage(j).start()

    def view(n, zb, yb):
        a, b = mine[n].shape[1:]
        block = zb * ctx_n + yb
        if kinds[n] == "col":
            return parts[n].at[:, pl.ds(pl.multiple_of(block * b, b), b)]
        if kinds[n] == "share":
            return parts[n].at[pl.ds(pl.multiple_of(block * a * tp_n + q * a, a), a), :]
        return parts[n].at[pl.ds(pl.multiple_of(block * a, a), a), :]

    def across(n, zb, dy):
        to = lax.rem(y + dy, ctx_n)
        return pltpu.make_async_remote_copy(
            src_ref=view(n, zb, to),
            dst_ref=other[n].at[dy - 1, zb],
            send_sem=col_send.at[n, zb, dy],
            recv_sem=col_recv.at[n, zb, dy],
            device_id=(fo, z, to, x, c),
            device_id_type=MESH_ID,
        )

    def load(n, zb):
        return pltpu.make_async_copy(view(n, zb, y), mine[n].at[zb], load_sem.at[n, zb])

    def block_turn(turn):
        high_first = z < fi_n // 2
        place = jnp.where(high_first, fi_n - 1 - z, z)
        at = turn + (place <= turn).astype(jnp.int32)
        far = jnp.where(high_first, fi_n - 1 - at, at)
        return z if turn == fi_n - 1 else far

    def send_turn(turn):
        zb = block_turn(turn)
        for n in range(count):
            for dy in range(1, ctx_n):
                across(n, zb, dy).start()
            load(n, zb).start()

    def sent_turn(turn):
        for n in range(count):
            for dy in range(1, ctx_n):
                across(n, block_turn(turn), dy).wait_send()

    send_turn(0)
    yield
    send_turn(1)
    for j in range(extra):
        stage(j).wait()
        spreads[j][1].start()

    def line(n, side, target):
        at = jnp.where(target == (z + 1 if side == 0 else z - 1), fi_n, target) if side == 1 else target
        return pltpu.make_async_remote_copy(
            src_ref=mine[n].at[target],
            dst_ref=coming[n].at[at],
            send_sem=line_send.at[n, side, target],
            recv_sem=line_recv.at[n, side, target],
            device_id=(fo, z + 1 if side == 0 else z - 1, y, x, c),
            device_id_type=MESH_ID,
        )

    def came(n, side, target, at):
        pltpu.make_async_remote_copy(
            src_ref=mine[n].at[target],
            dst_ref=coming[n].at[at],
            send_sem=line_send.at[n, side, target],
            recv_sem=line_recv.at[n, side, target],
            device_id=(fo, z, y, x, c),
            device_id_type=MESH_ID,
        ).wait_recv()

    def ready(n, target):
        load(n, target).wait()
        for dy in range(1, ctx_n):
            across(n, target, dy).wait_recv()

    def add(n, target, use, store):
        a = mine[n].shape[1]
        tile = math.gcd(a, 64)

        def rows(step, carry):
            at = pl.ds(pl.multiple_of(step * tile, tile), tile)
            summed = mine[n][target, at, :].astype(F32)
            for dy in range(1, ctx_n):
                summed = summed + other[n][dy - 1, target, at, :].astype(F32)
            for slot in use:
                summed = summed + coming[n][slot, at, :].astype(F32)
            store(at, summed.astype(BF16))
            return carry

        lax.fori_loop(0, a // tile, rows, 0)

    for step in range(fi_n - 1):
        for n in range(count):
            for side in (0, 1):
                depth = z if side == 0 else fi_n - 1 - z
                target = fi_n - 1 - step + z if side == 0 else step - (fi_n - 1) + z
                passes, inner = depth <= step, depth > 0

                def back(at, values, n=n, target=target):
                    mine[n][target, at, :] = values

                @pl.when(passes & inner)
                def _():
                    ready(n, target)
                    came(n, side, target, target)
                    add(n, target, (target,), back)
                    line(n, side, target).start()

                @pl.when(passes & jnp.logical_not(inner))
                def _():
                    ready(n, target)
                    add(n, target, (), back)
                    line(n, side, target).start()

        if step + 2 < fi_n:
            sent_turn(step)
            send_turn(step + 2)
        yield

    for n in range(count):
        ready(n, z)

        def out(at, values, n=n):
            if kinds[n] == "share":
                a = mine[n].shape[1]
                outs[n][q, at, :] = values
            elif kinds[n] == "sum":
                tiny[q, at, :] = values
            else:
                outs[n][at, :] = values

        @pl.when(z > 0)
        def _():
            came(n, 0, z, z)

        @pl.when(z < fi_n - 1)
        def _():
            came(n, 1, z, fi_n)

        @pl.when((z > 0) & (z < fi_n - 1))
        def _():
            add(n, z, (z, fi_n), out)

        @pl.when((z == 0) & (z < fi_n - 1))
        def _():
            add(n, z, (fi_n,), out)

        @pl.when((z > 0) & (z == fi_n - 1))
        def _():
            add(n, z, (z,), out)

        @pl.when((z == 0) & (z == fi_n - 1))
        def _():
            add(n, z, (), out)

        if kinds[n] in ("share", "sum"):
            held = outs[n] if kinds[n] == "share" else tiny
            for step in range(1, tp_n):
                peer = lax.rem(q + step, tp_n)
                pltpu.make_async_remote_copy(
                    src_ref=held.at[q],
                    dst_ref=held.at[q],
                    send_sem=tp_send.at[n, step],
                    recv_sem=tp_recv.at[n, step],
                    device_id=(fo, z, y, peer // tpc_n, lax.rem(peer, tpc_n)),
                    device_id_type=MESH_ID,
                ).start()

    yield
    for j in range(extra):
        spreads[j][2]()

    for n in range(count):
        if kinds[n] in ("share", "sum"):
            held = outs[n] if kinds[n] == "share" else tiny
            for step in range(1, tp_n):
                origin = lax.rem(q + tp_n - step, tp_n)
                copy = pltpu.make_async_remote_copy(
                    src_ref=held.at[q],
                    dst_ref=held.at[origin],
                    send_sem=tp_send.at[n, step],
                    recv_sem=tp_recv.at[n, step],
                    device_id=(fo, z, y, x, c),
                    device_id_type=MESH_ID,
                )
                copy.wait_send()
                copy.wait_recv()
            if kinds[n] == "sum":
                summed = tiny[0].astype(F32)
                for k in range(1, tp_n):
                    summed = summed + tiny[k].astype(F32)
                outs[n][...] = summed.astype(BF16)
        for target in range(fi_n):
            for side in (0, 1):

                @pl.when((z < target) if side == 0 else (z > target))
                def _():
                    line(n, side, target).wait_send()

    for turn in range(fi_n - 2, fi_n):
        sent_turn(turn)
    for j in range(extra):
        spreads[j][3]()


def finish_job(sizes, kinds, parts, quarters):
    fi_n, ctx_n, tpx_n, tpc_n = (sizes[n] for n in ("fi", "ctx", "tpx", "tpc"))
    tp_n = tpx_n * tpc_n
    blocks = fi_n * ctx_n
    count, extra = len(kinds), len(quarters)
    own, shapes = [], []
    sum_shape = (16, 256)
    for kind, part in zip(kinds, parts):
        a, b = part.shape
        if kind == "col":
            own.append((a, b // blocks))
            shapes.append(own[-1])
        elif kind == "share":
            own.append((a // (blocks * tp_n), b))
            shapes.append((tp_n,) + own[-1])
        else:
            own.append((a // blocks, b))
            shapes.append(own[-1])
        if kind == "sum":
            sum_shape = own[-1]
    wide = [(v.shape[0], v.shape[1] * tp_n) for v in quarters]
    some = max(extra, 1)
    shapes = [jax.ShapeDtypeStruct(shape, BF16) for shape in shapes + wide]
    return {
        "args": [(arg, HBM_SPEC) for arg in (*parts, *quarters)],
        "outs": list(zip(shapes, [VMEM_SPEC] * count + [HBM_SPEC] * extra)),
        "scratch": [pltpu.VMEM((fi_n,) + s, BF16) for s in own]
        + [pltpu.VMEM((max(ctx_n - 1, 1), fi_n) + s, BF16) for s in own]
        + [pltpu.VMEM((fi_n + 1,) + s, BF16) for s in own]
        + [pltpu.VMEM(v.shape, BF16) for v in quarters]
        + [
            pltpu.VMEM((tp_n,) + sum_shape, BF16),
            pltpu.SemaphoreType.DMA((count, fi_n)),
            pltpu.SemaphoreType.DMA((count, fi_n, ctx_n)),
            pltpu.SemaphoreType.DMA((count, fi_n, ctx_n)),
            pltpu.SemaphoreType.DMA((count, 2, fi_n)),
            pltpu.SemaphoreType.DMA((count, 2, fi_n)),
            pltpu.SemaphoreType.DMA((count, tp_n)),
            pltpu.SemaphoreType.DMA((count, tp_n)),
            pltpu.SemaphoreType.DMA((some,)),
            *(tp_spread_sems(sizes) * extra),
        ],
        "run": functools.partial(finish_run, tuple(kinds)),
    }


def products_job(sizes, lefts, rights, which):
    slots, hidden = lefts[0].shape
    width = rights[0].shape[1]
    tile = min(384, hidden)
    return {
        "args": [(arg, HBM_SPEC) for arg in (*lefts, *rights)],
        "outs": [(jax.ShapeDtypeStruct((hidden, width), BF16), HBM_SPEC)] * len(lefts),
        "scratch": [
            pltpu.VMEM((2, slots, tile), BF16),
            pltpu.VMEM((tile, slots), BF16),
            pltpu.VMEM((slots, width), BF16),
            pltpu.VMEM((2, tile, width), BF16),
            pltpu.SemaphoreType.DMA((2,)),
            pltpu.SemaphoreType.DMA,
            pltpu.SemaphoreType.DMA((2,)),
        ],
        "run": functools.partial(products_run, tuple(which), tile),
    }


def products_run(which, tile, sizes, args, outs, scratch):
    left_buf, turned, right_buf, out_buf, left_sem, right_sem, out_sem = scratch
    count = len(outs)
    lefts, rights = args[:count], args[count:]
    hidden = lefts[0].shape[1]
    width = right_buf.shape[1]
    cells = [(k, at, min(tile, hidden - at)) for k in range(count) for at in range(0, hidden, tile)]

    def load(n):
        k, at, size = cells[n]
        return pltpu.make_async_copy(
            lefts[k].at[:, pl.ds(at, size)],
            left_buf.at[n % 2, :, pl.ds(0, size)],
            left_sem.at[n % 2],
        )

    def fetch(k):
        return pltpu.make_async_copy(rights[which[k]], right_buf, right_sem)

    def store(n):
        k, at, size = cells[n]
        return pltpu.make_async_copy(
            out_buf.at[n % 2, pl.ds(0, size), :],
            outs[k].at[pl.ds(at, size), :],
            out_sem.at[n % 2],
        )

    columns = min(512, width)

    def products():
        for n, (k, at, size) in enumerate(cells):
            load(n).wait()
            if n + 1 < len(cells):
                load(n + 1).start()
            if at == 0 and (k == 0 or which[k] != which[k - 1]):
                if k > 0:
                    fetch(k).start()
                fetch(k).wait()
            if n >= 2:
                store(n - 2).wait()
            turned[pl.ds(0, size), :] = left_buf[n % 2, :, :size].T

            def one(step, carry, n=n, size=size):
                here = pl.ds(pl.multiple_of(step * columns, columns), columns)
                out_buf[n % 2, pl.ds(0, size), here] = jnp.dot(
                    turned[:size, :], right_buf[:, here], preferred_element_type=F32
                ).astype(BF16)
                return carry

            lax.fori_loop(0, width // columns, one, 0)
            store(n).start()
        for n in range(max(len(cells) - 2, 0), len(cells)):
            store(n).wait()

    fi_n = sizes["fi"]
    z = lax.axis_index("fi")
    inner = (z > 0) & (z < fi_n - 1)
    fetch(0).start()
    load(0).start()
    for phase in range(1, fi_n):
        yield
        if phase == 1:
            pl.when(inner)(products)
        if phase == fi_n - 1:
            pl.when(jnp.logical_not(inner))(products)


def reduce_job(sizes, both, parts):
    ctx_n, tpx_n, tpc_n = (sizes[n] for n in ("ctx", "tpx", "tpc"))
    tp_n = tpx_n * tpc_n
    tokens, quarter = parts.shape[1:]
    wide = both.shape[1]
    piece = (ctx_n, tokens // tp_n, wide)
    return {
        "args": [(both.reshape(ctx_n, tokens, wide), HBM_SPEC), (parts, HBM_SPEC)],
        "outs": [
            (jax.ShapeDtypeStruct((tokens, wide), BF16), VMEM_SPEC),
            (jax.ShapeDtypeStruct((tokens, quarter), F32), VMEM_SPEC),
        ],
        "scratch": [
            pltpu.VMEM((3, tpx_n) + piece, BF16),
            pltpu.VMEM((3, tpx_n, tokens, quarter), BF16),
            pltpu.VMEM((ctx_n,) + piece[1:], BF16),
            pltpu.SemaphoreType.DMA((2, tpx_n)),
            pltpu.SemaphoreType.DMA((2, tpx_n)),
            pltpu.SemaphoreType.DMA((2, tpx_n)),
            pltpu.SemaphoreType.DMA((2, tpx_n)),
            pltpu.SemaphoreType.DMA((2, tpx_n)),
            pltpu.SemaphoreType.DMA((2, ctx_n)),
            pltpu.SemaphoreType.DMA((2, tp_n)),
        ],
        "run": reduce_run,
    }


def reduce_run(sizes, args, outs, scratch):
    ctx_n, tpx_n, tpc_n = (sizes[n] for n in ("ctx", "tpx", "tpc"))
    tp_n = tpx_n * tpc_n
    both_ref, parts_ref = args
    both_out, parts_out = outs
    both_buf, parts_buf, halves = scratch[:3]
    load_sem, core_send, core_recv, x_send, x_recv, y_sem, tp_sem = scratch[3:]
    rows = halves.shape[1]
    fo, z, y, x, c = (lax.axis_index(n) for n in ("fo", "fi", "ctx", "tpx", "tpc"))
    q = x * tpc_n + c
    bufs = (both_buf, parts_buf)

    def view(kind, side, core):
        to = side * tpc_n + core
        if kind == 0:
            return both_ref.at[:, pl.ds(pl.multiple_of(to * rows, rows), rows), :]
        return parts_ref.at[to]

    def load(kind, side):
        return pltpu.make_async_copy(
            view(kind, side, c), bufs[kind].at[0, side], load_sem.at[kind, side]
        )

    def to_core(kind, side):
        return pltpu.make_async_remote_copy(
            src_ref=view(kind, side, 1 - c),
            dst_ref=bufs[kind].at[1, side],
            send_sem=core_send.at[kind, side],
            recv_sem=core_recv.at[kind, side],
            device_id=(fo, z, y, x, 1 - c),
            device_id_type=MESH_ID,
        )

    def to_chip(kind, side, slot):
        return pltpu.make_async_remote_copy(
            src_ref=bufs[kind].at[0, side],
            dst_ref=bufs[kind].at[2, slot],
            send_sem=x_send.at[kind, side],
            recv_sem=x_recv.at[kind, slot],
            device_id=(fo, z, y, side, c),
            device_id_type=MESH_ID,
        )

    def side_of(dx):
        return lax.rem(x + dx, tpx_n)

    def add(kind, side):
        count = bufs[kind].shape[2] if kind == 1 else bufs[kind].shape[3]
        tile = math.gcd(count, 64)

        def one(step, carry):
            at = pl.ds(pl.multiple_of(step * tile, tile), tile)
            if kind == 1:
                mine, other = parts_buf[0, side, at, :], parts_buf[1, side, at, :]
                parts_buf[0, side, at, :] = (mine.astype(F32) + other.astype(F32)).astype(BF16)
            else:
                for half in range(ctx_n):
                    mine = both_buf[0, side, half, at, :]
                    other = both_buf[1, side, half, at, :]
                    both_buf[0, side, half, at, :] = (
                        mine.astype(F32) + other.astype(F32)
                    ).astype(BF16)
            return carry

        lax.fori_loop(0, count // tile, one, 0)

    order = list(range(1, tpx_n)) + [0]
    for kind in (0, 1):
        for dx in order:
            to_core(kind, side_of(dx)).start()
            load(kind, side_of(dx)).start()
    yield
    for kind in (0, 1):
        for dx in order:
            side = side_of(dx)
            load(kind, side).wait()
            to_core(kind, side).wait_recv()
            add(kind, side)
            if dx > 0:
                to_chip(kind, side, x).start()
    yield

    for dx in range(1, tpx_n):
        to_chip(0, side_of(dx), side_of(dx)).wait_recv()
    tile = math.gcd(rows, 64)

    def over_x(step, carry):
        at = pl.ds(pl.multiple_of(step * tile, tile), tile)
        for half in range(ctx_n):
            summed = both_buf[0, x, half, at, :].astype(F32)
            for dx in range(1, tpx_n):
                summed = summed + both_buf[2, side_of(dx), half, at, :].astype(F32)
            both_buf[0, x, half, at, :] = summed.astype(BF16)
        return carry

    lax.fori_loop(0, rows // tile, over_x, 0)

    def to_y(dy, half, slot):
        return pltpu.make_async_remote_copy(
            src_ref=both_buf.at[0, x, half],
            dst_ref=halves.at[slot],
            send_sem=y_sem.at[0, dy],
            recv_sem=y_sem.at[1, dy],
            device_id=(fo, z, half, x, c),
            device_id_type=MESH_ID,
        )

    for dy in range(1, ctx_n):
        to_y(dy, lax.rem(y + dy, ctx_n), y).start()
    yield
    for dy in range(1, ctx_n):
        source = lax.rem(y + ctx_n - dy, ctx_n)
        to_y(dy, y, source).wait_recv()

    def over_y(step, carry):
        at = pl.ds(pl.multiple_of(step * tile, tile), tile)
        summed = both_buf[0, x, y, at, :].astype(F32)
        for dy in range(1, ctx_n):
            summed = summed + halves[lax.rem(y + ctx_n - dy, ctx_n), at, :].astype(F32)
        both_out[pl.ds(pl.multiple_of(q * rows + step * tile, tile), tile), :] = summed.astype(BF16)
        return carry

    lax.fori_loop(0, rows // tile, over_y, 0)

    def to_tp(step, owner):
        peer = lax.rem(q + step, tp_n)
        held = both_out.at[pl.ds(pl.multiple_of(owner * rows, rows), rows), :]
        return pltpu.make_async_remote_copy(
            src_ref=both_out.at[pl.ds(pl.multiple_of(q * rows, rows), rows), :],
            dst_ref=held,
            send_sem=tp_sem.at[0, step],
            recv_sem=tp_sem.at[1, step],
            device_id=(fo, z, y, peer // tpc_n, lax.rem(peer, tpc_n)),
            device_id_type=MESH_ID,
        )

    for step in range(1, tp_n):
        to_tp(step, q).start()
    yield
    for dx in range(1, tpx_n):
        to_chip(1, side_of(dx), side_of(dx)).wait_recv()
    tall = math.gcd(parts_out.shape[0], 64)

    def last(step, carry):
        at = pl.ds(pl.multiple_of(step * tall, tall), tall)
        summed = parts_buf[0, x, at, :].astype(F32)
        for dx in range(1, tpx_n):
            summed = summed + parts_buf[2, side_of(dx), at, :].astype(F32)
        parts_out[at, :] = summed
        return carry

    lax.fori_loop(0, parts_out.shape[0] // tall, last, 0)
    for step in range(1, tp_n):
        to_tp(step, q).wait_send()
        to_tp(step, lax.rem(q + tp_n - step, tp_n)).wait_recv()
    for dy in range(1, ctx_n):
        to_y(dy, lax.rem(y + dy, ctx_n), y).wait_send()
    for kind in (0, 1):
        for dx in range(tpx_n):
            to_core(kind, side_of(dx)).wait_send()
            if dx > 0:
                to_chip(kind, side_of(dx), x).wait_send()


def routed_body(
    rows_ref, grads_ref, gate_ref, gate_w, up_w, down_w, dgate_ref, dup_ref, act_ref, sum_ref, drows_ref
):
    gate_pre = dot_nt(rows_ref[...], gate_w[...])
    up_pre = dot_nt(rows_ref[...], up_w[...])
    silu, slope = silu_parts(gate_pre)
    act = (silu * up_pre).astype(BF16)
    act_ref[...] = act
    dact = dot_nt(grads_ref[...], down_w[...])
    sum_ref[...] = jnp.sum(act.astype(F32) * dact, axis=1, keepdims=True)
    dact = dact * gate_ref[...]
    dgate = (dact * up_pre * slope).astype(BF16)
    dup = (dact * silu).astype(BF16)
    dgate_ref[...] = dgate
    dup_ref[...] = dup
    drows_ref[...] = (dot(dgate, gate_w[...]) + dot(dup, up_w[...])).astype(BF16)


def routed(rows, grads, gate, gate_w, up_w, down_w):
    slots, width = rows.shape
    hidden = gate_w.shape[0]
    tile = math.gcd(slots, 256)

    def tiles(columns):
        return pl.BlockSpec((tile, columns), lambda i: (i, 0))

    held = pl.BlockSpec((hidden, width), lambda i: (0, 0), pipeline_mode=pl.Buffered(1))
    wide = jax.ShapeDtypeStruct((slots, hidden), BF16)
    return pl.pallas_call(
        routed_body,
        out_shape=(
            wide,
            wide,
            wide,
            jax.ShapeDtypeStruct((slots, 1), F32),
            jax.ShapeDtypeStruct((slots, width), BF16),
        ),
        grid=(slots // tile,),
        in_specs=[tiles(width), tiles(width), tiles(1), held, held, held],
        out_specs=[tiles(hidden), tiles(hidden), tiles(hidden), tiles(1), tiles(width)],
        compiler_params=pltpu.CompilerParams(vmem_limit_bytes=48 << 20),
        cost_estimate=pl.CostEstimate(
            flops=10 * slots * width * hidden,
            bytes_accessed=50_000_000,
            transcendentals=slots * hidden,
        ),
        name="routed",
    )(rows, grads, gate, gate_w, up_w, down_w)


def attend_body(place_ref, q_ref, kv_ref, rope_ref, out_ref, log_ref):
    block_rows, key_count = q_ref.shape[0], kv_ref.shape[0]
    first = place_ref[0] + pl.program_id(1) * block_rows
    keys = jnp.concatenate([kv_ref[:, :NOPE], rope_ref[...]], axis=1)
    scores = dot_nt(q_ref[...], keys)
    row = first + lax.broadcasted_iota(jnp.int32, (block_rows, 1), 0)
    limit = jnp.maximum(row, place_ref[1] - 1)
    key = lax.broadcasted_iota(jnp.int32, (block_rows, key_count), 1)
    scores = jnp.where(key <= limit, scores, -1e30)
    top = jnp.max(scores, axis=1, keepdims=True)
    exponent = jnp.exp(scores - top)
    row_total = jnp.sum(exponent, axis=1, keepdims=True)
    summed = jnp.dot(exponent.astype(BF16), kv_ref[:, NOPE:], preferred_element_type=F32)
    out_ref[...] = (summed / row_total).astype(BF16)
    log_total = jnp.broadcast_to(top + jnp.log(row_total), (block_rows, 128))
    log_ref[0] = log_total.T[:1]

def attend(place, query, key_value, rope, block_rows):
    rows, key_count = query.shape[0], key_value.shape[0]
    heads = query.shape[1] // HEAD
    return pl.pallas_call(
        attend_body,
        out_shape=(jax.ShapeDtypeStruct((rows, heads * VDIM), BF16), jax.ShapeDtypeStruct((heads, 1, rows), F32)),
        grid_spec=pltpu.PrefetchScalarGridSpec(
            num_scalar_prefetch=1,
            grid=(heads, rows // block_rows),
            in_specs=[
                pl.BlockSpec((block_rows, HEAD), lambda h, i, s: (i, h)),
                pl.BlockSpec((key_count, HEAD), lambda h, i, s: (0, h)),
                pl.BlockSpec((key_count, NOPE), lambda h, i, s: (0, 0)),
            ],
            out_specs=[
                pl.BlockSpec((block_rows, VDIM), lambda h, i, s: (i, h)),
                pl.BlockSpec((1, 1, block_rows), lambda h, i, s: (h, 0, i)),
            ],
        ),
        compiler_params=pltpu.CompilerParams(vmem_limit_bytes=48 << 20),
        cost_estimate=pl.CostEstimate(flops=4 * rows * key_count * heads * HEAD, bytes_accessed=20_000_000, transcendentals=rows * key_count * heads),
        name="attend",
    )(place, query, key_value, rope)

def attend_back_body(place_ref, q_ref, kv_ref, rope_ref, dout_ref, log_ref, table_ref, dq_ref, dkv_ref, drope_ref, keys_acc, values_acc):
    block_rows, key_count = q_ref.shape[0], kv_ref.shape[0]
    head, step = pl.program_id(0), pl.program_id(1)
    first = place_ref[0] + step * block_rows
    keys = jnp.concatenate([kv_ref[:, :NOPE], rope_ref[...]], axis=1)
    scores = dot_nt(keys, q_ref[...])
    row = first + lax.broadcasted_iota(jnp.int32, (1, block_rows), 1)
    limit = jnp.maximum(row, place_ref[1] - 1)
    key = lax.broadcasted_iota(jnp.int32, (key_count, block_rows), 0)
    soft = jnp.exp(jnp.where(key <= limit, scores, -1e30) - log_ref[0])
    soft_grad = dot_nt(kv_ref[:, NOPE:], dout_ref[...])
    mean = jnp.sum(soft * soft_grad, axis=0, keepdims=True)
    score_grad = (soft * (soft_grad - mean)).astype(BF16)
    values = jnp.dot(soft.astype(BF16), dout_ref[...], preferred_element_type=F32)
    keys_grad = jnp.dot(score_grad, q_ref[...], preferred_element_type=F32)
    dq_ref[...] = (dot_tn(score_grad, keys) * table_ref[...]).astype(BF16)

    @pl.when(step == 0)
    def _():
        keys_acc[...] = keys_grad
        values_acc[...] = values

    @pl.when(step > 0)
    def _():
        keys_acc[...] += keys_grad
        values_acc[...] += values

    @pl.when(step == pl.num_programs(1) - 1)
    def _():
        dkv_ref[...] = jnp.concatenate([keys_acc[:, :NOPE], values_acc[...]], axis=1).astype(BF16)

        @pl.when(head == 0)
        def _():
            drope_ref[...] = keys_acc[:, NOPE:]

        @pl.when(head > 0)
        def _():
            drope_ref[...] += keys_acc[:, NOPE:]

def attend_back(place, query, key_value, rope, dout, log_total, table, block_rows):
    rows, key_count = query.shape[0], key_value.shape[0]
    heads = query.shape[1] // HEAD
    return pl.pallas_call(
        attend_back_body,
        out_shape=(jax.ShapeDtypeStruct((rows, heads * HEAD), BF16), jax.ShapeDtypeStruct((key_count, heads * HEAD), BF16), jax.ShapeDtypeStruct((key_count, NOPE), F32)),
        grid_spec=pltpu.PrefetchScalarGridSpec(
            num_scalar_prefetch=1,
            grid=(heads, rows // block_rows),
            in_specs=[
                pl.BlockSpec((block_rows, HEAD), lambda h, i, s: (i, h)),
                pl.BlockSpec((key_count, HEAD), lambda h, i, s: (0, h)),
                pl.BlockSpec((key_count, NOPE), lambda h, i, s: (0, 0)),
                pl.BlockSpec((block_rows, VDIM), lambda h, i, s: (i, h)),
                pl.BlockSpec((1, 1, block_rows), lambda h, i, s: (h, 0, i)),
                pl.BlockSpec((block_rows, HEAD), lambda h, i, s: (i, 0)),
            ],
            out_specs=[
                pl.BlockSpec((block_rows, HEAD), lambda h, i, s: (i, h)),
                pl.BlockSpec((key_count, HEAD), lambda h, i, s: (0, h)),
                pl.BlockSpec((key_count, NOPE), lambda h, i, s: (0, 0)),
            ],
            scratch_shapes=[pltpu.VMEM((key_count, HEAD), F32), pltpu.VMEM((key_count, VDIM), F32)],
        ),
        compiler_params=pltpu.CompilerParams(vmem_limit_bytes=56 << 20),
        cost_estimate=pl.CostEstimate(
            flops=10 * rows * key_count * heads * HEAD,
            bytes_accessed=40_000_000,
            transcendentals=rows * key_count * heads,
        ),
        name="attend_back",
    )(place, query, key_value, rope, dout, log_total, table)


def build(sizes):
    fo_n, fi_n, ctx_n, tpx_n, tpc_n = (sizes[name] for name in ("fo", "fi", "ctx", "tpx", "tpc"))
    tp_n = tpx_n * tpc_n
    row_shards = fo_n * fi_n * ctx_n
    plane_experts = ctx_n * tpx_n
    z_part = fi_n // tpc_n

    def expert_weights(gate, up, down):
        local = jnp.stack([gate.transpose(0, 2, 1), up.transpose(0, 2, 1), down], axis=1)
        return lax.all_gather(local, "fo", axis=0) if fo_n > 1 else local[None]

    def shard_of(weight):
        return lax.all_gather(weight, "fo", axis=0) if fo_n > 1 else weight[None]

    def fo_sum(part, kind):
        if fo_n == 1:
            return part
        if kind == "col":
            a = part.shape[0]
            part = part.reshape(a, fo_n, -1)
            return lax.psum_scatter(part, "fo", scatter_dimension=1, tiled=True).reshape(a, -1)
        return lax.psum_scatter(part, "fo", scatter_dimension=0, tiled=True)

    def own_expert_grads(mine):
        mine = mine.reshape((fo_n, -1) + mine.shape[1:])
        got = lax.all_to_all(mine, CHIPS, split_axis=1, concat_axis=1, tiled=True)
        if fo_n > 1:
            got = lax.psum_scatter(got, "fo", scatter_dimension=0, tiled=True)
        got = got[0].astype(F32)
        return (got[:, 0].transpose(0, 2, 1), got[:, 1].transpose(0, 2, 1), got[:, 2])

    def shards(
        tokens,
        out_grad,
        routes,
        slot_index,
        prefix,
        attn_gain,
        query_weight,
        latent_down,
        latent_gain,
        latent_up,
        out_weight,
        moe_gain,
        router_weight,
        shared_gate,
        shared_up,
        shared_down,
        expert_gate,
        expert_up,
        expert_down,
    ):
        row_count, width = tokens.shape
        expert_count = expert_gate.shape[0]
        capacity = row_count * routes.shape[1] // expert_count
        quarter = width // tp_n
        tp_index = lax.axis_index(TP)
        own_expert = lax.axis_index(CHIPS)
        plane_base = lax.axis_index("fi") * plane_experts

        def columns(values):
            return lax.dynamic_slice_in_dim(values, tp_index * quarter, quarter, values.ndim - 1)

        depth = latent_down.shape[0]
        down_width = latent_down.shape[1]

        def turned(weight):
            half = weight.shape[-1] // 2
            return jnp.concatenate([-weight[..., half:], weight[..., :half]], axis=-1)

        small = jnp.concatenate(
            [
                latent_down,
                turned(latent_down[:, KVR:]),
                attn_gain[:, None],
                moe_gain[:, None],
                jnp.pad(latent_gain, (0, depth - latent_gain.shape[0]))[:, None],
                router_weight,
            ],
            axis=1,
        )
        used = small.shape[1]
        small = jnp.pad(small, ((0, 0), (0, -used % 128)))
        keys = jnp.where(slot_index < capacity, routes * capacity + slot_index, -1).T
        keys = jnp.pad(keys, ((0, 8 - keys.shape[0]), (0, 0)), constant_values=-1)
        (small, query_full, up_full, out_full, keys_all), *_ = exchange(
            sizes,
            [
                collect_job(
                    sizes,
                    ("share", "row", "row", "col", "row"),
                    [shard_of(w) for w in (small, query_weight, latent_up, out_weight, keys)],
                )
            ],
            4,
            "collect_attention",
            vmem=12,
        )
        local_weights, small = lax.optimization_barrier(
            (expert_weights(expert_gate, expert_up, expert_down), small)
        )
        routed_weights = lax.all_to_all(
            local_weights, CHIPS, split_axis=1, concat_axis=1, tiled=True
        )
        small = small.reshape(row_shards * depth, -1)
        wide_down = small[:, : down_width + ROPE]
        down_full = small[:, :down_width]
        gain_at = down_width + ROPE
        gain_one = small[:, gain_at].astype(F32)
        gain_two = small[:, gain_at + 1].astype(F32)
        gain_latent = (
            small[:, gain_at + 2]
            .reshape(row_shards, depth)[:, : latent_gain.shape[0]]
            .reshape(-1)
            .astype(F32)
        )
        router_full = small[:, gain_at + 3 : used]

        keys_all = lax.dynamic_slice_in_dim(
            keys_all, lax.axis_index("fo") * (fi_n * ctx_n * 8), fi_n * ctx_n * 8, 0
        ).reshape(fi_n, ctx_n, 8, row_count)
        keys_column = lax.dynamic_index_in_dim(keys_all, lax.axis_index("ctx"), 1, keepdims=False)
        first_keys = (plane_base + jnp.arange(plane_experts, dtype=jnp.int32)) * capacity
        rel = keys_column[:, None] - first_keys[:, None, None]
        plane_slots = jnp.max(jnp.where((rel >= 0) & (rel < capacity), rel, -1), axis=2)
        token_slots = plane_slots.transpose(0, 2, 1)

        def give_back(rows, gates, bases=None):
            rows = rows.reshape(z_part, ctx_n, capacity, width)
            return give_back_job(sizes, rows, token_slots, gates, bases)

        (slot_grads,), (shared_gate_full, shared_up_full, shared_down_full) = exchange(
            sizes,
            [
                dispatch_job(sizes, columns(out_grad), plane_slots, capacity),
                collect_job(
                    sizes,
                    ("row", "row", "col"),
                    [shard_of(w) for w in (shared_gate, shared_up, shared_down)],
                ),
            ],
            0,
            "dispatch_grads",
            vmem=28,
        )
        slot_grads = slot_grads.reshape(-1, width)

        head_count = query_full.shape[1] // (NOPE + ROPE)
        hidden = tokens.astype(F32)
        scale_one = rms_scale(hidden)
        normed_one = hidden * scale_one
        normed_in = (normed_one * gain_one).astype(BF16)
        seq_index = lax.axis_index(("fo", "fi"))
        prefix_len = lax.dynamic_index_in_dim(prefix, seq_index, keepdims=False)
        row_offset = lax.axis_index("ctx") * row_count
        query_pos = row_offset + jnp.arange(row_count, dtype=jnp.int32)
        cos_table, sin_table = rotation_tables(query_pos, ROPE // 2)
        score_scale = (NOPE + ROPE) ** (-0.5)
        cos_wide = jnp.concatenate([cos_table, cos_table], axis=1)
        sin_wide = jnp.concatenate([sin_table, sin_table], axis=1)
        table = score_scale * jnp.concatenate(
            [jnp.ones((row_count, NOPE), F32), cos_wide, sin_wide], axis=1
        )

        latent_raw = dot(normed_in, wide_down)
        latent_part = latent_raw[:, :KVR]
        scale_latent = rms_scale(latent_part)
        normed_latent = latent_part * scale_latent
        latent = (normed_latent * gain_latent).astype(BF16)
        key_rope = (
            latent_raw[:, KVR : KVR + ROPE] * cos_wide + latent_raw[:, KVR + ROPE :] * sin_wide
        ).astype(BF16)
        both = lax.all_gather(
            jnp.concatenate([latent, key_rope, key_rope], axis=1), "ctx", axis=0, tiled=True
        )
        latent_all, rope_all = both[:, :KVR], both[:, KVR:]
        query_heads = query_full.reshape(width, head_count, NOPE + ROPE)
        query_wide = jnp.concatenate(
            [query_heads, turned(query_heads[..., NOPE:])], axis=-1
        ).reshape(width, head_count * HEAD)
        query_in = (
            dot(normed_in, query_wide).reshape(row_count, head_count, HEAD) * table[:, None]
        ).astype(BF16).reshape(row_count, head_count * HEAD)
        key_value = dot(latent_all, up_full).astype(BF16)
        place = jnp.stack([row_offset, prefix_len]).astype(jnp.int32)
        block_rows = min(256, row_count)
        attended, log_totals = attend(place, query_in, key_value, rope_all, block_rows)

        def tp_scatter(parts):
            parts = jnp.stack([part.astype(BF16) for part in parts])
            return lax.psum_scatter(parts, TP, scatter_dimension=0, tiled=True)[0].astype(F32)

        def quarters(weight, axis):
            return jnp.split(weight, tp_n, axis=axis)

        attn_out = tp_scatter([dot(attended, part) for part in quarters(out_full, 1)])
        attn_out, slot_grads = lax.optimization_barrier((attn_out, slot_grads))
        residual = columns(tokens).astype(F32) + attn_out
        scale_two = lax.rsqrt(
            lax.psum(jnp.sum(residual * residual, axis=-1, keepdims=True), TP) / width + EPSILON
        )
        normed_two = residual * scale_two
        gain_two_part = columns(gain_two[None])
        mid_part = (normed_two * gain_two_part).astype(BF16)

        (slot_rows,), (gate_full, expert_up_full, down_weight), (normed_mid,) = exchange(
            sizes,
            [
                dispatch_job(sizes, mid_part, plane_slots, capacity),
                place_job(sizes, routed_weights),
                spread_job(sizes, mid_part),
            ],
            1,
            "dispatch_rows",
            vmem=36,
        )
        slot_rows = slot_rows.reshape(-1, width)

        logits = dot(normed_mid, router_full)
        router_prob = jax.nn.softmax(logits, axis=-1)
        slot_prob = jax.nn.softmax(dot(slot_rows, router_full), axis=-1)
        slot_gate = lax.dynamic_slice_in_dim(slot_prob, own_expert, 1, 1)

        gate_pre = dot(normed_mid, shared_gate_full)
        up_pre = dot(normed_mid, shared_up_full)
        shared_dact = dot_nt(out_grad, shared_down_full)
        shared_silu, shared_slope = silu_parts(gate_pre)
        shared_act = (shared_silu * up_pre).astype(BF16)
        shared_dgate = (shared_dact * up_pre * shared_slope).astype(BF16)
        shared_dup = (shared_dact * shared_silu).astype(BF16)
        mid_shared = tp_scatter(
            [
                dot_nt(shared_dgate, gate_part) + dot_nt(shared_dup, up_part)
                for gate_part, up_part in zip(
                    quarters(shared_gate_full, 0), quarters(shared_up_full, 0)
                )
            ]
        )
        out_shared = tp_scatter([dot(shared_act, part) for part in quarters(shared_down_full, 1)])

        expert_dgate, expert_dup, expert_act, slot_gate_grad, slot_drows = routed(
            slot_rows, slot_grads, slot_gate, gate_full, expert_up_full, down_weight
        )
        gate_rows = jnp.broadcast_to(
            slot_gate_grad.reshape(z_part, ctx_n, 1, capacity), (z_part, ctx_n, 8, capacity)
        )
        sdown_grad = dot_tn(shared_act, out_grad)
        sgate_grad = dot_tn(normed_mid, shared_dgate)
        sup_grad = dot_tn(normed_mid, shared_dup)
        shared_kinds = ("row", "row", "col")
        shared_parts = [
            fo_sum(part.astype(BF16), kind)
            for part, kind in zip((sgate_grad, sup_grad, sdown_grad), shared_kinds)
        ]
        slot_dout = (slot_grads.astype(F32) * slot_gate).astype(BF16)
        shared_own, (mid_routed, prob_grad), expert_grads = exchange(
            sizes,
            [
                finish_job(sizes, shared_kinds, shared_parts, []),
                give_back(slot_drows.astype(BF16), gate_rows),
                products_job(
                    sizes,
                    [expert_dgate, expert_dup, expert_act],
                    [slot_rows, slot_dout],
                    [0, 0, 1],
                ),
            ],
            2,
            "give_back_rows",
            vmem=60,
        )
        sgate_grad, sup_grad, sdown_grad = (part.astype(F32) for part in shared_own)
        prob_grad = prob_grad.T
        logit_grad = (
            router_prob * (prob_grad - jnp.sum(router_prob * prob_grad, axis=-1, keepdims=True))
        ).astype(BF16)

        mid_routed, mid_shared, out_shared = lax.optimization_barrier(
            (mid_routed, mid_shared, out_shared)
        )
        mid_total = mid_shared + mid_routed + dot_nt(logit_grad, columns(router_full.T).T)
        gain_two_grad = jnp.sum(mid_total * normed_two, axis=0)
        dn_two = mid_total * gain_two_part
        dot_two = lax.psum(jnp.sum(dn_two * normed_two, axis=-1, keepdims=True), TP) / width
        residual_grad = columns(out_grad).astype(F32) + scale_two * (dn_two - normed_two * dot_two)
        (routed_grads,), (attn_dout,) = exchange(
            sizes,
            [pair_job(sizes, expert_grads), spread_job(sizes, residual_grad.astype(BF16))],
            7,
            "pair_sum",
            vmem=32,
        )

        out_weight_grad = dot_tn(attended, attn_dout)
        attended_grad = dot_nt(attn_dout, out_full).astype(BF16)
        attended_grad, routed_grads = lax.optimization_barrier((attended_grad, routed_grads))
        egate_grad, eup_grad, edown_grad = own_expert_grads(routed_grads)
        query_grad, kv_grad, rope_grad = attend_back(
            place, query_in, key_value, rope_all, attended_grad, log_totals, table,
            min(512, row_count),
        )
        late_act, query_grad = lax.optimization_barrier((expert_act, query_grad))
        expert_out = (dot(late_act, down_weight) * slot_gate).astype(BF16)
        up_grad = dot_tn(latent_all, kv_grad)
        latent_grad = dot_nt(kv_grad, up_full)
        query_wide_grad = dot_tn(normed_in, query_grad).reshape(width, head_count, HEAD)
        query_weight_grad = jnp.concatenate(
            [
                query_wide_grad[..., :NOPE],
                query_wide_grad[..., NOPE : NOPE + ROPE] - turned(query_wide_grad[..., NOPE + ROPE :]),
            ],
            axis=-1,
        ).reshape(width, head_count * (NOPE + ROPE))
        input_parts = jnp.stack(
            [dot_nt(query_grad, part).astype(BF16) for part in quarters(query_wide, 0)]
        )
        ((both_grad, input_part),) = exchange(
            sizes,
            [
                reduce_job(
                    sizes,
                    jnp.concatenate([latent_grad, rope_grad], axis=1).astype(BF16),
                    input_parts,
                )
            ],
            6,
            "sum_inputs",
            vmem=28,
        )
        both_grad = both_grad.astype(F32)
        latent_own = both_grad[:, :KVR]
        rope_own = both_grad[:, KVR : KVR + ROPE] + both_grad[:, KVR + ROPE :]
        gain_latent_grad = jnp.sum(latent_own * normed_latent, axis=0)
        latent_raw_grad = norm_back(latent_own * gain_latent, normed_latent, scale_latent)
        down_out_grad = jnp.concatenate(
            [latent_raw_grad, rotate(rope_own, cos_table, -sin_table)], axis=-1
        ).astype(BF16)
        down_grad = dot_tn(normed_in, down_out_grad)
        input_total = input_part + dot_nt(
            down_out_grad, lax.dynamic_slice_in_dim(down_full, tp_index * quarter, quarter, 0)
        )
        normed_one_part = columns(normed_one)
        gain_one_grad = jnp.sum(input_total * normed_one_part, axis=0)
        dn_one = input_total * columns(gain_one[None])
        dot_one = lax.psum(jnp.sum(dn_one * normed_one_part, axis=-1, keepdims=True), TP) / width
        token_grad = residual_grad + scale_one * (dn_one - normed_one_part * dot_one)
        token_grad, egate_grad, eup_grad, edown_grad = lax.optimization_barrier(
            (token_grad, egate_grad, eup_grad, edown_grad)
        )
        router_grad = dot_tn(normed_mid, logit_grad)
        pack_grad = jnp.concatenate([down_grad, router_grad], axis=1)
        pack_used = pack_grad.shape[1]
        pack_grad = jnp.pad(pack_grad, ((0, 0), (0, -pack_used % 128)))
        gains = jnp.stack([gain_one_grad, gain_two_grad])
        gains = lax.dynamic_update_slice_in_dim(
            jnp.zeros((2, width), F32), gains, tp_index * quarter, 1
        )
        latent_rows = jnp.pad(
            gain_latent_grad.reshape(row_shards, -1),
            ((0, 0), (0, depth - latent_gain.shape[0])),
        ).reshape(1, width)
        gains = jnp.concatenate([gains, latent_rows * (tp_index == 0).astype(F32)], axis=0)
        gains = jnp.pad(
            gains.reshape(3, row_shards, depth).transpose(1, 0, 2), ((0, 0), (0, 13), (0, 0))
        ).reshape(row_shards * 16, depth)
        kinds = ("share", "sum", "row", "row", "col")
        partials = (pack_grad, gains, query_weight_grad, up_grad, out_weight_grad)
        (output,), done = exchange(
            sizes,
            [
                give_back(expert_out, None, (residual, out_shared)),
                finish_job(
                    sizes,
                    kinds,
                    [fo_sum(part.astype(BF16), kind) for part, kind in zip(partials, kinds)],
                    [token_grad.astype(BF16)],
                ),
            ],
            3,
            "finish_attention",
            vmem=50,
        )
        pack_own = done[0].reshape(depth, -1).astype(F32)
        gains_own = done[1].astype(F32)
        query_weight_grad, up_grad, out_weight_grad = (part.astype(F32) for part in done[2:5])
        token_grad = done[5].astype(F32)
        return (
            output,
            token_grad,
            gains_own[0],
            query_weight_grad,
            pack_own[:, :down_width],
            gains_own[2, : latent_gain.shape[0]],
            up_grad,
            out_weight_grad,
            gains_own[1],
            pack_own[:, down_width:pack_used],
            sgate_grad,
            sup_grad,
            sdown_grad,
            egate_grad,
            eup_grad,
            edown_grad,
        )

    return shards


EXPERTS = 16


def solution(mesh):
    ctx_n, tp_n = mesh.shape["ctx"], mesh.shape["tp"]
    tpc_n = 2
    tpx_n = tp_n // tpc_n
    fi_n = EXPERTS // (ctx_n * tpx_n)
    sizes = {
        "fo": mesh.shape["fsdp"] // fi_n,
        "fi": fi_n,
        "ctx": ctx_n,
        "tpx": tpx_n,
        "tpc": tpc_n,
    }
    fine = Mesh(mesh.devices.reshape(tuple(sizes.values())), tuple(sizes))
    rows = P(ROWS)
    rows_two = P(ROWS, None)
    rows_tp = P(ROWS, TP)
    tp_rows = P(TP, ROWS)
    wide_in = P(None, ROWS, TP)
    wide_out = P(None, TP, ROWS)
    weights = (
        rows,
        rows_tp,
        rows_two,
        rows,
        rows_tp,
        tp_rows,
        rows,
        rows_two,
        rows_tp,
        rows_tp,
        tp_rows,
        wide_in,
        wide_in,
        wide_out,
    )
    return jax.shard_map(
        build(sizes),
        mesh=fine,
        in_specs=(rows_two, rows_two, rows_two, rows_two, P()) + weights,
        out_specs=(rows_two, rows_two) + weights,
        check_vma=False,
    )
```
